128 devices in a mesh: seq: 64 (over x, y_lo, z, core), expert: 2 (over y_hi).
Axes of the slice: x: 4, y: 4 (y_hi: 2, y_lo: 2; y = y_hi * 2 + y_lo), z: 4, core: 2. Of those that a mesh axis runs over, the one named last changes fastest.
Arguments:
- tokens: bfloat16 [8192, 2048], P('seq'), may hold values from -6 to 6
- attn_gain: bfloat16 [2048], P(('seq', 'expert')), may hold values from 0.5 to 1.5
- kv_weight: bfloat16 [2048, 4096], P(('seq', 'expert')), may hold values from -0.125 to 0.125
- attn_router: bfloat16 [2048, 8], P(('seq', 'expert')), may hold values from -0.09375 to 0.09375
- query_weight: bfloat16 [2048, 16384], P(None, ('seq', 'expert')), may hold values from -0.125 to 0.125
- output_weight: bfloat16 [16384, 2048], P(('seq', 'expert')), may hold values from -1.5 to 1.5
- mlp_gain: bfloat16 [2048], P(('seq', 'expert')), may hold values from 0.5 to 1.5
- mlp_router: bfloat16 [2048, 8], P(('seq', 'expert')), may hold values from -0.09375 to 0.09375
- gate_weight: bfloat16 [2048, 45056], P(None, ('seq', 'expert')), may hold values from -0.125 to 0.125
- up_weight: bfloat16 [2048, 45056], P(None, ('seq', 'expert')), may hold values from -0.125 to 0.125
- down_weight: bfloat16 [45056, 2048], P(('seq', 'expert')), may hold values from -0.15625 to 0.15625
- attn_experts: int32 [8192, 2], P('seq'), may hold values from 0 to 7, all different within a row; in each aligned block of 64 rows (0 to 63, 64 to 127, ...) at most 18 rows name the same one
- mlp_experts: int32 [8192, 2], P('seq'), may hold values from 0 to 7, all different within a row
- priority: int32 [64, 128], P('seq'), may hold values from 0 to 127, each once within a row
- cotangent: bfloat16 [8192, 2048], P('seq'), may hold values from -6 to 6
Outputs:
- mixed: bfloat16 [8192, 2048], P('seq')
- tokens_grad: bfloat16 [8192, 2048], P('seq')
- attn_gain_grad: float32 [2048], P(('seq', 'expert'))
- kv_grad: float32 [2048, 4096], P(('seq', 'expert'))
- attn_router_grad: float32 [2048, 8], P(('seq', 'expert'))
- query_grad: float32 [2048, 16384], P(None, ('seq', 'expert'))
- output_grad: float32 [16384, 2048], P(('seq', 'expert'))
- mlp_gain_grad: float32 [2048], P(('seq', 'expert'))
- mlp_router_grad: float32 [2048, 8], P(('seq', 'expert'))
- gate_grad: float32 [2048, 45056], P(None, ('seq', 'expert'))
- up_grad: float32 [2048, 45056], P(None, ('seq', 'expert'))
- down_grad: float32 [45056, 2048], P(('seq', 'expert'))
The draws below stay inside these ranges and needn't reach their ends.
Inputs may be any that keep to these rules, and one draw needn't show every extreme that they name: `attn_experts`: each row names 2 different experts; in each aligned block of 64 rows no expert is named by more than 18 rows, and in some block one is named by exactly 18. `mlp_experts`: each row names 2 different experts. `priority`: each row holds every value of 0 to 127 once.
All inputs are finite; a program needn't handle non-finite values.
Results may differ from the reference program's by a relative error of at most 0.019.
Values may be sent and summed in bfloat16 or wider, within the bound.
No kernel may reach another device: no remote copies, remote signals or barrier semaphores. Data moves between devices by JAX's collectives and lax.ppermute only.
A program may use at most 320 MiB of HBM per device.

```python
import math
import jax
import jax.numpy as jnp
import numpy as np
from jax import lax

D = 2048
KV_HEADS = 16
HEAD = 128
EXPERTS = 8
TOPK = 2
FF = 5632
TOK_DEV = 128
BLOCK = 256
TOKENS = 8192
SEQ_LEN = 1024
SEQS = 8
ROWS_OWN = 64
CAP = 18


def block_scale(rng, extent, cuts, low, top_value):
    gain = 1.0
    for dim, shards_of in cuts:
        heights = jax.random.uniform(jax.random.fold_in(jax.random.fold_in(rng, 6), dim), (shards_of,), jnp.float32, low / len(cuts), top_value / len(cuts))
        gain = gain * jnp.repeat(jnp.exp(heights), extent[dim] // shards_of).reshape((-1,) + (1,) * (len(extent) - 1 - dim))
    return gain


def different_ones(rng, rows, count, top, lift):
    ranking = jax.random.permutation(jax.random.fold_in(rng, 1), count)
    pull = ranking
    for power in range(3):
        pull = pull * pull // count
    pull = pull * lift // count
    chance = jax.random.randint(jax.random.fold_in(rng, 2), (rows, count), 0, 4096) + pull
    sure = jax.random.permutation(jax.random.fold_in(rng, 3), rows)[jnp.arange(count) % rows]
    chance = jnp.where(jnp.arange(rows)[:, None] == sure[None, :], 1 << 14, chance)
    score = chance * count + jnp.arange(count)
    return lax.top_k(score.astype(jnp.int32), top)[1].astype(jnp.int32)


def routed_block(own_key, own, number, rows, count, top, reach, lean):
    order = jax.random.permutation(own_key, count)
    packed, common = portions_of(count, rows * top, reach, lean, True), portions_of(count, rows * top, reach, lean, False)
    places = jnp.arange(count)

    def named(tallies, turn):
        used = int((tallies > 0).sum())
        fixed = max(1, used // 4)
        moved = fixed + (places - fixed + turn * (used - fixed)) % max(1, count - fixed)
        return jnp.zeros((count,), jnp.int32).at[order[jnp.where(places < fixed, places, moved)]].set(jnp.asarray(tallies, jnp.int32))

    tallies = jnp.where(number % 4 == 0, named(packed, number // 4), named(common, number - number // 4 - 1))
    mixed = jax.random.permutation(jax.random.fold_in(own, 3), count)
    donor, sink = mixed[0:count // 2 * 2:2], mixed[1:count // 2 * 2:2]
    slack = jnp.minimum(tallies[donor] - 1, reach - tallies[sink]) // 2
    slack = jnp.where((donor == order[0]) | (sink == order[0]) | (tallies[sink] == 0), 0, jnp.maximum(slack, 0))
    moved = jax.random.randint(jax.random.fold_in(own, 4), (count // 2,), 0, 1 << 20) % (slack + 1)
    tallies = tallies.at[donor].add(-moved).at[sink].add(moved)
    members = jnp.searchsorted(jnp.cumsum(tallies), jnp.arange(rows * top), side="right").astype(jnp.int32)
    grid = members.reshape(top, rows).T
    grid = grid[jax.random.permutation(jax.random.fold_in(own, 1), rows)]
    turn = jax.random.randint(jax.random.fold_in(own, 2), (rows, 1), 0, top)
    return jnp.take_along_axis(grid, (jnp.arange(top)[None, :] + turn) % top, axis=1)


def portions_of(amount, total, reach, slope, full):
    portions = [(1 << 20) // math.isqrt(rank ** slope) + 1 for rank in range(1, amount + 1)]
    largest = reach if full else min(reach, max(-(-total // amount), total * portions[0] // sum(portions)))
    least = 1 if total - largest >= amount - 1 else 0
    holding, surplus = [largest] + [least] * (amount - 1), total - largest - least * (amount - 1)
    while surplus > 0:
        free = [i for i in range(1, amount) if holding[i] < largest] or [i for i in range(1, amount) if holding[i] < reach]
        whole, left = sum([portions[i] for i in free]), surplus
        for i in free:
            more = min(reach - holding[i], max(1, left * portions[i] // whole), surplus)
            holding[i] = holding[i] + more
            surplus = surplus - more
    return np.array(holding)


def normal_values(key, extent, scale, most, shards=(), kind=jnp.bfloat16):
    entries = jax.random.normal(key, extent, jnp.float32) * scale
    if len(shards) > 0:
        entries = block_scale(key, extent, shards, -0.22, 0.18) * entries
    return jnp.clip(entries, min=-most, max=most).astype(kind)


def setup_inputs(seed: int = 0) -> dict:
    key_of = jax.random.split(jax.random.key(seed), 16)
    tokens = normal_values(key_of[0], (TOKENS, D), 1.0, 6.0, ((0, 64),))
    attn_gain = jnp.clip(1.0 + 0.1 * jax.random.normal(key_of[1], (D,), jnp.float32), 0.5, 1.5).astype(jnp.bfloat16)
    kv_weight = normal_values(key_of[2], (D, 2 * KV_HEADS * HEAD), D ** -0.5, 0.125, ((0, 128),))
    attn_router = normal_values(key_of[3], (D, EXPERTS), (2 * D) ** -0.5, 0.09375, ((0, 128),))
    query_weight = normal_values(key_of[4], (D, EXPERTS * KV_HEADS * HEAD), D ** -0.5, 0.125, ((1, 128),))
    output_weight = normal_values(key_of[5], (EXPERTS * KV_HEADS * HEAD, D), (KV_HEADS * HEAD * 8 // SEQ_LEN) ** -0.5, 1.5, ((0, 128),))
    mlp_gain = jnp.clip(1.0 + 0.1 * jax.random.normal(key_of[6], (D,), jnp.float32), 0.5, 1.5).astype(jnp.bfloat16)
    mlp_router = normal_values(key_of[7], (D, EXPERTS), (2 * D) ** -0.5, 0.09375, ((0, 128),))
    gate_weight = normal_values(key_of[8], (D, EXPERTS * FF), D ** -0.5, 0.125, ((1, 128),))
    up_weight = normal_values(key_of[9], (D, EXPERTS * FF), D ** -0.5, 0.125, ((1, 128),))
    down_weight = normal_values(key_of[10], (EXPERTS * FF, D), (FF // 4) ** -0.5, 0.15625, ((0, 128),))
    attn_experts_keys = jax.random.split(jax.random.fold_in(key_of[11], 1), TOKENS // ROWS_OWN)
    attn_experts_turns = jax.random.permutation(jax.random.fold_in(key_of[11], 3), TOKENS // ROWS_OWN)
    attn_experts = jax.vmap(lambda own, number: routed_block(jax.random.fold_in(key_of[11], 2), own, number, ROWS_OWN, EXPERTS, TOPK, CAP, 2))(attn_experts_keys, attn_experts_turns).reshape((TOKENS, TOPK))
    mlp_experts = different_ones(key_of[12], TOKENS, EXPERTS, TOPK, 4096)
    priority = jax.vmap(lambda own: jax.random.permutation(own, TOK_DEV))(jax.random.split(key_of[13], (TOKENS // TOK_DEV))).reshape((TOKENS // TOK_DEV, TOK_DEV)).astype(jnp.int32)
    cotangent = normal_values(key_of[14], (TOKENS, D), 1.0, 6.0, ((0, 64),))
    return dict(tokens=tokens, attn_gain=attn_gain, kv_weight=kv_weight, attn_router=attn_router, query_weight=query_weight, output_weight=output_weight, mlp_gain=mlp_gain, mlp_router=mlp_router, gate_weight=gate_weight, up_weight=up_weight, down_weight=down_weight, attn_experts=attn_experts, mlp_experts=mlp_experts, priority=priority, cotangent=cotangent)


epsilon = 1e-06
masked_score = -1e+30
HIGHEST = lax.Precision.HIGHEST

@jax.custom_vjp
def low(v):
    return lax.optimization_barrier(v.astype(jnp.bfloat16)).astype(jnp.float32)

@jax.custom_vjp
def low_back(v):
    return v

def low_keep(v):
    return (low(v), None)

def low_pass(kept, grad):
    return (grad,)

def back_keep(v):
    return (v, None)

def back_low(kept, grad):
    return (low(grad),)
low.defvjp(low_keep, low_pass)
low_back.defvjp(back_keep, back_low)

def product(left, right):
    return jnp.dot(left, right, precision=HIGHEST, preferred_element_type=jnp.float32)

def rope_tables(positions, head_size):
    half_size = head_size // 2
    frequency = jnp.exp(jnp.arange(half_size, dtype=jnp.float32) * (-2.0 * math.log(10000.0) / head_size))
    angles = positions.astype(jnp.float32)[:, None] * frequency[None, :]
    return (jnp.cos(angles)[:, None, :], jnp.sin(angles)[:, None, :])

def rotate(values, cosines, sines):
    half_size = values.shape[-1] // 2
    first = values[..., :half_size]
    second = values[..., half_size:]
    return jnp.concatenate([first * cosines - second * sines, second * cosines + first * sines], axis=-1)

def slot_table(expert_ids, ranks, slot_cap):
    block_rows = expert_ids.shape[0]
    expert_range = jnp.arange(EXPERTS, dtype=jnp.int32)
    member = lax.optimization_barrier(jnp.sum((expert_ids[:, :, None] == expert_range[None, None, :]).astype(jnp.int32), axis=1))
    earlier = (ranks[:, None] < ranks[None, :]).astype(jnp.int32)
    places = lax.optimization_barrier(jnp.sum(earlier[:, :, None] * member[:, None, :], axis=0))
    kept = member * (places < slot_cap).astype(jnp.int32)
    slot_range = jnp.arange(slot_cap, dtype=jnp.int32)
    landing = kept[:, :, None] * (places[:, :, None] == slot_range[None, None, :]).astype(jnp.int32)
    row_range = jnp.arange(block_rows, dtype=jnp.int32)
    slot_token = lax.optimization_barrier(jnp.sum(landing * row_range[:, None, None], axis=0))
    slot_valid = lax.optimization_barrier(jnp.sum(landing, axis=0))
    return (places, kept, slot_token, slot_valid)

def attend(inputs):
    query_part, key_part, value_part, block_part = inputs
    scores = low_back(jnp.einsum('rhd,khd->hrk', query_part, key_part, precision=HIGHEST) * (1.0 / math.sqrt(HEAD)))
    key_blocks = jnp.arange(SEQ_LEN, dtype=jnp.int32) // BLOCK
    allowed = key_blocks[None, :] <= block_part[:, None]
    scores = jnp.where(allowed[None], scores, masked_score)
    probs = jax.nn.softmax(scores, axis=-1)
    mixed_part = jnp.einsum('hrk,khd->rhd', low(probs), value_part, precision=HIGHEST)
    return low(low_back(mixed_part))

def reference(tokens, attn_gain, kv_weight, attn_router, query_weight, output_weight, mlp_gain, mlp_router, gate_weight, up_weight, down_weight, attn_experts, mlp_experts, priority, cotangent):
    block_count = TOKENS // ROWS_OWN
    key_cols = KV_HEADS * HEAD
    token_order = jnp.arange(ROWS_OWN, dtype=jnp.int32)
    block_range = jnp.arange(block_count, dtype=jnp.int32)
    attn_blocks = attn_experts.reshape(block_count, ROWS_OWN, TOPK)
    mlp_blocks = mlp_experts.reshape(block_count, ROWS_OWN, TOPK)
    rank_blocks = priority.reshape(block_count, ROWS_OWN)
    attn_tables = jax.vmap(lambda block_ids: slot_table(block_ids, token_order, CAP))(attn_blocks)
    mlp_tables = jax.vmap(lambda block_ids, block_rank: slot_table(block_ids, block_rank, CAP))(mlp_blocks, rank_blocks)

    def combine(slot_out, expert_blocks, tables, logits):
        flat = jnp.moveaxis(slot_out.reshape(EXPERTS, block_count, CAP, D), 0, 1).reshape(block_count, EXPERTS * CAP, D)
        chosen_place = jnp.take_along_axis(tables[0], expert_blocks, axis=2)
        chosen_kept = jnp.take_along_axis(tables[1], expert_blocks, axis=2).astype(jnp.float32)
        index = expert_blocks * CAP + jnp.minimum(chosen_place, CAP - 1)
        picked = flat[block_range[:, None, None], index]
        gates = jax.nn.softmax(jnp.take_along_axis(logits, expert_blocks.reshape(TOKENS, TOPK), axis=1), axis=-1)
        weights = gates.reshape(block_count, ROWS_OWN, TOPK) * chosen_kept
        return lax.optimization_barrier(jnp.sum(picked * weights[..., None], axis=2)).reshape(TOKENS, D)

    def forward(input_f, gain_a, kv_w, router_a, query_w, output_w, gain_m, router_m, gate_w, up_w, down_w):
        inverse_one = lax.rsqrt(lax.optimization_barrier(jnp.mean(input_f * input_f, axis=-1, keepdims=True)) + epsilon)
        attn_input = low(input_f * inverse_one * gain_a)
        attn_logits = product(attn_input, router_a)
        key_value = low_back(product(attn_input, kv_w))
        positions = jnp.arange(TOKENS, dtype=jnp.int32) % SEQ_LEN
        cosines, sines = rope_tables(positions, HEAD)
        keys = low(rotate(key_value[:, :key_cols].reshape(TOKENS, KV_HEADS, HEAD), cosines, sines))
        values = low(key_value[:, key_cols:]).reshape(TOKENS, KV_HEADS, HEAD)
        seq_keys = keys.reshape(SEQS, SEQ_LEN, KV_HEADS, HEAD)
        seq_values = values.reshape(SEQS, SEQ_LEN, KV_HEADS, HEAD)
        attn_values = attn_input.reshape(block_count, ROWS_OWN, D)

        def attn_expert(inputs):
            query_e, output_e, token_e, valid_e = inputs
            slot_rows = jnp.where(valid_e[:, :, None] > 0, attn_values[block_range[:, None], token_e], 0.0).reshape(-1, D)
            queries = low_back(product(slot_rows, query_e))
            slot_positions = ((block_range[:, None] * ROWS_OWN + token_e) % SEQ_LEN).reshape(-1)
            slot_cos, slot_sin = rope_tables(slot_positions, HEAD)
            rotated = low(rotate(queries.reshape(-1, KV_HEADS, HEAD), slot_cos, slot_sin))
            seq_queries = rotated.reshape(SEQS, -1, KV_HEADS, HEAD)
            query_blocks = (slot_positions // BLOCK).reshape(SEQS, -1)
            mixed_rows = lax.map(jax.checkpoint(attend), (seq_queries, seq_keys, seq_values, query_blocks))
            return low_back(product(mixed_rows.reshape(-1, key_cols), output_e))
        query_stack = jnp.moveaxis(query_w.reshape(D, EXPERTS, key_cols), 1, 0)
        output_stack = output_w.reshape(EXPERTS, key_cols, D)
        attn_slots = lax.map(jax.checkpoint(attn_expert), (query_stack, output_stack, jnp.moveaxis(attn_tables[2], 1, 0), jnp.moveaxis(attn_tables[3], 1, 0)))
        hidden_state = input_f + combine(attn_slots, attn_blocks, attn_tables, attn_logits)
        inverse_two = lax.rsqrt(lax.optimization_barrier(jnp.mean(hidden_state * hidden_state, axis=-1, keepdims=True)) + epsilon)
        mlp_input = low(hidden_state * inverse_two * gain_m)
        mlp_logits = product(mlp_input, router_m)
        mlp_values = mlp_input.reshape(block_count, ROWS_OWN, D)

        def mlp_expert(inputs):
            gate_e, up_e, down_e, token_e, valid_e = inputs
            slot_rows = jnp.where(valid_e[:, :, None] > 0, mlp_values[block_range[:, None], token_e], 0.0).reshape(-1, D)
            gate_pre = low_back(product(slot_rows, gate_e))
            up_pre = low_back(product(slot_rows, up_e))
            inner_rows = low(jax.nn.silu(gate_pre) * up_pre)
            return low_back(product(inner_rows, down_e))
        gate_stack = jnp.moveaxis(gate_w.reshape(D, EXPERTS, FF), 1, 0)
        up_stack = jnp.moveaxis(up_w.reshape(D, EXPERTS, FF), 1, 0)
        down_stack = down_w.reshape(EXPERTS, FF, D)
        mlp_slots = lax.map(jax.checkpoint(mlp_expert), (gate_stack, up_stack, down_stack, jnp.moveaxis(mlp_tables[2], 1, 0), jnp.moveaxis(mlp_tables[3], 1, 0)))
        return hidden_state + combine(mlp_slots, mlp_blocks, mlp_tables, mlp_logits)
    floats = tuple((value.astype(jnp.float32) for value in (tokens, attn_gain, kv_weight, attn_router, query_weight, output_weight, mlp_gain, mlp_router, gate_weight, up_weight, down_weight)))
    result, pullback = jax.vjp(forward, *floats)
    grads = pullback(cotangent.astype(jnp.float32))
    return (result.astype(jnp.bfloat16), grads[0].astype(jnp.bfloat16), grads[1], grads[2], grads[3], grads[4], grads[5], grads[6], grads[7], grads[8], grads[9], grads[10])
```

```python
import math

import jax
import jax.numpy as jnp
from jax import lax
from jax.sharding import PartitionSpec as P

KV_HEADS = 16
HEAD = 128
EXPERTS = 8
TOPK = 2
PIECES = 8
BLOCK = 256


epsilon = 1e-06
masked_score = -1e30


def rope_tables(positions, head_size):
    half_size = head_size // 2
    frequency = jnp.exp(
        jnp.arange(half_size, dtype=jnp.float32) * (-2.0 * math.log(10000.0) / head_size)
    )
    angles = positions.astype(jnp.float32)[:, None] * frequency[None, :]
    return (jnp.cos(angles)[:, None, :], jnp.sin(angles)[:, None, :])


def rotate(values, cosines, sines):
    half_size = values.shape[-1] // 2
    first = values[..., :half_size]
    second = values[..., half_size:]
    return jnp.concatenate(
        [first * cosines - second * sines, second * cosines + first * sines], axis=-1
    )


def rotate_back(grads, cosines, sines):
    half_size = grads.shape[-1] // 2
    first = grads[..., :half_size]
    second = grads[..., half_size:]
    return jnp.concatenate(
        [first * cosines + second * sines, second * cosines - first * sines], axis=-1
    )


def slot_table(expert_ids, ranks, slot_cap):
    block_rows = expert_ids.shape[0]
    expert_range = jnp.arange(EXPERTS, dtype=jnp.int32)
    member = jnp.sum(
        (expert_ids[:, :, None] == expert_range[None, None, :]).astype(jnp.int32), axis=1
    )
    earlier = (ranks[:, None] < ranks[None, :]).astype(jnp.int32)
    places = jnp.sum(earlier[:, :, None] * member[:, None, :], axis=0)
    kept = member * (places < slot_cap).astype(jnp.int32)
    slot_range = jnp.arange(slot_cap, dtype=jnp.int32)
    landing = kept[:, :, None] * (places[:, :, None] == slot_range[None, None, :]).astype(jnp.int32)
    row_range = jnp.arange(block_rows, dtype=jnp.int32)
    slot_token = jnp.sum(landing * row_range[:, None, None], axis=0)
    slot_valid = jnp.sum(landing, axis=0)
    return (places, kept, slot_token, slot_valid)


def pair_index(expert_ids, places, kept, slot_cap):
    chosen_place = jnp.take_along_axis(places, expert_ids, axis=1)
    chosen_kept = jnp.take_along_axis(kept, expert_ids, axis=1)
    return (
        expert_ids * slot_cap + jnp.minimum(chosen_place, slot_cap - 1),
        chosen_kept.astype(jnp.float32),
    )


def pair_gates(logits, expert_ids):
    return jax.nn.softmax(jnp.take_along_axis(logits, expert_ids, axis=1), axis=-1)


def expert_onehot(expert_ids):
    expert_range = jnp.arange(EXPERTS, dtype=jnp.int32)
    return (expert_ids[:, :, None] == expert_range[None, None, :]).astype(jnp.float32)


def gates_back(gates, gate_grads, expert_ids):
    inner = jnp.sum(gates * gate_grads, axis=1, keepdims=True)
    chosen_grads = gates * (gate_grads - inner)
    return jnp.sum(chosen_grads[:, :, None] * expert_onehot(expert_ids), axis=1)


def slot_gates(gates, pair_kept, expert_ids, slot_token, slot_valid):
    per_expert = jnp.sum((gates * pair_kept)[:, :, None] * expert_onehot(expert_ids), axis=1)
    return jnp.take_along_axis(per_expert.T, slot_token, axis=1) * slot_valid.astype(jnp.float32)


def pick_slots(values, slot_token, slot_valid):
    return jnp.where(slot_valid[:, :, None] > 0, values[slot_token], jnp.zeros((), values.dtype))


def fan_out(slot_values, group_size):
    experts_here, slot_cap, width = slot_values.shape
    spread_out = jnp.broadcast_to(slot_values[:, None], (experts_here, group_size, slot_cap, width))
    return spread_out.reshape(experts_here * group_size, slot_cap, width)


def fold_group(received, group_size):
    count, slot_cap, width = received.shape
    return jnp.sum(received.reshape(count // group_size, group_size, slot_cap, width), axis=1)


def norm_back(normed_grad, gain, normed, inverse):
    scaled = normed_grad * gain
    gain_grad = jnp.sum(normed_grad * normed, axis=0)
    input_grad = inverse * (scaled - normed * jnp.mean(scaled * normed, axis=-1, keepdims=True))
    return (input_grad, gain_grad)


def shards(
    tokens,
    attn_gain,
    kv_weight,
    attn_router,
    query_weight,
    output_weight,
    mlp_gain,
    mlp_router,
    gate_weight,
    up_weight,
    down_weight,
    attn_experts,
    mlp_experts,
    priority,
    cotangent,
):
    devices = lax.axis_size(("seq", "expert"))
    halves = lax.axis_size("expert")
    device_index = lax.axis_index(("seq", "expert"))
    half_index = lax.axis_index("expert")
    seq_tokens, width = tokens.shape
    own_rows = seq_tokens // halves
    group_size = devices // EXPERTS
    head_cols = query_weight.shape[1]
    local_heads = head_cols // HEAD
    key_cols = KV_HEADS * HEAD
    all_tokens = own_rows * devices
    seq_length = seq_tokens * PIECES
    sequences = all_tokens // seq_length
    slot_cap = (9 * TOPK * own_rows + 8 * EXPERTS - 1) // (8 * EXPERTS)
    slot_rows = devices * slot_cap
    seq_rows = slot_rows // sequences
    my_expert = device_index // group_size
    scale = 1.0 / math.sqrt(HEAD)

    def slot_sums(partial_value):
        return fold_group(
            lax.all_to_all(
                partial_value, ("seq", "expert"), split_axis=0, concat_axis=0, tiled=True
            ),
            group_size,
        )

    start_row = half_index * own_rows
    own_input = lax.dynamic_slice_in_dim(tokens, start_row, own_rows, 0).astype(jnp.float32)
    own_cotangent = lax.dynamic_slice_in_dim(cotangent, start_row, own_rows, 0).astype(jnp.float32)
    own_attn = lax.dynamic_slice_in_dim(attn_experts, start_row, own_rows, 0)
    own_mlp = lax.dynamic_slice_in_dim(mlp_experts, start_row, own_rows, 0)
    own_rank = lax.dynamic_slice_in_dim(priority[0], start_row, own_rows, 0)
    token_order = jnp.arange(own_rows, dtype=jnp.int32)

    kv_rows, kv_width = kv_weight.shape
    id_cols = own_rows * TOPK // kv_rows
    extras = jnp.concatenate(
        [
            attn_gain[:, None],
            mlp_gain[:, None],
            attn_router,
            mlp_router,
            own_attn.reshape(kv_rows, id_cols).astype(jnp.bfloat16),
        ],
        axis=1,
    )
    extra_cols = extras.shape[1]
    extra_pad = -(-extra_cols // 128) * 128
    packed = jnp.concatenate(
        [kv_weight, jnp.pad(extras, ((0, 0), (0, extra_pad - extra_cols)))], axis=1
    )
    gathered = lax.all_gather(packed, ("seq", "expert"), axis=0, tiled=True)
    kv_full = gathered[:, :kv_width]
    gain_one = gathered[:, kv_width]
    gain_two = gathered[:, kv_width + 1]
    router_one = gathered[:, kv_width + 2 : kv_width + 2 + EXPERTS]
    router_two = gathered[:, kv_width + 2 + EXPERTS : kv_width + 2 + 2 * EXPERTS]
    routes_all = gathered[:, kv_width + 2 + 2 * EXPERTS : kv_width + extra_cols].astype(jnp.int32)
    inverse_one = lax.rsqrt(jnp.mean(own_input * own_input, axis=-1, keepdims=True) + epsilon)
    normed_one = own_input * inverse_one
    attn_input = (normed_one * gain_one.astype(jnp.float32)).astype(jnp.bfloat16)
    attn_logits = jnp.dot(attn_input, router_one, preferred_element_type=jnp.float32)
    key_value = jnp.dot(attn_input, kv_full, preferred_element_type=jnp.float32)
    own_positions = (device_index * own_rows + token_order) % seq_length
    own_cos, own_sin = rope_tables(own_positions, HEAD)
    own_keys = (
        rotate(key_value[:, :key_cols].reshape(own_rows, KV_HEADS, HEAD), own_cos, own_sin)
        .reshape(own_rows, key_cols)
        .astype(jnp.bfloat16)
    )
    own_values = key_value[:, key_cols:].astype(jnp.bfloat16)

    def spread(values):
        shaped = values.reshape(own_rows, 1, group_size, head_cols)
        return jnp.broadcast_to(shaped, (own_rows, EXPERTS, group_size, head_cols)).reshape(
            own_rows, devices, head_cols
        )

    head_keys, head_values = (
        lax.all_to_all(
            spread(own_keys), ("seq", "expert"), split_axis=1, concat_axis=0, tiled=True
        ),
        lax.all_to_all(
            spread(own_values), ("seq", "expert"), split_axis=1, concat_axis=0, tiled=True
        ),
    )
    seq_keys = head_keys.reshape(sequences, seq_length, local_heads, HEAD)
    seq_values = head_values.reshape(sequences, seq_length, local_heads, HEAD)
    attn_places, attn_kept, attn_token, attn_valid = slot_table(own_attn, token_order, slot_cap)
    mlp_places, mlp_kept, mlp_token, mlp_valid = slot_table(own_mlp, own_rank, slot_cap)
    block_routes = routes_all.reshape(devices, own_rows, TOPK)
    dest_tables = jax.vmap(lambda block_ids: slot_table(block_ids, token_order, slot_cap)[2])(
        block_routes
    )
    dest_token = jnp.take(dest_tables, my_expert, axis=1)
    attn_rows = lax.all_to_all(
        fan_out(pick_slots(attn_input, attn_token, attn_valid), group_size),
        ("seq", "expert"),
        split_axis=0,
        concat_axis=0,
        tiled=True,
    ).reshape(slot_rows, width)
    queries = jnp.dot(attn_rows, query_weight, preferred_element_type=jnp.float32)
    slot_positions = (
        (jnp.arange(devices, dtype=jnp.int32)[:, None] * own_rows + dest_token) % seq_length
    ).reshape(slot_rows)
    slot_cos, slot_sin = rope_tables(slot_positions, HEAD)
    rotated = rotate(queries.reshape(slot_rows, local_heads, HEAD), slot_cos, slot_sin).astype(
        jnp.bfloat16
    )
    seq_queries = rotated.reshape(sequences, seq_rows, local_heads, HEAD)
    query_blocks = (slot_positions // BLOCK).reshape(sequences, seq_rows)
    key_blocks = jnp.arange(seq_length, dtype=jnp.int32) // BLOCK

    def seq_scores(query_part, key_part, block_part):
        scores = (
            jnp.einsum("rhd,khd->hrk", query_part, key_part, preferred_element_type=jnp.float32)
            * scale
        )
        allowed = key_blocks[None, :] <= block_part[:, None]
        return jnp.where(allowed[None], scores, masked_score)

    def attend_forward(inputs):
        query_part, key_part, value_part, block_part = inputs
        scores = seq_scores(query_part, key_part, block_part)
        largest = jnp.max(scores, axis=-1, keepdims=True)
        weights = jnp.exp(scores - largest)
        totals = jnp.sum(weights, axis=-1, keepdims=True)
        probs = weights / totals
        mixed_part = jnp.einsum(
            "hrk,khd->rhd",
            probs.astype(jnp.bfloat16),
            value_part,
            preferred_element_type=jnp.float32,
        )
        return (mixed_part.astype(jnp.bfloat16), largest + jnp.log(totals))

    attn_mixed, log_totals = lax.map(
        attend_forward, (seq_queries, seq_keys, seq_values, query_blocks)
    )
    mixed_rows = attn_mixed.reshape(slot_rows, head_cols)
    attn_partial = jnp.dot(mixed_rows, output_weight, preferred_element_type=jnp.float32).reshape(
        devices, slot_cap, width
    )
    attn_slots = slot_sums(attn_partial)
    attn_gates = pair_gates(attn_logits, own_attn)
    attn_index, attn_pair_kept = pair_index(own_attn, attn_places, attn_kept, slot_cap)
    attn_picked = attn_slots.reshape(EXPERTS * slot_cap, width)[attn_index]
    hidden_state = own_input + jnp.sum(
        attn_picked * (attn_gates * attn_pair_kept)[:, :, None], axis=1
    )
    inverse_two = lax.rsqrt(jnp.mean(hidden_state * hidden_state, axis=-1, keepdims=True) + epsilon)
    normed_two = hidden_state * inverse_two
    mlp_input = (normed_two * gain_two.astype(jnp.float32)).astype(jnp.bfloat16)
    mlp_logits = jnp.dot(mlp_input, router_two, preferred_element_type=jnp.float32)
    mlp_rows = lax.all_to_all(
        fan_out(pick_slots(mlp_input, mlp_token, mlp_valid), group_size),
        ("seq", "expert"),
        split_axis=0,
        concat_axis=0,
        tiled=True,
    ).reshape(slot_rows, width)
    gate_pre = jnp.dot(mlp_rows, gate_weight, preferred_element_type=jnp.float32)
    up_pre = jnp.dot(mlp_rows, up_weight, preferred_element_type=jnp.float32)
    activated = jax.nn.silu(gate_pre)
    inner_rows = (activated * up_pre).astype(jnp.bfloat16)
    mlp_partial = jnp.dot(inner_rows, down_weight, preferred_element_type=jnp.float32).reshape(
        devices, slot_cap, width
    )
    mlp_slots = slot_sums(mlp_partial)
    mlp_gates = pair_gates(mlp_logits, own_mlp)
    mlp_index, mlp_pair_kept = pair_index(own_mlp, mlp_places, mlp_kept, slot_cap)
    mlp_picked = mlp_slots.reshape(EXPERTS * slot_cap, width)[mlp_index]
    own_output = hidden_state + jnp.sum(
        mlp_picked * (mlp_gates * mlp_pair_kept)[:, :, None], axis=1
    )
    mlp_gate_grad = jnp.sum(mlp_picked * own_cotangent[:, None, :], axis=-1) * mlp_pair_kept
    mlp_logit_grad = gates_back(mlp_gates, mlp_gate_grad, own_mlp)
    mlp_slot_grad = (
        own_cotangent[mlp_token]
        * slot_gates(mlp_gates, mlp_pair_kept, own_mlp, mlp_token, mlp_valid)[:, :, None]
    ).astype(jnp.bfloat16)
    down_rows = lax.all_to_all(
        fan_out(mlp_slot_grad, group_size),
        ("seq", "expert"),
        split_axis=0,
        concat_axis=0,
        tiled=True,
    ).reshape(slot_rows, width)
    inner_grad = jnp.einsum("rd,fd->rf", down_rows, down_weight, preferred_element_type=jnp.float32)
    down_grad = jnp.einsum("rf,rd->fd", inner_rows, down_rows, preferred_element_type=jnp.float32)
    sigmoid_gate = jax.nn.sigmoid(gate_pre)
    gate_pre_grad = (
        inner_grad * up_pre * sigmoid_gate * (1.0 + gate_pre * (1.0 - sigmoid_gate))
    ).astype(jnp.bfloat16)
    up_pre_grad = (inner_grad * activated).astype(jnp.bfloat16)
    gate_grad = jnp.einsum("rd,rf->df", mlp_rows, gate_pre_grad, preferred_element_type=jnp.float32)
    up_grad = jnp.einsum("rd,rf->df", mlp_rows, up_pre_grad, preferred_element_type=jnp.float32)
    row_grad = jnp.einsum(
        "rf,df->rd", gate_pre_grad, gate_weight, preferred_element_type=jnp.float32
    ) + jnp.einsum("rf,df->rd", up_pre_grad, up_weight, preferred_element_type=jnp.float32)
    mlp_row_grad = slot_sums(row_grad.reshape(devices, slot_cap, width))
    mlp_input_grad = jnp.sum(
        mlp_row_grad.reshape(EXPERTS * slot_cap, width)[mlp_index] * mlp_pair_kept[:, :, None],
        axis=1,
    )
    mlp_input_grad = mlp_input_grad + jnp.dot(
        mlp_logit_grad, router_two.astype(jnp.float32).T, precision=lax.Precision.HIGHEST
    )
    mlp_router_own = jnp.dot(
        mlp_input.astype(jnp.float32).T, mlp_logit_grad, precision=lax.Precision.HIGHEST
    )
    hidden_grad, gain_two_own = norm_back(
        mlp_input_grad, gain_two.astype(jnp.float32), normed_two, inverse_two
    )
    hidden_grad = hidden_grad + own_cotangent
    attn_gate_grad = jnp.sum(attn_picked * hidden_grad[:, None, :], axis=-1) * attn_pair_kept
    attn_logit_grad = gates_back(attn_gates, attn_gate_grad, own_attn)
    attn_slot_grad = (
        hidden_grad[attn_token]
        * slot_gates(attn_gates, attn_pair_kept, own_attn, attn_token, attn_valid)[:, :, None]
    ).astype(jnp.bfloat16)
    out_rows = lax.all_to_all(
        fan_out(attn_slot_grad, group_size),
        ("seq", "expert"),
        split_axis=0,
        concat_axis=0,
        tiled=True,
    ).reshape(slot_rows, width)
    output_grad = jnp.einsum("rw,rd->wd", mixed_rows, out_rows, preferred_element_type=jnp.float32)
    mixed_grad = jnp.einsum(
        "rd,wd->rw", out_rows, output_weight, preferred_element_type=jnp.float32
    ).astype(jnp.bfloat16)
    seq_mixed_grad = mixed_grad.reshape(sequences, seq_rows, local_heads, HEAD)

    def attend_backward(inputs):
        query_part, key_part, value_part, block_part, log_part, grad_part = inputs
        probs = jnp.exp(seq_scores(query_part, key_part, block_part) - log_part)
        prob_grad = jnp.einsum(
            "rhd,khd->hrk", grad_part, value_part, preferred_element_type=jnp.float32
        )
        inner = jnp.sum(probs * prob_grad, axis=-1, keepdims=True)
        score_grad = (probs * (prob_grad - inner)).astype(jnp.bfloat16)
        value_grad = jnp.einsum(
            "hrk,rhd->khd",
            probs.astype(jnp.bfloat16),
            grad_part,
            preferred_element_type=jnp.float32,
        )
        key_grad = (
            jnp.einsum("hrk,rhd->khd", score_grad, query_part, preferred_element_type=jnp.float32)
            * scale
        )
        query_part_grad = (
            jnp.einsum("hrk,khd->rhd", score_grad, key_part, preferred_element_type=jnp.float32)
            * scale
        )
        return (query_part_grad, key_grad, value_grad)

    seq_query_grad, seq_key_grad, seq_value_grad = lax.map(
        attend_backward,
        (seq_queries, seq_keys, seq_values, query_blocks, log_totals, seq_mixed_grad),
    )
    query_rot_grad = (
        rotate_back(seq_query_grad.reshape(slot_rows, local_heads, HEAD), slot_cos, slot_sin)
        .reshape(slot_rows, head_cols)
        .astype(jnp.bfloat16)
    )
    query_grad = jnp.einsum(
        "rd,rw->dw", attn_rows, query_rot_grad, preferred_element_type=jnp.float32
    )
    query_row_grad = jnp.einsum(
        "rw,dw->rd", query_rot_grad, query_weight, preferred_element_type=jnp.float32
    )
    attn_row_grad = slot_sums(query_row_grad.reshape(devices, slot_cap, width))
    key_back, value_back = (
        lax.all_to_all(
            seq_key_grad.reshape(devices, own_rows, 1, head_cols).astype(jnp.bfloat16),
            ("seq", "expert"),
            split_axis=0,
            concat_axis=2,
            tiled=True,
        ).astype(jnp.float32),
        lax.all_to_all(
            seq_value_grad.reshape(devices, own_rows, 1, head_cols).astype(jnp.bfloat16),
            ("seq", "expert"),
            split_axis=0,
            concat_axis=2,
            tiled=True,
        ).astype(jnp.float32),
    )
    own_key_grad = jnp.sum(key_back.reshape(own_rows, EXPERTS, group_size, head_cols), axis=1)
    own_value_grad = jnp.sum(
        value_back.reshape(own_rows, EXPERTS, group_size, head_cols), axis=1
    ).reshape(own_rows, key_cols)
    kv_own_grad = jnp.concatenate(
        [rotate_back(own_key_grad, own_cos, own_sin).reshape(own_rows, key_cols), own_value_grad],
        axis=1,
    ).astype(jnp.bfloat16)
    attn_input_grad = jnp.sum(
        attn_row_grad.reshape(EXPERTS * slot_cap, width)[attn_index] * attn_pair_kept[:, :, None],
        axis=1,
    )
    attn_input_grad = attn_input_grad + jnp.einsum(
        "rc,dc->rd", kv_own_grad, kv_full, preferred_element_type=jnp.float32
    )
    attn_input_grad = attn_input_grad + jnp.dot(
        attn_logit_grad, router_one.astype(jnp.float32).T, precision=lax.Precision.HIGHEST
    )
    kv_own_weight = jnp.einsum(
        "rd,rc->dc", attn_input, kv_own_grad, preferred_element_type=jnp.float32
    )
    attn_router_own = jnp.dot(
        attn_input.astype(jnp.float32).T, attn_logit_grad, precision=lax.Precision.HIGHEST
    )
    input_grad, gain_one_own = norm_back(
        attn_input_grad, gain_one.astype(jnp.float32), normed_one, inverse_one
    )
    input_grad = input_grad + hidden_grad
    grad_extras = jnp.concatenate(
        [gain_one_own[:, None], gain_two_own[:, None], attn_router_own, mlp_router_own], axis=1
    )
    packed_grad = jnp.concatenate(
        [
            kv_own_weight,
            jnp.pad(grad_extras, ((0, 0), (0, extra_pad - grad_extras.shape[1]))),
        ],
        axis=1,
    )
    scattered = lax.psum_scatter(packed_grad, ("seq", "expert"), scatter_dimension=0, tiled=True)
    kv_grad = scattered[:, :kv_width]
    gain_one_grad = scattered[:, kv_width]
    gain_two_grad = scattered[:, kv_width + 1]
    attn_router_grad = scattered[:, kv_width + 2 : kv_width + 2 + EXPERTS]
    mlp_router_grad = scattered[:, kv_width + 2 + EXPERTS : kv_width + 2 + 2 * EXPERTS]
    mixed_full, input_full = (
        lax.all_gather(own_output.astype(jnp.bfloat16), "expert", axis=0, tiled=True),
        lax.all_gather(input_grad.astype(jnp.bfloat16), "expert", axis=0, tiled=True),
    )
    return (
        mixed_full,
        input_full,
        gain_one_grad,
        kv_grad,
        attn_router_grad,
        query_grad,
        output_grad,
        gain_two_grad,
        mlp_router_grad,
        gate_grad,
        up_grad,
        down_grad,
    )


def solution(mesh):
    return jax.shard_map(
        shards,
        mesh=mesh,
        in_specs=(
            P("seq", None),
            P(("seq", "expert")),
            P(("seq", "expert"), None),
            P(("seq", "expert"), None),
            P(None, ("seq", "expert")),
            P(("seq", "expert"), None),
            P(("seq", "expert")),
            P(("seq", "expert"), None),
            P(None, ("seq", "expert")),
            P(None, ("seq", "expert")),
            P(("seq", "expert"), None),
            P("seq", None),
            P("seq", None),
            P("seq", None),
            P("seq", None),
        ),
        out_specs=(
            P("seq", None),
            P("seq", None),
            P(("seq", "expert")),
            P(("seq", "expert"), None),
            P(("seq", "expert"), None),
            P(None, ("seq", "expert")),
            P(("seq", "expert"), None),
            P(("seq", "expert")),
            P(("seq", "expert"), None),
            P(None, ("seq", "expert")),
            P(None, ("seq", "expert")),
            P(("seq", "expert"), None),
        ),
        check_vma=False,
    )
```

```python
import math

import jax
import jax.numpy as jnp
from jax import lax
from jax.sharding import PartitionSpec as P

KV_HEADS = 16
HEAD = 128
EXPERTS = 8
TOPK = 2
PIECES = 8
BLOCK = 256


epsilon = 1e-06
masked_score = -1e30


def rope_tables(positions, head_size):
    half_size = head_size // 2
    frequency = jnp.exp(
        jnp.arange(half_size, dtype=jnp.float32) * (-2.0 * math.log(10000.0) / head_size)
    )
    angles = positions.astype(jnp.float32)[:, None] * frequency[None, :]
    return (jnp.cos(angles)[:, None, :], jnp.sin(angles)[:, None, :])


def rotate(values, cosines, sines):
    half_size = values.shape[-1] // 2
    first = values[..., :half_size]
    second = values[..., half_size:]
    return jnp.concatenate(
        [first * cosines - second * sines, second * cosines + first * sines], axis=-1
    )


def rotate_back(grads, cosines, sines):
    half_size = grads.shape[-1] // 2
    first = grads[..., :half_size]
    second = grads[..., half_size:]
    return jnp.concatenate(
        [first * cosines + second * sines, second * cosines - first * sines], axis=-1
    )


def slot_table(expert_ids, ranks, slot_cap):
    block_rows = expert_ids.shape[0]
    expert_range = jnp.arange(EXPERTS, dtype=jnp.int32)
    member = jnp.sum(
        (expert_ids[:, :, None] == expert_range[None, None, :]).astype(jnp.int32), axis=1
    )
    earlier = (ranks[:, None] < ranks[None, :]).astype(jnp.int32)
    places = jnp.sum(earlier[:, :, None] * member[:, None, :], axis=0)
    kept = member * (places < slot_cap).astype(jnp.int32)
    slot_range = jnp.arange(slot_cap, dtype=jnp.int32)
    landing = kept[:, :, None] * (places[:, :, None] == slot_range[None, None, :]).astype(jnp.int32)
    row_range = jnp.arange(block_rows, dtype=jnp.int32)
    slot_token = jnp.sum(landing * row_range[:, None, None], axis=0)
    slot_valid = jnp.sum(landing, axis=0)
    return (places, kept, slot_token, slot_valid)


def pair_index(expert_ids, places, kept, slot_cap):
    chosen_place = jnp.take_along_axis(places, expert_ids, axis=1)
    chosen_kept = jnp.take_along_axis(kept, expert_ids, axis=1)
    return (
        expert_ids * slot_cap + jnp.minimum(chosen_place, slot_cap - 1),
        chosen_kept.astype(jnp.float32),
    )


def pair_gates(logits, expert_ids):
    return jax.nn.softmax(jnp.take_along_axis(logits, expert_ids, axis=1), axis=-1)


def expert_onehot(expert_ids):
    expert_range = jnp.arange(EXPERTS, dtype=jnp.int32)
    return (expert_ids[:, :, None] == expert_range[None, None, :]).astype(jnp.float32)


def gates_back(gates, gate_grads, expert_ids):
    inner = jnp.sum(gates * gate_grads, axis=1, keepdims=True)
    chosen_grads = gates * (gate_grads - inner)
    return jnp.sum(chosen_grads[:, :, None] * expert_onehot(expert_ids), axis=1)


def slot_gates(gates, pair_kept, expert_ids, slot_token, slot_valid):
    per_expert = jnp.sum((gates * pair_kept)[:, :, None] * expert_onehot(expert_ids), axis=1)
    return jnp.take_along_axis(per_expert.T, slot_token, axis=1) * slot_valid.astype(jnp.float32)


def pick_slots(values, slot_token, slot_valid):
    return jnp.where(slot_valid[:, :, None] > 0, values[slot_token], jnp.zeros((), values.dtype))


def fan_out(slot_values, group_size):
    experts_here, slot_cap, width = slot_values.shape
    spread_out = jnp.broadcast_to(slot_values[:, None], (experts_here, group_size, slot_cap, width))
    return spread_out.reshape(experts_here * group_size, slot_cap, width)


def fold_group(received, group_size):
    count, slot_cap, width = received.shape
    return jnp.sum(received.reshape(count // group_size, group_size, slot_cap, width), axis=1)


def norm_back(normed_grad, gain, normed, inverse):
    scaled = normed_grad * gain
    gain_grad = jnp.sum(normed_grad * normed, axis=0)
    input_grad = inverse * (scaled - normed * jnp.mean(scaled * normed, axis=-1, keepdims=True))
    return (input_grad, gain_grad)


def shards(
    tokens,
    attn_gain,
    kv_weight,
    attn_router,
    query_weight,
    output_weight,
    mlp_gain,
    mlp_router,
    gate_weight,
    up_weight,
    down_weight,
    attn_experts,
    mlp_experts,
    priority,
    cotangent,
):
    devices = lax.axis_size(("seq", "expert"))
    halves = lax.axis_size("expert")
    device_index = lax.axis_index(("seq", "expert"))
    half_index = lax.axis_index("expert")
    seq_tokens, width = tokens.shape
    own_rows = seq_tokens // halves
    group_size = devices // EXPERTS
    head_cols = query_weight.shape[1]
    local_heads = head_cols // HEAD
    key_cols = KV_HEADS * HEAD
    all_tokens = own_rows * devices
    seq_length = seq_tokens * PIECES
    sequences = all_tokens // seq_length
    slot_cap = (9 * TOPK * own_rows + 8 * EXPERTS - 1) // (8 * EXPERTS)
    slot_rows = devices * slot_cap
    seq_rows = slot_rows // sequences
    my_expert = device_index // group_size
    scale = 1.0 / math.sqrt(HEAD)

    def slot_sums(partial_value):
        return fold_group(
            lax.all_to_all(
                partial_value.astype(jnp.bfloat16),
                ("seq", "expert"),
                split_axis=0,
                concat_axis=0,
                tiled=True,
            ).astype(jnp.float32),
            group_size,
        )

    start_row = half_index * own_rows
    own_input = lax.dynamic_slice_in_dim(tokens, start_row, own_rows, 0).astype(jnp.float32)
    own_cotangent = lax.dynamic_slice_in_dim(cotangent, start_row, own_rows, 0).astype(jnp.float32)
    own_attn = lax.dynamic_slice_in_dim(attn_experts, start_row, own_rows, 0)
    own_mlp = lax.dynamic_slice_in_dim(mlp_experts, start_row, own_rows, 0)
    own_rank = lax.dynamic_slice_in_dim(priority[0], start_row, own_rows, 0)
    token_order = jnp.arange(own_rows, dtype=jnp.int32)

    kv_rows, kv_width = kv_weight.shape
    id_cols = own_rows * TOPK // kv_rows
    extras = jnp.concatenate(
        [
            attn_gain[:, None],
            mlp_gain[:, None],
            attn_router,
            mlp_router,
            own_attn.reshape(kv_rows, id_cols).astype(jnp.bfloat16),
        ],
        axis=1,
    )
    extra_cols = extras.shape[1]
    extra_pad = -(-extra_cols // 128) * 128
    packed = jnp.concatenate(
        [kv_weight, jnp.pad(extras, ((0, 0), (0, extra_pad - extra_cols)))], axis=1
    )
    gathered = lax.all_gather(packed, ("seq", "expert"), axis=0, tiled=True)
    kv_full = gathered[:, :kv_width]
    gain_one = gathered[:, kv_width]
    gain_two = gathered[:, kv_width + 1]
    router_one = gathered[:, kv_width + 2 : kv_width + 2 + EXPERTS]
    router_two = gathered[:, kv_width + 2 + EXPERTS : kv_width + 2 + 2 * EXPERTS]
    routes_all = gathered[:, kv_width + 2 + 2 * EXPERTS : kv_width + extra_cols].astype(jnp.int32)
    inverse_one = lax.rsqrt(jnp.mean(own_input * own_input, axis=-1, keepdims=True) + epsilon)
    normed_one = own_input * inverse_one
    attn_input = (normed_one * gain_one.astype(jnp.float32)).astype(jnp.bfloat16)
    attn_logits = jnp.dot(attn_input, router_one, preferred_element_type=jnp.float32)
    key_value = jnp.dot(attn_input, kv_full, preferred_element_type=jnp.float32)
    own_positions = (device_index * own_rows + token_order) % seq_length
    own_cos, own_sin = rope_tables(own_positions, HEAD)
    own_keys = (
        rotate(key_value[:, :key_cols].reshape(own_rows, KV_HEADS, HEAD), own_cos, own_sin)
        .reshape(own_rows, key_cols)
        .astype(jnp.bfloat16)
    )
    own_values = key_value[:, key_cols:].astype(jnp.bfloat16)

    def spread(values):
        shaped = values.reshape(own_rows, 1, group_size, head_cols)
        return jnp.broadcast_to(shaped, (own_rows, EXPERTS, group_size, head_cols)).reshape(
            own_rows, devices, head_cols
        )

    head_keys, head_values = (
        lax.all_to_all(
            spread(own_keys), ("seq", "expert"), split_axis=1, concat_axis=0, tiled=True
        ),
        lax.all_to_all(
            spread(own_values), ("seq", "expert"), split_axis=1, concat_axis=0, tiled=True
        ),
    )
    seq_keys = head_keys.reshape(sequences, seq_length, local_heads, HEAD)
    seq_values = head_values.reshape(sequences, seq_length, local_heads, HEAD)
    attn_places, attn_kept, attn_token, attn_valid = slot_table(own_attn, token_order, slot_cap)
    mlp_places, mlp_kept, mlp_token, mlp_valid = slot_table(own_mlp, own_rank, slot_cap)
    block_routes = routes_all.reshape(devices, own_rows, TOPK)
    dest_tables = jax.vmap(lambda block_ids: slot_table(block_ids, token_order, slot_cap)[2])(
        block_routes
    )
    dest_token = jnp.take(dest_tables, my_expert, axis=1)
    attn_rows = lax.all_to_all(
        fan_out(pick_slots(attn_input, attn_token, attn_valid), group_size),
        ("seq", "expert"),
        split_axis=0,
        concat_axis=0,
        tiled=True,
    ).reshape(slot_rows, width)
    queries = jnp.dot(attn_rows, query_weight, preferred_element_type=jnp.float32)
    slot_positions = (
        (jnp.arange(devices, dtype=jnp.int32)[:, None] * own_rows + dest_token) % seq_length
    ).reshape(slot_rows)
    slot_cos, slot_sin = rope_tables(slot_positions, HEAD)
    rotated = rotate(queries.reshape(slot_rows, local_heads, HEAD), slot_cos, slot_sin).astype(
        jnp.bfloat16
    )
    seq_queries = rotated.reshape(sequences, seq_rows, local_heads, HEAD)
    query_blocks = (slot_positions // BLOCK).reshape(sequences, seq_rows)
    key_blocks = jnp.arange(seq_length, dtype=jnp.int32) // BLOCK

    def seq_scores(query_part, key_part, block_part):
        scores = (
            jnp.einsum("rhd,khd->hrk", query_part, key_part, preferred_element_type=jnp.float32)
            * scale
        )
        allowed = key_blocks[None, :] <= block_part[:, None]
        return jnp.where(allowed[None], scores, masked_score)

    def attend_forward(inputs):
        query_part, key_part, value_part, block_part = inputs
        scores = seq_scores(query_part, key_part, block_part)
        largest = jnp.max(scores, axis=-1, keepdims=True)
        weights = jnp.exp(scores - largest)
        totals = jnp.sum(weights, axis=-1, keepdims=True)
        probs = weights / totals
        mixed_part = jnp.einsum(
            "hrk,khd->rhd",
            probs.astype(jnp.bfloat16),
            value_part,
            preferred_element_type=jnp.float32,
        )
        return (mixed_part.astype(jnp.bfloat16), largest + jnp.log(totals))

    attn_mixed, log_totals = lax.map(
        attend_forward, (seq_queries, seq_keys, seq_values, query_blocks)
    )
    mixed_rows = attn_mixed.reshape(slot_rows, head_cols)
    attn_partial = jnp.dot(mixed_rows, output_weight, preferred_element_type=jnp.float32).reshape(
        devices, slot_cap, width
    )
    attn_slots = slot_sums(attn_partial)
    attn_gates = pair_gates(attn_logits, own_attn)
    attn_index, attn_pair_kept = pair_index(own_attn, attn_places, attn_kept, slot_cap)
    attn_picked = attn_slots.reshape(EXPERTS * slot_cap, width)[attn_index]
    hidden_state = own_input + jnp.sum(
        attn_picked * (attn_gates * attn_pair_kept)[:, :, None], axis=1
    )
    inverse_two = lax.rsqrt(jnp.mean(hidden_state * hidden_state, axis=-1, keepdims=True) + epsilon)
    normed_two = hidden_state * inverse_two
    mlp_input = (normed_two * gain_two.astype(jnp.float32)).astype(jnp.bfloat16)
    mlp_logits = jnp.dot(mlp_input, router_two, preferred_element_type=jnp.float32)
    mlp_rows = lax.all_to_all(
        fan_out(pick_slots(mlp_input, mlp_token, mlp_valid), group_size),
        ("seq", "expert"),
        split_axis=0,
        concat_axis=0,
        tiled=True,
    ).reshape(slot_rows, width)
    gate_pre = jnp.dot(mlp_rows, gate_weight, preferred_element_type=jnp.float32)
    up_pre = jnp.dot(mlp_rows, up_weight, preferred_element_type=jnp.float32)
    activated = jax.nn.silu(gate_pre)
    inner_rows = (activated * up_pre).astype(jnp.bfloat16)
    mlp_partial = jnp.dot(inner_rows, down_weight, preferred_element_type=jnp.float32).reshape(
        devices, slot_cap, width
    )
    mlp_slots = slot_sums(mlp_partial)
    mlp_gates = pair_gates(mlp_logits, own_mlp)
    mlp_index, mlp_pair_kept = pair_index(own_mlp, mlp_places, mlp_kept, slot_cap)
    mlp_picked = mlp_slots.reshape(EXPERTS * slot_cap, width)[mlp_index]
    own_output = hidden_state + jnp.sum(
        mlp_picked * (mlp_gates * mlp_pair_kept)[:, :, None], axis=1
    )
    mlp_gate_grad = jnp.sum(mlp_picked * own_cotangent[:, None, :], axis=-1) * mlp_pair_kept
    mlp_logit_grad = gates_back(mlp_gates, mlp_gate_grad, own_mlp)
    mlp_slot_grad = (
        own_cotangent[mlp_token]
        * slot_gates(mlp_gates, mlp_pair_kept, own_mlp, mlp_token, mlp_valid)[:, :, None]
    ).astype(jnp.bfloat16)
    down_rows = lax.all_to_all(
        fan_out(mlp_slot_grad, group_size),
        ("seq", "expert"),
        split_axis=0,
        concat_axis=0,
        tiled=True,
    ).reshape(slot_rows, width)
    inner_grad = jnp.einsum("rd,fd->rf", down_rows, down_weight, preferred_element_type=jnp.float32)
    down_grad = jnp.einsum("rf,rd->fd", inner_rows, down_rows, preferred_element_type=jnp.float32)
    sigmoid_gate = jax.nn.sigmoid(gate_pre)
    gate_pre_grad = (
        inner_grad * up_pre * sigmoid_gate * (1.0 + gate_pre * (1.0 - sigmoid_gate))
    ).astype(jnp.bfloat16)
    up_pre_grad = (inner_grad * activated).astype(jnp.bfloat16)
    gate_grad = jnp.einsum("rd,rf->df", mlp_rows, gate_pre_grad, preferred_element_type=jnp.float32)
    up_grad = jnp.einsum("rd,rf->df", mlp_rows, up_pre_grad, preferred_element_type=jnp.float32)
    row_grad = jnp.einsum(
        "rf,df->rd", gate_pre_grad, gate_weight, preferred_element_type=jnp.float32
    ) + jnp.einsum("rf,df->rd", up_pre_grad, up_weight, preferred_element_type=jnp.float32)
    mlp_row_grad = slot_sums(row_grad.reshape(devices, slot_cap, width))
    mlp_input_grad = jnp.sum(
        mlp_row_grad.reshape(EXPERTS * slot_cap, width)[mlp_index] * mlp_pair_kept[:, :, None],
        axis=1,
    )
    mlp_input_grad = mlp_input_grad + jnp.dot(
        mlp_logit_grad, router_two.astype(jnp.float32).T, precision=lax.Precision.HIGHEST
    )
    mlp_router_own = jnp.dot(
        mlp_input.astype(jnp.float32).T, mlp_logit_grad, precision=lax.Precision.HIGHEST
    )
    hidden_grad, gain_two_own = norm_back(
        mlp_input_grad, gain_two.astype(jnp.float32), normed_two, inverse_two
    )
    hidden_grad = hidden_grad + own_cotangent
    attn_gate_grad = jnp.sum(attn_picked * hidden_grad[:, None, :], axis=-1) * attn_pair_kept
    attn_logit_grad = gates_back(attn_gates, attn_gate_grad, own_attn)
    attn_slot_grad = (
        hidden_grad[attn_token]
        * slot_gates(attn_gates, attn_pair_kept, own_attn, attn_token, attn_valid)[:, :, None]
    ).astype(jnp.bfloat16)
    out_rows = lax.all_to_all(
        fan_out(attn_slot_grad, group_size),
        ("seq", "expert"),
        split_axis=0,
        concat_axis=0,
        tiled=True,
    ).reshape(slot_rows, width)
    output_grad = jnp.einsum("rw,rd->wd", mixed_rows, out_rows, preferred_element_type=jnp.float32)
    mixed_grad = jnp.einsum(
        "rd,wd->rw", out_rows, output_weight, preferred_element_type=jnp.float32
    ).astype(jnp.bfloat16)
    seq_mixed_grad = mixed_grad.reshape(sequences, seq_rows, local_heads, HEAD)

    def attend_backward(inputs):
        query_part, key_part, value_part, block_part, log_part, grad_part = inputs
        probs = jnp.exp(seq_scores(query_part, key_part, block_part) - log_part)
        prob_grad = jnp.einsum(
            "rhd,khd->hrk", grad_part, value_part, preferred_element_type=jnp.float32
        )
        inner = jnp.sum(probs * prob_grad, axis=-1, keepdims=True)
        score_grad = (probs * (prob_grad - inner)).astype(jnp.bfloat16)
        value_grad = jnp.einsum(
            "hrk,rhd->khd",
            probs.astype(jnp.bfloat16),
            grad_part,
            preferred_element_type=jnp.float32,
        )
        key_grad = (
            jnp.einsum("hrk,rhd->khd", score_grad, query_part, preferred_element_type=jnp.float32)
            * scale
        )
        query_part_grad = (
            jnp.einsum("hrk,khd->rhd", score_grad, key_part, preferred_element_type=jnp.float32)
            * scale
        )
        return (query_part_grad, key_grad, value_grad)

    seq_query_grad, seq_key_grad, seq_value_grad = lax.map(
        attend_backward,
        (seq_queries, seq_keys, seq_values, query_blocks, log_totals, seq_mixed_grad),
    )
    query_rot_grad = (
        rotate_back(seq_query_grad.reshape(slot_rows, local_heads, HEAD), slot_cos, slot_sin)
        .reshape(slot_rows, head_cols)
        .astype(jnp.bfloat16)
    )
    query_grad = jnp.einsum(
        "rd,rw->dw", attn_rows, query_rot_grad, preferred_element_type=jnp.float32
    )
    query_row_grad = jnp.einsum(
        "rw,dw->rd", query_rot_grad, query_weight, preferred_element_type=jnp.float32
    )
    attn_row_grad = slot_sums(query_row_grad.reshape(devices, slot_cap, width))
    key_back, value_back = (
        lax.all_to_all(
            seq_key_grad.reshape(devices, own_rows, 1, head_cols).astype(jnp.bfloat16),
            ("seq", "expert"),
            split_axis=0,
            concat_axis=2,
            tiled=True,
        ).astype(jnp.float32),
        lax.all_to_all(
            seq_value_grad.reshape(devices, own_rows, 1, head_cols).astype(jnp.bfloat16),
            ("seq", "expert"),
            split_axis=0,
            concat_axis=2,
            tiled=True,
        ).astype(jnp.float32),
    )
    own_key_grad = jnp.sum(key_back.reshape(own_rows, EXPERTS, group_size, head_cols), axis=1)
    own_value_grad = jnp.sum(
        value_back.reshape(own_rows, EXPERTS, group_size, head_cols), axis=1
    ).reshape(own_rows, key_cols)
    kv_own_grad = jnp.concatenate(
        [rotate_back(own_key_grad, own_cos, own_sin).reshape(own_rows, key_cols), own_value_grad],
        axis=1,
    ).astype(jnp.bfloat16)
    attn_input_grad = jnp.sum(
        attn_row_grad.reshape(EXPERTS * slot_cap, width)[attn_index] * attn_pair_kept[:, :, None],
        axis=1,
    )
    attn_input_grad = attn_input_grad + jnp.einsum(
        "rc,dc->rd", kv_own_grad, kv_full, preferred_element_type=jnp.float32
    )
    attn_input_grad = attn_input_grad + jnp.dot(
        attn_logit_grad, router_one.astype(jnp.float32).T, precision=lax.Precision.HIGHEST
    )
    kv_own_weight = jnp.einsum(
        "rd,rc->dc", attn_input, kv_own_grad, preferred_element_type=jnp.float32
    )
    attn_router_own = jnp.dot(
        attn_input.astype(jnp.float32).T, attn_logit_grad, precision=lax.Precision.HIGHEST
    )
    input_grad, gain_one_own = norm_back(
        attn_input_grad, gain_one.astype(jnp.float32), normed_one, inverse_one
    )
    input_grad = input_grad + hidden_grad
    grad_extras = jnp.concatenate(
        [gain_one_own[:, None], gain_two_own[:, None], attn_router_own, mlp_router_own], axis=1
    )
    packed_grad = jnp.concatenate(
        [
            kv_own_weight,
            jnp.pad(grad_extras, ((0, 0), (0, extra_pad - grad_extras.shape[1]))),
        ],
        axis=1,
    )
    scattered = lax.psum_scatter(packed_grad, ("seq", "expert"), scatter_dimension=0, tiled=True)
    kv_grad = scattered[:, :kv_width]
    gain_one_grad = scattered[:, kv_width]
    gain_two_grad = scattered[:, kv_width + 1]
    attn_router_grad = scattered[:, kv_width + 2 : kv_width + 2 + EXPERTS]
    mlp_router_grad = scattered[:, kv_width + 2 + EXPERTS : kv_width + 2 + 2 * EXPERTS]
    mixed_full, input_full = (
        lax.all_gather(own_output.astype(jnp.bfloat16), "expert", axis=0, tiled=True),
        lax.all_gather(input_grad.astype(jnp.bfloat16), "expert", axis=0, tiled=True),
    )
    return (
        mixed_full,
        input_full,
        gain_one_grad,
        kv_grad,
        attn_router_grad,
        query_grad,
        output_grad,
        gain_two_grad,
        mlp_router_grad,
        gate_grad,
        up_grad,
        down_grad,
    )


def solution(mesh):
    return jax.shard_map(
        shards,
        mesh=mesh,
        in_specs=(
            P("seq", None),
            P(("seq", "expert")),
            P(("seq", "expert"), None),
            P(("seq", "expert"), None),
            P(None, ("seq", "expert")),
            P(("seq", "expert"), None),
            P(("seq", "expert")),
            P(("seq", "expert"), None),
            P(None, ("seq", "expert")),
            P(None, ("seq", "expert")),
            P(("seq", "expert"), None),
            P("seq", None),
            P("seq", None),
            P("seq", None),
            P("seq", None),
        ),
        out_specs=(
            P("seq", None),
            P("seq", None),
            P(("seq", "expert")),
            P(("seq", "expert"), None),
            P(("seq", "expert"), None),
            P(None, ("seq", "expert")),
            P(("seq", "expert"), None),
            P(("seq", "expert")),
            P(("seq", "expert"), None),
            P(None, ("seq", "expert")),
            P(None, ("seq", "expert")),
            P(("seq", "expert"), None),
        ),
        check_vma=False,
    )
```

```python
import math

import jax
import jax.numpy as jnp
from jax import lax
from jax.sharding import PartitionSpec as P

ALL_AXES = ("grp", "sub", "expert")
SEQ_AXES = ("grp", "sub")
GROUP_AXES = ("sub", "expert")
KV_HEADS = 16
HEAD = 128
EXPERTS = 8
TOPK = 2
PIECES = 8
BLOCK = 256


epsilon = 1e-06
masked_score = -1e30


def rope_tables(positions, head_size):
    half_size = head_size // 2
    frequency = jnp.exp(
        jnp.arange(half_size, dtype=jnp.float32) * (-2.0 * math.log(10000.0) / head_size)
    )
    angles = positions.astype(jnp.float32)[:, None] * frequency[None, :]
    return (jnp.cos(angles)[:, None, :], jnp.sin(angles)[:, None, :])


def rotate(values, cosines, sines):
    half_size = values.shape[-1] // 2
    first = values[..., :half_size]
    second = values[..., half_size:]
    return jnp.concatenate(
        [first * cosines - second * sines, second * cosines + first * sines], axis=-1
    )


def rotate_back(grads, cosines, sines):
    half_size = grads.shape[-1] // 2
    first = grads[..., :half_size]
    second = grads[..., half_size:]
    return jnp.concatenate(
        [first * cosines + second * sines, second * cosines - first * sines], axis=-1
    )


def slot_table(expert_ids, ranks, slot_cap):
    block_rows = expert_ids.shape[0]
    expert_range = jnp.arange(EXPERTS, dtype=jnp.int32)
    member = jnp.sum(
        (expert_ids[:, :, None] == expert_range[None, None, :]).astype(jnp.int32), axis=1
    )
    earlier = (ranks[:, None] < ranks[None, :]).astype(jnp.int32)
    places = jnp.sum(earlier[:, :, None] * member[:, None, :], axis=0)
    kept = member * (places < slot_cap).astype(jnp.int32)
    slot_range = jnp.arange(slot_cap, dtype=jnp.int32)
    landing = kept[:, :, None] * (places[:, :, None] == slot_range[None, None, :]).astype(jnp.int32)
    row_range = jnp.arange(block_rows, dtype=jnp.int32)
    slot_token = jnp.sum(landing * row_range[:, None, None], axis=0)
    slot_valid = jnp.sum(landing, axis=0)
    return (places, kept, slot_token, slot_valid)


def pair_index(expert_ids, places, kept, slot_cap):
    chosen_place = jnp.take_along_axis(places, expert_ids, axis=1)
    chosen_kept = jnp.take_along_axis(kept, expert_ids, axis=1)
    return (
        expert_ids * slot_cap + jnp.minimum(chosen_place, slot_cap - 1),
        chosen_kept.astype(jnp.float32),
    )


def pair_gates(logits, expert_ids):
    return jax.nn.softmax(jnp.take_along_axis(logits, expert_ids, axis=1), axis=-1)


def expert_onehot(expert_ids):
    expert_range = jnp.arange(EXPERTS, dtype=jnp.int32)
    return (expert_ids[:, :, None] == expert_range[None, None, :]).astype(jnp.float32)


def gates_back(gates, gate_grads, expert_ids):
    inner = jnp.sum(gates * gate_grads, axis=1, keepdims=True)
    chosen_grads = gates * (gate_grads - inner)
    return jnp.sum(chosen_grads[:, :, None] * expert_onehot(expert_ids), axis=1)


def slot_gates(gates, pair_kept, expert_ids, slot_token, slot_valid):
    per_expert = jnp.sum((gates * pair_kept)[:, :, None] * expert_onehot(expert_ids), axis=1)
    return jnp.take_along_axis(per_expert.T, slot_token, axis=1) * slot_valid.astype(jnp.float32)


def pick_slots(values, slot_token, slot_valid):
    return jnp.where(slot_valid[:, :, None] > 0, values[slot_token], jnp.zeros((), values.dtype))


def fan_out(slot_values, group_size):
    experts_here, slot_cap, width = slot_values.shape
    spread_out = jnp.broadcast_to(slot_values[:, None], (experts_here, group_size, slot_cap, width))
    return spread_out.reshape(experts_here * group_size, slot_cap, width)


def fold_group(received, group_size):
    count, slot_cap, width = received.shape
    return jnp.sum(received.reshape(count // group_size, group_size, slot_cap, width), axis=1)


def norm_back(normed_grad, gain, normed, inverse):
    scaled = normed_grad * gain
    gain_grad = jnp.sum(normed_grad * normed, axis=0)
    input_grad = inverse * (scaled - normed * jnp.mean(scaled * normed, axis=-1, keepdims=True))
    return (input_grad, gain_grad)


def shards(
    tokens,
    attn_gain,
    kv_weight,
    attn_router,
    query_weight,
    output_weight,
    mlp_gain,
    mlp_router,
    gate_weight,
    up_weight,
    down_weight,
    attn_experts,
    mlp_experts,
    priority,
    cotangent,
):
    devices = lax.axis_size(ALL_AXES)
    halves = lax.axis_size("expert")
    device_index = lax.axis_index(ALL_AXES)
    half_index = lax.axis_index("expert")
    seq_tokens, width = tokens.shape
    own_rows = seq_tokens // halves
    group_size = devices // EXPERTS
    head_cols = query_weight.shape[1]
    local_heads = head_cols // HEAD
    key_cols = KV_HEADS * HEAD
    all_tokens = own_rows * devices
    seq_length = seq_tokens * PIECES
    sequences = all_tokens // seq_length
    slot_cap = (9 * TOPK * own_rows + 8 * EXPERTS - 1) // (8 * EXPERTS)
    slot_rows = devices * slot_cap
    seq_rows = slot_rows // sequences
    my_expert = device_index // group_size
    scale = 1.0 / math.sqrt(HEAD)

    def slot_sums(partial_value):
        return fold_group(
            lax.all_to_all(
                partial_value.astype(jnp.bfloat16),
                ALL_AXES,
                split_axis=0,
                concat_axis=0,
                tiled=True,
            ).astype(jnp.float32),
            group_size,
        )

    start_row = half_index * own_rows
    own_input = lax.dynamic_slice_in_dim(tokens, start_row, own_rows, 0).astype(jnp.float32)
    own_cotangent = lax.dynamic_slice_in_dim(cotangent, start_row, own_rows, 0).astype(jnp.float32)
    own_attn = lax.dynamic_slice_in_dim(attn_experts, start_row, own_rows, 0)
    own_mlp = lax.dynamic_slice_in_dim(mlp_experts, start_row, own_rows, 0)
    own_rank = lax.dynamic_slice_in_dim(priority[0], start_row, own_rows, 0)
    token_order = jnp.arange(own_rows, dtype=jnp.int32)

    kv_rows, kv_width = kv_weight.shape
    id_cols = own_rows * TOPK // kv_rows
    extras = jnp.concatenate(
        [
            attn_gain[:, None],
            mlp_gain[:, None],
            attn_router,
            mlp_router,
            own_attn.reshape(kv_rows, id_cols).astype(jnp.bfloat16),
        ],
        axis=1,
    )
    extra_cols = extras.shape[1]
    extra_pad = -(-extra_cols // 128) * 128
    packed = jnp.concatenate(
        [kv_weight, jnp.pad(extras, ((0, 0), (0, extra_pad - extra_cols)))], axis=1
    )
    gathered = lax.all_gather(packed, ALL_AXES, axis=0, tiled=True)
    kv_full = gathered[:, :kv_width]
    gain_one = gathered[:, kv_width]
    gain_two = gathered[:, kv_width + 1]
    router_one = gathered[:, kv_width + 2 : kv_width + 2 + EXPERTS]
    router_two = gathered[:, kv_width + 2 + EXPERTS : kv_width + 2 + 2 * EXPERTS]
    routes_all = gathered[:, kv_width + 2 + 2 * EXPERTS : kv_width + extra_cols].astype(jnp.int32)
    inverse_one = lax.rsqrt(jnp.mean(own_input * own_input, axis=-1, keepdims=True) + epsilon)
    normed_one = own_input * inverse_one
    attn_input = (normed_one * gain_one.astype(jnp.float32)).astype(jnp.bfloat16)
    attn_logits = jnp.dot(attn_input, router_one, preferred_element_type=jnp.float32)
    seq_input = lax.all_gather(attn_input, GROUP_AXES, axis=0, tiled=True)
    key_value = jnp.dot(attn_input, kv_full, preferred_element_type=jnp.float32)
    own_positions = (device_index * own_rows + token_order) % seq_length
    own_cos, own_sin = rope_tables(own_positions, HEAD)
    own_keys = (
        rotate(key_value[:, :key_cols].reshape(own_rows, KV_HEADS, HEAD), own_cos, own_sin)
        .reshape(own_rows, key_cols)
        .astype(jnp.bfloat16)
    )
    own_values = key_value[:, key_cols:].astype(jnp.bfloat16)

    def spread(values):
        shaped = values.reshape(own_rows, 1, group_size, head_cols)
        return jnp.broadcast_to(shaped, (own_rows, EXPERTS, group_size, head_cols)).reshape(
            own_rows, devices, head_cols
        )

    head_keys, head_values = (
        lax.all_to_all(
            spread(own_keys), ALL_AXES, split_axis=1, concat_axis=0, tiled=True
        ),
        lax.all_to_all(
            spread(own_values), ALL_AXES, split_axis=1, concat_axis=0, tiled=True
        ),
    )
    seq_keys = head_keys.reshape(sequences, seq_length, local_heads, HEAD)
    seq_values = head_values.reshape(sequences, seq_length, local_heads, HEAD)
    attn_places, attn_kept, attn_token, attn_valid = slot_table(own_attn, token_order, slot_cap)
    mlp_places, mlp_kept, mlp_token, mlp_valid = slot_table(own_mlp, own_rank, slot_cap)
    block_routes = routes_all.reshape(devices, own_rows, TOPK)
    dest_tables = jax.vmap(lambda block_ids: slot_table(block_ids, token_order, slot_cap)[2])(
        block_routes
    )
    dest_token = jnp.take(dest_tables, my_expert, axis=1)
    attn_rows = lax.all_to_all(
        fan_out(pick_slots(attn_input, attn_token, attn_valid), group_size),
        ALL_AXES,
        split_axis=0,
        concat_axis=0,
        tiled=True,
    ).reshape(slot_rows, width)
    queries = jnp.dot(attn_rows, query_weight, preferred_element_type=jnp.float32)
    slot_positions = (
        (jnp.arange(devices, dtype=jnp.int32)[:, None] * own_rows + dest_token) % seq_length
    ).reshape(slot_rows)
    slot_cos, slot_sin = rope_tables(slot_positions, HEAD)
    rotated = rotate(queries.reshape(slot_rows, local_heads, HEAD), slot_cos, slot_sin).astype(
        jnp.bfloat16
    )
    seq_queries = rotated.reshape(sequences, seq_rows, local_heads, HEAD)
    query_blocks = (slot_positions // BLOCK).reshape(sequences, seq_rows)
    key_blocks = jnp.arange(seq_length, dtype=jnp.int32) // BLOCK

    def seq_scores(query_part, key_part, block_part):
        scores = (
            jnp.einsum("rhd,khd->hrk", query_part, key_part, preferred_element_type=jnp.float32)
            * scale
        )
        allowed = key_blocks[None, :] <= block_part[:, None]
        return jnp.where(allowed[None], scores, masked_score)

    def attend_forward(inputs):
        query_part, key_part, value_part, block_part = inputs
        scores = seq_scores(query_part, key_part, block_part)
        largest = jnp.max(scores, axis=-1, keepdims=True)
        weights = jnp.exp(scores - largest)
        totals = jnp.sum(weights, axis=-1, keepdims=True)
        probs = weights / totals
        mixed_part = jnp.einsum(
            "hrk,khd->rhd",
            probs.astype(jnp.bfloat16),
            value_part,
            preferred_element_type=jnp.float32,
        )
        return (mixed_part.astype(jnp.bfloat16), largest + jnp.log(totals))

    attn_mixed, log_totals = lax.map(
        attend_forward, (seq_queries, seq_keys, seq_values, query_blocks)
    )
    mixed_rows = attn_mixed.reshape(slot_rows, head_cols)
    attn_partial = jnp.dot(mixed_rows, output_weight, preferred_element_type=jnp.float32).reshape(
        devices, slot_cap, width
    )
    attn_slots = slot_sums(attn_partial)
    attn_gates = pair_gates(attn_logits, own_attn)
    attn_index, attn_pair_kept = pair_index(own_attn, attn_places, attn_kept, slot_cap)
    attn_picked = attn_slots.reshape(EXPERTS * slot_cap, width)[attn_index]
    hidden_state = own_input + jnp.sum(
        attn_picked * (attn_gates * attn_pair_kept)[:, :, None], axis=1
    )
    inverse_two = lax.rsqrt(jnp.mean(hidden_state * hidden_state, axis=-1, keepdims=True) + epsilon)
    normed_two = hidden_state * inverse_two
    mlp_input = (normed_two * gain_two.astype(jnp.float32)).astype(jnp.bfloat16)
    mlp_logits = jnp.dot(mlp_input, router_two, preferred_element_type=jnp.float32)
    mlp_rows = lax.all_to_all(
        fan_out(pick_slots(mlp_input, mlp_token, mlp_valid), group_size),
        ALL_AXES,
        split_axis=0,
        concat_axis=0,
        tiled=True,
    ).reshape(slot_rows, width)
    gate_pre = jnp.dot(mlp_rows, gate_weight, preferred_element_type=jnp.float32)
    up_pre = jnp.dot(mlp_rows, up_weight, preferred_element_type=jnp.float32)
    activated = jax.nn.silu(gate_pre)
    inner_rows = (activated * up_pre).astype(jnp.bfloat16)
    mlp_partial = jnp.dot(inner_rows, down_weight, preferred_element_type=jnp.float32).reshape(
        devices, slot_cap, width
    )
    mlp_slots = slot_sums(mlp_partial)
    mlp_gates = pair_gates(mlp_logits, own_mlp)
    mlp_index, mlp_pair_kept = pair_index(own_mlp, mlp_places, mlp_kept, slot_cap)
    mlp_picked = mlp_slots.reshape(EXPERTS * slot_cap, width)[mlp_index]
    own_output = hidden_state + jnp.sum(
        mlp_picked * (mlp_gates * mlp_pair_kept)[:, :, None], axis=1
    )
    mlp_gate_grad = jnp.sum(mlp_picked * own_cotangent[:, None, :], axis=-1) * mlp_pair_kept
    mlp_logit_grad = gates_back(mlp_gates, mlp_gate_grad, own_mlp)
    mlp_slot_grad = (
        own_cotangent[mlp_token]
        * slot_gates(mlp_gates, mlp_pair_kept, own_mlp, mlp_token, mlp_valid)[:, :, None]
    ).astype(jnp.bfloat16)
    down_rows = lax.all_to_all(
        fan_out(mlp_slot_grad, group_size),
        ALL_AXES,
        split_axis=0,
        concat_axis=0,
        tiled=True,
    ).reshape(slot_rows, width)
    inner_grad = jnp.einsum("rd,fd->rf", down_rows, down_weight, preferred_element_type=jnp.float32)
    down_grad = jnp.einsum("rf,rd->fd", inner_rows, down_rows, preferred_element_type=jnp.float32)
    sigmoid_gate = jax.nn.sigmoid(gate_pre)
    gate_pre_grad = (
        inner_grad * up_pre * sigmoid_gate * (1.0 + gate_pre * (1.0 - sigmoid_gate))
    ).astype(jnp.bfloat16)
    up_pre_grad = (inner_grad * activated).astype(jnp.bfloat16)
    gate_grad = jnp.einsum("rd,rf->df", mlp_rows, gate_pre_grad, preferred_element_type=jnp.float32)
    up_grad = jnp.einsum("rd,rf->df", mlp_rows, up_pre_grad, preferred_element_type=jnp.float32)
    row_grad = jnp.einsum(
        "rf,df->rd", gate_pre_grad, gate_weight, preferred_element_type=jnp.float32
    ) + jnp.einsum("rf,df->rd", up_pre_grad, up_weight, preferred_element_type=jnp.float32)
    mlp_row_grad = slot_sums(row_grad.reshape(devices, slot_cap, width))
    mlp_input_grad = jnp.sum(
        mlp_row_grad.reshape(EXPERTS * slot_cap, width)[mlp_index] * mlp_pair_kept[:, :, None],
        axis=1,
    )
    mlp_input_grad = mlp_input_grad + jnp.dot(
        mlp_logit_grad, router_two.astype(jnp.float32).T, precision=lax.Precision.HIGHEST
    )
    mlp_router_own = jnp.dot(
        mlp_input.astype(jnp.float32).T, mlp_logit_grad, precision=lax.Precision.HIGHEST
    )
    hidden_grad, gain_two_own = norm_back(
        mlp_input_grad, gain_two.astype(jnp.float32), normed_two, inverse_two
    )
    hidden_grad = hidden_grad + own_cotangent
    attn_gate_grad = jnp.sum(attn_picked * hidden_grad[:, None, :], axis=-1) * attn_pair_kept
    attn_logit_grad = gates_back(attn_gates, attn_gate_grad, own_attn)
    attn_slot_grad = (
        hidden_grad[attn_token]
        * slot_gates(attn_gates, attn_pair_kept, own_attn, attn_token, attn_valid)[:, :, None]
    ).astype(jnp.bfloat16)
    out_rows = lax.all_to_all(
        fan_out(attn_slot_grad, group_size),
        ALL_AXES,
        split_axis=0,
        concat_axis=0,
        tiled=True,
    ).reshape(slot_rows, width)
    output_grad = jnp.einsum("rw,rd->wd", mixed_rows, out_rows, preferred_element_type=jnp.float32)
    mixed_grad = jnp.einsum(
        "rd,wd->rw", out_rows, output_weight, preferred_element_type=jnp.float32
    ).astype(jnp.bfloat16)
    seq_mixed_grad = mixed_grad.reshape(sequences, seq_rows, local_heads, HEAD)

    def attend_backward(inputs):
        query_part, key_part, value_part, block_part, log_part, grad_part = inputs
        probs = jnp.exp(seq_scores(query_part, key_part, block_part) - log_part)
        prob_grad = jnp.einsum(
            "rhd,khd->hrk", grad_part, value_part, preferred_element_type=jnp.float32
        )
        inner = jnp.sum(probs * prob_grad, axis=-1, keepdims=True)
        score_grad = (probs * (prob_grad - inner)).astype(jnp.bfloat16)
        value_grad = jnp.einsum(
            "hrk,rhd->khd",
            probs.astype(jnp.bfloat16),
            grad_part,
            preferred_element_type=jnp.float32,
        )
        key_grad = (
            jnp.einsum("hrk,rhd->khd", score_grad, query_part, preferred_element_type=jnp.float32)
            * scale
        )
        query_part_grad = (
            jnp.einsum("hrk,khd->rhd", score_grad, key_part, preferred_element_type=jnp.float32)
            * scale
        )
        return (query_part_grad, key_grad, value_grad)

    seq_query_grad, seq_key_grad, seq_value_grad = lax.map(
        attend_backward,
        (seq_queries, seq_keys, seq_values, query_blocks, log_totals, seq_mixed_grad),
    )
    query_rot_grad = (
        rotate_back(seq_query_grad.reshape(slot_rows, local_heads, HEAD), slot_cos, slot_sin)
        .reshape(slot_rows, head_cols)
        .astype(jnp.bfloat16)
    )
    query_grad = jnp.einsum(
        "rd,rw->dw", attn_rows, query_rot_grad, preferred_element_type=jnp.float32
    )
    query_row_grad = jnp.einsum(
        "rw,dw->rd", query_rot_grad, query_weight, preferred_element_type=jnp.float32
    )
    attn_row_grad = slot_sums(query_row_grad.reshape(devices, slot_cap, width))
    key_back, value_back = (
        lax.all_to_all(
            seq_key_grad.reshape(devices, own_rows, 1, head_cols).astype(jnp.bfloat16),
            ALL_AXES,
            split_axis=0,
            concat_axis=2,
            tiled=True,
        ).astype(jnp.float32),
        lax.all_to_all(
            seq_value_grad.reshape(devices, own_rows, 1, head_cols).astype(jnp.bfloat16),
            ALL_AXES,
            split_axis=0,
            concat_axis=2,
            tiled=True,
        ).astype(jnp.float32),
    )
    own_key_grad = jnp.sum(key_back.reshape(own_rows, EXPERTS, group_size, head_cols), axis=1)
    own_value_grad = jnp.sum(
        value_back.reshape(own_rows, EXPERTS, group_size, head_cols), axis=1
    ).reshape(own_rows, key_cols)
    kv_own_grad = jnp.concatenate(
        [rotate_back(own_key_grad, own_cos, own_sin).reshape(own_rows, key_cols), own_value_grad],
        axis=1,
    ).astype(jnp.bfloat16)
    attn_input_grad = jnp.sum(
        attn_row_grad.reshape(EXPERTS * slot_cap, width)[attn_index] * attn_pair_kept[:, :, None],
        axis=1,
    )
    attn_input_grad = attn_input_grad + jnp.einsum(
        "rc,dc->rd", kv_own_grad, kv_full, preferred_element_type=jnp.float32
    )
    attn_input_grad = attn_input_grad + jnp.dot(
        attn_logit_grad, router_one.astype(jnp.float32).T, precision=lax.Precision.HIGHEST
    )
    col_block = kv_width // group_size
    kv_col_grad = lax.all_to_all(
        kv_own_grad.reshape(own_rows, group_size, col_block),
        GROUP_AXES,
        split_axis=1,
        concat_axis=0,
        tiled=True,
    ).reshape(own_rows * group_size, col_block)
    kv_col_weight = jnp.einsum(
        "rd,rc->dc", seq_input, kv_col_grad, preferred_element_type=jnp.float32
    )
    attn_router_own = jnp.dot(
        attn_input.astype(jnp.float32).T, attn_logit_grad, precision=lax.Precision.HIGHEST
    )
    input_grad, gain_one_own = norm_back(
        attn_input_grad, gain_one.astype(jnp.float32), normed_one, inverse_one
    )
    input_grad = input_grad + hidden_grad
    grad_extras = jnp.concatenate(
        [gain_one_own[:, None], gain_two_own[:, None], attn_router_own, mlp_router_own], axis=1
    )
    packed_grad = jnp.concatenate(
        [
            kv_col_weight,
            jnp.pad(grad_extras, ((0, 0), (0, extra_pad - grad_extras.shape[1]))),
        ],
        axis=1,
    )
    group_sum = lax.psum_scatter(packed_grad, "grp", scatter_dimension=0, tiled=True)
    dealt = lax.all_to_all(
        group_sum.reshape(group_size, kv_rows, col_block + extra_pad),
        GROUP_AXES,
        split_axis=0,
        concat_axis=0,
        tiled=True,
    )
    kv_grad = jnp.moveaxis(dealt[:, :, :col_block], 0, 1).reshape(kv_rows, kv_width)
    extra_grad = jnp.sum(dealt[:, :, col_block:], axis=0)
    gain_one_grad = extra_grad[:, 0]
    gain_two_grad = extra_grad[:, 1]
    attn_router_grad = extra_grad[:, 2 : 2 + EXPERTS]
    mlp_router_grad = extra_grad[:, 2 + EXPERTS : 2 + 2 * EXPERTS]
    mixed_full, input_full = (
        lax.all_gather(own_output.astype(jnp.bfloat16), "expert", axis=0, tiled=True),
        lax.all_gather(input_grad.astype(jnp.bfloat16), "expert", axis=0, tiled=True),
    )
    return (
        mixed_full,
        input_full,
        gain_one_grad,
        kv_grad,
        attn_router_grad,
        query_grad,
        output_grad,
        gain_two_grad,
        mlp_router_grad,
        gate_grad,
        up_grad,
        down_grad,
    )


def solution(mesh):
    seq_size, halves = mesh.devices.shape
    grouped = jax.sharding.Mesh(
        mesh.devices.reshape(EXPERTS, seq_size // EXPERTS, halves), ALL_AXES
    )
    return jax.shard_map(
        shards,
        mesh=grouped,
        in_specs=(
            P(SEQ_AXES, None),
            P(ALL_AXES),
            P(ALL_AXES, None),
            P(ALL_AXES, None),
            P(None, ALL_AXES),
            P(ALL_AXES, None),
            P(ALL_AXES),
            P(ALL_AXES, None),
            P(None, ALL_AXES),
            P(None, ALL_AXES),
            P(ALL_AXES, None),
            P(SEQ_AXES, None),
            P(SEQ_AXES, None),
            P(SEQ_AXES, None),
            P(SEQ_AXES, None),
        ),
        out_specs=(
            P(SEQ_AXES, None),
            P(SEQ_AXES, None),
            P(ALL_AXES),
            P(ALL_AXES, None),
            P(ALL_AXES, None),
            P(None, ALL_AXES),
            P(ALL_AXES, None),
            P(ALL_AXES),
            P(ALL_AXES, None),
            P(None, ALL_AXES),
            P(None, ALL_AXES),
            P(ALL_AXES, None),
        ),
        check_vma=False,
    )
```

```python
import math

import jax
import jax.numpy as jnp
from jax import lax
from jax.sharding import PartitionSpec as P

ALL_AXES = ("grp", "sub", "expert")
SEQ_AXES = ("grp", "sub")
GROUP_AXES = ("sub", "expert")
KV_HEADS = 16
HEAD = 128
EXPERTS = 8
TOPK = 2
PIECES = 8
BLOCK = 256


epsilon = 1e-06
masked_score = -1e30


def rope_tables(positions, head_size):
    half_size = head_size // 2
    frequency = jnp.exp(
        jnp.arange(half_size, dtype=jnp.float32) * (-2.0 * math.log(10000.0) / head_size)
    )
    angles = positions.astype(jnp.float32)[:, None] * frequency[None, :]
    return (jnp.cos(angles)[:, None, :], jnp.sin(angles)[:, None, :])


def rotate(values, cosines, sines):
    half_size = values.shape[-1] // 2
    first = values[..., :half_size]
    second = values[..., half_size:]
    return jnp.concatenate(
        [first * cosines - second * sines, second * cosines + first * sines], axis=-1
    )


def rotate_back(grads, cosines, sines):
    half_size = grads.shape[-1] // 2
    first = grads[..., :half_size]
    second = grads[..., half_size:]
    return jnp.concatenate(
        [first * cosines + second * sines, second * cosines - first * sines], axis=-1
    )


def slot_table(expert_ids, ranks, slot_cap):
    block_rows = expert_ids.shape[0]
    expert_range = jnp.arange(EXPERTS, dtype=jnp.int32)
    member = jnp.sum(
        (expert_ids[:, :, None] == expert_range[None, None, :]).astype(jnp.int32), axis=1
    )
    earlier = (ranks[:, None] < ranks[None, :]).astype(jnp.int32)
    places = jnp.sum(earlier[:, :, None] * member[:, None, :], axis=0)
    kept = member * (places < slot_cap).astype(jnp.int32)
    slot_range = jnp.arange(slot_cap, dtype=jnp.int32)
    landing = kept[:, :, None] * (places[:, :, None] == slot_range[None, None, :]).astype(jnp.int32)
    row_range = jnp.arange(block_rows, dtype=jnp.int32)
    slot_token = jnp.sum(landing * row_range[:, None, None], axis=0)
    slot_valid = jnp.sum(landing, axis=0)
    return (places, kept, slot_token, slot_valid)


def pair_index(expert_ids, places, kept, slot_cap):
    chosen_place = jnp.take_along_axis(places, expert_ids, axis=1)
    chosen_kept = jnp.take_along_axis(kept, expert_ids, axis=1)
    return (
        expert_ids * slot_cap + jnp.minimum(chosen_place, slot_cap - 1),
        chosen_kept.astype(jnp.float32),
    )


def pair_gates(logits, expert_ids):
    return jax.nn.softmax(jnp.take_along_axis(logits, expert_ids, axis=1), axis=-1)


def expert_onehot(expert_ids):
    expert_range = jnp.arange(EXPERTS, dtype=jnp.int32)
    return (expert_ids[:, :, None] == expert_range[None, None, :]).astype(jnp.float32)


def gates_back(gates, gate_grads, expert_ids):
    inner = jnp.sum(gates * gate_grads, axis=1, keepdims=True)
    chosen_grads = gates * (gate_grads - inner)
    return jnp.sum(chosen_grads[:, :, None] * expert_onehot(expert_ids), axis=1)


def slot_gates(gates, pair_kept, expert_ids, slot_token, slot_valid):
    per_expert = jnp.sum((gates * pair_kept)[:, :, None] * expert_onehot(expert_ids), axis=1)
    return jnp.take_along_axis(per_expert.T, slot_token, axis=1) * slot_valid.astype(jnp.float32)


def pick_slots(values, slot_token, slot_valid):
    return jnp.where(slot_valid[:, :, None] > 0, values[slot_token], jnp.zeros((), values.dtype))


def fan_out(slot_values, group_size):
    experts_here, slot_cap, width = slot_values.shape
    spread_out = jnp.broadcast_to(slot_values[:, None], (experts_here, group_size, slot_cap, width))
    return spread_out.reshape(experts_here * group_size, slot_cap, width)


def fold_group(received, group_size):
    count, slot_cap, width = received.shape
    return jnp.sum(received.reshape(count // group_size, group_size, slot_cap, width), axis=1)


def norm_back(normed_grad, gain, normed, inverse):
    scaled = normed_grad * gain
    gain_grad = jnp.sum(normed_grad * normed, axis=0)
    input_grad = inverse * (scaled - normed * jnp.mean(scaled * normed, axis=-1, keepdims=True))
    return (input_grad, gain_grad)


def shards(
    tokens,
    attn_gain,
    kv_weight,
    attn_router,
    query_weight,
    output_weight,
    mlp_gain,
    mlp_router,
    gate_weight,
    up_weight,
    down_weight,
    attn_experts,
    mlp_experts,
    priority,
    cotangent,
):
    devices = lax.axis_size(ALL_AXES)
    halves = lax.axis_size("expert")
    device_index = lax.axis_index(ALL_AXES)
    half_index = lax.axis_index("expert")
    seq_tokens, width = tokens.shape
    own_rows = seq_tokens // halves
    group_size = devices // EXPERTS
    head_cols = query_weight.shape[1]
    local_heads = head_cols // HEAD
    key_cols = KV_HEADS * HEAD
    all_tokens = own_rows * devices
    seq_length = seq_tokens * PIECES
    sequences = all_tokens // seq_length
    slot_cap = (9 * TOPK * own_rows + 8 * EXPERTS - 1) // (8 * EXPERTS)
    slot_rows = devices * slot_cap
    seq_rows = slot_rows // sequences
    my_expert = device_index // group_size
    groups = lax.axis_size("grp")
    head_index = device_index % group_size

    def dispatch(slot_values):
        by_group = lax.all_to_all(slot_values, "grp", split_axis=0, concat_axis=0, tiled=True)
        return lax.all_gather(by_group, GROUP_AXES, axis=0, tiled=True).reshape(slot_rows, width)

    def combine(partial_value):
        parts = lax.all_to_all(
            partial_value.astype(jnp.bfloat16).reshape(group_size, groups * slot_cap, width),
            GROUP_AXES,
            split_axis=0,
            concat_axis=0,
            tiled=True,
        )
        summed = jnp.sum(parts.astype(jnp.float32), axis=0).reshape(groups, slot_cap, width)
        return lax.all_to_all(summed, "grp", split_axis=0, concat_axis=0, tiled=True)

    def to_gj(rows):
        shaped = rows.reshape((group_size, groups, slot_cap) + rows.shape[1:])
        return jnp.swapaxes(shaped, 0, 1).reshape(rows.shape)

    def to_jg(rows):
        shaped = rows.reshape((groups, group_size, slot_cap) + rows.shape[1:])
        return jnp.swapaxes(shaped, 0, 1).reshape(rows.shape)
    scale = 1.0 / math.sqrt(HEAD)

    start_row = half_index * own_rows
    own_input = lax.dynamic_slice_in_dim(tokens, start_row, own_rows, 0).astype(jnp.float32)
    own_cotangent = lax.dynamic_slice_in_dim(cotangent, start_row, own_rows, 0).astype(jnp.float32)
    own_attn = lax.dynamic_slice_in_dim(attn_experts, start_row, own_rows, 0)
    own_mlp = lax.dynamic_slice_in_dim(mlp_experts, start_row, own_rows, 0)
    own_rank = lax.dynamic_slice_in_dim(priority[0], start_row, own_rows, 0)
    token_order = jnp.arange(own_rows, dtype=jnp.int32)

    kv_rows, kv_width = kv_weight.shape
    id_cols = own_rows * TOPK // kv_rows
    extras = jnp.concatenate(
        [
            attn_gain[:, None],
            mlp_gain[:, None],
            attn_router,
            mlp_router,
            own_attn.reshape(kv_rows, id_cols).astype(jnp.bfloat16),
        ],
        axis=1,
    )
    extra_cols = extras.shape[1]
    extra_pad = -(-extra_cols // 128) * 128
    packed = jnp.concatenate(
        [kv_weight, jnp.pad(extras, ((0, 0), (0, extra_pad - extra_cols)))], axis=1
    )
    gathered = lax.all_gather(
        lax.all_gather(packed, "grp", axis=0, tiled=True), GROUP_AXES, axis=0, tiled=True
    )
    gathered = jnp.swapaxes(
        gathered.reshape(group_size, groups, kv_rows, extra_pad + kv_width), 0, 1
    ).reshape(devices * kv_rows, extra_pad + kv_width)
    kv_full = gathered[:, :kv_width]
    gain_one = gathered[:, kv_width]
    gain_two = gathered[:, kv_width + 1]
    router_one = gathered[:, kv_width + 2 : kv_width + 2 + EXPERTS]
    router_two = gathered[:, kv_width + 2 + EXPERTS : kv_width + 2 + 2 * EXPERTS]
    routes_all = gathered[:, kv_width + 2 + 2 * EXPERTS : kv_width + extra_cols].astype(jnp.int32)
    inverse_one = lax.rsqrt(jnp.mean(own_input * own_input, axis=-1, keepdims=True) + epsilon)
    normed_one = own_input * inverse_one
    attn_input = (normed_one * gain_one.astype(jnp.float32)).astype(jnp.bfloat16)
    attn_logits = jnp.dot(attn_input, router_one, preferred_element_type=jnp.float32)
    seq_input = lax.all_gather(attn_input, GROUP_AXES, axis=0, tiled=True)
    own_positions = (device_index * own_rows + token_order) % seq_length
    own_cos, own_sin = rope_tables(own_positions, HEAD)
    head_kv = jnp.concatenate(
        [
            lax.dynamic_slice_in_dim(kv_full, head_index * head_cols, head_cols, axis=1),
            lax.dynamic_slice_in_dim(kv_full, key_cols + head_index * head_cols, head_cols, axis=1),
        ],
        axis=1,
    )
    seq_kv = jnp.dot(seq_input, head_kv, preferred_element_type=jnp.float32)
    seq_cos, seq_sin = rope_tables(jnp.arange(seq_length, dtype=jnp.int32), HEAD)
    seq_pair = jnp.concatenate(
        [
            rotate(seq_kv[:, :head_cols].reshape(seq_length, local_heads, HEAD), seq_cos, seq_sin)
            .reshape(seq_length, head_cols)
            .astype(jnp.bfloat16),
            seq_kv[:, head_cols:].astype(jnp.bfloat16),
        ],
        axis=1,
    )
    all_pairs = lax.all_gather(seq_pair, "grp", axis=0, tiled=True)
    seq_keys = all_pairs[:, :head_cols].reshape(sequences, seq_length, local_heads, HEAD)
    seq_values = all_pairs[:, head_cols:].reshape(sequences, seq_length, local_heads, HEAD)
    attn_places, attn_kept, attn_token, attn_valid = slot_table(own_attn, token_order, slot_cap)
    mlp_places, mlp_kept, mlp_token, mlp_valid = slot_table(own_mlp, own_rank, slot_cap)
    block_routes = routes_all.reshape(devices, own_rows, TOPK)
    dest_tables = jax.vmap(lambda block_ids: slot_table(block_ids, token_order, slot_cap)[2])(
        block_routes
    )
    dest_token = jnp.take(dest_tables, my_expert, axis=1)
    attn_rows = dispatch(pick_slots(attn_input, attn_token, attn_valid))
    queries = to_gj(jnp.dot(attn_rows, query_weight, preferred_element_type=jnp.float32))
    slot_positions = (
        (jnp.arange(devices, dtype=jnp.int32)[:, None] * own_rows + dest_token) % seq_length
    ).reshape(slot_rows)
    slot_cos, slot_sin = rope_tables(slot_positions, HEAD)
    rotated = rotate(queries.reshape(slot_rows, local_heads, HEAD), slot_cos, slot_sin).astype(
        jnp.bfloat16
    )
    seq_queries = rotated.reshape(sequences, seq_rows, local_heads, HEAD)
    query_blocks = (slot_positions // BLOCK).reshape(sequences, seq_rows)
    key_blocks = jnp.arange(seq_length, dtype=jnp.int32) // BLOCK

    def seq_scores(query_part, key_part, block_part):
        scores = (
            jnp.einsum("rhd,khd->hrk", query_part, key_part, preferred_element_type=jnp.float32)
            * scale
        )
        allowed = key_blocks[None, :] <= block_part[:, None]
        return jnp.where(allowed[None], scores, masked_score)

    def attend_forward(inputs):
        query_part, key_part, value_part, block_part = inputs
        scores = seq_scores(query_part, key_part, block_part)
        largest = jnp.max(scores, axis=-1, keepdims=True)
        weights = jnp.exp(scores - largest)
        totals = jnp.sum(weights, axis=-1, keepdims=True)
        probs = weights / totals
        mixed_part = jnp.einsum(
            "hrk,khd->rhd",
            probs.astype(jnp.bfloat16),
            value_part,
            preferred_element_type=jnp.float32,
        )
        return (mixed_part.astype(jnp.bfloat16), largest + jnp.log(totals))

    attn_mixed, log_totals = lax.map(
        attend_forward, (seq_queries, seq_keys, seq_values, query_blocks)
    )
    mixed_rows = to_jg(attn_mixed.reshape(slot_rows, head_cols))
    attn_partial = jnp.dot(mixed_rows, output_weight, preferred_element_type=jnp.float32)
    attn_slots = combine(attn_partial)
    attn_gates = pair_gates(attn_logits, own_attn)
    attn_index, attn_pair_kept = pair_index(own_attn, attn_places, attn_kept, slot_cap)
    attn_picked = attn_slots.reshape(EXPERTS * slot_cap, width)[attn_index]
    hidden_state = own_input + jnp.sum(
        attn_picked * (attn_gates * attn_pair_kept)[:, :, None], axis=1
    )
    inverse_two = lax.rsqrt(jnp.mean(hidden_state * hidden_state, axis=-1, keepdims=True) + epsilon)
    normed_two = hidden_state * inverse_two
    mlp_input = (normed_two * gain_two.astype(jnp.float32)).astype(jnp.bfloat16)
    mlp_logits = jnp.dot(mlp_input, router_two, preferred_element_type=jnp.float32)
    mlp_rows = dispatch(pick_slots(mlp_input, mlp_token, mlp_valid))
    gate_pre = jnp.dot(mlp_rows, gate_weight, preferred_element_type=jnp.float32)
    up_pre = jnp.dot(mlp_rows, up_weight, preferred_element_type=jnp.float32)
    activated = jax.nn.silu(gate_pre)
    inner_rows = (activated * up_pre).astype(jnp.bfloat16)
    mlp_partial = jnp.dot(inner_rows, down_weight, preferred_element_type=jnp.float32)
    mlp_slots = combine(mlp_partial)
    mlp_gates = pair_gates(mlp_logits, own_mlp)
    mlp_index, mlp_pair_kept = pair_index(own_mlp, mlp_places, mlp_kept, slot_cap)
    mlp_picked = mlp_slots.reshape(EXPERTS * slot_cap, width)[mlp_index]
    own_output = hidden_state + jnp.sum(
        mlp_picked * (mlp_gates * mlp_pair_kept)[:, :, None], axis=1
    )
    mlp_gate_grad = jnp.sum(mlp_picked * own_cotangent[:, None, :], axis=-1) * mlp_pair_kept
    mlp_logit_grad = gates_back(mlp_gates, mlp_gate_grad, own_mlp)
    mlp_slot_grad = (
        own_cotangent[mlp_token]
        * slot_gates(mlp_gates, mlp_pair_kept, own_mlp, mlp_token, mlp_valid)[:, :, None]
    ).astype(jnp.bfloat16)
    down_rows = dispatch(mlp_slot_grad)
    inner_grad = jnp.einsum("rd,fd->rf", down_rows, down_weight, preferred_element_type=jnp.float32)
    down_grad = jnp.einsum("rf,rd->fd", inner_rows, down_rows, preferred_element_type=jnp.float32)
    sigmoid_gate = jax.nn.sigmoid(gate_pre)
    gate_pre_grad = (
        inner_grad * up_pre * sigmoid_gate * (1.0 + gate_pre * (1.0 - sigmoid_gate))
    ).astype(jnp.bfloat16)
    up_pre_grad = (inner_grad * activated).astype(jnp.bfloat16)
    gate_grad = jnp.einsum("rd,rf->df", mlp_rows, gate_pre_grad, preferred_element_type=jnp.float32)
    up_grad = jnp.einsum("rd,rf->df", mlp_rows, up_pre_grad, preferred_element_type=jnp.float32)
    row_grad = jnp.einsum(
        "rf,df->rd", gate_pre_grad, gate_weight, preferred_element_type=jnp.float32
    ) + jnp.einsum("rf,df->rd", up_pre_grad, up_weight, preferred_element_type=jnp.float32)
    mlp_row_grad = combine(row_grad)
    mlp_input_grad = jnp.sum(
        mlp_row_grad.reshape(EXPERTS * slot_cap, width)[mlp_index] * mlp_pair_kept[:, :, None],
        axis=1,
    )
    mlp_input_grad = mlp_input_grad + jnp.dot(
        mlp_logit_grad, router_two.astype(jnp.float32).T, precision=lax.Precision.HIGHEST
    )
    mlp_router_own = jnp.dot(
        mlp_input.astype(jnp.float32).T, mlp_logit_grad, precision=lax.Precision.HIGHEST
    )
    hidden_grad, gain_two_own = norm_back(
        mlp_input_grad, gain_two.astype(jnp.float32), normed_two, inverse_two
    )
    hidden_grad = hidden_grad + own_cotangent
    attn_gate_grad = jnp.sum(attn_picked * hidden_grad[:, None, :], axis=-1) * attn_pair_kept
    attn_logit_grad = gates_back(attn_gates, attn_gate_grad, own_attn)
    attn_slot_grad = (
        hidden_grad[attn_token]
        * slot_gates(attn_gates, attn_pair_kept, own_attn, attn_token, attn_valid)[:, :, None]
    ).astype(jnp.bfloat16)
    out_rows = dispatch(attn_slot_grad)
    output_grad = jnp.einsum("rw,rd->wd", mixed_rows, out_rows, preferred_element_type=jnp.float32)
    mixed_grad = jnp.einsum(
        "rd,wd->rw", out_rows, output_weight, preferred_element_type=jnp.float32
    ).astype(jnp.bfloat16)
    seq_mixed_grad = to_gj(mixed_grad).reshape(sequences, seq_rows, local_heads, HEAD)

    def attend_backward(inputs):
        query_part, key_part, value_part, block_part, log_part, grad_part = inputs
        probs = jnp.exp(seq_scores(query_part, key_part, block_part) - log_part)
        prob_grad = jnp.einsum(
            "rhd,khd->hrk", grad_part, value_part, preferred_element_type=jnp.float32
        )
        inner = jnp.sum(probs * prob_grad, axis=-1, keepdims=True)
        score_grad = (probs * (prob_grad - inner)).astype(jnp.bfloat16)
        value_grad = jnp.einsum(
            "hrk,rhd->khd",
            probs.astype(jnp.bfloat16),
            grad_part,
            preferred_element_type=jnp.float32,
        )
        key_grad = (
            jnp.einsum("hrk,rhd->khd", score_grad, query_part, preferred_element_type=jnp.float32)
            * scale
        )
        query_part_grad = (
            jnp.einsum("hrk,khd->rhd", score_grad, key_part, preferred_element_type=jnp.float32)
            * scale
        )
        return (query_part_grad, key_grad, value_grad)

    seq_query_grad, seq_key_grad, seq_value_grad = lax.map(
        attend_backward,
        (seq_queries, seq_keys, seq_values, query_blocks, log_totals, seq_mixed_grad),
    )
    query_rot_grad = to_jg(
        rotate_back(seq_query_grad.reshape(slot_rows, local_heads, HEAD), slot_cos, slot_sin)
        .reshape(slot_rows, head_cols)
        .astype(jnp.bfloat16)
    )
    query_grad = jnp.einsum(
        "rd,rw->dw", attn_rows, query_rot_grad, preferred_element_type=jnp.float32
    )
    query_row_grad = jnp.einsum(
        "rw,dw->rd", query_rot_grad, query_weight, preferred_element_type=jnp.float32
    )
    attn_row_grad = combine(query_row_grad)
    key_back, value_back = (
        lax.all_to_all(
            seq_key_grad.reshape(devices, own_rows, 1, head_cols).astype(jnp.bfloat16),
            ALL_AXES,
            split_axis=0,
            concat_axis=2,
            tiled=True,
        ).astype(jnp.float32),
        lax.all_to_all(
            seq_value_grad.reshape(devices, own_rows, 1, head_cols).astype(jnp.bfloat16),
            ALL_AXES,
            split_axis=0,
            concat_axis=2,
            tiled=True,
        ).astype(jnp.float32),
    )
    own_key_grad = jnp.sum(key_back.reshape(own_rows, EXPERTS, group_size, head_cols), axis=1)
    own_value_grad = jnp.sum(
        value_back.reshape(own_rows, EXPERTS, group_size, head_cols), axis=1
    ).reshape(own_rows, key_cols)
    kv_own_grad = jnp.concatenate(
        [rotate_back(own_key_grad, own_cos, own_sin).reshape(own_rows, key_cols), own_value_grad],
        axis=1,
    ).astype(jnp.bfloat16)
    attn_input_grad = jnp.sum(
        attn_row_grad.reshape(EXPERTS * slot_cap, width)[attn_index] * attn_pair_kept[:, :, None],
        axis=1,
    )
    attn_input_grad = attn_input_grad + jnp.einsum(
        "rc,dc->rd", kv_own_grad, kv_full, preferred_element_type=jnp.float32
    )
    attn_input_grad = attn_input_grad + jnp.dot(
        attn_logit_grad, router_one.astype(jnp.float32).T, precision=lax.Precision.HIGHEST
    )
    col_block = kv_width // group_size
    kv_col_grad = lax.all_to_all(
        kv_own_grad.reshape(own_rows, group_size, col_block),
        GROUP_AXES,
        split_axis=1,
        concat_axis=0,
        tiled=True,
    ).reshape(own_rows * group_size, col_block)
    kv_col_weight = jnp.einsum(
        "rd,rc->dc", seq_input, kv_col_grad, preferred_element_type=jnp.float32
    )
    attn_router_own = jnp.dot(
        attn_input.astype(jnp.float32).T, attn_logit_grad, precision=lax.Precision.HIGHEST
    )
    input_grad, gain_one_own = norm_back(
        attn_input_grad, gain_one.astype(jnp.float32), normed_one, inverse_one
    )
    input_grad = input_grad + hidden_grad
    grad_extras = jnp.concatenate(
        [gain_one_own[:, None], gain_two_own[:, None], attn_router_own, mlp_router_own], axis=1
    )
    packed_grad = jnp.concatenate(
        [
            kv_col_weight,
            jnp.pad(grad_extras, ((0, 0), (0, extra_pad - grad_extras.shape[1]))),
        ],
        axis=1,
    )
    group_sum = lax.psum_scatter(packed_grad, "grp", scatter_dimension=0, tiled=True)
    dealt = lax.all_to_all(
        group_sum.reshape(group_size, kv_rows, col_block + extra_pad),
        GROUP_AXES,
        split_axis=0,
        concat_axis=0,
        tiled=True,
    )
    kv_grad = jnp.moveaxis(dealt[:, :, :col_block], 0, 1).reshape(kv_rows, kv_width)
    extra_grad = jnp.sum(dealt[:, :, col_block:], axis=0)
    gain_one_grad = extra_grad[:, 0]
    gain_two_grad = extra_grad[:, 1]
    attn_router_grad = extra_grad[:, 2 : 2 + EXPERTS]
    mlp_router_grad = extra_grad[:, 2 + EXPERTS : 2 + 2 * EXPERTS]
    mixed_full, input_full = (
        lax.all_gather(own_output.astype(jnp.bfloat16), "expert", axis=0, tiled=True),
        lax.all_gather(input_grad.astype(jnp.bfloat16), "expert", axis=0, tiled=True),
    )
    return (
        mixed_full,
        input_full,
        gain_one_grad,
        kv_grad,
        attn_router_grad,
        query_grad,
        output_grad,
        gain_two_grad,
        mlp_router_grad,
        gate_grad,
        up_grad,
        down_grad,
    )


def solution(mesh):
    seq_size, halves = mesh.devices.shape
    grouped = jax.sharding.Mesh(
        mesh.devices.reshape(EXPERTS, seq_size // EXPERTS, halves), ALL_AXES
    )
    return jax.shard_map(
        shards,
        mesh=grouped,
        in_specs=(
            P(SEQ_AXES, None),
            P(ALL_AXES),
            P(ALL_AXES, None),
            P(ALL_AXES, None),
            P(None, ALL_AXES),
            P(ALL_AXES, None),
            P(ALL_AXES),
            P(ALL_AXES, None),
            P(None, ALL_AXES),
            P(None, ALL_AXES),
            P(ALL_AXES, None),
            P(SEQ_AXES, None),
            P(SEQ_AXES, None),
            P(SEQ_AXES, None),
            P(SEQ_AXES, None),
        ),
        out_specs=(
            P(SEQ_AXES, None),
            P(SEQ_AXES, None),
            P(ALL_AXES),
            P(ALL_AXES, None),
            P(ALL_AXES, None),
            P(None, ALL_AXES),
            P(ALL_AXES, None),
            P(ALL_AXES),
            P(ALL_AXES, None),
            P(None, ALL_AXES),
            P(None, ALL_AXES),
            P(ALL_AXES, None),
        ),
        check_vma=False,
    )
```

```python
import math

import jax
import jax.numpy as jnp
from jax import lax
from jax.sharding import PartitionSpec as P

ALL_AXES = ("grp", "sub", "expert")
SEQ_AXES = ("grp", "sub")
GROUP_AXES = ("sub", "expert")
KV_HEADS = 16
HEAD = 128
EXPERTS = 8
TOPK = 2
PIECES = 8
BLOCK = 256


epsilon = 1e-06
masked_score = -1e30


def rope_tables(positions, head_size):
    half_size = head_size // 2
    frequency = jnp.exp(
        jnp.arange(half_size, dtype=jnp.float32) * (-2.0 * math.log(10000.0) / head_size)
    )
    angles = positions.astype(jnp.float32)[:, None] * frequency[None, :]
    return (jnp.cos(angles)[:, None, :], jnp.sin(angles)[:, None, :])


def rotate(values, cosines, sines):
    half_size = values.shape[-1] // 2
    first = values[..., :half_size]
    second = values[..., half_size:]
    return jnp.concatenate(
        [first * cosines - second * sines, second * cosines + first * sines], axis=-1
    )


def rotate_back(grads, cosines, sines):
    half_size = grads.shape[-1] // 2
    first = grads[..., :half_size]
    second = grads[..., half_size:]
    return jnp.concatenate(
        [first * cosines + second * sines, second * cosines - first * sines], axis=-1
    )


def slot_table(expert_ids, ranks, slot_cap):
    block_rows = expert_ids.shape[0]
    expert_range = jnp.arange(EXPERTS, dtype=jnp.int32)
    member = jnp.sum(
        (expert_ids[:, :, None] == expert_range[None, None, :]).astype(jnp.int32), axis=1
    )
    earlier = (ranks[:, None] < ranks[None, :]).astype(jnp.int32)
    places = jnp.sum(earlier[:, :, None] * member[:, None, :], axis=0)
    kept = member * (places < slot_cap).astype(jnp.int32)
    slot_range = jnp.arange(slot_cap, dtype=jnp.int32)
    landing = kept[:, :, None] * (places[:, :, None] == slot_range[None, None, :]).astype(jnp.int32)
    row_range = jnp.arange(block_rows, dtype=jnp.int32)
    slot_token = jnp.sum(landing * row_range[:, None, None], axis=0)
    slot_valid = jnp.sum(landing, axis=0)
    return (places, kept, slot_token, slot_valid)


def pair_index(expert_ids, places, kept, slot_cap):
    chosen_place = jnp.take_along_axis(places, expert_ids, axis=1)
    chosen_kept = jnp.take_along_axis(kept, expert_ids, axis=1)
    return (
        expert_ids * slot_cap + jnp.minimum(chosen_place, slot_cap - 1),
        chosen_kept.astype(jnp.float32),
    )


def pair_gates(logits, expert_ids):
    return jax.nn.softmax(jnp.take_along_axis(logits, expert_ids, axis=1), axis=-1)


def expert_onehot(expert_ids):
    expert_range = jnp.arange(EXPERTS, dtype=jnp.int32)
    return (expert_ids[:, :, None] == expert_range[None, None, :]).astype(jnp.float32)


def gates_back(gates, gate_grads, expert_ids):
    inner = jnp.sum(gates * gate_grads, axis=1, keepdims=True)
    chosen_grads = gates * (gate_grads - inner)
    return jnp.sum(chosen_grads[:, :, None] * expert_onehot(expert_ids), axis=1)


def slot_gates(gates, pair_kept, expert_ids, slot_token, slot_valid):
    per_expert = jnp.sum((gates * pair_kept)[:, :, None] * expert_onehot(expert_ids), axis=1)
    return jnp.take_along_axis(per_expert.T, slot_token, axis=1) * slot_valid.astype(jnp.float32)


def pick_slots(values, slot_token, slot_valid):
    return jnp.where(slot_valid[:, :, None] > 0, values[slot_token], jnp.zeros((), values.dtype))


def fan_out(slot_values, group_size):
    experts_here, slot_cap, width = slot_values.shape
    spread_out = jnp.broadcast_to(slot_values[:, None], (experts_here, group_size, slot_cap, width))
    return spread_out.reshape(experts_here * group_size, slot_cap, width)


def fold_group(received, group_size):
    count, slot_cap, width = received.shape
    return jnp.sum(received.reshape(count // group_size, group_size, slot_cap, width), axis=1)


def norm_back(normed_grad, gain, normed, inverse):
    scaled = normed_grad * gain
    gain_grad = jnp.sum(normed_grad * normed, axis=0)
    input_grad = inverse * (scaled - normed * jnp.mean(scaled * normed, axis=-1, keepdims=True))
    return (input_grad, gain_grad)


def shards(
    tokens,
    attn_gain,
    kv_weight,
    attn_router,
    query_weight,
    output_weight,
    mlp_gain,
    mlp_router,
    gate_weight,
    up_weight,
    down_weight,
    attn_experts,
    mlp_experts,
    priority,
    cotangent,
):
    devices = lax.axis_size(ALL_AXES)
    halves = lax.axis_size("expert")
    device_index = lax.axis_index(ALL_AXES)
    half_index = lax.axis_index("expert")
    seq_tokens, width = tokens.shape
    own_rows = seq_tokens // halves
    group_size = devices // EXPERTS
    head_cols = query_weight.shape[1]
    local_heads = head_cols // HEAD
    key_cols = KV_HEADS * HEAD
    all_tokens = own_rows * devices
    seq_length = seq_tokens * PIECES
    sequences = all_tokens // seq_length
    slot_cap = (9 * TOPK * own_rows + 8 * EXPERTS - 1) // (8 * EXPERTS)
    slot_rows = devices * slot_cap
    seq_rows = slot_rows // sequences
    my_expert = device_index // group_size
    groups = lax.axis_size("grp")
    head_index = device_index % group_size

    def dispatch(slot_values):
        by_group = lax.all_to_all(slot_values, "grp", split_axis=0, concat_axis=0, tiled=True)
        return lax.all_gather(
            by_group.reshape(groups * slot_cap, width), GROUP_AXES, axis=0, tiled=True
        )

    def combine(partial_value):
        parts = lax.all_to_all(
            partial_value.astype(jnp.bfloat16).reshape(group_size, groups * slot_cap, width),
            GROUP_AXES,
            split_axis=0,
            concat_axis=0,
            tiled=True,
        )
        summed = jnp.sum(parts.astype(jnp.float32), axis=0).reshape(groups, slot_cap, width)
        return lax.all_to_all(summed, "grp", split_axis=0, concat_axis=0, tiled=True)

    def to_gj(rows):
        shaped = rows.reshape((group_size, groups, slot_cap) + rows.shape[1:])
        return jnp.swapaxes(shaped, 0, 1).reshape(rows.shape)

    def to_jg(rows):
        shaped = rows.reshape((groups, group_size, slot_cap) + rows.shape[1:])
        return jnp.swapaxes(shaped, 0, 1).reshape(rows.shape)
    scale = 1.0 / math.sqrt(HEAD)

    start_row = half_index * own_rows
    own_input = lax.dynamic_slice_in_dim(tokens, start_row, own_rows, 0).astype(jnp.float32)
    own_cotangent = lax.dynamic_slice_in_dim(cotangent, start_row, own_rows, 0).astype(jnp.float32)
    own_attn = lax.dynamic_slice_in_dim(attn_experts, start_row, own_rows, 0)
    own_mlp = lax.dynamic_slice_in_dim(mlp_experts, start_row, own_rows, 0)
    own_rank = lax.dynamic_slice_in_dim(priority[0], start_row, own_rows, 0)
    token_order = jnp.arange(own_rows, dtype=jnp.int32)

    kv_rows, kv_width = kv_weight.shape
    id_cols = own_rows * TOPK // kv_rows
    extras = jnp.concatenate(
        [
            attn_gain[:, None],
            mlp_gain[:, None],
            attn_router,
            mlp_router,
            own_attn.reshape(kv_rows, id_cols).astype(jnp.bfloat16),
        ],
        axis=1,
    )
    extra_cols = extras.shape[1]
    extra_pad = -(-extra_cols // 128) * 128
    packed = jnp.concatenate(
        [kv_weight, jnp.pad(extras, ((0, 0), (0, extra_pad - extra_cols)))], axis=1
    )
    gathered = lax.all_gather(
        lax.all_gather(packed, "grp", axis=0, tiled=True), GROUP_AXES, axis=0, tiled=True
    )
    gathered = jnp.swapaxes(
        gathered.reshape(group_size, groups, kv_rows, extra_pad + kv_width), 0, 1
    ).reshape(devices * kv_rows, extra_pad + kv_width)
    kv_full = gathered[:, :kv_width]
    gain_one = gathered[:, kv_width]
    gain_two = gathered[:, kv_width + 1]
    router_one = gathered[:, kv_width + 2 : kv_width + 2 + EXPERTS]
    router_two = gathered[:, kv_width + 2 + EXPERTS : kv_width + 2 + 2 * EXPERTS]
    routes_all = gathered[:, kv_width + 2 + 2 * EXPERTS : kv_width + extra_cols].astype(jnp.int32)
    inverse_one = lax.rsqrt(jnp.mean(own_input * own_input, axis=-1, keepdims=True) + epsilon)
    normed_one = own_input * inverse_one
    attn_input = (normed_one * gain_one.astype(jnp.float32)).astype(jnp.bfloat16)
    attn_logits = jnp.dot(attn_input, router_one, preferred_element_type=jnp.float32)
    seq_input = lax.all_gather(attn_input, GROUP_AXES, axis=0, tiled=True)
    own_positions = (device_index * own_rows + token_order) % seq_length
    own_cos, own_sin = rope_tables(own_positions, HEAD)
    head_kv = jnp.concatenate(
        [
            lax.dynamic_slice_in_dim(kv_full, head_index * head_cols, head_cols, axis=1),
            lax.dynamic_slice_in_dim(kv_full, key_cols + head_index * head_cols, head_cols, axis=1),
        ],
        axis=1,
    )
    seq_kv = jnp.dot(seq_input, head_kv, preferred_element_type=jnp.float32)
    seq_cos, seq_sin = rope_tables(jnp.arange(seq_length, dtype=jnp.int32), HEAD)
    seq_pair = jnp.concatenate(
        [
            rotate(seq_kv[:, :head_cols].reshape(seq_length, local_heads, HEAD), seq_cos, seq_sin)
            .reshape(seq_length, head_cols)
            .astype(jnp.bfloat16),
            seq_kv[:, head_cols:].astype(jnp.bfloat16),
        ],
        axis=1,
    )
    all_pairs = lax.all_gather(seq_pair, "grp", axis=0, tiled=True)
    seq_keys = all_pairs[:, :head_cols].reshape(sequences, seq_length, local_heads, HEAD)
    seq_values = all_pairs[:, head_cols:].reshape(sequences, seq_length, local_heads, HEAD)
    attn_places, attn_kept, attn_token, attn_valid = slot_table(own_attn, token_order, slot_cap)
    mlp_places, mlp_kept, mlp_token, mlp_valid = slot_table(own_mlp, own_rank, slot_cap)
    block_routes = routes_all.reshape(devices, own_rows, TOPK)
    dest_tables = jax.vmap(lambda block_ids: slot_table(block_ids, token_order, slot_cap)[2])(
        block_routes
    )
    dest_token = jnp.take(dest_tables, my_expert, axis=1)
    attn_rows = dispatch(pick_slots(attn_input, attn_token, attn_valid))
    queries = to_gj(jnp.dot(attn_rows, query_weight, preferred_element_type=jnp.float32))
    slot_positions = (
        (jnp.arange(devices, dtype=jnp.int32)[:, None] * own_rows + dest_token) % seq_length
    ).reshape(slot_rows)
    slot_cos, slot_sin = rope_tables(slot_positions, HEAD)
    rotated = rotate(queries.reshape(slot_rows, local_heads, HEAD), slot_cos, slot_sin).astype(
        jnp.bfloat16
    )
    seq_queries = rotated.reshape(sequences, seq_rows, local_heads, HEAD)
    query_blocks = (slot_positions // BLOCK).reshape(sequences, seq_rows)
    key_blocks = jnp.arange(seq_length, dtype=jnp.int32) // BLOCK

    def seq_scores(query_part, key_part, block_part):
        scores = (
            jnp.einsum("rhd,khd->hrk", query_part, key_part, preferred_element_type=jnp.float32)
            * scale
        )
        allowed = key_blocks[None, :] <= block_part[:, None]
        return jnp.where(allowed[None], scores, masked_score)

    def attend_forward(inputs):
        query_part, key_part, value_part, block_part = inputs
        scores = seq_scores(query_part, key_part, block_part)
        largest = jnp.max(scores, axis=-1, keepdims=True)
        weights = jnp.exp(scores - largest)
        totals = jnp.sum(weights, axis=-1, keepdims=True)
        probs = weights / totals
        mixed_part = jnp.einsum(
            "hrk,khd->rhd",
            probs.astype(jnp.bfloat16),
            value_part,
            preferred_element_type=jnp.float32,
        )
        return (mixed_part.astype(jnp.bfloat16), largest + jnp.log(totals))

    attn_mixed, log_totals = lax.map(
        attend_forward, (seq_queries, seq_keys, seq_values, query_blocks)
    )
    mixed_rows = to_jg(attn_mixed.reshape(slot_rows, head_cols))
    attn_partial = jnp.dot(mixed_rows, output_weight, preferred_element_type=jnp.float32)
    attn_slots = combine(attn_partial)
    attn_gates = pair_gates(attn_logits, own_attn)
    attn_index, attn_pair_kept = pair_index(own_attn, attn_places, attn_kept, slot_cap)
    attn_picked = attn_slots.reshape(EXPERTS * slot_cap, width)[attn_index]
    hidden_state = own_input + jnp.sum(
        attn_picked * (attn_gates * attn_pair_kept)[:, :, None], axis=1
    )
    inverse_two = lax.rsqrt(jnp.mean(hidden_state * hidden_state, axis=-1, keepdims=True) + epsilon)
    normed_two = hidden_state * inverse_two
    mlp_input = (normed_two * gain_two.astype(jnp.float32)).astype(jnp.bfloat16)
    mlp_logits = jnp.dot(mlp_input, router_two, preferred_element_type=jnp.float32)
    mlp_rows = dispatch(pick_slots(mlp_input, mlp_token, mlp_valid))
    gate_pre = jnp.dot(mlp_rows, gate_weight, preferred_element_type=jnp.float32)
    up_pre = jnp.dot(mlp_rows, up_weight, preferred_element_type=jnp.float32)
    activated = jax.nn.silu(gate_pre)
    inner_rows = (activated * up_pre).astype(jnp.bfloat16)
    mlp_partial = jnp.dot(inner_rows, down_weight, preferred_element_type=jnp.float32)
    mlp_slots = combine(mlp_partial)
    mlp_gates = pair_gates(mlp_logits, own_mlp)
    mlp_index, mlp_pair_kept = pair_index(own_mlp, mlp_places, mlp_kept, slot_cap)
    mlp_picked = mlp_slots.reshape(EXPERTS * slot_cap, width)[mlp_index]
    own_output = hidden_state + jnp.sum(
        mlp_picked * (mlp_gates * mlp_pair_kept)[:, :, None], axis=1
    )
    mlp_gate_grad = jnp.sum(mlp_picked * own_cotangent[:, None, :], axis=-1) * mlp_pair_kept
    mlp_logit_grad = gates_back(mlp_gates, mlp_gate_grad, own_mlp)
    mlp_slot_grad = (
        own_cotangent[mlp_token]
        * slot_gates(mlp_gates, mlp_pair_kept, own_mlp, mlp_token, mlp_valid)[:, :, None]
    ).astype(jnp.bfloat16)
    down_rows = dispatch(mlp_slot_grad)
    inner_grad = jnp.einsum("rd,fd->rf", down_rows, down_weight, preferred_element_type=jnp.float32)
    down_grad = jnp.einsum("rf,rd->fd", inner_rows, down_rows, preferred_element_type=jnp.float32)
    sigmoid_gate = jax.nn.sigmoid(gate_pre)
    gate_pre_grad = (
        inner_grad * up_pre * sigmoid_gate * (1.0 + gate_pre * (1.0 - sigmoid_gate))
    ).astype(jnp.bfloat16)
    up_pre_grad = (inner_grad * activated).astype(jnp.bfloat16)
    gate_grad = jnp.einsum("rd,rf->df", mlp_rows, gate_pre_grad, preferred_element_type=jnp.float32)
    up_grad = jnp.einsum("rd,rf->df", mlp_rows, up_pre_grad, preferred_element_type=jnp.float32)
    row_grad = jnp.einsum(
        "rf,df->rd", gate_pre_grad, gate_weight, preferred_element_type=jnp.float32
    ) + jnp.einsum("rf,df->rd", up_pre_grad, up_weight, preferred_element_type=jnp.float32)
    mlp_row_grad = combine(row_grad)
    mlp_input_grad = jnp.sum(
        mlp_row_grad.reshape(EXPERTS * slot_cap, width)[mlp_index] * mlp_pair_kept[:, :, None],
        axis=1,
    )
    mlp_input_grad = mlp_input_grad + jnp.dot(
        mlp_logit_grad, router_two.astype(jnp.float32).T, precision=lax.Precision.HIGHEST
    )
    mlp_router_own = jnp.dot(
        mlp_input.astype(jnp.float32).T, mlp_logit_grad, precision=lax.Precision.HIGHEST
    )
    hidden_grad, gain_two_own = norm_back(
        mlp_input_grad, gain_two.astype(jnp.float32), normed_two, inverse_two
    )
    hidden_grad = hidden_grad + own_cotangent
    attn_gate_grad = jnp.sum(attn_picked * hidden_grad[:, None, :], axis=-1) * attn_pair_kept
    attn_logit_grad = gates_back(attn_gates, attn_gate_grad, own_attn)
    attn_slot_grad = (
        hidden_grad[attn_token]
        * slot_gates(attn_gates, attn_pair_kept, own_attn, attn_token, attn_valid)[:, :, None]
    ).astype(jnp.bfloat16)
    out_rows = dispatch(attn_slot_grad)
    output_grad = jnp.einsum("rw,rd->wd", mixed_rows, out_rows, preferred_element_type=jnp.float32)
    mixed_grad = jnp.einsum(
        "rd,wd->rw", out_rows, output_weight, preferred_element_type=jnp.float32
    ).astype(jnp.bfloat16)
    seq_mixed_grad = to_gj(mixed_grad).reshape(sequences, seq_rows, local_heads, HEAD)

    def attend_backward(inputs):
        query_part, key_part, value_part, block_part, log_part, grad_part = inputs
        probs = jnp.exp(seq_scores(query_part, key_part, block_part) - log_part)
        prob_grad = jnp.einsum(
            "rhd,khd->hrk", grad_part, value_part, preferred_element_type=jnp.float32
        )
        inner = jnp.sum(probs * prob_grad, axis=-1, keepdims=True)
        score_grad = (probs * (prob_grad - inner)).astype(jnp.bfloat16)
        value_grad = jnp.einsum(
            "hrk,rhd->khd",
            probs.astype(jnp.bfloat16),
            grad_part,
            preferred_element_type=jnp.float32,
        )
        key_grad = (
            jnp.einsum("hrk,rhd->khd", score_grad, query_part, preferred_element_type=jnp.float32)
            * scale
        )
        query_part_grad = (
            jnp.einsum("hrk,khd->rhd", score_grad, key_part, preferred_element_type=jnp.float32)
            * scale
        )
        return (query_part_grad, key_grad, value_grad)

    seq_query_grad, seq_key_grad, seq_value_grad = lax.map(
        attend_backward,
        (seq_queries, seq_keys, seq_values, query_blocks, log_totals, seq_mixed_grad),
    )
    query_rot_grad = to_jg(
        rotate_back(seq_query_grad.reshape(slot_rows, local_heads, HEAD), slot_cos, slot_sin)
        .reshape(slot_rows, head_cols)
        .astype(jnp.bfloat16)
    )
    query_grad = jnp.einsum(
        "rd,rw->dw", attn_rows, query_rot_grad, preferred_element_type=jnp.float32
    )
    query_row_grad = jnp.einsum(
        "rw,dw->rd", query_rot_grad, query_weight, preferred_element_type=jnp.float32
    )
    attn_row_grad = combine(query_row_grad)
    key_back, value_back = (
        lax.all_to_all(
            seq_key_grad.reshape(devices, own_rows, 1, head_cols).astype(jnp.bfloat16),
            ALL_AXES,
            split_axis=0,
            concat_axis=2,
            tiled=True,
        ).astype(jnp.float32),
        lax.all_to_all(
            seq_value_grad.reshape(devices, own_rows, 1, head_cols).astype(jnp.bfloat16),
            ALL_AXES,
            split_axis=0,
            concat_axis=2,
            tiled=True,
        ).astype(jnp.float32),
    )
    own_key_grad = jnp.sum(key_back.reshape(own_rows, EXPERTS, group_size, head_cols), axis=1)
    own_value_grad = jnp.sum(
        value_back.reshape(own_rows, EXPERTS, group_size, head_cols), axis=1
    ).reshape(own_rows, key_cols)
    kv_own_grad = jnp.concatenate(
        [rotate_back(own_key_grad, own_cos, own_sin).reshape(own_rows, key_cols), own_value_grad],
        axis=1,
    ).astype(jnp.bfloat16)
    attn_input_grad = jnp.sum(
        attn_row_grad.reshape(EXPERTS * slot_cap, width)[attn_index] * attn_pair_kept[:, :, None],
        axis=1,
    )
    attn_input_grad = attn_input_grad + jnp.einsum(
        "rc,dc->rd", kv_own_grad, kv_full, preferred_element_type=jnp.float32
    )
    attn_input_grad = attn_input_grad + jnp.dot(
        attn_logit_grad, router_one.astype(jnp.float32).T, precision=lax.Precision.HIGHEST
    )
    col_block = kv_width // group_size
    kv_col_grad = lax.all_to_all(
        kv_own_grad.reshape(own_rows, group_size, col_block),
        GROUP_AXES,
        split_axis=1,
        concat_axis=0,
        tiled=True,
    ).reshape(own_rows * group_size, col_block)
    kv_col_weight = jnp.einsum(
        "rd,rc->dc", seq_input, kv_col_grad, preferred_element_type=jnp.float32
    )
    attn_router_own = jnp.dot(
        attn_input.astype(jnp.float32).T, attn_logit_grad, precision=lax.Precision.HIGHEST
    )
    input_grad, gain_one_own = norm_back(
        attn_input_grad, gain_one.astype(jnp.float32), normed_one, inverse_one
    )
    input_grad = input_grad + hidden_grad
    grad_extras = jnp.concatenate(
        [gain_one_own[:, None], gain_two_own[:, None], attn_router_own, mlp_router_own], axis=1
    )
    packed_grad = jnp.concatenate(
        [
            kv_col_weight,
            jnp.pad(grad_extras, ((0, 0), (0, extra_pad - grad_extras.shape[1]))),
        ],
        axis=1,
    )
    group_sum = lax.psum_scatter(packed_grad, "grp", scatter_dimension=0, tiled=True)
    dealt = lax.all_to_all(
        group_sum.reshape(group_size, kv_rows, col_block + extra_pad),
        GROUP_AXES,
        split_axis=0,
        concat_axis=0,
        tiled=True,
    )
    kv_grad = jnp.moveaxis(dealt[:, :, :col_block], 0, 1).reshape(kv_rows, kv_width)
    extra_grad = jnp.sum(dealt[:, :, col_block:], axis=0)
    gain_one_grad = extra_grad[:, 0]
    gain_two_grad = extra_grad[:, 1]
    attn_router_grad = extra_grad[:, 2 : 2 + EXPERTS]
    mlp_router_grad = extra_grad[:, 2 + EXPERTS : 2 + 2 * EXPERTS]
    both_full = lax.all_gather(
        jnp.concatenate(
            [own_output.astype(jnp.bfloat16), input_grad.astype(jnp.bfloat16)], axis=1
        ),
        "expert",
        axis=0,
        tiled=True,
    )
    mixed_full, input_full = both_full[:, :width], both_full[:, width:]
    return (
        mixed_full,
        input_full,
        gain_one_grad,
        kv_grad,
        attn_router_grad,
        query_grad,
        output_grad,
        gain_two_grad,
        mlp_router_grad,
        gate_grad,
        up_grad,
        down_grad,
    )


def solution(mesh):
    seq_size, halves = mesh.devices.shape
    grouped = jax.sharding.Mesh(
        mesh.devices.reshape(EXPERTS, seq_size // EXPERTS, halves), ALL_AXES
    )
    return jax.shard_map(
        shards,
        mesh=grouped,
        in_specs=(
            P(SEQ_AXES, None),
            P(ALL_AXES),
            P(ALL_AXES, None),
            P(ALL_AXES, None),
            P(None, ALL_AXES),
            P(ALL_AXES, None),
            P(ALL_AXES),
            P(ALL_AXES, None),
            P(None, ALL_AXES),
            P(None, ALL_AXES),
            P(ALL_AXES, None),
            P(SEQ_AXES, None),
            P(SEQ_AXES, None),
            P(SEQ_AXES, None),
            P(SEQ_AXES, None),
        ),
        out_specs=(
            P(SEQ_AXES, None),
            P(SEQ_AXES, None),
            P(ALL_AXES),
            P(ALL_AXES, None),
            P(ALL_AXES, None),
            P(None, ALL_AXES),
            P(ALL_AXES, None),
            P(ALL_AXES),
            P(ALL_AXES, None),
            P(None, ALL_AXES),
            P(None, ALL_AXES),
            P(ALL_AXES, None),
        ),
        check_vma=False,
    )
```

```python
import functools
import math

import jax
import jax.numpy as jnp
from jax import lax
from jax.experimental import pallas as pl
from jax.sharding import PartitionSpec as P

ALL_AXES = ("grp", "sub", "expert")
SEQ_AXES = ("grp", "sub")
GROUP_AXES = ("sub", "expert")
KV_HEADS = 16
HEAD = 128
EXPERTS = 8
TOPK = 2
PIECES = 8
BLOCK = 256


epsilon = 1e-06
masked_score = -1e30


def _scores(q, k, qb, scale):
    s = lax.dot_general(q, k, (((1,), (1,)), ((), ())), preferred_element_type=jnp.float32) * scale
    kblock = lax.broadcasted_iota(jnp.int32, s.shape, 1) // BLOCK
    return jnp.where(kblock <= qb, s, masked_score)

def _fwd_kernel(scale, q_ref, k_ref, v_ref, qb_ref, o_ref, lse_ref):
    s = _scores(q_ref[...], k_ref[...], qb_ref[...], scale)
    largest = jnp.max(s, axis=-1, keepdims=True)
    weights = jnp.exp(s - largest)
    totals = jnp.sum(weights, axis=-1, keepdims=True)
    probs = weights / totals
    o_ref[...] = jnp.dot(probs.astype(jnp.bfloat16), v_ref[...],
                         preferred_element_type=jnp.float32).astype(o_ref.dtype)
    lse_ref[...] = largest + jnp.log(totals)

def _bwd_kernel(scale, q_ref, k_ref, v_ref, qb_ref, lse_ref, do_ref, dq_ref, dk_ref, dv_ref):
    q = q_ref[...]; k = k_ref[...]; v = v_ref[...]; do = do_ref[...]
    probs = jnp.exp(_scores(q, k, qb_ref[...], scale) - lse_ref[...])
    dp = lax.dot_general(do, v, (((1,), (1,)), ((), ())), preferred_element_type=jnp.float32)
    inner = jnp.sum(probs * dp, axis=-1, keepdims=True)
    ds = (probs * (dp - inner)).astype(jnp.bfloat16)
    dv_ref[...] = lax.dot_general(probs.astype(jnp.bfloat16), do, (((0,), (0,)), ((), ())),
                                  preferred_element_type=jnp.float32)
    dk_ref[...] = lax.dot_general(ds, q, (((0,), (0,)), ((), ())),
                                  preferred_element_type=jnp.float32) * scale
    dq_ref[...] = jnp.dot(ds, k, preferred_element_type=jnp.float32) * scale

def attn_fwd(q, k, v, qb):
    n, rows, d = q.shape; keys = k.shape[1]
    scale = 1.0 / math.sqrt(d)
    rspec = pl.BlockSpec((None, rows, d), lambda i: (i, 0, 0))
    kspec = pl.BlockSpec((None, keys, d), lambda i: (i, 0, 0))
    cspec = pl.BlockSpec((None, rows, 1), lambda i: (i, 0, 0))
    return pl.pallas_call(
        functools.partial(_fwd_kernel, scale),
        grid=(n,),
        in_specs=[rspec, kspec, kspec, cspec],
        out_specs=[rspec, cspec],
        out_shape=[jax.ShapeDtypeStruct((n, rows, d), jnp.bfloat16),
                   jax.ShapeDtypeStruct((n, rows, 1), jnp.float32)],
        cost_estimate=pl.CostEstimate(flops=4 * n * rows * keys * d,
                                      transcendentals=n * rows * keys,
                                      bytes_accessed=2 * n * (2 * rows * d + 2 * keys * d)),
    )(q, k, v, qb)

def attn_bwd(q, k, v, qb, lse, do):
    n, rows, d = q.shape; keys = k.shape[1]
    scale = 1.0 / math.sqrt(d)
    rspec = pl.BlockSpec((None, rows, d), lambda i: (i, 0, 0))
    kspec = pl.BlockSpec((None, keys, d), lambda i: (i, 0, 0))
    cspec = pl.BlockSpec((None, rows, 1), lambda i: (i, 0, 0))
    return pl.pallas_call(
        functools.partial(_bwd_kernel, scale),
        grid=(n,),
        in_specs=[rspec, kspec, kspec, cspec, cspec, rspec],
        out_specs=[rspec, kspec, kspec],
        out_shape=[jax.ShapeDtypeStruct((n, rows, d), jnp.float32),
                   jax.ShapeDtypeStruct((n, keys, d), jnp.float32),
                   jax.ShapeDtypeStruct((n, keys, d), jnp.float32)],
        cost_estimate=pl.CostEstimate(flops=10 * n * rows * keys * d,
                                      transcendentals=n * rows * keys,
                                      bytes_accessed=2 * n * (3 * rows * d + 2 * keys * d) + 8 * n * (rows * d + 2 * keys * d)),
    )(q, k, v, qb, lse, do)


def rope_tables(positions, head_size):
    half_size = head_size // 2
    frequency = jnp.exp(
        jnp.arange(half_size, dtype=jnp.float32) * (-2.0 * math.log(10000.0) / head_size)
    )
    angles = positions.astype(jnp.float32)[:, None] * frequency[None, :]
    return (jnp.cos(angles)[:, None, :], jnp.sin(angles)[:, None, :])


def rotate(values, cosines, sines):
    half_size = values.shape[-1] // 2
    first = values[..., :half_size]
    second = values[..., half_size:]
    return jnp.concatenate(
        [first * cosines - second * sines, second * cosines + first * sines], axis=-1
    )


def rotate_back(grads, cosines, sines):
    half_size = grads.shape[-1] // 2
    first = grads[..., :half_size]
    second = grads[..., half_size:]
    return jnp.concatenate(
        [first * cosines + second * sines, second * cosines - first * sines], axis=-1
    )


def slot_table(expert_ids, ranks, slot_cap):
    block_rows = expert_ids.shape[0]
    expert_range = jnp.arange(EXPERTS, dtype=jnp.int32)
    member = jnp.sum(
        (expert_ids[:, :, None] == expert_range[None, None, :]).astype(jnp.int32), axis=1
    )
    earlier = (ranks[:, None] < ranks[None, :]).astype(jnp.int32)
    places = jnp.sum(earlier[:, :, None] * member[:, None, :], axis=0)
    kept = member * (places < slot_cap).astype(jnp.int32)
    slot_range = jnp.arange(slot_cap, dtype=jnp.int32)
    landing = kept[:, :, None] * (places[:, :, None] == slot_range[None, None, :]).astype(jnp.int32)
    row_range = jnp.arange(block_rows, dtype=jnp.int32)
    slot_token = jnp.sum(landing * row_range[:, None, None], axis=0)
    slot_valid = jnp.sum(landing, axis=0)
    return (places, kept, slot_token, slot_valid)


def pair_index(expert_ids, places, kept, slot_cap):
    chosen_place = jnp.take_along_axis(places, expert_ids, axis=1)
    chosen_kept = jnp.take_along_axis(kept, expert_ids, axis=1)
    return (
        expert_ids * slot_cap + jnp.minimum(chosen_place, slot_cap - 1),
        chosen_kept.astype(jnp.float32),
    )


def pair_gates(logits, expert_ids):
    return jax.nn.softmax(jnp.take_along_axis(logits, expert_ids, axis=1), axis=-1)


def expert_onehot(expert_ids):
    expert_range = jnp.arange(EXPERTS, dtype=jnp.int32)
    return (expert_ids[:, :, None] == expert_range[None, None, :]).astype(jnp.float32)


def gates_back(gates, gate_grads, expert_ids):
    inner = jnp.sum(gates * gate_grads, axis=1, keepdims=True)
    chosen_grads = gates * (gate_grads - inner)
    return jnp.sum(chosen_grads[:, :, None] * expert_onehot(expert_ids), axis=1)


def slot_gates(gates, pair_kept, expert_ids, slot_token, slot_valid):
    per_expert = jnp.sum((gates * pair_kept)[:, :, None] * expert_onehot(expert_ids), axis=1)
    return jnp.take_along_axis(per_expert.T, slot_token, axis=1) * slot_valid.astype(jnp.float32)


def pick_slots(values, slot_token, slot_valid):
    return jnp.where(slot_valid[:, :, None] > 0, values[slot_token], jnp.zeros((), values.dtype))


def fan_out(slot_values, group_size):
    experts_here, slot_cap, width = slot_values.shape
    spread_out = jnp.broadcast_to(slot_values[:, None], (experts_here, group_size, slot_cap, width))
    return spread_out.reshape(experts_here * group_size, slot_cap, width)


def fold_group(received, group_size):
    count, slot_cap, width = received.shape
    return jnp.sum(received.reshape(count // group_size, group_size, slot_cap, width), axis=1)


def norm_back(normed_grad, gain, normed, inverse):
    scaled = normed_grad * gain
    gain_grad = jnp.sum(normed_grad * normed, axis=0)
    input_grad = inverse * (scaled - normed * jnp.mean(scaled * normed, axis=-1, keepdims=True))
    return (input_grad, gain_grad)


def shards(
    tokens,
    attn_gain,
    kv_weight,
    attn_router,
    query_weight,
    output_weight,
    mlp_gain,
    mlp_router,
    gate_weight,
    up_weight,
    down_weight,
    attn_experts,
    mlp_experts,
    priority,
    cotangent,
):
    devices = lax.axis_size(ALL_AXES)
    halves = lax.axis_size("expert")
    device_index = lax.axis_index(ALL_AXES)
    half_index = lax.axis_index("expert")
    seq_tokens, width = tokens.shape
    own_rows = seq_tokens // halves
    group_size = devices // EXPERTS
    head_cols = query_weight.shape[1]
    local_heads = head_cols // HEAD
    key_cols = KV_HEADS * HEAD
    all_tokens = own_rows * devices
    seq_length = seq_tokens * PIECES
    sequences = all_tokens // seq_length
    slot_cap = (9 * TOPK * own_rows + 8 * EXPERTS - 1) // (8 * EXPERTS)
    slot_rows = devices * slot_cap
    seq_rows = slot_rows // sequences
    my_expert = device_index // group_size
    groups = lax.axis_size("grp")
    head_index = device_index % group_size

    def dispatch(slot_values):
        by_group = lax.all_to_all(slot_values, "grp", split_axis=0, concat_axis=0, tiled=True)
        return lax.all_gather(
            by_group.reshape(groups * slot_cap, width), GROUP_AXES, axis=0, tiled=True
        )

    def combine(partial_value):
        parts = lax.all_to_all(
            partial_value.astype(jnp.bfloat16).reshape(group_size, groups * slot_cap, width),
            GROUP_AXES,
            split_axis=0,
            concat_axis=0,
            tiled=True,
        )
        summed = jnp.sum(parts.astype(jnp.float32), axis=0).reshape(groups, slot_cap, width)
        return lax.all_to_all(summed, "grp", split_axis=0, concat_axis=0, tiled=True)

    def to_gj(rows):
        shaped = rows.reshape((group_size, groups, slot_cap) + rows.shape[1:])
        return jnp.swapaxes(shaped, 0, 1).reshape(rows.shape)

    def to_jg(rows):
        shaped = rows.reshape((groups, group_size, slot_cap) + rows.shape[1:])
        return jnp.swapaxes(shaped, 0, 1).reshape(rows.shape)
    scale = 1.0 / math.sqrt(HEAD)

    start_row = half_index * own_rows
    own_input = lax.dynamic_slice_in_dim(tokens, start_row, own_rows, 0).astype(jnp.float32)
    own_cotangent = lax.dynamic_slice_in_dim(cotangent, start_row, own_rows, 0).astype(jnp.float32)
    own_attn = lax.dynamic_slice_in_dim(attn_experts, start_row, own_rows, 0)
    own_mlp = lax.dynamic_slice_in_dim(mlp_experts, start_row, own_rows, 0)
    own_rank = lax.dynamic_slice_in_dim(priority[0], start_row, own_rows, 0)
    token_order = jnp.arange(own_rows, dtype=jnp.int32)

    kv_rows, kv_width = kv_weight.shape
    id_cols = own_rows * TOPK // kv_rows
    extras = jnp.concatenate(
        [
            attn_gain[:, None],
            mlp_gain[:, None],
            attn_router,
            mlp_router,
            own_attn.reshape(kv_rows, id_cols).astype(jnp.bfloat16),
        ],
        axis=1,
    )
    extra_cols = extras.shape[1]
    extra_pad = -(-extra_cols // 128) * 128
    packed = jnp.concatenate(
        [kv_weight, jnp.pad(extras, ((0, 0), (0, extra_pad - extra_cols)))], axis=1
    )
    gathered = lax.all_gather(
        lax.all_gather(packed, "grp", axis=0, tiled=True), GROUP_AXES, axis=0, tiled=True
    )
    gathered = jnp.swapaxes(
        gathered.reshape(group_size, groups, kv_rows, extra_pad + kv_width), 0, 1
    ).reshape(devices * kv_rows, extra_pad + kv_width)
    kv_full = gathered[:, :kv_width]
    gain_one = gathered[:, kv_width]
    gain_two = gathered[:, kv_width + 1]
    router_one = gathered[:, kv_width + 2 : kv_width + 2 + EXPERTS]
    router_two = gathered[:, kv_width + 2 + EXPERTS : kv_width + 2 + 2 * EXPERTS]
    routes_all = gathered[:, kv_width + 2 + 2 * EXPERTS : kv_width + extra_cols].astype(jnp.int32)
    inverse_one = lax.rsqrt(jnp.mean(own_input * own_input, axis=-1, keepdims=True) + epsilon)
    normed_one = own_input * inverse_one
    attn_input = (normed_one * gain_one.astype(jnp.float32)).astype(jnp.bfloat16)
    attn_logits = jnp.dot(attn_input, router_one, preferred_element_type=jnp.float32)
    seq_input = lax.all_gather(attn_input, GROUP_AXES, axis=0, tiled=True)
    own_positions = (device_index * own_rows + token_order) % seq_length
    own_cos, own_sin = rope_tables(own_positions, HEAD)
    head_kv = jnp.concatenate(
        [
            lax.dynamic_slice_in_dim(kv_full, head_index * head_cols, head_cols, axis=1),
            lax.dynamic_slice_in_dim(kv_full, key_cols + head_index * head_cols, head_cols, axis=1),
        ],
        axis=1,
    )
    seq_kv = jnp.dot(seq_input, head_kv, preferred_element_type=jnp.float32)
    seq_cos, seq_sin = rope_tables(jnp.arange(seq_length, dtype=jnp.int32), HEAD)
    seq_pair = jnp.concatenate(
        [
            rotate(seq_kv[:, :head_cols].reshape(seq_length, local_heads, HEAD), seq_cos, seq_sin)
            .reshape(seq_length, head_cols)
            .astype(jnp.bfloat16),
            seq_kv[:, head_cols:].astype(jnp.bfloat16),
        ],
        axis=1,
    )
    all_pairs = lax.all_gather(seq_pair, "grp", axis=0, tiled=True)
    seq_keys = all_pairs[:, :head_cols].reshape(sequences, seq_length, local_heads, HEAD)
    seq_values = all_pairs[:, head_cols:].reshape(sequences, seq_length, local_heads, HEAD)
    attn_places, attn_kept, attn_token, attn_valid = slot_table(own_attn, token_order, slot_cap)
    mlp_places, mlp_kept, mlp_token, mlp_valid = slot_table(own_mlp, own_rank, slot_cap)
    block_routes = routes_all.reshape(devices, own_rows, TOPK)
    dest_tables = jax.vmap(lambda block_ids: slot_table(block_ids, token_order, slot_cap)[2])(
        block_routes
    )
    dest_token = jnp.take(dest_tables, my_expert, axis=1)
    attn_rows = dispatch(pick_slots(attn_input, attn_token, attn_valid))
    queries = to_gj(jnp.dot(attn_rows, query_weight, preferred_element_type=jnp.float32))
    slot_positions = (
        (jnp.arange(devices, dtype=jnp.int32)[:, None] * own_rows + dest_token) % seq_length
    ).reshape(slot_rows)
    slot_cos, slot_sin = rope_tables(slot_positions, HEAD)
    rotated = rotate(queries.reshape(slot_rows, local_heads, HEAD), slot_cos, slot_sin).astype(
        jnp.bfloat16
    )
    seq_queries = rotated.reshape(sequences, seq_rows, local_heads, HEAD)
    query_blocks = (slot_positions // BLOCK).reshape(sequences, seq_rows)
    key_blocks = jnp.arange(seq_length, dtype=jnp.int32) // BLOCK

    attn_mixed, log_totals = attn_fwd(
        seq_queries.reshape(sequences, seq_rows, HEAD),
        seq_keys.reshape(sequences, seq_length, HEAD),
        seq_values.reshape(sequences, seq_length, HEAD),
        query_blocks[:, :, None],
    )
    mixed_rows = to_jg(attn_mixed.reshape(slot_rows, head_cols))
    attn_partial = jnp.dot(mixed_rows, output_weight, preferred_element_type=jnp.float32)
    attn_slots = combine(attn_partial)
    attn_gates = pair_gates(attn_logits, own_attn)
    attn_index, attn_pair_kept = pair_index(own_attn, attn_places, attn_kept, slot_cap)
    attn_picked = attn_slots.reshape(EXPERTS * slot_cap, width)[attn_index]
    hidden_state = own_input + jnp.sum(
        attn_picked * (attn_gates * attn_pair_kept)[:, :, None], axis=1
    )
    inverse_two = lax.rsqrt(jnp.mean(hidden_state * hidden_state, axis=-1, keepdims=True) + epsilon)
    normed_two = hidden_state * inverse_two
    mlp_input = (normed_two * gain_two.astype(jnp.float32)).astype(jnp.bfloat16)
    mlp_logits = jnp.dot(mlp_input, router_two, preferred_element_type=jnp.float32)
    mlp_rows = dispatch(pick_slots(mlp_input, mlp_token, mlp_valid))
    gate_pre = jnp.dot(mlp_rows, gate_weight, preferred_element_type=jnp.float32)
    up_pre = jnp.dot(mlp_rows, up_weight, preferred_element_type=jnp.float32)
    activated = jax.nn.silu(gate_pre)
    inner_rows = (activated * up_pre).astype(jnp.bfloat16)
    mlp_partial = jnp.dot(inner_rows, down_weight, preferred_element_type=jnp.float32)
    mlp_slots = combine(mlp_partial)
    mlp_gates = pair_gates(mlp_logits, own_mlp)
    mlp_index, mlp_pair_kept = pair_index(own_mlp, mlp_places, mlp_kept, slot_cap)
    mlp_picked = mlp_slots.reshape(EXPERTS * slot_cap, width)[mlp_index]
    own_output = hidden_state + jnp.sum(
        mlp_picked * (mlp_gates * mlp_pair_kept)[:, :, None], axis=1
    )
    mlp_gate_grad = jnp.sum(mlp_picked * own_cotangent[:, None, :], axis=-1) * mlp_pair_kept
    mlp_logit_grad = gates_back(mlp_gates, mlp_gate_grad, own_mlp)
    mlp_slot_grad = (
        own_cotangent[mlp_token]
        * slot_gates(mlp_gates, mlp_pair_kept, own_mlp, mlp_token, mlp_valid)[:, :, None]
    ).astype(jnp.bfloat16)
    down_rows = dispatch(mlp_slot_grad)
    inner_grad = jnp.einsum("rd,fd->rf", down_rows, down_weight, preferred_element_type=jnp.float32)
    down_grad = jnp.einsum("rf,rd->fd", inner_rows, down_rows, preferred_element_type=jnp.float32)
    sigmoid_gate = jax.nn.sigmoid(gate_pre)
    gate_pre_grad = (
        inner_grad * up_pre * sigmoid_gate * (1.0 + gate_pre * (1.0 - sigmoid_gate))
    ).astype(jnp.bfloat16)
    up_pre_grad = (inner_grad * activated).astype(jnp.bfloat16)
    gate_grad = jnp.einsum("rd,rf->df", mlp_rows, gate_pre_grad, preferred_element_type=jnp.float32)
    up_grad = jnp.einsum("rd,rf->df", mlp_rows, up_pre_grad, preferred_element_type=jnp.float32)
    row_grad = jnp.einsum(
        "rf,df->rd", gate_pre_grad, gate_weight, preferred_element_type=jnp.float32
    ) + jnp.einsum("rf,df->rd", up_pre_grad, up_weight, preferred_element_type=jnp.float32)
    mlp_row_grad = combine(row_grad)
    mlp_input_grad = jnp.sum(
        mlp_row_grad.reshape(EXPERTS * slot_cap, width)[mlp_index] * mlp_pair_kept[:, :, None],
        axis=1,
    )
    mlp_input_grad = mlp_input_grad + jnp.dot(
        mlp_logit_grad, router_two.astype(jnp.float32).T, precision=lax.Precision.HIGHEST
    )
    mlp_router_own = jnp.dot(
        mlp_input.astype(jnp.float32).T, mlp_logit_grad, precision=lax.Precision.HIGHEST
    )
    hidden_grad, gain_two_own = norm_back(
        mlp_input_grad, gain_two.astype(jnp.float32), normed_two, inverse_two
    )
    hidden_grad = hidden_grad + own_cotangent
    attn_gate_grad = jnp.sum(attn_picked * hidden_grad[:, None, :], axis=-1) * attn_pair_kept
    attn_logit_grad = gates_back(attn_gates, attn_gate_grad, own_attn)
    attn_slot_grad = (
        hidden_grad[attn_token]
        * slot_gates(attn_gates, attn_pair_kept, own_attn, attn_token, attn_valid)[:, :, None]
    ).astype(jnp.bfloat16)
    out_rows = dispatch(attn_slot_grad)
    output_grad = jnp.einsum("rw,rd->wd", mixed_rows, out_rows, preferred_element_type=jnp.float32)
    mixed_grad = jnp.einsum(
        "rd,wd->rw", out_rows, output_weight, preferred_element_type=jnp.float32
    ).astype(jnp.bfloat16)
    seq_mixed_grad = to_gj(mixed_grad).reshape(sequences, seq_rows, local_heads, HEAD)

    seq_query_grad, seq_key_grad, seq_value_grad = attn_bwd(
        seq_queries.reshape(sequences, seq_rows, HEAD),
        seq_keys.reshape(sequences, seq_length, HEAD),
        seq_values.reshape(sequences, seq_length, HEAD),
        query_blocks[:, :, None],
        log_totals,
        seq_mixed_grad.reshape(sequences, seq_rows, HEAD),
    )
    query_rot_grad = to_jg(
        rotate_back(seq_query_grad.reshape(slot_rows, local_heads, HEAD), slot_cos, slot_sin)
        .reshape(slot_rows, head_cols)
        .astype(jnp.bfloat16)
    )
    query_grad = jnp.einsum(
        "rd,rw->dw", attn_rows, query_rot_grad, preferred_element_type=jnp.float32
    )
    query_row_grad = jnp.einsum(
        "rw,dw->rd", query_rot_grad, query_weight, preferred_element_type=jnp.float32
    )
    attn_row_grad = combine(query_row_grad)
    key_back, value_back = (
        lax.all_to_all(
            seq_key_grad.reshape(devices, own_rows, 1, head_cols).astype(jnp.bfloat16),
            ALL_AXES,
            split_axis=0,
            concat_axis=2,
            tiled=True,
        ).astype(jnp.float32),
        lax.all_to_all(
            seq_value_grad.reshape(devices, own_rows, 1, head_cols).astype(jnp.bfloat16),
            ALL_AXES,
            split_axis=0,
            concat_axis=2,
            tiled=True,
        ).astype(jnp.float32),
    )
    own_key_grad = jnp.sum(key_back.reshape(own_rows, EXPERTS, group_size, head_cols), axis=1)
    own_value_grad = jnp.sum(
        value_back.reshape(own_rows, EXPERTS, group_size, head_cols), axis=1
    ).reshape(own_rows, key_cols)
    kv_own_grad = jnp.concatenate(
        [rotate_back(own_key_grad, own_cos, own_sin).reshape(own_rows, key_cols), own_value_grad],
        axis=1,
    ).astype(jnp.bfloat16)
    attn_input_grad = jnp.sum(
        attn_row_grad.reshape(EXPERTS * slot_cap, width)[attn_index] * attn_pair_kept[:, :, None],
        axis=1,
    )
    attn_input_grad = attn_input_grad + jnp.einsum(
        "rc,dc->rd", kv_own_grad, kv_full, preferred_element_type=jnp.float32
    )
    attn_input_grad = attn_input_grad + jnp.dot(
        attn_logit_grad, router_one.astype(jnp.float32).T, precision=lax.Precision.HIGHEST
    )
    col_block = kv_width // group_size
    kv_col_grad = lax.all_to_all(
        kv_own_grad.reshape(own_rows, group_size, col_block),
        GROUP_AXES,
        split_axis=1,
        concat_axis=0,
        tiled=True,
    ).reshape(own_rows * group_size, col_block)
    kv_col_weight = jnp.einsum(
        "rd,rc->dc", seq_input, kv_col_grad, preferred_element_type=jnp.float32
    )
    attn_router_own = jnp.dot(
        attn_input.astype(jnp.float32).T, attn_logit_grad, precision=lax.Precision.HIGHEST
    )
    input_grad, gain_one_own = norm_back(
        attn_input_grad, gain_one.astype(jnp.float32), normed_one, inverse_one
    )
    input_grad = input_grad + hidden_grad
    grad_extras = jnp.concatenate(
        [gain_one_own[:, None], gain_two_own[:, None], attn_router_own, mlp_router_own], axis=1
    )
    packed_grad = jnp.concatenate(
        [
            kv_col_weight,
            jnp.pad(grad_extras, ((0, 0), (0, extra_pad - grad_extras.shape[1]))),
        ],
        axis=1,
    )
    group_sum = lax.psum_scatter(packed_grad, "grp", scatter_dimension=0, tiled=True)
    dealt = lax.all_to_all(
        group_sum.reshape(group_size, kv_rows, col_block + extra_pad),
        GROUP_AXES,
        split_axis=0,
        concat_axis=0,
        tiled=True,
    )
    kv_grad = jnp.moveaxis(dealt[:, :, :col_block], 0, 1).reshape(kv_rows, kv_width)
    extra_grad = jnp.sum(dealt[:, :, col_block:], axis=0)
    gain_one_grad = extra_grad[:, 0]
    gain_two_grad = extra_grad[:, 1]
    attn_router_grad = extra_grad[:, 2 : 2 + EXPERTS]
    mlp_router_grad = extra_grad[:, 2 + EXPERTS : 2 + 2 * EXPERTS]
    both_full = lax.all_gather(
        jnp.concatenate(
            [own_output.astype(jnp.bfloat16), input_grad.astype(jnp.bfloat16)], axis=1
        ),
        "expert",
        axis=0,
        tiled=True,
    )
    mixed_full, input_full = both_full[:, :width], both_full[:, width:]
    return (
        mixed_full,
        input_full,
        gain_one_grad,
        kv_grad,
        attn_router_grad,
        query_grad,
        output_grad,
        gain_two_grad,
        mlp_router_grad,
        gate_grad,
        up_grad,
        down_grad,
    )


def solution(mesh):
    seq_size, halves = mesh.devices.shape
    grouped = jax.sharding.Mesh(
        mesh.devices.reshape(EXPERTS, seq_size // EXPERTS, halves), ALL_AXES
    )
    return jax.shard_map(
        shards,
        mesh=grouped,
        in_specs=(
            P(SEQ_AXES, None),
            P(ALL_AXES),
            P(ALL_AXES, None),
            P(ALL_AXES, None),
            P(None, ALL_AXES),
            P(ALL_AXES, None),
            P(ALL_AXES),
            P(ALL_AXES, None),
            P(None, ALL_AXES),
            P(None, ALL_AXES),
            P(ALL_AXES, None),
            P(SEQ_AXES, None),
            P(SEQ_AXES, None),
            P(SEQ_AXES, None),
            P(SEQ_AXES, None),
        ),
        out_specs=(
            P(SEQ_AXES, None),
            P(SEQ_AXES, None),
            P(ALL_AXES),
            P(ALL_AXES, None),
            P(ALL_AXES, None),
            P(None, ALL_AXES),
            P(ALL_AXES, None),
            P(ALL_AXES),
            P(ALL_AXES, None),
            P(None, ALL_AXES),
            P(None, ALL_AXES),
            P(ALL_AXES, None),
        ),
        check_vma=False,
    )
```

```python
import functools
import math

import jax
import jax.numpy as jnp
from jax import lax
from jax.experimental import pallas as pl
from jax.sharding import PartitionSpec as P

ALL_AXES = ("grp", "sub", "expert")
SEQ_AXES = ("grp", "sub")
GROUP_AXES = ("sub", "expert")
KV_HEADS = 16
HEAD = 128
EXPERTS = 8
TOPK = 2
PIECES = 8
BLOCK = 256


epsilon = 1e-06
masked_score = -1e30


def _scores(q, k, qb, scale):
    s = lax.dot_general(q, k, (((1,), (1,)), ((), ())), preferred_element_type=jnp.float32) * scale
    kblock = lax.broadcasted_iota(jnp.int32, s.shape, 1) // BLOCK
    return jnp.where(kblock <= qb, s, masked_score)

def _fwd_kernel(scale, q_ref, k_ref, v_ref, qb_ref, o_ref, lse_ref):
    s = _scores(q_ref[...], k_ref[...], qb_ref[...], scale)
    largest = jnp.max(s, axis=-1, keepdims=True)
    weights = jnp.exp(s - largest)
    totals = jnp.sum(weights, axis=-1, keepdims=True)
    probs = weights / totals
    o_ref[...] = jnp.dot(probs.astype(jnp.bfloat16), v_ref[...],
                         preferred_element_type=jnp.float32).astype(o_ref.dtype)
    lse_ref[...] = largest + jnp.log(totals)

def _bwd_kernel(scale, q_ref, k_ref, v_ref, qb_ref, lse_ref, do_ref, dq_ref, dk_ref, dv_ref):
    q = q_ref[...]; k = k_ref[...]; v = v_ref[...]; do = do_ref[...]
    probs = jnp.exp(_scores(q, k, qb_ref[...], scale) - lse_ref[...])
    dp = lax.dot_general(do, v, (((1,), (1,)), ((), ())), preferred_element_type=jnp.float32)
    inner = jnp.sum(probs * dp, axis=-1, keepdims=True)
    ds = (probs * (dp - inner)).astype(jnp.bfloat16)
    dv_ref[...] = lax.dot_general(probs.astype(jnp.bfloat16), do, (((0,), (0,)), ((), ())),
                                  preferred_element_type=jnp.float32)
    dk_ref[...] = lax.dot_general(ds, q, (((0,), (0,)), ((), ())),
                                  preferred_element_type=jnp.float32) * scale
    dq_ref[...] = jnp.dot(ds, k, preferred_element_type=jnp.float32) * scale

def attn_fwd(q, k, v, qb):
    n, rows, d = q.shape; keys = k.shape[1]
    scale = 1.0 / math.sqrt(d)
    rspec = pl.BlockSpec((None, rows, d), lambda i: (i, 0, 0))
    kspec = pl.BlockSpec((None, keys, d), lambda i: (i, 0, 0))
    cspec = pl.BlockSpec((None, rows, 1), lambda i: (i, 0, 0))
    return pl.pallas_call(
        functools.partial(_fwd_kernel, scale),
        grid=(n,),
        in_specs=[rspec, kspec, kspec, cspec],
        out_specs=[rspec, cspec],
        out_shape=[jax.ShapeDtypeStruct((n, rows, d), jnp.bfloat16),
                   jax.ShapeDtypeStruct((n, rows, 1), jnp.float32)],
        cost_estimate=pl.CostEstimate(flops=4 * n * rows * keys * d,
                                      transcendentals=n * rows * keys,
                                      bytes_accessed=2 * n * (2 * rows * d + 2 * keys * d)),
    )(q, k, v, qb)

def attn_bwd(q, k, v, qb, lse, do):
    n, rows, d = q.shape; keys = k.shape[1]
    scale = 1.0 / math.sqrt(d)
    rspec = pl.BlockSpec((None, rows, d), lambda i: (i, 0, 0))
    kspec = pl.BlockSpec((None, keys, d), lambda i: (i, 0, 0))
    cspec = pl.BlockSpec((None, rows, 1), lambda i: (i, 0, 0))
    return pl.pallas_call(
        functools.partial(_bwd_kernel, scale),
        grid=(n,),
        in_specs=[rspec, kspec, kspec, cspec, cspec, rspec],
        out_specs=[rspec, kspec, kspec],
        out_shape=[jax.ShapeDtypeStruct((n, rows, d), jnp.float32),
                   jax.ShapeDtypeStruct((n, keys, d), jnp.float32),
                   jax.ShapeDtypeStruct((n, keys, d), jnp.float32)],
        cost_estimate=pl.CostEstimate(flops=10 * n * rows * keys * d,
                                      transcendentals=n * rows * keys,
                                      bytes_accessed=2 * n * (3 * rows * d + 2 * keys * d) + 8 * n * (rows * d + 2 * keys * d)),
    )(q, k, v, qb, lse, do)


def rope_tables(positions, head_size):
    half_size = head_size // 2
    frequency = jnp.exp(
        jnp.arange(half_size, dtype=jnp.float32) * (-2.0 * math.log(10000.0) / head_size)
    )
    angles = positions.astype(jnp.float32)[:, None] * frequency[None, :]
    return (jnp.cos(angles)[:, None, :], jnp.sin(angles)[:, None, :])


def rotate(values, cosines, sines):
    half_size = values.shape[-1] // 2
    first = values[..., :half_size]
    second = values[..., half_size:]
    return jnp.concatenate(
        [first * cosines - second * sines, second * cosines + first * sines], axis=-1
    )


def rotate_back(grads, cosines, sines):
    half_size = grads.shape[-1] // 2
    first = grads[..., :half_size]
    second = grads[..., half_size:]
    return jnp.concatenate(
        [first * cosines + second * sines, second * cosines - first * sines], axis=-1
    )


def slot_table(expert_ids, ranks, slot_cap):
    block_rows = expert_ids.shape[0]
    expert_range = jnp.arange(EXPERTS, dtype=jnp.int32)
    member = jnp.sum(
        (expert_ids[:, :, None] == expert_range[None, None, :]).astype(jnp.int32), axis=1
    )
    earlier = (ranks[:, None] < ranks[None, :]).astype(jnp.int32)
    places = jnp.sum(earlier[:, :, None] * member[:, None, :], axis=0)
    kept = member * (places < slot_cap).astype(jnp.int32)
    slot_range = jnp.arange(slot_cap, dtype=jnp.int32)
    landing = kept[:, :, None] * (places[:, :, None] == slot_range[None, None, :]).astype(jnp.int32)
    row_range = jnp.arange(block_rows, dtype=jnp.int32)
    slot_token = jnp.sum(landing * row_range[:, None, None], axis=0)
    slot_valid = jnp.sum(landing, axis=0)
    return (places, kept, slot_token, slot_valid)


def pair_index(expert_ids, places, kept, slot_cap):
    chosen_place = jnp.take_along_axis(places, expert_ids, axis=1)
    chosen_kept = jnp.take_along_axis(kept, expert_ids, axis=1)
    return (
        expert_ids * slot_cap + jnp.minimum(chosen_place, slot_cap - 1),
        chosen_kept.astype(jnp.float32),
    )


def pair_gates(logits, expert_ids):
    return jax.nn.softmax(jnp.take_along_axis(logits, expert_ids, axis=1), axis=-1)


def expert_onehot(expert_ids):
    expert_range = jnp.arange(EXPERTS, dtype=jnp.int32)
    return (expert_ids[:, :, None] == expert_range[None, None, :]).astype(jnp.float32)


def gates_back(gates, gate_grads, expert_ids):
    inner = jnp.sum(gates * gate_grads, axis=1, keepdims=True)
    chosen_grads = gates * (gate_grads - inner)
    return jnp.sum(chosen_grads[:, :, None] * expert_onehot(expert_ids), axis=1)


def slot_gates(gates, pair_kept, expert_ids, slot_token, slot_valid):
    per_expert = jnp.sum((gates * pair_kept)[:, :, None] * expert_onehot(expert_ids), axis=1)
    return jnp.take_along_axis(per_expert.T, slot_token, axis=1) * slot_valid.astype(jnp.float32)


def pick_slots(values, slot_token, slot_valid):
    return jnp.where(slot_valid[:, :, None] > 0, values[slot_token], jnp.zeros((), values.dtype))


def fan_out(slot_values, group_size):
    experts_here, slot_cap, width = slot_values.shape
    spread_out = jnp.broadcast_to(slot_values[:, None], (experts_here, group_size, slot_cap, width))
    return spread_out.reshape(experts_here * group_size, slot_cap, width)


def fold_group(received, group_size):
    count, slot_cap, width = received.shape
    return jnp.sum(received.reshape(count // group_size, group_size, slot_cap, width), axis=1)


def norm_back(normed_grad, gain, normed, inverse):
    scaled = normed_grad * gain
    gain_grad = jnp.sum(normed_grad * normed, axis=0)
    input_grad = inverse * (scaled - normed * jnp.mean(scaled * normed, axis=-1, keepdims=True))
    return (input_grad, gain_grad)


def shards(
    tokens,
    attn_gain,
    kv_weight,
    attn_router,
    query_weight,
    output_weight,
    mlp_gain,
    mlp_router,
    gate_weight,
    up_weight,
    down_weight,
    attn_experts,
    mlp_experts,
    priority,
    cotangent,
):
    devices = lax.axis_size(ALL_AXES)
    halves = lax.axis_size("expert")
    device_index = lax.axis_index(ALL_AXES)
    half_index = lax.axis_index("expert")
    seq_tokens, width = tokens.shape
    own_rows = seq_tokens // halves
    group_size = devices // EXPERTS
    head_cols = query_weight.shape[1]
    local_heads = head_cols // HEAD
    key_cols = KV_HEADS * HEAD
    all_tokens = own_rows * devices
    seq_length = seq_tokens * PIECES
    sequences = all_tokens // seq_length
    slot_cap = (9 * TOPK * own_rows + 8 * EXPERTS - 1) // (8 * EXPERTS)
    slot_rows = devices * slot_cap
    seq_rows = slot_rows // sequences
    my_expert = device_index // group_size
    groups = lax.axis_size("grp")
    head_index = device_index % group_size

    def dispatch(slot_values):
        by_group = lax.all_to_all(slot_values, "grp", split_axis=0, concat_axis=0, tiled=True)
        return lax.all_gather(
            by_group.reshape(groups * slot_cap, width), GROUP_AXES, axis=0, tiled=True
        )

    def combine(partial_value):
        parts = lax.all_to_all(
            partial_value.astype(jnp.bfloat16).reshape(group_size, groups * slot_cap, width),
            GROUP_AXES,
            split_axis=0,
            concat_axis=0,
            tiled=True,
        )
        summed = jnp.sum(parts.astype(jnp.float32), axis=0).reshape(groups, slot_cap, width)
        return lax.all_to_all(summed, "grp", split_axis=0, concat_axis=0, tiled=True)

    def to_rows(per_head):
        parts = lax.all_to_all(
            per_head.reshape(group_size, groups * slot_cap, head_cols),
            GROUP_AXES,
            split_axis=0,
            concat_axis=0,
            tiled=True,
        )
        return jnp.swapaxes(parts, 0, 1).reshape(groups * slot_cap, group_size * head_cols)

    def to_owners(row_values):
        return lax.all_to_all(
            row_values.reshape(groups, slot_cap, width), "grp", split_axis=0, concat_axis=0, tiled=True
        )

    def to_gj(rows):
        shaped = rows.reshape((group_size, groups, slot_cap) + rows.shape[1:])
        return jnp.swapaxes(shaped, 0, 1).reshape(rows.shape)

    def to_jg(rows):
        shaped = rows.reshape((groups, group_size, slot_cap) + rows.shape[1:])
        return jnp.swapaxes(shaped, 0, 1).reshape(rows.shape)
    scale = 1.0 / math.sqrt(HEAD)

    start_row = half_index * own_rows
    own_input = lax.dynamic_slice_in_dim(tokens, start_row, own_rows, 0).astype(jnp.float32)
    own_cotangent = lax.dynamic_slice_in_dim(cotangent, start_row, own_rows, 0).astype(jnp.float32)
    own_attn = lax.dynamic_slice_in_dim(attn_experts, start_row, own_rows, 0)
    own_mlp = lax.dynamic_slice_in_dim(mlp_experts, start_row, own_rows, 0)
    own_rank = lax.dynamic_slice_in_dim(priority[0], start_row, own_rows, 0)
    token_order = jnp.arange(own_rows, dtype=jnp.int32)

    kv_rows, kv_width = kv_weight.shape
    id_cols = own_rows * TOPK // kv_rows
    extras = jnp.concatenate(
        [
            attn_gain[:, None],
            mlp_gain[:, None],
            attn_router,
            mlp_router,
            own_attn.reshape(kv_rows, id_cols).astype(jnp.bfloat16),
        ],
        axis=1,
    )
    extra_cols = extras.shape[1]
    extra_pad = -(-extra_cols // 128) * 128
    packed = jnp.concatenate(
        [kv_weight, jnp.pad(extras, ((0, 0), (0, extra_pad - extra_cols)))], axis=1
    )
    gathered = lax.all_gather(
        lax.all_gather(packed, "grp", axis=0, tiled=True), GROUP_AXES, axis=0, tiled=True
    )
    gathered = jnp.swapaxes(
        gathered.reshape(group_size, groups, kv_rows, extra_pad + kv_width), 0, 1
    ).reshape(devices * kv_rows, extra_pad + kv_width)
    kv_full = gathered[:, :kv_width]
    gain_one = gathered[:, kv_width]
    gain_two = gathered[:, kv_width + 1]
    router_one = gathered[:, kv_width + 2 : kv_width + 2 + EXPERTS]
    router_two = gathered[:, kv_width + 2 + EXPERTS : kv_width + 2 + 2 * EXPERTS]
    routes_all = gathered[:, kv_width + 2 + 2 * EXPERTS : kv_width + extra_cols].astype(jnp.int32)
    inverse_one = lax.rsqrt(jnp.mean(own_input * own_input, axis=-1, keepdims=True) + epsilon)
    normed_one = own_input * inverse_one
    attn_input = (normed_one * gain_one.astype(jnp.float32)).astype(jnp.bfloat16)
    attn_logits = jnp.dot(attn_input, router_one, preferred_element_type=jnp.float32)
    seq_input = lax.all_gather(attn_input, GROUP_AXES, axis=0, tiled=True)
    own_positions = (device_index * own_rows + token_order) % seq_length
    own_cos, own_sin = rope_tables(own_positions, HEAD)
    head_kv = jnp.concatenate(
        [
            lax.dynamic_slice_in_dim(kv_full, head_index * head_cols, head_cols, axis=1),
            lax.dynamic_slice_in_dim(kv_full, key_cols + head_index * head_cols, head_cols, axis=1),
        ],
        axis=1,
    )
    seq_kv = jnp.dot(seq_input, head_kv, preferred_element_type=jnp.float32)
    seq_cos, seq_sin = rope_tables(jnp.arange(seq_length, dtype=jnp.int32), HEAD)
    seq_pair = jnp.concatenate(
        [
            rotate(seq_kv[:, :head_cols].reshape(seq_length, local_heads, HEAD), seq_cos, seq_sin)
            .reshape(seq_length, head_cols)
            .astype(jnp.bfloat16),
            seq_kv[:, head_cols:].astype(jnp.bfloat16),
        ],
        axis=1,
    )
    all_pairs = lax.all_gather(seq_pair, "grp", axis=0, tiled=True)
    seq_keys = all_pairs[:, :head_cols].reshape(sequences, seq_length, local_heads, HEAD)
    seq_values = all_pairs[:, head_cols:].reshape(sequences, seq_length, local_heads, HEAD)
    attn_places, attn_kept, attn_token, attn_valid = slot_table(own_attn, token_order, slot_cap)
    mlp_places, mlp_kept, mlp_token, mlp_valid = slot_table(own_mlp, own_rank, slot_cap)
    block_routes = routes_all.reshape(devices, own_rows, TOPK)
    dest_tables = jax.vmap(lambda block_ids: slot_table(block_ids, token_order, slot_cap)[2])(
        block_routes
    )
    dest_token = jnp.take(dest_tables, my_expert, axis=1)
    attn_rows = dispatch(pick_slots(attn_input, attn_token, attn_valid))
    queries = to_gj(jnp.dot(attn_rows, query_weight, preferred_element_type=jnp.float32))
    slot_positions = (
        (jnp.arange(devices, dtype=jnp.int32)[:, None] * own_rows + dest_token) % seq_length
    ).reshape(slot_rows)
    slot_cos, slot_sin = rope_tables(slot_positions, HEAD)
    rotated = rotate(queries.reshape(slot_rows, local_heads, HEAD), slot_cos, slot_sin).astype(
        jnp.bfloat16
    )
    seq_queries = rotated.reshape(sequences, seq_rows, local_heads, HEAD)
    query_blocks = (slot_positions // BLOCK).reshape(sequences, seq_rows)
    key_blocks = jnp.arange(seq_length, dtype=jnp.int32) // BLOCK

    attn_mixed, log_totals = attn_fwd(
        seq_queries.reshape(sequences, seq_rows, HEAD),
        seq_keys.reshape(sequences, seq_length, HEAD),
        seq_values.reshape(sequences, seq_length, HEAD),
        query_blocks[:, :, None],
    )
    mixed_rows = to_jg(attn_mixed.reshape(slot_rows, head_cols))
    output_stack = lax.all_gather(output_weight, GROUP_AXES, axis=0, tiled=True)
    attn_slots = to_owners(
        jnp.dot(to_rows(mixed_rows), output_stack, preferred_element_type=jnp.float32)
    )
    attn_gates = pair_gates(attn_logits, own_attn)
    attn_index, attn_pair_kept = pair_index(own_attn, attn_places, attn_kept, slot_cap)
    attn_picked = attn_slots.reshape(EXPERTS * slot_cap, width)[attn_index]
    hidden_state = own_input + jnp.sum(
        attn_picked * (attn_gates * attn_pair_kept)[:, :, None], axis=1
    )
    inverse_two = lax.rsqrt(jnp.mean(hidden_state * hidden_state, axis=-1, keepdims=True) + epsilon)
    normed_two = hidden_state * inverse_two
    mlp_input = (normed_two * gain_two.astype(jnp.float32)).astype(jnp.bfloat16)
    mlp_logits = jnp.dot(mlp_input, router_two, preferred_element_type=jnp.float32)
    mlp_rows = dispatch(pick_slots(mlp_input, mlp_token, mlp_valid))
    gate_pre = jnp.dot(mlp_rows, gate_weight, preferred_element_type=jnp.float32)
    up_pre = jnp.dot(mlp_rows, up_weight, preferred_element_type=jnp.float32)
    activated = jax.nn.silu(gate_pre)
    inner_rows = (activated * up_pre).astype(jnp.bfloat16)
    mlp_partial = jnp.dot(inner_rows, down_weight, preferred_element_type=jnp.float32)
    mlp_slots = combine(mlp_partial)
    mlp_gates = pair_gates(mlp_logits, own_mlp)
    mlp_index, mlp_pair_kept = pair_index(own_mlp, mlp_places, mlp_kept, slot_cap)
    mlp_picked = mlp_slots.reshape(EXPERTS * slot_cap, width)[mlp_index]
    own_output = hidden_state + jnp.sum(
        mlp_picked * (mlp_gates * mlp_pair_kept)[:, :, None], axis=1
    )
    mlp_gate_grad = jnp.sum(mlp_picked * own_cotangent[:, None, :], axis=-1) * mlp_pair_kept
    mlp_logit_grad = gates_back(mlp_gates, mlp_gate_grad, own_mlp)
    mlp_slot_grad = (
        own_cotangent[mlp_token]
        * slot_gates(mlp_gates, mlp_pair_kept, own_mlp, mlp_token, mlp_valid)[:, :, None]
    ).astype(jnp.bfloat16)
    down_rows = dispatch(mlp_slot_grad)
    inner_grad = jnp.einsum("rd,fd->rf", down_rows, down_weight, preferred_element_type=jnp.float32)
    down_grad = jnp.einsum("rf,rd->fd", inner_rows, down_rows, preferred_element_type=jnp.float32)
    sigmoid_gate = jax.nn.sigmoid(gate_pre)
    gate_pre_grad = (
        inner_grad * up_pre * sigmoid_gate * (1.0 + gate_pre * (1.0 - sigmoid_gate))
    ).astype(jnp.bfloat16)
    up_pre_grad = (inner_grad * activated).astype(jnp.bfloat16)
    gate_grad = jnp.einsum("rd,rf->df", mlp_rows, gate_pre_grad, preferred_element_type=jnp.float32)
    up_grad = jnp.einsum("rd,rf->df", mlp_rows, up_pre_grad, preferred_element_type=jnp.float32)
    row_grad = jnp.einsum(
        "rf,df->rd", gate_pre_grad, gate_weight, preferred_element_type=jnp.float32
    ) + jnp.einsum("rf,df->rd", up_pre_grad, up_weight, preferred_element_type=jnp.float32)
    mlp_row_grad = combine(row_grad)
    mlp_input_grad = jnp.sum(
        mlp_row_grad.reshape(EXPERTS * slot_cap, width)[mlp_index] * mlp_pair_kept[:, :, None],
        axis=1,
    )
    mlp_input_grad = mlp_input_grad + jnp.dot(
        mlp_logit_grad, router_two.astype(jnp.float32).T, precision=lax.Precision.HIGHEST
    )
    mlp_router_own = jnp.dot(
        mlp_input.astype(jnp.float32).T, mlp_logit_grad, precision=lax.Precision.HIGHEST
    )
    hidden_grad, gain_two_own = norm_back(
        mlp_input_grad, gain_two.astype(jnp.float32), normed_two, inverse_two
    )
    hidden_grad = hidden_grad + own_cotangent
    attn_gate_grad = jnp.sum(attn_picked * hidden_grad[:, None, :], axis=-1) * attn_pair_kept
    attn_logit_grad = gates_back(attn_gates, attn_gate_grad, own_attn)
    attn_slot_grad = (
        hidden_grad[attn_token]
        * slot_gates(attn_gates, attn_pair_kept, own_attn, attn_token, attn_valid)[:, :, None]
    ).astype(jnp.bfloat16)
    out_rows = dispatch(attn_slot_grad)
    output_grad = jnp.einsum("rw,rd->wd", mixed_rows, out_rows, preferred_element_type=jnp.float32)
    mixed_grad = jnp.einsum(
        "rd,wd->rw", out_rows, output_weight, preferred_element_type=jnp.float32
    ).astype(jnp.bfloat16)
    seq_mixed_grad = to_gj(mixed_grad).reshape(sequences, seq_rows, local_heads, HEAD)

    seq_query_grad, seq_key_grad, seq_value_grad = attn_bwd(
        seq_queries.reshape(sequences, seq_rows, HEAD),
        seq_keys.reshape(sequences, seq_length, HEAD),
        seq_values.reshape(sequences, seq_length, HEAD),
        query_blocks[:, :, None],
        log_totals,
        seq_mixed_grad.reshape(sequences, seq_rows, HEAD),
    )
    query_rot_grad = to_jg(
        rotate_back(seq_query_grad.reshape(slot_rows, local_heads, HEAD), slot_cos, slot_sin)
        .reshape(slot_rows, head_cols)
        .astype(jnp.bfloat16)
    )
    query_grad = jnp.einsum(
        "rd,rw->dw", attn_rows, query_rot_grad, preferred_element_type=jnp.float32
    )
    query_stack = lax.all_gather(query_weight, GROUP_AXES, axis=1, tiled=True)
    attn_row_grad = to_owners(
        jnp.einsum(
            "rw,dw->rd", to_rows(query_rot_grad), query_stack, preferred_element_type=jnp.float32
        )
    )
    key_back, value_back = (
        lax.all_to_all(
            seq_key_grad.reshape(devices, own_rows, 1, head_cols).astype(jnp.bfloat16),
            ALL_AXES,
            split_axis=0,
            concat_axis=2,
            tiled=True,
        ).astype(jnp.float32),
        lax.all_to_all(
            seq_value_grad.reshape(devices, own_rows, 1, head_cols).astype(jnp.bfloat16),
            ALL_AXES,
            split_axis=0,
            concat_axis=2,
            tiled=True,
        ).astype(jnp.float32),
    )
    own_key_grad = jnp.sum(key_back.reshape(own_rows, EXPERTS, group_size, head_cols), axis=1)
    own_value_grad = jnp.sum(
        value_back.reshape(own_rows, EXPERTS, group_size, head_cols), axis=1
    ).reshape(own_rows, key_cols)
    kv_own_grad = jnp.concatenate(
        [rotate_back(own_key_grad, own_cos, own_sin).reshape(own_rows, key_cols), own_value_grad],
        axis=1,
    ).astype(jnp.bfloat16)
    attn_input_grad = jnp.sum(
        attn_row_grad.reshape(EXPERTS * slot_cap, width)[attn_index] * attn_pair_kept[:, :, None],
        axis=1,
    )
    attn_input_grad = attn_input_grad + jnp.einsum(
        "rc,dc->rd", kv_own_grad, kv_full, preferred_element_type=jnp.float32
    )
    attn_input_grad = attn_input_grad + jnp.dot(
        attn_logit_grad, router_one.astype(jnp.float32).T, precision=lax.Precision.HIGHEST
    )
    col_block = kv_width // group_size
    kv_col_grad = lax.all_to_all(
        kv_own_grad.reshape(own_rows, group_size, col_block),
        GROUP_AXES,
        split_axis=1,
        concat_axis=0,
        tiled=True,
    ).reshape(own_rows * group_size, col_block)
    kv_col_weight = jnp.einsum(
        "rd,rc->dc", seq_input, kv_col_grad, preferred_element_type=jnp.float32
    )
    attn_router_own = jnp.dot(
        attn_input.astype(jnp.float32).T, attn_logit_grad, precision=lax.Precision.HIGHEST
    )
    input_grad, gain_one_own = norm_back(
        attn_input_grad, gain_one.astype(jnp.float32), normed_one, inverse_one
    )
    input_grad = input_grad + hidden_grad
    grad_extras = jnp.concatenate(
        [gain_one_own[:, None], gain_two_own[:, None], attn_router_own, mlp_router_own], axis=1
    )
    packed_grad = jnp.concatenate(
        [
            kv_col_weight,
            jnp.pad(grad_extras, ((0, 0), (0, extra_pad - grad_extras.shape[1]))),
        ],
        axis=1,
    )
    group_sum = lax.psum_scatter(packed_grad, "grp", scatter_dimension=0, tiled=True)
    dealt = lax.all_to_all(
        group_sum.reshape(group_size, kv_rows, col_block + extra_pad),
        GROUP_AXES,
        split_axis=0,
        concat_axis=0,
        tiled=True,
    )
    kv_grad = jnp.moveaxis(dealt[:, :, :col_block], 0, 1).reshape(kv_rows, kv_width)
    extra_grad = jnp.sum(dealt[:, :, col_block:], axis=0)
    gain_one_grad = extra_grad[:, 0]
    gain_two_grad = extra_grad[:, 1]
    attn_router_grad = extra_grad[:, 2 : 2 + EXPERTS]
    mlp_router_grad = extra_grad[:, 2 + EXPERTS : 2 + 2 * EXPERTS]
    both_full = lax.all_gather(
        jnp.concatenate(
            [own_output.astype(jnp.bfloat16), input_grad.astype(jnp.bfloat16)], axis=1
        ),
        "expert",
        axis=0,
        tiled=True,
    )
    mixed_full, input_full = both_full[:, :width], both_full[:, width:]
    return (
        mixed_full,
        input_full,
        gain_one_grad,
        kv_grad,
        attn_router_grad,
        query_grad,
        output_grad,
        gain_two_grad,
        mlp_router_grad,
        gate_grad,
        up_grad,
        down_grad,
    )


def solution(mesh):
    seq_size, halves = mesh.devices.shape
    grouped = jax.sharding.Mesh(
        mesh.devices.reshape(EXPERTS, seq_size // EXPERTS, halves), ALL_AXES
    )
    return jax.shard_map(
        shards,
        mesh=grouped,
        in_specs=(
            P(SEQ_AXES, None),
            P(ALL_AXES),
            P(ALL_AXES, None),
            P(ALL_AXES, None),
            P(None, ALL_AXES),
            P(ALL_AXES, None),
            P(ALL_AXES),
            P(ALL_AXES, None),
            P(None, ALL_AXES),
            P(None, ALL_AXES),
            P(ALL_AXES, None),
            P(SEQ_AXES, None),
            P(SEQ_AXES, None),
            P(SEQ_AXES, None),
            P(SEQ_AXES, None),
        ),
        out_specs=(
            P(SEQ_AXES, None),
            P(SEQ_AXES, None),
            P(ALL_AXES),
            P(ALL_AXES, None),
            P(ALL_AXES, None),
            P(None, ALL_AXES),
            P(ALL_AXES, None),
            P(ALL_AXES),
            P(ALL_AXES, None),
            P(None, ALL_AXES),
            P(None, ALL_AXES),
            P(ALL_AXES, None),
        ),
        check_vma=False,
    )
```

```python
import functools
import math

import jax
import jax.numpy as jnp
from jax import lax
from jax.experimental import pallas as pl
from jax.sharding import PartitionSpec as P

ALL_AXES = ("grp", "sub", "expert")
SEQ_AXES = ("grp", "sub")
GROUP_AXES = ("sub", "expert")
KV_HEADS = 16
HEAD = 128
EXPERTS = 8
TOPK = 2
PIECES = 8
BLOCK = 256


epsilon = 1e-06
masked_score = -1e30


def _scores(q, k, qb, scale):
    s = lax.dot_general(q, k, (((1,), (1,)), ((), ())), preferred_element_type=jnp.float32) * scale
    kblock = lax.broadcasted_iota(jnp.int32, s.shape, 1) // BLOCK
    return jnp.where(kblock <= qb, s, masked_score)

def _fwd_kernel(scale, q_ref, k_ref, v_ref, qb_ref, o_ref, lse_ref):
    s = _scores(q_ref[...], k_ref[...], qb_ref[...], scale)
    largest = jnp.max(s, axis=-1, keepdims=True)
    weights = jnp.exp(s - largest)
    totals = jnp.sum(weights, axis=-1, keepdims=True)
    probs = weights / totals
    o_ref[...] = jnp.dot(probs.astype(jnp.bfloat16), v_ref[...],
                         preferred_element_type=jnp.float32).astype(o_ref.dtype)
    lse_ref[...] = largest + jnp.log(totals)

def _bwd_kernel(scale, q_ref, k_ref, v_ref, qb_ref, lse_ref, do_ref, dq_ref, dk_ref, dv_ref):
    q = q_ref[...]; k = k_ref[...]; v = v_ref[...]; do = do_ref[...]
    probs = jnp.exp(_scores(q, k, qb_ref[...], scale) - lse_ref[...])
    dp = lax.dot_general(do, v, (((1,), (1,)), ((), ())), preferred_element_type=jnp.float32)
    inner = jnp.sum(probs * dp, axis=-1, keepdims=True)
    ds = (probs * (dp - inner)).astype(jnp.bfloat16)
    dv_ref[...] = lax.dot_general(probs.astype(jnp.bfloat16), do, (((0,), (0,)), ((), ())),
                                  preferred_element_type=jnp.float32)
    dk_ref[...] = lax.dot_general(ds, q, (((0,), (0,)), ((), ())),
                                  preferred_element_type=jnp.float32) * scale
    dq_ref[...] = jnp.dot(ds, k, preferred_element_type=jnp.float32) * scale

def attn_fwd(q, k, v, qb):
    n, rows, d = q.shape; keys = k.shape[1]
    scale = 1.0 / math.sqrt(d)
    rspec = pl.BlockSpec((None, rows, d), lambda i: (i, 0, 0))
    kspec = pl.BlockSpec((None, keys, d), lambda i: (i, 0, 0))
    cspec = pl.BlockSpec((None, rows, 1), lambda i: (i, 0, 0))
    return pl.pallas_call(
        functools.partial(_fwd_kernel, scale),
        grid=(n,),
        in_specs=[rspec, kspec, kspec, cspec],
        out_specs=[rspec, cspec],
        out_shape=[jax.ShapeDtypeStruct((n, rows, d), jnp.bfloat16),
                   jax.ShapeDtypeStruct((n, rows, 1), jnp.float32)],
        cost_estimate=pl.CostEstimate(flops=4 * n * rows * keys * d,
                                      transcendentals=n * rows * keys,
                                      bytes_accessed=2 * n * (2 * rows * d + 2 * keys * d)),
    )(q, k, v, qb)

def attn_bwd(q, k, v, qb, lse, do):
    n, rows, d = q.shape; keys = k.shape[1]
    scale = 1.0 / math.sqrt(d)
    rspec = pl.BlockSpec((None, rows, d), lambda i: (i, 0, 0))
    kspec = pl.BlockSpec((None, keys, d), lambda i: (i, 0, 0))
    cspec = pl.BlockSpec((None, rows, 1), lambda i: (i, 0, 0))
    return pl.pallas_call(
        functools.partial(_bwd_kernel, scale),
        grid=(n,),
        in_specs=[rspec, kspec, kspec, cspec, cspec, rspec],
        out_specs=[rspec, kspec, kspec],
        out_shape=[jax.ShapeDtypeStruct((n, rows, d), jnp.float32),
                   jax.ShapeDtypeStruct((n, keys, d), jnp.float32),
                   jax.ShapeDtypeStruct((n, keys, d), jnp.float32)],
        cost_estimate=pl.CostEstimate(flops=10 * n * rows * keys * d,
                                      transcendentals=n * rows * keys,
                                      bytes_accessed=2 * n * (3 * rows * d + 2 * keys * d) + 8 * n * (rows * d + 2 * keys * d)),
    )(q, k, v, qb, lse, do)


def rope_tables(positions, head_size):
    half_size = head_size // 2
    frequency = jnp.exp(
        jnp.arange(half_size, dtype=jnp.float32) * (-2.0 * math.log(10000.0) / head_size)
    )
    angles = positions.astype(jnp.float32)[:, None] * frequency[None, :]
    return (jnp.cos(angles)[:, None, :], jnp.sin(angles)[:, None, :])


def rotate(values, cosines, sines):
    half_size = values.shape[-1] // 2
    first = values[..., :half_size]
    second = values[..., half_size:]
    return jnp.concatenate(
        [first * cosines - second * sines, second * cosines + first * sines], axis=-1
    )


def rotate_back(grads, cosines, sines):
    half_size = grads.shape[-1] // 2
    first = grads[..., :half_size]
    second = grads[..., half_size:]
    return jnp.concatenate(
        [first * cosines + second * sines, second * cosines - first * sines], axis=-1
    )


def slot_table(expert_ids, ranks, slot_cap):
    block_rows = expert_ids.shape[0]
    expert_range = jnp.arange(EXPERTS, dtype=jnp.int32)
    member = jnp.sum(
        (expert_ids[:, :, None] == expert_range[None, None, :]).astype(jnp.int32), axis=1
    )
    earlier = (ranks[:, None] < ranks[None, :]).astype(jnp.int32)
    places = jnp.sum(earlier[:, :, None] * member[:, None, :], axis=0)
    kept = member * (places < slot_cap).astype(jnp.int32)
    slot_range = jnp.arange(slot_cap, dtype=jnp.int32)
    landing = kept[:, :, None] * (places[:, :, None] == slot_range[None, None, :]).astype(jnp.int32)
    row_range = jnp.arange(block_rows, dtype=jnp.int32)
    slot_token = jnp.sum(landing * row_range[:, None, None], axis=0)
    slot_valid = jnp.sum(landing, axis=0)
    return (places, kept, slot_token, slot_valid)


def pair_index(expert_ids, places, kept, slot_cap):
    chosen_place = jnp.take_along_axis(places, expert_ids, axis=1)
    chosen_kept = jnp.take_along_axis(kept, expert_ids, axis=1)
    return (
        expert_ids * slot_cap + jnp.minimum(chosen_place, slot_cap - 1),
        chosen_kept.astype(jnp.float32),
    )


def pair_gates(logits, expert_ids):
    return jax.nn.softmax(jnp.take_along_axis(logits, expert_ids, axis=1), axis=-1)


def expert_onehot(expert_ids):
    expert_range = jnp.arange(EXPERTS, dtype=jnp.int32)
    return (expert_ids[:, :, None] == expert_range[None, None, :]).astype(jnp.float32)


def gates_back(gates, gate_grads, expert_ids):
    inner = jnp.sum(gates * gate_grads, axis=1, keepdims=True)
    chosen_grads = gates * (gate_grads - inner)
    return jnp.sum(chosen_grads[:, :, None] * expert_onehot(expert_ids), axis=1)


def slot_gates(gates, pair_kept, expert_ids, slot_token, slot_valid):
    per_expert = jnp.sum((gates * pair_kept)[:, :, None] * expert_onehot(expert_ids), axis=1)
    return jnp.take_along_axis(per_expert.T, slot_token, axis=1) * slot_valid.astype(jnp.float32)


def pick_slots(values, slot_token, slot_valid):
    return jnp.where(slot_valid[:, :, None] > 0, values[slot_token], jnp.zeros((), values.dtype))


def fan_out(slot_values, group_size):
    experts_here, slot_cap, width = slot_values.shape
    spread_out = jnp.broadcast_to(slot_values[:, None], (experts_here, group_size, slot_cap, width))
    return spread_out.reshape(experts_here * group_size, slot_cap, width)


def fold_group(received, group_size):
    count, slot_cap, width = received.shape
    return jnp.sum(received.reshape(count // group_size, group_size, slot_cap, width), axis=1)


def norm_back(normed_grad, gain, normed, inverse):
    scaled = normed_grad * gain
    gain_grad = jnp.sum(normed_grad * normed, axis=0)
    input_grad = inverse * (scaled - normed * jnp.mean(scaled * normed, axis=-1, keepdims=True))
    return (input_grad, gain_grad)


def shards(
    tokens,
    attn_gain,
    kv_weight,
    attn_router,
    query_weight,
    output_weight,
    mlp_gain,
    mlp_router,
    gate_weight,
    up_weight,
    down_weight,
    attn_experts,
    mlp_experts,
    priority,
    cotangent,
):
    devices = lax.axis_size(ALL_AXES)
    halves = lax.axis_size("expert")
    device_index = lax.axis_index(ALL_AXES)
    half_index = lax.axis_index("expert")
    seq_tokens, width = tokens.shape
    own_rows = seq_tokens // halves
    group_size = devices // EXPERTS
    head_cols = query_weight.shape[1]
    local_heads = head_cols // HEAD
    key_cols = KV_HEADS * HEAD
    all_tokens = own_rows * devices
    seq_length = seq_tokens * PIECES
    sequences = all_tokens // seq_length
    slot_cap = (9 * TOPK * own_rows + 8 * EXPERTS - 1) // (8 * EXPERTS)
    slot_rows = devices * slot_cap
    seq_rows = slot_rows // sequences
    my_expert = device_index // group_size
    groups = lax.axis_size("grp")
    head_index = device_index % group_size

    def dispatch(slot_values):
        by_group = lax.all_to_all(slot_values, "grp", split_axis=0, concat_axis=0, tiled=True)
        return lax.all_gather(
            by_group.reshape(groups * slot_cap, width), GROUP_AXES, axis=0, tiled=True
        )

    def combine(partial_value):
        parts = lax.all_to_all(
            partial_value.astype(jnp.bfloat16).reshape(group_size, groups * slot_cap, width),
            GROUP_AXES,
            split_axis=0,
            concat_axis=0,
            tiled=True,
        )
        summed = jnp.sum(parts.astype(jnp.float32), axis=0).reshape(groups, slot_cap, width)
        return lax.all_to_all(summed, "grp", split_axis=0, concat_axis=0, tiled=True)

    def to_rows(per_head):
        parts = lax.all_to_all(
            per_head.reshape(group_size, groups * slot_cap, head_cols),
            GROUP_AXES,
            split_axis=0,
            concat_axis=0,
            tiled=True,
        )
        return jnp.swapaxes(parts, 0, 1).reshape(groups * slot_cap, group_size * head_cols)

    def to_owners(row_values):
        return lax.all_to_all(
            row_values.reshape(groups, slot_cap, width), "grp", split_axis=0, concat_axis=0, tiled=True
        )

    def to_gj(rows):
        shaped = rows.reshape((group_size, groups, slot_cap) + rows.shape[1:])
        return jnp.swapaxes(shaped, 0, 1).reshape(rows.shape)

    def to_jg(rows):
        shaped = rows.reshape((groups, group_size, slot_cap) + rows.shape[1:])
        return jnp.swapaxes(shaped, 0, 1).reshape(rows.shape)
    scale = 1.0 / math.sqrt(HEAD)

    start_row = half_index * own_rows
    own_input = lax.dynamic_slice_in_dim(tokens, start_row, own_rows, 0).astype(jnp.float32)
    own_cotangent = lax.dynamic_slice_in_dim(cotangent, start_row, own_rows, 0).astype(jnp.float32)
    own_attn = lax.dynamic_slice_in_dim(attn_experts, start_row, own_rows, 0)
    own_mlp = lax.dynamic_slice_in_dim(mlp_experts, start_row, own_rows, 0)
    own_rank = lax.dynamic_slice_in_dim(priority[0], start_row, own_rows, 0)
    token_order = jnp.arange(own_rows, dtype=jnp.int32)

    kv_rows, kv_width = kv_weight.shape
    id_cols = own_rows * TOPK // kv_rows
    extras = jnp.concatenate(
        [
            attn_gain[:, None],
            mlp_gain[:, None],
            attn_router,
            mlp_router,
            own_attn.reshape(kv_rows, id_cols).astype(jnp.bfloat16),
        ],
        axis=1,
    )
    extra_cols = extras.shape[1]
    extra_pad = -(-extra_cols // 128) * 128
    packed = jnp.concatenate(
        [kv_weight, jnp.pad(extras, ((0, 0), (0, extra_pad - extra_cols)))], axis=1
    )
    gathered = lax.all_gather(
        lax.all_gather(packed, "grp", axis=0, tiled=True), GROUP_AXES, axis=0, tiled=True
    )
    gathered = jnp.swapaxes(
        gathered.reshape(group_size, groups, kv_rows, extra_pad + kv_width), 0, 1
    ).reshape(devices * kv_rows, extra_pad + kv_width)
    kv_full = gathered[:, :kv_width]
    gain_one = gathered[:, kv_width]
    gain_two = gathered[:, kv_width + 1]
    router_one = gathered[:, kv_width + 2 : kv_width + 2 + EXPERTS]
    router_two = gathered[:, kv_width + 2 + EXPERTS : kv_width + 2 + 2 * EXPERTS]
    routes_all = gathered[:, kv_width + 2 + 2 * EXPERTS : kv_width + extra_cols].astype(jnp.int32)
    inverse_one = lax.rsqrt(jnp.mean(own_input * own_input, axis=-1, keepdims=True) + epsilon)
    normed_one = own_input * inverse_one
    attn_input = (normed_one * gain_one.astype(jnp.float32)).astype(jnp.bfloat16)
    attn_logits = jnp.dot(attn_input, router_one, preferred_element_type=jnp.float32)
    seq_input = lax.all_gather(attn_input, GROUP_AXES, axis=0, tiled=True)
    own_positions = (device_index * own_rows + token_order) % seq_length
    own_cos, own_sin = rope_tables(own_positions, HEAD)
    head_kv = jnp.concatenate(
        [
            lax.dynamic_slice_in_dim(kv_full, head_index * head_cols, head_cols, axis=1),
            lax.dynamic_slice_in_dim(kv_full, key_cols + head_index * head_cols, head_cols, axis=1),
        ],
        axis=1,
    )
    seq_kv = jnp.dot(seq_input, head_kv, preferred_element_type=jnp.float32)
    seq_cos, seq_sin = rope_tables(jnp.arange(seq_length, dtype=jnp.int32), HEAD)
    seq_pair = jnp.concatenate(
        [
            rotate(seq_kv[:, :head_cols].reshape(seq_length, local_heads, HEAD), seq_cos, seq_sin)
            .reshape(seq_length, head_cols)
            .astype(jnp.bfloat16),
            seq_kv[:, head_cols:].astype(jnp.bfloat16),
        ],
        axis=1,
    )
    all_pairs = lax.all_to_all(
        jnp.broadcast_to(seq_pair[None], (groups,) + seq_pair.shape),
        "grp",
        split_axis=0,
        concat_axis=0,
        tiled=True,
    ).reshape(groups * seq_length, 2 * head_cols)
    seq_keys = all_pairs[:, :head_cols].reshape(sequences, seq_length, local_heads, HEAD)
    seq_values = all_pairs[:, head_cols:].reshape(sequences, seq_length, local_heads, HEAD)
    attn_places, attn_kept, attn_token, attn_valid = slot_table(own_attn, token_order, slot_cap)
    mlp_places, mlp_kept, mlp_token, mlp_valid = slot_table(own_mlp, own_rank, slot_cap)
    block_routes = routes_all.reshape(devices, own_rows, TOPK)
    dest_tables = jax.vmap(lambda block_ids: slot_table(block_ids, token_order, slot_cap)[2])(
        block_routes
    )
    dest_token = jnp.take(dest_tables, my_expert, axis=1)
    attn_rows = dispatch(pick_slots(attn_input, attn_token, attn_valid))
    queries = to_gj(jnp.dot(attn_rows, query_weight, preferred_element_type=jnp.float32))
    slot_positions = (
        (jnp.arange(devices, dtype=jnp.int32)[:, None] * own_rows + dest_token) % seq_length
    ).reshape(slot_rows)
    slot_cos, slot_sin = rope_tables(slot_positions, HEAD)
    rotated = rotate(queries.reshape(slot_rows, local_heads, HEAD), slot_cos, slot_sin).astype(
        jnp.bfloat16
    )
    seq_queries = rotated.reshape(sequences, seq_rows, local_heads, HEAD)
    query_blocks = (slot_positions // BLOCK).reshape(sequences, seq_rows)
    key_blocks = jnp.arange(seq_length, dtype=jnp.int32) // BLOCK

    attn_mixed, log_totals = attn_fwd(
        seq_queries.reshape(sequences, seq_rows, HEAD),
        seq_keys.reshape(sequences, seq_length, HEAD),
        seq_values.reshape(sequences, seq_length, HEAD),
        query_blocks[:, :, None],
    )
    mixed_rows = to_jg(attn_mixed.reshape(slot_rows, head_cols))
    output_stack = lax.all_gather(output_weight, GROUP_AXES, axis=0, tiled=True)
    attn_slots = to_owners(
        jnp.dot(to_rows(mixed_rows), output_stack, preferred_element_type=jnp.float32)
    )
    attn_gates = pair_gates(attn_logits, own_attn)
    attn_index, attn_pair_kept = pair_index(own_attn, attn_places, attn_kept, slot_cap)
    attn_picked = attn_slots.reshape(EXPERTS * slot_cap, width)[attn_index]
    hidden_state = own_input + jnp.sum(
        attn_picked * (attn_gates * attn_pair_kept)[:, :, None], axis=1
    )
    inverse_two = lax.rsqrt(jnp.mean(hidden_state * hidden_state, axis=-1, keepdims=True) + epsilon)
    normed_two = hidden_state * inverse_two
    mlp_input = (normed_two * gain_two.astype(jnp.float32)).astype(jnp.bfloat16)
    mlp_logits = jnp.dot(mlp_input, router_two, preferred_element_type=jnp.float32)
    mlp_gates = pair_gates(mlp_logits, own_mlp)
    mlp_index, mlp_pair_kept = pair_index(own_mlp, mlp_places, mlp_kept, slot_cap)
    mlp_slot_grad = (
        own_cotangent[mlp_token]
        * slot_gates(mlp_gates, mlp_pair_kept, own_mlp, mlp_token, mlp_valid)[:, :, None]
    ).astype(jnp.bfloat16)
    mlp_by_group = lax.all_to_all(
        jnp.concatenate([pick_slots(mlp_input, mlp_token, mlp_valid), mlp_slot_grad], axis=1),
        "grp",
        split_axis=0,
        concat_axis=0,
        tiled=True,
    )
    mlp_rows = lax.all_gather(
        mlp_by_group[:, :slot_cap].reshape(groups * slot_cap, width),
        GROUP_AXES,
        axis=0,
        tiled=True,
    )
    down_rows = lax.all_gather(
        mlp_by_group[:, slot_cap:].reshape(groups * slot_cap, width),
        GROUP_AXES,
        axis=0,
        tiled=True,
    )
    gate_pre = jnp.dot(mlp_rows, gate_weight, preferred_element_type=jnp.float32)
    up_pre = jnp.dot(mlp_rows, up_weight, preferred_element_type=jnp.float32)
    activated = jax.nn.silu(gate_pre)
    inner_rows = (activated * up_pre).astype(jnp.bfloat16)
    mlp_partial = jnp.dot(inner_rows, down_weight, preferred_element_type=jnp.float32)
    mlp_slots = combine(mlp_partial)
    mlp_picked = mlp_slots.reshape(EXPERTS * slot_cap, width)[mlp_index]
    own_output = hidden_state + jnp.sum(
        mlp_picked * (mlp_gates * mlp_pair_kept)[:, :, None], axis=1
    )
    mlp_gate_grad = jnp.sum(mlp_picked * own_cotangent[:, None, :], axis=-1) * mlp_pair_kept
    mlp_logit_grad = gates_back(mlp_gates, mlp_gate_grad, own_mlp)
    inner_grad = jnp.einsum("rd,fd->rf", down_rows, down_weight, preferred_element_type=jnp.float32)
    down_grad = jnp.einsum("rf,rd->fd", inner_rows, down_rows, preferred_element_type=jnp.float32)
    sigmoid_gate = jax.nn.sigmoid(gate_pre)
    gate_pre_grad = (
        inner_grad * up_pre * sigmoid_gate * (1.0 + gate_pre * (1.0 - sigmoid_gate))
    ).astype(jnp.bfloat16)
    up_pre_grad = (inner_grad * activated).astype(jnp.bfloat16)
    gate_grad = jnp.einsum("rd,rf->df", mlp_rows, gate_pre_grad, preferred_element_type=jnp.float32)
    up_grad = jnp.einsum("rd,rf->df", mlp_rows, up_pre_grad, preferred_element_type=jnp.float32)
    row_grad = jnp.einsum(
        "rf,df->rd", gate_pre_grad, gate_weight, preferred_element_type=jnp.float32
    ) + jnp.einsum("rf,df->rd", up_pre_grad, up_weight, preferred_element_type=jnp.float32)
    mlp_row_grad = combine(row_grad)
    mlp_input_grad = jnp.sum(
        mlp_row_grad.reshape(EXPERTS * slot_cap, width)[mlp_index] * mlp_pair_kept[:, :, None],
        axis=1,
    )
    mlp_input_grad = mlp_input_grad + jnp.dot(
        mlp_logit_grad, router_two.astype(jnp.float32).T, precision=lax.Precision.HIGHEST
    )
    mlp_router_own = jnp.dot(
        mlp_input.astype(jnp.float32).T, mlp_logit_grad, precision=lax.Precision.HIGHEST
    )
    hidden_grad, gain_two_own = norm_back(
        mlp_input_grad, gain_two.astype(jnp.float32), normed_two, inverse_two
    )
    hidden_grad = hidden_grad + own_cotangent
    attn_gate_grad = jnp.sum(attn_picked * hidden_grad[:, None, :], axis=-1) * attn_pair_kept
    attn_logit_grad = gates_back(attn_gates, attn_gate_grad, own_attn)
    attn_slot_grad = (
        hidden_grad[attn_token]
        * slot_gates(attn_gates, attn_pair_kept, own_attn, attn_token, attn_valid)[:, :, None]
    ).astype(jnp.bfloat16)
    out_rows = dispatch(attn_slot_grad)
    output_grad = jnp.einsum("rw,rd->wd", mixed_rows, out_rows, preferred_element_type=jnp.float32)
    mixed_grad = jnp.einsum(
        "rd,wd->rw", out_rows, output_weight, preferred_element_type=jnp.float32
    ).astype(jnp.bfloat16)
    seq_mixed_grad = to_gj(mixed_grad).reshape(sequences, seq_rows, local_heads, HEAD)

    seq_query_grad, seq_key_grad, seq_value_grad = attn_bwd(
        seq_queries.reshape(sequences, seq_rows, HEAD),
        seq_keys.reshape(sequences, seq_length, HEAD),
        seq_values.reshape(sequences, seq_length, HEAD),
        query_blocks[:, :, None],
        log_totals,
        seq_mixed_grad.reshape(sequences, seq_rows, HEAD),
    )
    query_rot_grad = to_jg(
        rotate_back(seq_query_grad.reshape(slot_rows, local_heads, HEAD), slot_cos, slot_sin)
        .reshape(slot_rows, head_cols)
        .astype(jnp.bfloat16)
    )
    query_grad = jnp.einsum(
        "rd,rw->dw", attn_rows, query_rot_grad, preferred_element_type=jnp.float32
    )
    query_stack = lax.all_gather(query_weight, GROUP_AXES, axis=1, tiled=True)
    attn_row_grad = to_owners(
        jnp.einsum(
            "rw,dw->rd", to_rows(query_rot_grad), query_stack, preferred_element_type=jnp.float32
        )
    )
    key_back, value_back = (
        lax.all_to_all(
            seq_key_grad.reshape(devices, own_rows, 1, head_cols).astype(jnp.bfloat16),
            ALL_AXES,
            split_axis=0,
            concat_axis=2,
            tiled=True,
        ).astype(jnp.float32),
        lax.all_to_all(
            seq_value_grad.reshape(devices, own_rows, 1, head_cols).astype(jnp.bfloat16),
            ALL_AXES,
            split_axis=0,
            concat_axis=2,
            tiled=True,
        ).astype(jnp.float32),
    )
    own_key_grad = jnp.sum(key_back.reshape(own_rows, EXPERTS, group_size, head_cols), axis=1)
    own_value_grad = jnp.sum(
        value_back.reshape(own_rows, EXPERTS, group_size, head_cols), axis=1
    ).reshape(own_rows, key_cols)
    kv_own_grad = jnp.concatenate(
        [rotate_back(own_key_grad, own_cos, own_sin).reshape(own_rows, key_cols), own_value_grad],
        axis=1,
    ).astype(jnp.bfloat16)
    attn_input_grad = jnp.sum(
        attn_row_grad.reshape(EXPERTS * slot_cap, width)[attn_index] * attn_pair_kept[:, :, None],
        axis=1,
    )
    attn_input_grad = attn_input_grad + jnp.einsum(
        "rc,dc->rd", kv_own_grad, kv_full, preferred_element_type=jnp.float32
    )
    attn_input_grad = attn_input_grad + jnp.dot(
        attn_logit_grad, router_one.astype(jnp.float32).T, precision=lax.Precision.HIGHEST
    )
    col_block = kv_width // group_size
    kv_col_grad = lax.all_to_all(
        kv_own_grad.reshape(own_rows, group_size, col_block),
        GROUP_AXES,
        split_axis=1,
        concat_axis=0,
        tiled=True,
    ).reshape(own_rows * group_size, col_block)
    kv_col_weight = jnp.einsum(
        "rd,rc->dc", seq_input, kv_col_grad, preferred_element_type=jnp.float32
    )
    attn_router_own = jnp.dot(
        attn_input.astype(jnp.float32).T, attn_logit_grad, precision=lax.Precision.HIGHEST
    )
    input_grad, gain_one_own = norm_back(
        attn_input_grad, gain_one.astype(jnp.float32), normed_one, inverse_one
    )
    input_grad = input_grad + hidden_grad
    grad_extras = jnp.concatenate(
        [gain_one_own[:, None], gain_two_own[:, None], attn_router_own, mlp_router_own], axis=1
    )
    packed_grad = jnp.concatenate(
        [
            kv_col_weight,
            jnp.pad(grad_extras, ((0, 0), (0, extra_pad - grad_extras.shape[1]))),
        ],
        axis=1,
    )
    group_sum = lax.psum_scatter(packed_grad, "grp", scatter_dimension=0, tiled=True)
    dealt = lax.all_to_all(
        group_sum.reshape(group_size, kv_rows, col_block + extra_pad),
        GROUP_AXES,
        split_axis=0,
        concat_axis=0,
        tiled=True,
    )
    kv_grad = jnp.moveaxis(dealt[:, :, :col_block], 0, 1).reshape(kv_rows, kv_width)
    extra_grad = jnp.sum(dealt[:, :, col_block:], axis=0)
    gain_one_grad = extra_grad[:, 0]
    gain_two_grad = extra_grad[:, 1]
    attn_router_grad = extra_grad[:, 2 : 2 + EXPERTS]
    mlp_router_grad = extra_grad[:, 2 + EXPERTS : 2 + 2 * EXPERTS]
    both_full = lax.all_gather(
        jnp.concatenate(
            [own_output.astype(jnp.bfloat16), input_grad.astype(jnp.bfloat16)], axis=1
        ),
        "expert",
        axis=0,
        tiled=True,
    )
    mixed_full, input_full = both_full[:, :width], both_full[:, width:]
    return (
        mixed_full,
        input_full,
        gain_one_grad,
        kv_grad,
        attn_router_grad,
        query_grad,
        output_grad,
        gain_two_grad,
        mlp_router_grad,
        gate_grad,
        up_grad,
        down_grad,
    )


def solution(mesh):
    seq_size, halves = mesh.devices.shape
    grouped = jax.sharding.Mesh(
        mesh.devices.reshape(EXPERTS, seq_size // EXPERTS, halves), ALL_AXES
    )
    return jax.shard_map(
        shards,
        mesh=grouped,
        in_specs=(
            P(SEQ_AXES, None),
            P(ALL_AXES),
            P(ALL_AXES, None),
            P(ALL_AXES, None),
            P(None, ALL_AXES),
            P(ALL_AXES, None),
            P(ALL_AXES),
            P(ALL_AXES, None),
            P(None, ALL_AXES),
            P(None, ALL_AXES),
            P(ALL_AXES, None),
            P(SEQ_AXES, None),
            P(SEQ_AXES, None),
            P(SEQ_AXES, None),
            P(SEQ_AXES, None),
        ),
        out_specs=(
            P(SEQ_AXES, None),
            P(SEQ_AXES, None),
            P(ALL_AXES),
            P(ALL_AXES, None),
            P(ALL_AXES, None),
            P(None, ALL_AXES),
            P(ALL_AXES, None),
            P(ALL_AXES),
            P(ALL_AXES, None),
            P(None, ALL_AXES),
            P(None, ALL_AXES),
            P(ALL_AXES, None),
        ),
        check_vma=False,
    )
```

```python
import functools
import math

import jax
import jax.numpy as jnp
from jax import lax
from jax.experimental import pallas as pl
from jax.sharding import PartitionSpec as P

ALL_AXES = ("grp", "sub", "expert")
SEQ_AXES = ("grp", "sub")
GROUP_AXES = ("sub", "expert")
KV_HEADS = 16
HEAD = 128
EXPERTS = 8
TOPK = 2
PIECES = 8
BLOCK = 256


epsilon = 1e-06
masked_score = -1e30


def _scores(q, k, qb, scale):
    s = lax.dot_general(q, k, (((1,), (1,)), ((), ())), preferred_element_type=jnp.float32) * scale
    kblock = lax.broadcasted_iota(jnp.int32, s.shape, 1) // BLOCK
    return jnp.where(kblock <= qb, s, masked_score)

def _fwd_kernel(scale, q_ref, k_ref, v_ref, qb_ref, o_ref, lse_ref):
    s = _scores(q_ref[...], k_ref[...], qb_ref[...], scale)
    largest = jnp.max(s, axis=-1, keepdims=True)
    weights = jnp.exp(s - largest)
    totals = jnp.sum(weights, axis=-1, keepdims=True)
    probs = weights / totals
    o_ref[...] = jnp.dot(probs.astype(jnp.bfloat16), v_ref[...],
                         preferred_element_type=jnp.float32).astype(o_ref.dtype)
    lse_ref[...] = largest + jnp.log(totals)

def _bwd_kernel(scale, q_ref, k_ref, v_ref, qb_ref, lse_ref, do_ref, dq_ref, dk_ref, dv_ref):
    q = q_ref[...]; k = k_ref[...]; v = v_ref[...]; do = do_ref[...]
    probs = jnp.exp(_scores(q, k, qb_ref[...], scale) - lse_ref[...])
    dp = lax.dot_general(do, v, (((1,), (1,)), ((), ())), preferred_element_type=jnp.float32)
    inner = jnp.sum(probs * dp, axis=-1, keepdims=True)
    ds = (probs * (dp - inner)).astype(jnp.bfloat16)
    dv_ref[...] = lax.dot_general(probs.astype(jnp.bfloat16), do, (((0,), (0,)), ((), ())),
                                  preferred_element_type=jnp.float32)
    dk_ref[...] = lax.dot_general(ds, q, (((0,), (0,)), ((), ())),
                                  preferred_element_type=jnp.float32) * scale
    dq_ref[...] = jnp.dot(ds, k, preferred_element_type=jnp.float32) * scale

def attn_fwd(q, k, v, qb):
    n, rows, d = q.shape; keys = k.shape[1]
    scale = 1.0 / math.sqrt(d)
    rspec = pl.BlockSpec((None, rows, d), lambda i: (i, 0, 0))
    kspec = pl.BlockSpec((None, keys, d), lambda i: (i, 0, 0))
    cspec = pl.BlockSpec((None, rows, 1), lambda i: (i, 0, 0))
    return pl.pallas_call(
        functools.partial(_fwd_kernel, scale),
        grid=(n,),
        in_specs=[rspec, kspec, kspec, cspec],
        out_specs=[rspec, cspec],
        out_shape=[jax.ShapeDtypeStruct((n, rows, d), jnp.bfloat16),
                   jax.ShapeDtypeStruct((n, rows, 1), jnp.float32)],
        cost_estimate=pl.CostEstimate(flops=4 * n * rows * keys * d,
                                      transcendentals=n * rows * keys,
                                      bytes_accessed=2 * n * (2 * rows * d + 2 * keys * d)),
    )(q, k, v, qb)

def attn_bwd(q, k, v, qb, lse, do):
    n, rows, d = q.shape; keys = k.shape[1]
    scale = 1.0 / math.sqrt(d)
    rspec = pl.BlockSpec((None, rows, d), lambda i: (i, 0, 0))
    kspec = pl.BlockSpec((None, keys, d), lambda i: (i, 0, 0))
    cspec = pl.BlockSpec((None, rows, 1), lambda i: (i, 0, 0))
    return pl.pallas_call(
        functools.partial(_bwd_kernel, scale),
        grid=(n,),
        in_specs=[rspec, kspec, kspec, cspec, cspec, rspec],
        out_specs=[rspec, kspec, kspec],
        out_shape=[jax.ShapeDtypeStruct((n, rows, d), jnp.float32),
                   jax.ShapeDtypeStruct((n, keys, d), jnp.float32),
                   jax.ShapeDtypeStruct((n, keys, d), jnp.float32)],
        cost_estimate=pl.CostEstimate(flops=10 * n * rows * keys * d,
                                      transcendentals=n * rows * keys,
                                      bytes_accessed=2 * n * (3 * rows * d + 2 * keys * d) + 8 * n * (rows * d + 2 * keys * d)),
    )(q, k, v, qb, lse, do)


def rope_tables(positions, head_size):
    half_size = head_size // 2
    frequency = jnp.exp(
        jnp.arange(half_size, dtype=jnp.float32) * (-2.0 * math.log(10000.0) / head_size)
    )
    angles = positions.astype(jnp.float32)[:, None] * frequency[None, :]
    return (jnp.cos(angles)[:, None, :], jnp.sin(angles)[:, None, :])


def rotate(values, cosines, sines):
    half_size = values.shape[-1] // 2
    first = values[..., :half_size]
    second = values[..., half_size:]
    return jnp.concatenate(
        [first * cosines - second * sines, second * cosines + first * sines], axis=-1
    )


def rotate_back(grads, cosines, sines):
    half_size = grads.shape[-1] // 2
    first = grads[..., :half_size]
    second = grads[..., half_size:]
    return jnp.concatenate(
        [first * cosines + second * sines, second * cosines - first * sines], axis=-1
    )


def slot_table(expert_ids, ranks, slot_cap):
    block_rows = expert_ids.shape[0]
    expert_range = jnp.arange(EXPERTS, dtype=jnp.int32)
    member = jnp.sum(
        (expert_ids[:, :, None] == expert_range[None, None, :]).astype(jnp.int32), axis=1
    )
    earlier = (ranks[:, None] < ranks[None, :]).astype(jnp.int32)
    places = jnp.sum(earlier[:, :, None] * member[:, None, :], axis=0)
    kept = member * (places < slot_cap).astype(jnp.int32)
    slot_range = jnp.arange(slot_cap, dtype=jnp.int32)
    landing = kept[:, :, None] * (places[:, :, None] == slot_range[None, None, :]).astype(jnp.int32)
    row_range = jnp.arange(block_rows, dtype=jnp.int32)
    slot_token = jnp.sum(landing * row_range[:, None, None], axis=0)
    slot_valid = jnp.sum(landing, axis=0)
    return (places, kept, slot_token, slot_valid)


def pair_index(expert_ids, places, kept, slot_cap):
    chosen_place = jnp.take_along_axis(places, expert_ids, axis=1)
    chosen_kept = jnp.take_along_axis(kept, expert_ids, axis=1)
    return (
        expert_ids * slot_cap + jnp.minimum(chosen_place, slot_cap - 1),
        chosen_kept.astype(jnp.float32),
    )


def pair_gates(logits, expert_ids):
    return jax.nn.softmax(jnp.take_along_axis(logits, expert_ids, axis=1), axis=-1)


def expert_onehot(expert_ids):
    expert_range = jnp.arange(EXPERTS, dtype=jnp.int32)
    return (expert_ids[:, :, None] == expert_range[None, None, :]).astype(jnp.float32)


def gates_back(gates, gate_grads, expert_ids):
    inner = jnp.sum(gates * gate_grads, axis=1, keepdims=True)
    chosen_grads = gates * (gate_grads - inner)
    return jnp.sum(chosen_grads[:, :, None] * expert_onehot(expert_ids), axis=1)


def slot_gates(gates, pair_kept, expert_ids, slot_token, slot_valid):
    per_expert = jnp.sum((gates * pair_kept)[:, :, None] * expert_onehot(expert_ids), axis=1)
    return jnp.take_along_axis(per_expert.T, slot_token, axis=1) * slot_valid.astype(jnp.float32)


def pick_slots(values, slot_token, slot_valid):
    return jnp.where(slot_valid[:, :, None] > 0, values[slot_token], jnp.zeros((), values.dtype))


def fan_out(slot_values, group_size):
    experts_here, slot_cap, width = slot_values.shape
    spread_out = jnp.broadcast_to(slot_values[:, None], (experts_here, group_size, slot_cap, width))
    return spread_out.reshape(experts_here * group_size, slot_cap, width)


def fold_group(received, group_size):
    count, slot_cap, width = received.shape
    return jnp.sum(received.reshape(count // group_size, group_size, slot_cap, width), axis=1)


def norm_back(normed_grad, gain, normed, inverse):
    scaled = normed_grad * gain
    gain_grad = jnp.sum(normed_grad * normed, axis=0)
    input_grad = inverse * (scaled - normed * jnp.mean(scaled * normed, axis=-1, keepdims=True))
    return (input_grad, gain_grad)


def shards(
    tokens,
    attn_gain,
    kv_weight,
    attn_router,
    query_weight,
    output_weight,
    mlp_gain,
    mlp_router,
    gate_weight,
    up_weight,
    down_weight,
    attn_experts,
    mlp_experts,
    priority,
    cotangent,
):
    devices = lax.axis_size(ALL_AXES)
    halves = lax.axis_size("expert")
    device_index = lax.axis_index(ALL_AXES)
    half_index = lax.axis_index("expert")
    seq_tokens, width = tokens.shape
    own_rows = seq_tokens // halves
    group_size = devices // EXPERTS
    head_cols = query_weight.shape[1]
    local_heads = head_cols // HEAD
    key_cols = KV_HEADS * HEAD
    all_tokens = own_rows * devices
    seq_length = seq_tokens * PIECES
    sequences = all_tokens // seq_length
    slot_cap = (9 * TOPK * own_rows + 8 * EXPERTS - 1) // (8 * EXPERTS)
    slot_rows = devices * slot_cap
    seq_rows = slot_rows // sequences
    my_expert = device_index // group_size
    groups = lax.axis_size("grp")

    def dispatch(slot_values):
        by_group = lax.all_to_all(slot_values, "grp", split_axis=0, concat_axis=0, tiled=True)
        return lax.all_gather(
            by_group.reshape(groups * slot_cap, width), GROUP_AXES, axis=0, tiled=True
        )

    def combine(partial_value):
        parts = lax.all_to_all(
            partial_value.astype(jnp.bfloat16).reshape(group_size, groups * slot_cap, width),
            GROUP_AXES,
            split_axis=0,
            concat_axis=0,
            tiled=True,
        )
        summed = jnp.sum(parts.astype(jnp.float32), axis=0).reshape(groups, slot_cap, width)
        return lax.all_to_all(summed, "grp", split_axis=0, concat_axis=0, tiled=True)

    def to_rows(per_head):
        parts = lax.all_to_all(
            per_head.reshape(group_size, groups * slot_cap, head_cols),
            GROUP_AXES,
            split_axis=0,
            concat_axis=0,
            tiled=True,
        )
        return jnp.swapaxes(parts, 0, 1).reshape(groups * slot_cap, group_size * head_cols)

    def to_owners(row_values):
        return lax.all_to_all(
            row_values.reshape(groups, slot_cap, width), "grp", split_axis=0, concat_axis=0, tiled=True
        )

    def to_gj(rows):
        shaped = rows.reshape((group_size, groups, slot_cap) + rows.shape[1:])
        return jnp.swapaxes(shaped, 0, 1).reshape(rows.shape)

    def to_jg(rows):
        shaped = rows.reshape((groups, group_size, slot_cap) + rows.shape[1:])
        return jnp.swapaxes(shaped, 0, 1).reshape(rows.shape)
    scale = 1.0 / math.sqrt(HEAD)

    start_row = half_index * own_rows
    own_input = lax.dynamic_slice_in_dim(tokens, start_row, own_rows, 0).astype(jnp.float32)
    own_cotangent = lax.dynamic_slice_in_dim(cotangent, start_row, own_rows, 0).astype(jnp.float32)
    own_attn = lax.dynamic_slice_in_dim(attn_experts, start_row, own_rows, 0)
    own_mlp = lax.dynamic_slice_in_dim(mlp_experts, start_row, own_rows, 0)
    own_rank = lax.dynamic_slice_in_dim(priority[0], start_row, own_rows, 0)
    token_order = jnp.arange(own_rows, dtype=jnp.int32)

    kv_rows, kv_width = kv_weight.shape
    id_cols = own_rows * TOPK // kv_rows
    extras = jnp.concatenate(
        [
            attn_gain[:, None],
            mlp_gain[:, None],
            attn_router,
            mlp_router,
            own_attn.reshape(kv_rows, id_cols).astype(jnp.bfloat16),
        ],
        axis=1,
    )
    extra_cols = extras.shape[1]
    extra_pad = -(-extra_cols // 128) * 128
    pair_cols = 2 * head_cols
    head_blocks = jnp.transpose(
        kv_weight.reshape(kv_rows, 2, group_size, head_cols), (2, 0, 1, 3)
    ).reshape(group_size, kv_rows, pair_cols)
    padded_extras = jnp.pad(extras, ((0, 0), (0, extra_pad - extra_cols)))
    dealt_rows = lax.all_to_all(
        jnp.concatenate(
            [
                head_blocks,
                jnp.broadcast_to(padded_extras[None], (group_size, kv_rows, extra_pad)),
            ],
            axis=2,
        ),
        GROUP_AXES,
        split_axis=0,
        concat_axis=0,
        tiled=True,
    )
    gathered = lax.all_gather(
        dealt_rows.reshape(group_size * kv_rows, pair_cols + extra_pad), "grp", axis=0, tiled=True
    )
    head_kv = gathered[:, :pair_cols]
    gain_one = gathered[:, pair_cols]
    gain_two = gathered[:, pair_cols + 1]
    router_one = gathered[:, pair_cols + 2 : pair_cols + 2 + EXPERTS]
    router_two = gathered[:, pair_cols + 2 + EXPERTS : pair_cols + 2 + 2 * EXPERTS]
    routes_all = gathered[:, pair_cols + 2 + 2 * EXPERTS : pair_cols + extra_cols].astype(jnp.int32)
    inverse_one = lax.rsqrt(jnp.mean(own_input * own_input, axis=-1, keepdims=True) + epsilon)
    normed_one = own_input * inverse_one
    attn_input = (normed_one * gain_one.astype(jnp.float32)).astype(jnp.bfloat16)
    attn_logits = jnp.dot(attn_input, router_one, preferred_element_type=jnp.float32)
    seq_input = lax.all_gather(attn_input, GROUP_AXES, axis=0, tiled=True)
    seq_kv = jnp.dot(seq_input, head_kv, preferred_element_type=jnp.float32)
    seq_cos, seq_sin = rope_tables(jnp.arange(seq_length, dtype=jnp.int32), HEAD)
    seq_pair = jnp.concatenate(
        [
            rotate(seq_kv[:, :head_cols].reshape(seq_length, local_heads, HEAD), seq_cos, seq_sin)
            .reshape(seq_length, head_cols)
            .astype(jnp.bfloat16),
            seq_kv[:, head_cols:].astype(jnp.bfloat16),
        ],
        axis=1,
    )
    all_pairs = lax.all_to_all(
        jnp.broadcast_to(seq_pair[None], (groups,) + seq_pair.shape),
        "grp",
        split_axis=0,
        concat_axis=0,
        tiled=True,
    ).reshape(groups * seq_length, 2 * head_cols)
    seq_keys = all_pairs[:, :head_cols].reshape(sequences, seq_length, local_heads, HEAD)
    seq_values = all_pairs[:, head_cols:].reshape(sequences, seq_length, local_heads, HEAD)
    attn_places, attn_kept, attn_token, attn_valid = slot_table(own_attn, token_order, slot_cap)
    mlp_places, mlp_kept, mlp_token, mlp_valid = slot_table(own_mlp, own_rank, slot_cap)
    block_routes = routes_all.reshape(devices, own_rows, TOPK)
    dest_tables = jax.vmap(lambda block_ids: slot_table(block_ids, token_order, slot_cap)[2])(
        block_routes
    )
    dest_token = jnp.take(dest_tables, my_expert, axis=1)
    attn_rows = dispatch(pick_slots(attn_input, attn_token, attn_valid))
    queries = to_gj(jnp.dot(attn_rows, query_weight, preferred_element_type=jnp.float32))
    slot_positions = (
        (jnp.arange(devices, dtype=jnp.int32)[:, None] * own_rows + dest_token) % seq_length
    ).reshape(slot_rows)
    slot_cos, slot_sin = rope_tables(slot_positions, HEAD)
    rotated = rotate(queries.reshape(slot_rows, local_heads, HEAD), slot_cos, slot_sin).astype(
        jnp.bfloat16
    )
    seq_queries = rotated.reshape(sequences, seq_rows, local_heads, HEAD)
    query_blocks = (slot_positions // BLOCK).reshape(sequences, seq_rows)
    key_blocks = jnp.arange(seq_length, dtype=jnp.int32) // BLOCK

    attn_mixed, log_totals = attn_fwd(
        seq_queries.reshape(sequences, seq_rows, HEAD),
        seq_keys.reshape(sequences, seq_length, HEAD),
        seq_values.reshape(sequences, seq_length, HEAD),
        query_blocks[:, :, None],
    )
    mixed_rows = to_jg(attn_mixed.reshape(slot_rows, head_cols))
    output_stack = lax.all_gather(output_weight, GROUP_AXES, axis=0, tiled=True)
    attn_slots = to_owners(
        jnp.dot(to_rows(mixed_rows), output_stack, preferred_element_type=jnp.float32)
    )
    attn_gates = pair_gates(attn_logits, own_attn)
    attn_index, attn_pair_kept = pair_index(own_attn, attn_places, attn_kept, slot_cap)
    attn_picked = attn_slots.reshape(EXPERTS * slot_cap, width)[attn_index]
    hidden_state = own_input + jnp.sum(
        attn_picked * (attn_gates * attn_pair_kept)[:, :, None], axis=1
    )
    inverse_two = lax.rsqrt(jnp.mean(hidden_state * hidden_state, axis=-1, keepdims=True) + epsilon)
    normed_two = hidden_state * inverse_two
    mlp_input = (normed_two * gain_two.astype(jnp.float32)).astype(jnp.bfloat16)
    mlp_logits = jnp.dot(mlp_input, router_two, preferred_element_type=jnp.float32)
    mlp_gates = pair_gates(mlp_logits, own_mlp)
    mlp_index, mlp_pair_kept = pair_index(own_mlp, mlp_places, mlp_kept, slot_cap)
    mlp_slot_grad = (
        own_cotangent[mlp_token]
        * slot_gates(mlp_gates, mlp_pair_kept, own_mlp, mlp_token, mlp_valid)[:, :, None]
    ).astype(jnp.bfloat16)
    mlp_by_group = lax.all_to_all(
        jnp.concatenate([pick_slots(mlp_input, mlp_token, mlp_valid), mlp_slot_grad], axis=1),
        "grp",
        split_axis=0,
        concat_axis=0,
        tiled=True,
    )
    mlp_rows = lax.all_gather(
        mlp_by_group[:, :slot_cap].reshape(groups * slot_cap, width),
        GROUP_AXES,
        axis=0,
        tiled=True,
    )
    down_rows = lax.all_gather(
        mlp_by_group[:, slot_cap:].reshape(groups * slot_cap, width),
        GROUP_AXES,
        axis=0,
        tiled=True,
    )
    gate_pre = jnp.dot(mlp_rows, gate_weight, preferred_element_type=jnp.float32)
    up_pre = jnp.dot(mlp_rows, up_weight, preferred_element_type=jnp.float32)
    activated = jax.nn.silu(gate_pre)
    inner_rows = (activated * up_pre).astype(jnp.bfloat16)
    mlp_partial = jnp.dot(inner_rows, down_weight, preferred_element_type=jnp.float32)
    mlp_slots = combine(mlp_partial)
    mlp_picked = mlp_slots.reshape(EXPERTS * slot_cap, width)[mlp_index]
    own_output = hidden_state + jnp.sum(
        mlp_picked * (mlp_gates * mlp_pair_kept)[:, :, None], axis=1
    )
    mlp_gate_grad = jnp.sum(mlp_picked * own_cotangent[:, None, :], axis=-1) * mlp_pair_kept
    mlp_logit_grad = gates_back(mlp_gates, mlp_gate_grad, own_mlp)
    inner_grad = jnp.einsum("rd,fd->rf", down_rows, down_weight, preferred_element_type=jnp.float32)
    down_grad = jnp.einsum("rf,rd->fd", inner_rows, down_rows, preferred_element_type=jnp.float32)
    sigmoid_gate = jax.nn.sigmoid(gate_pre)
    gate_pre_grad = (
        inner_grad * up_pre * sigmoid_gate * (1.0 + gate_pre * (1.0 - sigmoid_gate))
    ).astype(jnp.bfloat16)
    up_pre_grad = (inner_grad * activated).astype(jnp.bfloat16)
    gate_grad = jnp.einsum("rd,rf->df", mlp_rows, gate_pre_grad, preferred_element_type=jnp.float32)
    up_grad = jnp.einsum("rd,rf->df", mlp_rows, up_pre_grad, preferred_element_type=jnp.float32)
    row_grad = jnp.einsum(
        "rf,df->rd", gate_pre_grad, gate_weight, preferred_element_type=jnp.float32
    ) + jnp.einsum("rf,df->rd", up_pre_grad, up_weight, preferred_element_type=jnp.float32)
    mlp_row_grad = combine(row_grad)
    mlp_input_grad = jnp.sum(
        mlp_row_grad.reshape(EXPERTS * slot_cap, width)[mlp_index] * mlp_pair_kept[:, :, None],
        axis=1,
    )
    mlp_input_grad = mlp_input_grad + jnp.dot(
        mlp_logit_grad, router_two.astype(jnp.float32).T, precision=lax.Precision.HIGHEST
    )
    mlp_router_own = jnp.dot(
        mlp_input.astype(jnp.float32).T, mlp_logit_grad, precision=lax.Precision.HIGHEST
    )
    hidden_grad, gain_two_own = norm_back(
        mlp_input_grad, gain_two.astype(jnp.float32), normed_two, inverse_two
    )
    hidden_grad = hidden_grad + own_cotangent
    attn_gate_grad = jnp.sum(attn_picked * hidden_grad[:, None, :], axis=-1) * attn_pair_kept
    attn_logit_grad = gates_back(attn_gates, attn_gate_grad, own_attn)
    attn_slot_grad = (
        hidden_grad[attn_token]
        * slot_gates(attn_gates, attn_pair_kept, own_attn, attn_token, attn_valid)[:, :, None]
    ).astype(jnp.bfloat16)
    out_rows = dispatch(attn_slot_grad)
    output_grad = jnp.einsum("rw,rd->wd", mixed_rows, out_rows, preferred_element_type=jnp.float32)
    mixed_grad = jnp.einsum(
        "rd,wd->rw", out_rows, output_weight, preferred_element_type=jnp.float32
    ).astype(jnp.bfloat16)
    seq_mixed_grad = to_gj(mixed_grad).reshape(sequences, seq_rows, local_heads, HEAD)

    seq_query_grad, seq_key_grad, seq_value_grad = attn_bwd(
        seq_queries.reshape(sequences, seq_rows, HEAD),
        seq_keys.reshape(sequences, seq_length, HEAD),
        seq_values.reshape(sequences, seq_length, HEAD),
        query_blocks[:, :, None],
        log_totals,
        seq_mixed_grad.reshape(sequences, seq_rows, HEAD),
    )
    query_rot_grad = to_jg(
        rotate_back(seq_query_grad.reshape(slot_rows, local_heads, HEAD), slot_cos, slot_sin)
        .reshape(slot_rows, head_cols)
        .astype(jnp.bfloat16)
    )
    query_grad = jnp.einsum(
        "rd,rw->dw", attn_rows, query_rot_grad, preferred_element_type=jnp.float32
    )
    query_stack = lax.all_gather(query_weight, GROUP_AXES, axis=1, tiled=True)
    attn_row_grad = to_owners(
        jnp.einsum(
            "rw,dw->rd", to_rows(query_rot_grad), query_stack, preferred_element_type=jnp.float32
        )
    )
    pair_back = lax.all_to_all(
        jnp.concatenate([seq_key_grad, seq_value_grad], axis=2).astype(jnp.bfloat16),
        "grp",
        split_axis=0,
        concat_axis=0,
        tiled=True,
    )
    seq_pair_grad = jnp.sum(pair_back.astype(jnp.float32), axis=0)
    kv_col_grad = jnp.concatenate(
        [
            rotate_back(
                seq_pair_grad[:, :head_cols].reshape(seq_length, local_heads, HEAD),
                seq_cos,
                seq_sin,
            ).reshape(seq_length, head_cols),
            seq_pair_grad[:, head_cols:],
        ],
        axis=1,
    ).astype(jnp.bfloat16)
    kv_col_weight = jnp.einsum(
        "rd,rc->dc", seq_input, kv_col_grad, preferred_element_type=jnp.float32
    )
    kv_input_parts = lax.all_to_all(
        jnp.einsum("rc,dc->rd", kv_col_grad, head_kv, preferred_element_type=jnp.float32)
        .astype(jnp.bfloat16)
        .reshape(group_size, own_rows, width),
        GROUP_AXES,
        split_axis=0,
        concat_axis=0,
        tiled=True,
    )
    attn_input_grad = jnp.sum(
        attn_row_grad.reshape(EXPERTS * slot_cap, width)[attn_index] * attn_pair_kept[:, :, None],
        axis=1,
    )
    attn_input_grad = attn_input_grad + jnp.sum(kv_input_parts.astype(jnp.float32), axis=0)
    attn_input_grad = attn_input_grad + jnp.dot(
        attn_logit_grad, router_one.astype(jnp.float32).T, precision=lax.Precision.HIGHEST
    )
    attn_router_own = jnp.dot(
        attn_input.astype(jnp.float32).T, attn_logit_grad, precision=lax.Precision.HIGHEST
    )
    input_grad, gain_one_own = norm_back(
        attn_input_grad, gain_one.astype(jnp.float32), normed_one, inverse_one
    )
    input_grad = input_grad + hidden_grad
    grad_extras = jnp.concatenate(
        [gain_one_own[:, None], gain_two_own[:, None], attn_router_own, mlp_router_own], axis=1
    )
    packed_grad = jnp.concatenate(
        [
            kv_col_weight,
            jnp.pad(grad_extras, ((0, 0), (0, extra_pad - grad_extras.shape[1]))),
        ],
        axis=1,
    )
    group_sum = lax.psum_scatter(packed_grad, "grp", scatter_dimension=0, tiled=True)
    dealt = lax.all_to_all(
        group_sum.reshape(group_size, kv_rows, pair_cols + extra_pad),
        GROUP_AXES,
        split_axis=0,
        concat_axis=0,
        tiled=True,
    )
    kv_grad = jnp.transpose(
        dealt[:, :, :pair_cols].reshape(group_size, kv_rows, 2, head_cols), (1, 2, 0, 3)
    ).reshape(kv_rows, kv_width)
    extra_grad = jnp.sum(dealt[:, :, pair_cols:], axis=0)
    gain_one_grad = extra_grad[:, 0]
    gain_two_grad = extra_grad[:, 1]
    attn_router_grad = extra_grad[:, 2 : 2 + EXPERTS]
    mlp_router_grad = extra_grad[:, 2 + EXPERTS : 2 + 2 * EXPERTS]
    both_full = lax.all_gather(
        jnp.concatenate(
            [own_output.astype(jnp.bfloat16), input_grad.astype(jnp.bfloat16)], axis=1
        ),
        "expert",
        axis=0,
        tiled=True,
    )
    mixed_full, input_full = both_full[:, :width], both_full[:, width:]
    return (
        mixed_full,
        input_full,
        gain_one_grad,
        kv_grad,
        attn_router_grad,
        query_grad,
        output_grad,
        gain_two_grad,
        mlp_router_grad,
        gate_grad,
        up_grad,
        down_grad,
    )


def solution(mesh):
    seq_size, halves = mesh.devices.shape
    grouped = jax.sharding.Mesh(
        mesh.devices.reshape(EXPERTS, seq_size // EXPERTS, halves), ALL_AXES
    )
    return jax.shard_map(
        shards,
        mesh=grouped,
        in_specs=(
            P(SEQ_AXES, None),
            P(ALL_AXES),
            P(ALL_AXES, None),
            P(ALL_AXES, None),
            P(None, ALL_AXES),
            P(ALL_AXES, None),
            P(ALL_AXES),
            P(ALL_AXES, None),
            P(None, ALL_AXES),
            P(None, ALL_AXES),
            P(ALL_AXES, None),
            P(SEQ_AXES, None),
            P(SEQ_AXES, None),
            P(SEQ_AXES, None),
            P(SEQ_AXES, None),
        ),
        out_specs=(
            P(SEQ_AXES, None),
            P(SEQ_AXES, None),
            P(ALL_AXES),
            P(ALL_AXES, None),
            P(ALL_AXES, None),
            P(None, ALL_AXES),
            P(ALL_AXES, None),
            P(ALL_AXES),
            P(ALL_AXES, None),
            P(None, ALL_AXES),
            P(None, ALL_AXES),
            P(ALL_AXES, None),
        ),
        check_vma=False,
    )
```

```python
import functools
import math

import jax
import jax.numpy as jnp
from jax import lax
from jax.experimental import pallas as pl
from jax.sharding import PartitionSpec as P

ALL_AXES = ("grp", "sub", "expert")
SEQ_AXES = ("grp", "sub")
GROUP_AXES = ("sub", "expert")
KV_HEADS = 16
HEAD = 128
EXPERTS = 8
TOPK = 2
PIECES = 8
BLOCK = 256


epsilon = 1e-06
masked_score = -1e30


def _scores(q, k, qb, scale):
    s = lax.dot_general(q, k, (((1,), (1,)), ((), ())), preferred_element_type=jnp.float32) * scale
    kblock = lax.broadcasted_iota(jnp.int32, s.shape, 1) // BLOCK
    return jnp.where(kblock <= qb, s, masked_score)

def _fwd_kernel(scale, q_ref, k_ref, v_ref, qb_ref, o_ref, lse_ref):
    s = _scores(q_ref[...], k_ref[...], qb_ref[...], scale)
    largest = jnp.max(s, axis=-1, keepdims=True)
    weights = jnp.exp(s - largest)
    totals = jnp.sum(weights, axis=-1, keepdims=True)
    probs = weights / totals
    o_ref[...] = jnp.dot(probs.astype(jnp.bfloat16), v_ref[...],
                         preferred_element_type=jnp.float32).astype(o_ref.dtype)
    lse_ref[...] = largest + jnp.log(totals)

def _bwd_kernel(scale, q_ref, k_ref, v_ref, qb_ref, lse_ref, do_ref, dq_ref, dk_ref, dv_ref):
    q = q_ref[...]; k = k_ref[...]; v = v_ref[...]; do = do_ref[...]
    probs = jnp.exp(_scores(q, k, qb_ref[...], scale) - lse_ref[...])
    dp = lax.dot_general(do, v, (((1,), (1,)), ((), ())), preferred_element_type=jnp.float32)
    inner = jnp.sum(probs * dp, axis=-1, keepdims=True)
    ds = (probs * (dp - inner)).astype(jnp.bfloat16)
    dv_ref[...] = lax.dot_general(probs.astype(jnp.bfloat16), do, (((0,), (0,)), ((), ())),
                                  preferred_element_type=jnp.float32)
    dk_ref[...] = lax.dot_general(ds, q, (((0,), (0,)), ((), ())),
                                  preferred_element_type=jnp.float32) * scale
    dq_ref[...] = jnp.dot(ds, k, preferred_element_type=jnp.float32) * scale

def attn_fwd(q, k, v, qb):
    n, rows, d = q.shape; keys = k.shape[1]
    scale = 1.0 / math.sqrt(d)
    rspec = pl.BlockSpec((None, rows, d), lambda i: (i, 0, 0))
    kspec = pl.BlockSpec((None, keys, d), lambda i: (i, 0, 0))
    cspec = pl.BlockSpec((None, rows, 1), lambda i: (i, 0, 0))
    return pl.pallas_call(
        functools.partial(_fwd_kernel, scale),
        grid=(n,),
        in_specs=[rspec, kspec, kspec, cspec],
        out_specs=[rspec, cspec],
        out_shape=[jax.ShapeDtypeStruct((n, rows, d), jnp.bfloat16),
                   jax.ShapeDtypeStruct((n, rows, 1), jnp.float32)],
        cost_estimate=pl.CostEstimate(flops=4 * n * rows * keys * d,
                                      transcendentals=n * rows * keys,
                                      bytes_accessed=2 * n * (2 * rows * d + 2 * keys * d)),
    )(q, k, v, qb)

def attn_bwd(q, k, v, qb, lse, do):
    n, rows, d = q.shape; keys = k.shape[1]
    scale = 1.0 / math.sqrt(d)
    rspec = pl.BlockSpec((None, rows, d), lambda i: (i, 0, 0))
    kspec = pl.BlockSpec((None, keys, d), lambda i: (i, 0, 0))
    cspec = pl.BlockSpec((None, rows, 1), lambda i: (i, 0, 0))
    return pl.pallas_call(
        functools.partial(_bwd_kernel, scale),
        grid=(n,),
        in_specs=[rspec, kspec, kspec, cspec, cspec, rspec],
        out_specs=[rspec, kspec, kspec],
        out_shape=[jax.ShapeDtypeStruct((n, rows, d), jnp.float32),
                   jax.ShapeDtypeStruct((n, keys, d), jnp.float32),
                   jax.ShapeDtypeStruct((n, keys, d), jnp.float32)],
        cost_estimate=pl.CostEstimate(flops=10 * n * rows * keys * d,
                                      transcendentals=n * rows * keys,
                                      bytes_accessed=2 * n * (3 * rows * d + 2 * keys * d) + 8 * n * (rows * d + 2 * keys * d)),
    )(q, k, v, qb, lse, do)


def rope_tables(positions, head_size):
    half_size = head_size // 2
    frequency = jnp.exp(
        jnp.arange(half_size, dtype=jnp.float32) * (-2.0 * math.log(10000.0) / head_size)
    )
    angles = positions.astype(jnp.float32)[:, None] * frequency[None, :]
    return (jnp.cos(angles)[:, None, :], jnp.sin(angles)[:, None, :])


def rotate(values, cosines, sines):
    half_size = values.shape[-1] // 2
    first = values[..., :half_size]
    second = values[..., half_size:]
    return jnp.concatenate(
        [first * cosines - second * sines, second * cosines + first * sines], axis=-1
    )


def rotate_back(grads, cosines, sines):
    half_size = grads.shape[-1] // 2
    first = grads[..., :half_size]
    second = grads[..., half_size:]
    return jnp.concatenate(
        [first * cosines + second * sines, second * cosines - first * sines], axis=-1
    )


def slot_table(expert_ids, ranks, slot_cap):
    block_rows = expert_ids.shape[0]
    expert_range = jnp.arange(EXPERTS, dtype=jnp.int32)
    member = jnp.sum(
        (expert_ids[:, :, None] == expert_range[None, None, :]).astype(jnp.int32), axis=1
    )
    earlier = (ranks[:, None] < ranks[None, :]).astype(jnp.int32)
    places = jnp.sum(earlier[:, :, None] * member[:, None, :], axis=0)
    kept = member * (places < slot_cap).astype(jnp.int32)
    slot_range = jnp.arange(slot_cap, dtype=jnp.int32)
    landing = kept[:, :, None] * (places[:, :, None] == slot_range[None, None, :]).astype(jnp.int32)
    row_range = jnp.arange(block_rows, dtype=jnp.int32)
    slot_token = jnp.sum(landing * row_range[:, None, None], axis=0)
    slot_valid = jnp.sum(landing, axis=0)
    return (places, kept, slot_token, slot_valid)


def pair_index(expert_ids, places, kept, slot_cap):
    chosen_place = jnp.take_along_axis(places, expert_ids, axis=1)
    chosen_kept = jnp.take_along_axis(kept, expert_ids, axis=1)
    return (
        expert_ids * slot_cap + jnp.minimum(chosen_place, slot_cap - 1),
        chosen_kept.astype(jnp.float32),
    )


def pair_gates(logits, expert_ids):
    return jax.nn.softmax(jnp.take_along_axis(logits, expert_ids, axis=1), axis=-1)


def expert_onehot(expert_ids):
    expert_range = jnp.arange(EXPERTS, dtype=jnp.int32)
    return (expert_ids[:, :, None] == expert_range[None, None, :]).astype(jnp.float32)


def gates_back(gates, gate_grads, expert_ids):
    inner = jnp.sum(gates * gate_grads, axis=1, keepdims=True)
    chosen_grads = gates * (gate_grads - inner)
    return jnp.sum(chosen_grads[:, :, None] * expert_onehot(expert_ids), axis=1)


def slot_gates(gates, pair_kept, expert_ids, slot_token, slot_valid):
    per_expert = jnp.sum((gates * pair_kept)[:, :, None] * expert_onehot(expert_ids), axis=1)
    return jnp.take_along_axis(per_expert.T, slot_token, axis=1) * slot_valid.astype(jnp.float32)


def pick_slots(values, slot_token, slot_valid):
    return jnp.where(slot_valid[:, :, None] > 0, values[slot_token], jnp.zeros((), values.dtype))


def fan_out(slot_values, group_size):
    experts_here, slot_cap, width = slot_values.shape
    spread_out = jnp.broadcast_to(slot_values[:, None], (experts_here, group_size, slot_cap, width))
    return spread_out.reshape(experts_here * group_size, slot_cap, width)


def fold_group(received, group_size):
    count, slot_cap, width = received.shape
    return jnp.sum(received.reshape(count // group_size, group_size, slot_cap, width), axis=1)


def norm_back(normed_grad, gain, normed, inverse):
    scaled = normed_grad * gain
    gain_grad = jnp.sum(normed_grad * normed, axis=0)
    input_grad = inverse * (scaled - normed * jnp.mean(scaled * normed, axis=-1, keepdims=True))
    return (input_grad, gain_grad)


def shards(
    tokens,
    attn_gain,
    kv_weight,
    attn_router,
    query_weight,
    output_weight,
    mlp_gain,
    mlp_router,
    gate_weight,
    up_weight,
    down_weight,
    attn_experts,
    mlp_experts,
    priority,
    cotangent,
):
    devices = lax.axis_size(ALL_AXES)
    halves = lax.axis_size("expert")
    device_index = lax.axis_index(ALL_AXES)
    half_index = lax.axis_index("expert")
    seq_tokens, width = tokens.shape
    own_rows = seq_tokens // halves
    group_size = devices // EXPERTS
    head_cols = query_weight.shape[1]
    local_heads = head_cols // HEAD
    key_cols = KV_HEADS * HEAD
    all_tokens = own_rows * devices
    seq_length = seq_tokens * PIECES
    sequences = all_tokens // seq_length
    slot_cap = (9 * TOPK * own_rows + 8 * EXPERTS - 1) // (8 * EXPERTS)
    slot_rows = devices * slot_cap
    seq_rows = slot_rows // sequences
    my_expert = device_index // group_size
    groups = lax.axis_size("grp")

    def dispatch(slot_values):
        by_group = lax.all_to_all(slot_values, "grp", split_axis=0, concat_axis=0, tiled=True)
        return lax.all_gather(
            by_group.reshape(groups * slot_cap, width), GROUP_AXES, axis=0, tiled=True
        )

    def combine(partial_value):
        parts = lax.all_to_all(
            partial_value.astype(jnp.bfloat16).reshape(group_size, groups * slot_cap, width),
            GROUP_AXES,
            split_axis=0,
            concat_axis=0,
            tiled=True,
        )
        summed = jnp.sum(parts.astype(jnp.float32), axis=0).reshape(groups, slot_cap, width)
        return lax.all_to_all(summed, "grp", split_axis=0, concat_axis=0, tiled=True)

    def to_rows(per_head):
        parts = lax.all_to_all(
            per_head.reshape(group_size, groups * slot_cap, head_cols),
            GROUP_AXES,
            split_axis=0,
            concat_axis=0,
            tiled=True,
        )
        return jnp.swapaxes(parts, 0, 1).reshape(groups * slot_cap, group_size * head_cols)

    def to_owners(row_values):
        return lax.all_to_all(
            row_values.reshape(groups, slot_cap, width), "grp", split_axis=0, concat_axis=0, tiled=True
        )

    def to_gj(rows):
        shaped = rows.reshape((group_size, groups, slot_cap) + rows.shape[1:])
        return jnp.swapaxes(shaped, 0, 1).reshape(rows.shape)

    def to_jg(rows):
        shaped = rows.reshape((groups, group_size, slot_cap) + rows.shape[1:])
        return jnp.swapaxes(shaped, 0, 1).reshape(rows.shape)
    scale = 1.0 / math.sqrt(HEAD)

    start_row = half_index * own_rows
    own_input = lax.dynamic_slice_in_dim(tokens, start_row, own_rows, 0).astype(jnp.float32)
    own_cotangent = lax.dynamic_slice_in_dim(cotangent, start_row, own_rows, 0).astype(jnp.float32)
    own_attn = lax.dynamic_slice_in_dim(attn_experts, start_row, own_rows, 0)
    own_mlp = lax.dynamic_slice_in_dim(mlp_experts, start_row, own_rows, 0)
    own_rank = lax.dynamic_slice_in_dim(priority[0], start_row, own_rows, 0)
    token_order = jnp.arange(own_rows, dtype=jnp.int32)

    kv_rows, kv_width = kv_weight.shape
    id_cols = own_rows * TOPK // kv_rows
    extras = jnp.concatenate(
        [
            attn_gain[:, None],
            mlp_gain[:, None],
            attn_router,
            mlp_router,
            own_attn.reshape(kv_rows, id_cols).astype(jnp.bfloat16),
        ],
        axis=1,
    )
    extra_cols = extras.shape[1]
    extra_pad = -(-extra_cols // 128) * 128
    pair_cols = 2 * head_cols
    head_blocks = jnp.transpose(
        kv_weight.reshape(kv_rows, 2, group_size, head_cols), (2, 0, 1, 3)
    ).reshape(group_size, kv_rows, pair_cols)
    padded_extras = jnp.pad(extras, ((0, 0), (0, extra_pad - extra_cols)))
    dealt_rows = lax.all_to_all(
        jnp.concatenate(
            [
                head_blocks,
                jnp.broadcast_to(padded_extras[None], (group_size, kv_rows, extra_pad)),
            ],
            axis=2,
        ),
        GROUP_AXES,
        split_axis=0,
        concat_axis=0,
        tiled=True,
    )
    gathered = lax.all_to_all(
        jnp.broadcast_to(
            dealt_rows.reshape(1, group_size * kv_rows, pair_cols + extra_pad),
            (groups, group_size * kv_rows, pair_cols + extra_pad),
        ),
        "grp",
        split_axis=0,
        concat_axis=0,
        tiled=True,
    ).reshape(devices * kv_rows, pair_cols + extra_pad)
    head_kv = gathered[:, :pair_cols]
    gain_one = gathered[:, pair_cols]
    gain_two = gathered[:, pair_cols + 1]
    router_one = gathered[:, pair_cols + 2 : pair_cols + 2 + EXPERTS]
    router_two = gathered[:, pair_cols + 2 + EXPERTS : pair_cols + 2 + 2 * EXPERTS]
    routes_all = gathered[:, pair_cols + 2 + 2 * EXPERTS : pair_cols + extra_cols].astype(jnp.int32)
    inverse_one = lax.rsqrt(jnp.mean(own_input * own_input, axis=-1, keepdims=True) + epsilon)
    normed_one = own_input * inverse_one
    attn_input = (normed_one * gain_one.astype(jnp.float32)).astype(jnp.bfloat16)
    attn_logits = jnp.dot(attn_input, router_one, preferred_element_type=jnp.float32)
    seq_input = lax.all_gather(attn_input, GROUP_AXES, axis=0, tiled=True)
    seq_kv = jnp.dot(seq_input, head_kv, preferred_element_type=jnp.float32)
    seq_cos, seq_sin = rope_tables(jnp.arange(seq_length, dtype=jnp.int32), HEAD)
    seq_pair = jnp.concatenate(
        [
            rotate(seq_kv[:, :head_cols].reshape(seq_length, local_heads, HEAD), seq_cos, seq_sin)
            .reshape(seq_length, head_cols)
            .astype(jnp.bfloat16),
            seq_kv[:, head_cols:].astype(jnp.bfloat16),
        ],
        axis=1,
    )
    all_pairs = lax.all_to_all(
        jnp.broadcast_to(seq_pair[None], (groups,) + seq_pair.shape),
        "grp",
        split_axis=0,
        concat_axis=0,
        tiled=True,
    ).reshape(groups * seq_length, 2 * head_cols)
    seq_keys = all_pairs[:, :head_cols].reshape(sequences, seq_length, local_heads, HEAD)
    seq_values = all_pairs[:, head_cols:].reshape(sequences, seq_length, local_heads, HEAD)
    attn_places, attn_kept, attn_token, attn_valid = slot_table(own_attn, token_order, slot_cap)
    mlp_places, mlp_kept, mlp_token, mlp_valid = slot_table(own_mlp, own_rank, slot_cap)
    block_routes = routes_all.reshape(devices, own_rows, TOPK)
    dest_tables = jax.vmap(lambda block_ids: slot_table(block_ids, token_order, slot_cap)[2])(
        block_routes
    )
    dest_token = jnp.take(dest_tables, my_expert, axis=1)
    attn_rows = dispatch(pick_slots(attn_input, attn_token, attn_valid))
    queries = to_gj(jnp.dot(attn_rows, query_weight, preferred_element_type=jnp.float32))
    slot_positions = (
        (jnp.arange(devices, dtype=jnp.int32)[:, None] * own_rows + dest_token) % seq_length
    ).reshape(slot_rows)
    slot_cos, slot_sin = rope_tables(slot_positions, HEAD)
    rotated = rotate(queries.reshape(slot_rows, local_heads, HEAD), slot_cos, slot_sin).astype(
        jnp.bfloat16
    )
    seq_queries = rotated.reshape(sequences, seq_rows, local_heads, HEAD)
    query_blocks = (slot_positions // BLOCK).reshape(sequences, seq_rows)
    key_blocks = jnp.arange(seq_length, dtype=jnp.int32) // BLOCK

    attn_mixed, log_totals = attn_fwd(
        seq_queries.reshape(sequences, seq_rows, HEAD),
        seq_keys.reshape(sequences, seq_length, HEAD),
        seq_values.reshape(sequences, seq_length, HEAD),
        query_blocks[:, :, None],
    )
    mixed_rows = to_jg(attn_mixed.reshape(slot_rows, head_cols))
    output_stack = lax.all_gather(output_weight, GROUP_AXES, axis=0, tiled=True)
    attn_slots = to_owners(
        jnp.dot(to_rows(mixed_rows), output_stack, preferred_element_type=jnp.float32)
    )
    attn_gates = pair_gates(attn_logits, own_attn)
    attn_index, attn_pair_kept = pair_index(own_attn, attn_places, attn_kept, slot_cap)
    attn_picked = attn_slots.reshape(EXPERTS * slot_cap, width)[attn_index]
    hidden_state = own_input + jnp.sum(
        attn_picked * (attn_gates * attn_pair_kept)[:, :, None], axis=1
    )
    inverse_two = lax.rsqrt(jnp.mean(hidden_state * hidden_state, axis=-1, keepdims=True) + epsilon)
    normed_two = hidden_state * inverse_two
    mlp_input = (normed_two * gain_two.astype(jnp.float32)).astype(jnp.bfloat16)
    mlp_logits = jnp.dot(mlp_input, router_two, preferred_element_type=jnp.float32)
    mlp_gates = pair_gates(mlp_logits, own_mlp)
    mlp_index, mlp_pair_kept = pair_index(own_mlp, mlp_places, mlp_kept, slot_cap)
    mlp_slot_grad = (
        own_cotangent[mlp_token]
        * slot_gates(mlp_gates, mlp_pair_kept, own_mlp, mlp_token, mlp_valid)[:, :, None]
    ).astype(jnp.bfloat16)
    mlp_by_group = lax.all_to_all(
        jnp.concatenate([pick_slots(mlp_input, mlp_token, mlp_valid), mlp_slot_grad], axis=1),
        "grp",
        split_axis=0,
        concat_axis=0,
        tiled=True,
    )
    mlp_rows = lax.all_gather(
        mlp_by_group[:, :slot_cap].reshape(groups * slot_cap, width),
        GROUP_AXES,
        axis=0,
        tiled=True,
    )
    down_rows = lax.all_gather(
        mlp_by_group[:, slot_cap:].reshape(groups * slot_cap, width),
        GROUP_AXES,
        axis=0,
        tiled=True,
    )
    gate_pre = jnp.dot(mlp_rows, gate_weight, preferred_element_type=jnp.float32)
    up_pre = jnp.dot(mlp_rows, up_weight, preferred_element_type=jnp.float32)
    activated = jax.nn.silu(gate_pre)
    inner_rows = (activated * up_pre).astype(jnp.bfloat16)
    mlp_partial = jnp.dot(inner_rows, down_weight, preferred_element_type=jnp.float32)
    mlp_slots = combine(mlp_partial)
    query_stack = lax.all_gather(query_weight, GROUP_AXES, axis=1, tiled=True)
    mlp_slots, query_stack = lax.optimization_barrier((mlp_slots, query_stack))
    mlp_picked = mlp_slots.reshape(EXPERTS * slot_cap, width)[mlp_index]
    own_output = hidden_state + jnp.sum(
        mlp_picked * (mlp_gates * mlp_pair_kept)[:, :, None], axis=1
    )
    mlp_gate_grad = jnp.sum(mlp_picked * own_cotangent[:, None, :], axis=-1) * mlp_pair_kept
    mlp_logit_grad = gates_back(mlp_gates, mlp_gate_grad, own_mlp)
    inner_grad = jnp.einsum("rd,fd->rf", down_rows, down_weight, preferred_element_type=jnp.float32)
    down_grad = jnp.einsum("rf,rd->fd", inner_rows, down_rows, preferred_element_type=jnp.float32)
    sigmoid_gate = jax.nn.sigmoid(gate_pre)
    gate_pre_grad = (
        inner_grad * up_pre * sigmoid_gate * (1.0 + gate_pre * (1.0 - sigmoid_gate))
    ).astype(jnp.bfloat16)
    up_pre_grad = (inner_grad * activated).astype(jnp.bfloat16)
    gate_grad = jnp.einsum("rd,rf->df", mlp_rows, gate_pre_grad, preferred_element_type=jnp.float32)
    up_grad = jnp.einsum("rd,rf->df", mlp_rows, up_pre_grad, preferred_element_type=jnp.float32)
    row_grad = jnp.einsum(
        "rf,df->rd", gate_pre_grad, gate_weight, preferred_element_type=jnp.float32
    ) + jnp.einsum("rf,df->rd", up_pre_grad, up_weight, preferred_element_type=jnp.float32)
    mlp_row_grad = combine(row_grad)
    mlp_input_grad = jnp.sum(
        mlp_row_grad.reshape(EXPERTS * slot_cap, width)[mlp_index] * mlp_pair_kept[:, :, None],
        axis=1,
    )
    mlp_input_grad = mlp_input_grad + jnp.dot(
        mlp_logit_grad, router_two.astype(jnp.float32).T, precision=lax.Precision.HIGHEST
    )
    mlp_router_own = jnp.dot(
        mlp_input.astype(jnp.float32).T, mlp_logit_grad, precision=lax.Precision.HIGHEST
    )
    hidden_grad, gain_two_own = norm_back(
        mlp_input_grad, gain_two.astype(jnp.float32), normed_two, inverse_two
    )
    hidden_grad = hidden_grad + own_cotangent
    attn_gate_grad = jnp.sum(attn_picked * hidden_grad[:, None, :], axis=-1) * attn_pair_kept
    attn_logit_grad = gates_back(attn_gates, attn_gate_grad, own_attn)
    attn_slot_grad = (
        hidden_grad[attn_token]
        * slot_gates(attn_gates, attn_pair_kept, own_attn, attn_token, attn_valid)[:, :, None]
    ).astype(jnp.bfloat16)
    out_rows = dispatch(attn_slot_grad)
    output_grad = jnp.einsum("rw,rd->wd", mixed_rows, out_rows, preferred_element_type=jnp.float32)
    mixed_grad = jnp.einsum(
        "rd,wd->rw", out_rows, output_weight, preferred_element_type=jnp.float32
    ).astype(jnp.bfloat16)
    seq_mixed_grad = to_gj(mixed_grad).reshape(sequences, seq_rows, local_heads, HEAD)

    seq_query_grad, seq_key_grad, seq_value_grad = attn_bwd(
        seq_queries.reshape(sequences, seq_rows, HEAD),
        seq_keys.reshape(sequences, seq_length, HEAD),
        seq_values.reshape(sequences, seq_length, HEAD),
        query_blocks[:, :, None],
        log_totals,
        seq_mixed_grad.reshape(sequences, seq_rows, HEAD),
    )
    query_rot_grad = to_jg(
        rotate_back(seq_query_grad.reshape(slot_rows, local_heads, HEAD), slot_cos, slot_sin)
        .reshape(slot_rows, head_cols)
        .astype(jnp.bfloat16)
    )
    query_grad = jnp.einsum(
        "rd,rw->dw", attn_rows, query_rot_grad, preferred_element_type=jnp.float32
    )
    attn_row_grad = to_owners(
        jnp.einsum(
            "rw,dw->rd", to_rows(query_rot_grad), query_stack, preferred_element_type=jnp.float32
        )
    )
    pair_back = lax.all_to_all(
        jnp.concatenate([seq_key_grad, seq_value_grad], axis=2).astype(jnp.bfloat16),
        "grp",
        split_axis=0,
        concat_axis=0,
        tiled=True,
    )
    seq_pair_grad = jnp.sum(pair_back.astype(jnp.float32), axis=0)
    kv_col_grad = jnp.concatenate(
        [
            rotate_back(
                seq_pair_grad[:, :head_cols].reshape(seq_length, local_heads, HEAD),
                seq_cos,
                seq_sin,
            ).reshape(seq_length, head_cols),
            seq_pair_grad[:, head_cols:],
        ],
        axis=1,
    ).astype(jnp.bfloat16)
    kv_col_weight = jnp.einsum(
        "rd,rc->dc", seq_input, kv_col_grad, preferred_element_type=jnp.float32
    )
    kv_input_parts = lax.all_to_all(
        jnp.einsum("rc,dc->rd", kv_col_grad, head_kv, preferred_element_type=jnp.float32)
        .astype(jnp.bfloat16)
        .reshape(group_size, own_rows, width),
        GROUP_AXES,
        split_axis=0,
        concat_axis=0,
        tiled=True,
    )
    attn_input_grad = jnp.sum(
        attn_row_grad.reshape(EXPERTS * slot_cap, width)[attn_index] * attn_pair_kept[:, :, None],
        axis=1,
    )
    attn_input_grad = attn_input_grad + jnp.sum(kv_input_parts.astype(jnp.float32), axis=0)
    attn_input_grad = attn_input_grad + jnp.dot(
        attn_logit_grad, router_one.astype(jnp.float32).T, precision=lax.Precision.HIGHEST
    )
    attn_router_own = jnp.dot(
        attn_input.astype(jnp.float32).T, attn_logit_grad, precision=lax.Precision.HIGHEST
    )
    input_grad, gain_one_own = norm_back(
        attn_input_grad, gain_one.astype(jnp.float32), normed_one, inverse_one
    )
    input_grad = input_grad + hidden_grad
    grad_extras = jnp.concatenate(
        [gain_one_own[:, None], gain_two_own[:, None], attn_router_own, mlp_router_own], axis=1
    )
    packed_grad = jnp.concatenate(
        [
            kv_col_weight,
            jnp.pad(grad_extras, ((0, 0), (0, extra_pad - grad_extras.shape[1]))),
        ],
        axis=1,
    )
    group_sum = lax.psum_scatter(packed_grad, "grp", scatter_dimension=0, tiled=True)
    dealt = lax.all_to_all(
        group_sum.reshape(group_size, kv_rows, pair_cols + extra_pad),
        GROUP_AXES,
        split_axis=0,
        concat_axis=0,
        tiled=True,
    )
    kv_grad = jnp.transpose(
        dealt[:, :, :pair_cols].reshape(group_size, kv_rows, 2, head_cols), (1, 2, 0, 3)
    ).reshape(kv_rows, kv_width)
    extra_grad = jnp.sum(dealt[:, :, pair_cols:], axis=0)
    gain_one_grad = extra_grad[:, 0]
    gain_two_grad = extra_grad[:, 1]
    attn_router_grad = extra_grad[:, 2 : 2 + EXPERTS]
    mlp_router_grad = extra_grad[:, 2 + EXPERTS : 2 + 2 * EXPERTS]
    both_full = lax.all_gather(
        jnp.concatenate(
            [own_output.astype(jnp.bfloat16), input_grad.astype(jnp.bfloat16)], axis=1
        ),
        "expert",
        axis=0,
        tiled=True,
    )
    mixed_full, input_full = both_full[:, :width], both_full[:, width:]
    return (
        mixed_full,
        input_full,
        gain_one_grad,
        kv_grad,
        attn_router_grad,
        query_grad,
        output_grad,
        gain_two_grad,
        mlp_router_grad,
        gate_grad,
        up_grad,
        down_grad,
    )


def solution(mesh):
    seq_size, halves = mesh.devices.shape
    grouped = jax.sharding.Mesh(
        mesh.devices.reshape(EXPERTS, seq_size // EXPERTS, halves), ALL_AXES
    )
    return jax.shard_map(
        shards,
        mesh=grouped,
        in_specs=(
            P(SEQ_AXES, None),
            P(ALL_AXES),
            P(ALL_AXES, None),
            P(ALL_AXES, None),
            P(None, ALL_AXES),
            P(ALL_AXES, None),
            P(ALL_AXES),
            P(ALL_AXES, None),
            P(None, ALL_AXES),
            P(None, ALL_AXES),
            P(ALL_AXES, None),
            P(SEQ_AXES, None),
            P(SEQ_AXES, None),
            P(SEQ_AXES, None),
            P(SEQ_AXES, None),
        ),
        out_specs=(
            P(SEQ_AXES, None),
            P(SEQ_AXES, None),
            P(ALL_AXES),
            P(ALL_AXES, None),
            P(ALL_AXES, None),
            P(None, ALL_AXES),
            P(ALL_AXES, None),
            P(ALL_AXES),
            P(ALL_AXES, None),
            P(None, ALL_AXES),
            P(None, ALL_AXES),
            P(ALL_AXES, None),
        ),
        check_vma=False,
    )
```

```python
import functools
import math

import jax
import jax.numpy as jnp
from jax import lax
from jax.experimental import pallas as pl
from jax.sharding import PartitionSpec as P

ALL_AXES = ("grp", "sub", "expert")
SEQ_AXES = ("grp", "sub")
GROUP_AXES = ("sub", "expert")
KV_HEADS = 16
HEAD = 128
EXPERTS = 8
TOPK = 2
PIECES = 8
BLOCK = 256


epsilon = 1e-06
masked_score = -1e30


def _scores(q, k, qb, scale):
    s = lax.dot_general(q, k, (((1,), (1,)), ((), ())), preferred_element_type=jnp.float32) * scale
    kblock = lax.broadcasted_iota(jnp.int32, s.shape, 1) // BLOCK
    return jnp.where(kblock <= qb, s, masked_score)

def _fwd_kernel(scale, q_ref, k_ref, v_ref, qb_ref, o_ref, lse_ref):
    s = _scores(q_ref[...], k_ref[...], qb_ref[...], scale)
    largest = jnp.max(s, axis=-1, keepdims=True)
    weights = jnp.exp(s - largest)
    totals = jnp.sum(weights, axis=-1, keepdims=True)
    probs = weights / totals
    o_ref[...] = jnp.dot(probs.astype(jnp.bfloat16), v_ref[...],
                         preferred_element_type=jnp.float32).astype(o_ref.dtype)
    lse_ref[...] = largest + jnp.log(totals)

def _bwd_kernel(scale, q_ref, k_ref, v_ref, qb_ref, lse_ref, do_ref, dq_ref, dk_ref, dv_ref):
    q = q_ref[...]; k = k_ref[...]; v = v_ref[...]; do = do_ref[...]
    probs = jnp.exp(_scores(q, k, qb_ref[...], scale) - lse_ref[...])
    dp = lax.dot_general(do, v, (((1,), (1,)), ((), ())), preferred_element_type=jnp.float32)
    inner = jnp.sum(probs * dp, axis=-1, keepdims=True)
    ds = (probs * (dp - inner)).astype(jnp.bfloat16)
    dv_ref[...] = lax.dot_general(probs.astype(jnp.bfloat16), do, (((0,), (0,)), ((), ())),
                                  preferred_element_type=jnp.float32)
    dk_ref[...] = lax.dot_general(ds, q, (((0,), (0,)), ((), ())),
                                  preferred_element_type=jnp.float32) * scale
    dq_ref[...] = jnp.dot(ds, k, preferred_element_type=jnp.float32) * scale

def attn_fwd(q, k, v, qb):
    n, rows, d = q.shape; keys = k.shape[1]
    scale = 1.0 / math.sqrt(d)
    rspec = pl.BlockSpec((None, rows, d), lambda i: (i, 0, 0))
    kspec = pl.BlockSpec((None, keys, d), lambda i: (i, 0, 0))
    cspec = pl.BlockSpec((None, rows, 1), lambda i: (i, 0, 0))
    return pl.pallas_call(
        functools.partial(_fwd_kernel, scale),
        grid=(n,),
        in_specs=[rspec, kspec, kspec, cspec],
        out_specs=[rspec, cspec],
        out_shape=[jax.ShapeDtypeStruct((n, rows, d), jnp.bfloat16),
                   jax.ShapeDtypeStruct((n, rows, 1), jnp.float32)],
        cost_estimate=pl.CostEstimate(flops=4 * n * rows * keys * d,
                                      transcendentals=n * rows * keys,
                                      bytes_accessed=2 * n * (2 * rows * d + 2 * keys * d)),
    )(q, k, v, qb)

def attn_bwd(q, k, v, qb, lse, do):
    n, rows, d = q.shape; keys = k.shape[1]
    scale = 1.0 / math.sqrt(d)
    rspec = pl.BlockSpec((None, rows, d), lambda i: (i, 0, 0))
    kspec = pl.BlockSpec((None, keys, d), lambda i: (i, 0, 0))
    cspec = pl.BlockSpec((None, rows, 1), lambda i: (i, 0, 0))
    return pl.pallas_call(
        functools.partial(_bwd_kernel, scale),
        grid=(n,),
        in_specs=[rspec, kspec, kspec, cspec, cspec, rspec],
        out_specs=[rspec, kspec, kspec],
        out_shape=[jax.ShapeDtypeStruct((n, rows, d), jnp.float32),
                   jax.ShapeDtypeStruct((n, keys, d), jnp.float32),
                   jax.ShapeDtypeStruct((n, keys, d), jnp.float32)],
        cost_estimate=pl.CostEstimate(flops=10 * n * rows * keys * d,
                                      transcendentals=n * rows * keys,
                                      bytes_accessed=2 * n * (3 * rows * d + 2 * keys * d) + 8 * n * (rows * d + 2 * keys * d)),
    )(q, k, v, qb, lse, do)


def rope_tables(positions, head_size):
    half_size = head_size // 2
    frequency = jnp.exp(
        jnp.arange(half_size, dtype=jnp.float32) * (-2.0 * math.log(10000.0) / head_size)
    )
    angles = positions.astype(jnp.float32)[:, None] * frequency[None, :]
    return (jnp.cos(angles)[:, None, :], jnp.sin(angles)[:, None, :])


def rotate(values, cosines, sines):
    half_size = values.shape[-1] // 2
    first = values[..., :half_size]
    second = values[..., half_size:]
    return jnp.concatenate(
        [first * cosines - second * sines, second * cosines + first * sines], axis=-1
    )


def rotate_back(grads, cosines, sines):
    half_size = grads.shape[-1] // 2
    first = grads[..., :half_size]
    second = grads[..., half_size:]
    return jnp.concatenate(
        [first * cosines + second * sines, second * cosines - first * sines], axis=-1
    )


def slot_table(expert_ids, ranks, slot_cap):
    block_rows = expert_ids.shape[0]
    expert_range = jnp.arange(EXPERTS, dtype=jnp.int32)
    member = jnp.sum(
        (expert_ids[:, :, None] == expert_range[None, None, :]).astype(jnp.int32), axis=1
    )
    earlier = (ranks[:, None] < ranks[None, :]).astype(jnp.int32)
    places = jnp.sum(earlier[:, :, None] * member[:, None, :], axis=0)
    kept = member * (places < slot_cap).astype(jnp.int32)
    slot_range = jnp.arange(slot_cap, dtype=jnp.int32)
    landing = kept[:, :, None] * (places[:, :, None] == slot_range[None, None, :]).astype(jnp.int32)
    row_range = jnp.arange(block_rows, dtype=jnp.int32)
    slot_token = jnp.sum(landing * row_range[:, None, None], axis=0)
    slot_valid = jnp.sum(landing, axis=0)
    return (places, kept, slot_token, slot_valid)


def pair_index(expert_ids, places, kept, slot_cap):
    chosen_place = jnp.take_along_axis(places, expert_ids, axis=1)
    chosen_kept = jnp.take_along_axis(kept, expert_ids, axis=1)
    return (
        expert_ids * slot_cap + jnp.minimum(chosen_place, slot_cap - 1),
        chosen_kept.astype(jnp.float32),
    )


def pair_gates(logits, expert_ids):
    return jax.nn.softmax(jnp.take_along_axis(logits, expert_ids, axis=1), axis=-1)


def expert_onehot(expert_ids):
    expert_range = jnp.arange(EXPERTS, dtype=jnp.int32)
    return (expert_ids[:, :, None] == expert_range[None, None, :]).astype(jnp.float32)


def gates_back(gates, gate_grads, expert_ids):
    inner = jnp.sum(gates * gate_grads, axis=1, keepdims=True)
    chosen_grads = gates * (gate_grads - inner)
    return jnp.sum(chosen_grads[:, :, None] * expert_onehot(expert_ids), axis=1)


def slot_gates(gates, pair_kept, expert_ids, slot_token, slot_valid):
    per_expert = jnp.sum((gates * pair_kept)[:, :, None] * expert_onehot(expert_ids), axis=1)
    return jnp.take_along_axis(per_expert.T, slot_token, axis=1) * slot_valid.astype(jnp.float32)


def pick_slots(values, slot_token, slot_valid):
    return jnp.where(slot_valid[:, :, None] > 0, values[slot_token], jnp.zeros((), values.dtype))


def fan_out(slot_values, group_size):
    experts_here, slot_cap, width = slot_values.shape
    spread_out = jnp.broadcast_to(slot_values[:, None], (experts_here, group_size, slot_cap, width))
    return spread_out.reshape(experts_here * group_size, slot_cap, width)


def fold_group(received, group_size):
    count, slot_cap, width = received.shape
    return jnp.sum(received.reshape(count // group_size, group_size, slot_cap, width), axis=1)


def norm_back(normed_grad, gain, normed, inverse):
    scaled = normed_grad * gain
    gain_grad = jnp.sum(normed_grad * normed, axis=0)
    input_grad = inverse * (scaled - normed * jnp.mean(scaled * normed, axis=-1, keepdims=True))
    return (input_grad, gain_grad)


def shards(
    tokens,
    attn_gain,
    kv_weight,
    attn_router,
    query_weight,
    output_weight,
    mlp_gain,
    mlp_router,
    gate_weight,
    up_weight,
    down_weight,
    attn_experts,
    mlp_experts,
    priority,
    cotangent,
):
    devices = lax.axis_size(ALL_AXES)
    halves = lax.axis_size("expert")
    device_index = lax.axis_index(ALL_AXES)
    half_index = lax.axis_index("expert")
    seq_tokens, width = tokens.shape
    own_rows = seq_tokens // halves
    group_size = devices // EXPERTS
    head_cols = query_weight.shape[1]
    local_heads = head_cols // HEAD
    key_cols = KV_HEADS * HEAD
    all_tokens = own_rows * devices
    seq_length = seq_tokens * PIECES
    sequences = all_tokens // seq_length
    slot_cap = (9 * TOPK * own_rows + 8 * EXPERTS - 1) // (8 * EXPERTS)
    slot_rows = devices * slot_cap
    seq_rows = slot_rows // sequences
    my_expert = device_index // group_size
    groups = lax.axis_size("grp")

    def dispatch(slot_values):
        by_group = lax.all_to_all(slot_values, "grp", split_axis=0, concat_axis=0, tiled=True)
        return lax.all_gather(
            by_group.reshape(groups * slot_cap, width), GROUP_AXES, axis=0, tiled=True
        )

    def combine(partial_value):
        parts = lax.all_to_all(
            partial_value.astype(jnp.bfloat16).reshape(group_size, groups * slot_cap, width),
            GROUP_AXES,
            split_axis=0,
            concat_axis=0,
            tiled=True,
        )
        summed = jnp.sum(parts.astype(jnp.float32), axis=0).reshape(groups, slot_cap, width)
        return lax.all_to_all(summed, "grp", split_axis=0, concat_axis=0, tiled=True)

    def combine_scattered(partial_value):
        summed = lax.psum_scatter(
            partial_value.astype(jnp.bfloat16), GROUP_AXES, scatter_dimension=0, tiled=True
        )
        return lax.all_to_all(
            summed.astype(jnp.float32).reshape(groups, slot_cap, width),
            "grp",
            split_axis=0,
            concat_axis=0,
            tiled=True,
        )

    def to_rows(per_head):
        parts = lax.all_to_all(
            per_head.reshape(group_size, groups * slot_cap, head_cols),
            GROUP_AXES,
            split_axis=0,
            concat_axis=0,
            tiled=True,
        )
        return jnp.swapaxes(parts, 0, 1).reshape(groups * slot_cap, group_size * head_cols)

    def to_owners(row_values):
        return lax.all_to_all(
            row_values.reshape(groups, slot_cap, width), "grp", split_axis=0, concat_axis=0, tiled=True
        )

    def to_gj(rows):
        shaped = rows.reshape((group_size, groups, slot_cap) + rows.shape[1:])
        return jnp.swapaxes(shaped, 0, 1).reshape(rows.shape)

    def to_jg(rows):
        shaped = rows.reshape((groups, group_size, slot_cap) + rows.shape[1:])
        return jnp.swapaxes(shaped, 0, 1).reshape(rows.shape)
    scale = 1.0 / math.sqrt(HEAD)

    start_row = half_index * own_rows
    own_input = lax.dynamic_slice_in_dim(tokens, start_row, own_rows, 0).astype(jnp.float32)
    own_cotangent = lax.dynamic_slice_in_dim(cotangent, start_row, own_rows, 0).astype(jnp.float32)
    own_attn = lax.dynamic_slice_in_dim(attn_experts, start_row, own_rows, 0)
    own_mlp = lax.dynamic_slice_in_dim(mlp_experts, start_row, own_rows, 0)
    own_rank = lax.dynamic_slice_in_dim(priority[0], start_row, own_rows, 0)
    token_order = jnp.arange(own_rows, dtype=jnp.int32)

    kv_rows, kv_width = kv_weight.shape
    id_cols = own_rows * TOPK // kv_rows
    extras = jnp.concatenate(
        [
            attn_gain[:, None],
            mlp_gain[:, None],
            attn_router,
            mlp_router,
            own_attn.reshape(kv_rows, id_cols).astype(jnp.bfloat16),
        ],
        axis=1,
    )
    extra_cols = extras.shape[1]
    extra_pad = -(-extra_cols // 128) * 128
    pair_cols = 2 * head_cols
    head_blocks = jnp.transpose(
        kv_weight.reshape(kv_rows, 2, group_size, head_cols), (2, 0, 1, 3)
    ).reshape(group_size, kv_rows, pair_cols)
    padded_extras = jnp.pad(extras, ((0, 0), (0, extra_pad - extra_cols)))
    dealt_rows = lax.all_to_all(
        jnp.concatenate(
            [
                head_blocks,
                jnp.broadcast_to(padded_extras[None], (group_size, kv_rows, extra_pad)),
            ],
            axis=2,
        ),
        GROUP_AXES,
        split_axis=0,
        concat_axis=0,
        tiled=True,
    )
    gathered = lax.all_to_all(
        jnp.broadcast_to(
            dealt_rows.reshape(1, group_size * kv_rows, pair_cols + extra_pad),
            (groups, group_size * kv_rows, pair_cols + extra_pad),
        ),
        "grp",
        split_axis=0,
        concat_axis=0,
        tiled=True,
    ).reshape(devices * kv_rows, pair_cols + extra_pad)
    head_kv = gathered[:, :pair_cols]
    gain_one = gathered[:, pair_cols]
    gain_two = gathered[:, pair_cols + 1]
    router_one = gathered[:, pair_cols + 2 : pair_cols + 2 + EXPERTS]
    router_two = gathered[:, pair_cols + 2 + EXPERTS : pair_cols + 2 + 2 * EXPERTS]
    routes_all = gathered[:, pair_cols + 2 + 2 * EXPERTS : pair_cols + extra_cols].astype(jnp.int32)
    inverse_one = lax.rsqrt(jnp.mean(own_input * own_input, axis=-1, keepdims=True) + epsilon)
    normed_one = own_input * inverse_one
    attn_input = (normed_one * gain_one.astype(jnp.float32)).astype(jnp.bfloat16)
    attn_logits = jnp.dot(attn_input, router_one, preferred_element_type=jnp.float32)
    seq_input = lax.all_gather(attn_input, GROUP_AXES, axis=0, tiled=True)
    seq_kv = jnp.dot(seq_input, head_kv, preferred_element_type=jnp.float32)
    seq_cos, seq_sin = rope_tables(jnp.arange(seq_length, dtype=jnp.int32), HEAD)
    seq_pair = jnp.concatenate(
        [
            rotate(seq_kv[:, :head_cols].reshape(seq_length, local_heads, HEAD), seq_cos, seq_sin)
            .reshape(seq_length, head_cols)
            .astype(jnp.bfloat16),
            seq_kv[:, head_cols:].astype(jnp.bfloat16),
        ],
        axis=1,
    )
    all_pairs = lax.all_to_all(
        jnp.broadcast_to(seq_pair[None], (groups,) + seq_pair.shape),
        "grp",
        split_axis=0,
        concat_axis=0,
        tiled=True,
    ).reshape(groups * seq_length, 2 * head_cols)
    seq_keys = all_pairs[:, :head_cols].reshape(sequences, seq_length, local_heads, HEAD)
    seq_values = all_pairs[:, head_cols:].reshape(sequences, seq_length, local_heads, HEAD)
    attn_places, attn_kept, attn_token, attn_valid = slot_table(own_attn, token_order, slot_cap)
    mlp_places, mlp_kept, mlp_token, mlp_valid = slot_table(own_mlp, own_rank, slot_cap)
    block_routes = routes_all.reshape(devices, own_rows, TOPK)
    dest_tables = jax.vmap(lambda block_ids: slot_table(block_ids, token_order, slot_cap)[2])(
        block_routes
    )
    dest_token = jnp.take(dest_tables, my_expert, axis=1)
    attn_rows = dispatch(pick_slots(attn_input, attn_token, attn_valid))
    queries = to_gj(jnp.dot(attn_rows, query_weight, preferred_element_type=jnp.float32))
    slot_positions = (
        (jnp.arange(devices, dtype=jnp.int32)[:, None] * own_rows + dest_token) % seq_length
    ).reshape(slot_rows)
    slot_cos, slot_sin = rope_tables(slot_positions, HEAD)
    rotated = rotate(queries.reshape(slot_rows, local_heads, HEAD), slot_cos, slot_sin).astype(
        jnp.bfloat16
    )
    seq_queries = rotated.reshape(sequences, seq_rows, local_heads, HEAD)
    query_blocks = (slot_positions // BLOCK).reshape(sequences, seq_rows)
    key_blocks = jnp.arange(seq_length, dtype=jnp.int32) // BLOCK

    attn_mixed, log_totals = attn_fwd(
        seq_queries.reshape(sequences, seq_rows, HEAD),
        seq_keys.reshape(sequences, seq_length, HEAD),
        seq_values.reshape(sequences, seq_length, HEAD),
        query_blocks[:, :, None],
    )
    mixed_rows = to_jg(attn_mixed.reshape(slot_rows, head_cols))
    output_stack = lax.all_gather(output_weight, GROUP_AXES, axis=0, tiled=True)
    attn_slots = to_owners(
        jnp.dot(to_rows(mixed_rows), output_stack, preferred_element_type=jnp.float32)
    )
    attn_gates = pair_gates(attn_logits, own_attn)
    attn_index, attn_pair_kept = pair_index(own_attn, attn_places, attn_kept, slot_cap)
    attn_picked = attn_slots.reshape(EXPERTS * slot_cap, width)[attn_index]
    hidden_state = own_input + jnp.sum(
        attn_picked * (attn_gates * attn_pair_kept)[:, :, None], axis=1
    )
    inverse_two = lax.rsqrt(jnp.mean(hidden_state * hidden_state, axis=-1, keepdims=True) + epsilon)
    normed_two = hidden_state * inverse_two
    mlp_input = (normed_two * gain_two.astype(jnp.float32)).astype(jnp.bfloat16)
    mlp_logits = jnp.dot(mlp_input, router_two, preferred_element_type=jnp.float32)
    mlp_gates = pair_gates(mlp_logits, own_mlp)
    mlp_index, mlp_pair_kept = pair_index(own_mlp, mlp_places, mlp_kept, slot_cap)
    mlp_slot_grad = (
        own_cotangent[mlp_token]
        * slot_gates(mlp_gates, mlp_pair_kept, own_mlp, mlp_token, mlp_valid)[:, :, None]
    ).astype(jnp.bfloat16)
    mlp_by_group = lax.all_to_all(
        jnp.concatenate([pick_slots(mlp_input, mlp_token, mlp_valid), mlp_slot_grad], axis=1),
        "grp",
        split_axis=0,
        concat_axis=0,
        tiled=True,
    )
    mlp_rows = lax.all_gather(
        mlp_by_group[:, :slot_cap].reshape(groups * slot_cap, width),
        GROUP_AXES,
        axis=0,
        tiled=True,
    )
    down_rows = lax.all_gather(
        mlp_by_group[:, slot_cap:].reshape(groups * slot_cap, width),
        GROUP_AXES,
        axis=0,
        tiled=True,
    )
    gate_pre = jnp.dot(mlp_rows, gate_weight, preferred_element_type=jnp.float32)
    up_pre = jnp.dot(mlp_rows, up_weight, preferred_element_type=jnp.float32)
    activated = jax.nn.silu(gate_pre)
    inner_rows = (activated * up_pre).astype(jnp.bfloat16)
    mlp_partial = jnp.dot(inner_rows, down_weight, preferred_element_type=jnp.float32)
    mlp_slots = combine_scattered(mlp_partial)
    query_stack = lax.all_gather(query_weight, GROUP_AXES, axis=1, tiled=True)
    mlp_slots, query_stack = lax.optimization_barrier((mlp_slots, query_stack))
    mlp_picked = mlp_slots.reshape(EXPERTS * slot_cap, width)[mlp_index]
    own_output = hidden_state + jnp.sum(
        mlp_picked * (mlp_gates * mlp_pair_kept)[:, :, None], axis=1
    )
    mlp_gate_grad = jnp.sum(mlp_picked * own_cotangent[:, None, :], axis=-1) * mlp_pair_kept
    mlp_logit_grad = gates_back(mlp_gates, mlp_gate_grad, own_mlp)
    inner_grad = jnp.einsum("rd,fd->rf", down_rows, down_weight, preferred_element_type=jnp.float32)
    down_grad = jnp.einsum("rf,rd->fd", inner_rows, down_rows, preferred_element_type=jnp.float32)
    sigmoid_gate = jax.nn.sigmoid(gate_pre)
    gate_pre_grad = (
        inner_grad * up_pre * sigmoid_gate * (1.0 + gate_pre * (1.0 - sigmoid_gate))
    ).astype(jnp.bfloat16)
    up_pre_grad = (inner_grad * activated).astype(jnp.bfloat16)
    gate_grad = jnp.einsum("rd,rf->df", mlp_rows, gate_pre_grad, preferred_element_type=jnp.float32)
    up_grad = jnp.einsum("rd,rf->df", mlp_rows, up_pre_grad, preferred_element_type=jnp.float32)
    row_grad = jnp.einsum(
        "rf,df->rd", gate_pre_grad, gate_weight, preferred_element_type=jnp.float32
    ) + jnp.einsum("rf,df->rd", up_pre_grad, up_weight, preferred_element_type=jnp.float32)
    mlp_row_grad = combine(row_grad)
    mlp_input_grad = jnp.sum(
        mlp_row_grad.reshape(EXPERTS * slot_cap, width)[mlp_index] * mlp_pair_kept[:, :, None],
        axis=1,
    )
    mlp_input_grad = mlp_input_grad + jnp.dot(
        mlp_logit_grad, router_two.astype(jnp.float32).T, precision=lax.Precision.HIGHEST
    )
    mlp_router_own = jnp.dot(
        mlp_input.astype(jnp.float32).T, mlp_logit_grad, precision=lax.Precision.HIGHEST
    )
    hidden_grad, gain_two_own = norm_back(
        mlp_input_grad, gain_two.astype(jnp.float32), normed_two, inverse_two
    )
    hidden_grad = hidden_grad + own_cotangent
    attn_gate_grad = jnp.sum(attn_picked * hidden_grad[:, None, :], axis=-1) * attn_pair_kept
    attn_logit_grad = gates_back(attn_gates, attn_gate_grad, own_attn)
    attn_slot_grad = (
        hidden_grad[attn_token]
        * slot_gates(attn_gates, attn_pair_kept, own_attn, attn_token, attn_valid)[:, :, None]
    ).astype(jnp.bfloat16)
    out_rows = dispatch(attn_slot_grad)
    output_grad = jnp.einsum("rw,rd->wd", mixed_rows, out_rows, preferred_element_type=jnp.float32)
    mixed_grad = jnp.einsum(
        "rd,wd->rw", out_rows, output_weight, preferred_element_type=jnp.float32
    ).astype(jnp.bfloat16)
    seq_mixed_grad = to_gj(mixed_grad).reshape(sequences, seq_rows, local_heads, HEAD)

    seq_query_grad, seq_key_grad, seq_value_grad = attn_bwd(
        seq_queries.reshape(sequences, seq_rows, HEAD),
        seq_keys.reshape(sequences, seq_length, HEAD),
        seq_values.reshape(sequences, seq_length, HEAD),
        query_blocks[:, :, None],
        log_totals,
        seq_mixed_grad.reshape(sequences, seq_rows, HEAD),
    )
    query_rot_grad = to_jg(
        rotate_back(seq_query_grad.reshape(slot_rows, local_heads, HEAD), slot_cos, slot_sin)
        .reshape(slot_rows, head_cols)
        .astype(jnp.bfloat16)
    )
    query_grad = jnp.einsum(
        "rd,rw->dw", attn_rows, query_rot_grad, preferred_element_type=jnp.float32
    )
    attn_row_grad = to_owners(
        jnp.einsum(
            "rw,dw->rd", to_rows(query_rot_grad), query_stack, preferred_element_type=jnp.float32
        )
    )
    pair_back = lax.all_to_all(
        jnp.concatenate([seq_key_grad, seq_value_grad], axis=2).astype(jnp.bfloat16),
        "grp",
        split_axis=0,
        concat_axis=0,
        tiled=True,
    )
    seq_pair_grad = jnp.sum(pair_back.astype(jnp.float32), axis=0)
    kv_col_grad = jnp.concatenate(
        [
            rotate_back(
                seq_pair_grad[:, :head_cols].reshape(seq_length, local_heads, HEAD),
                seq_cos,
                seq_sin,
            ).reshape(seq_length, head_cols),
            seq_pair_grad[:, head_cols:],
        ],
        axis=1,
    ).astype(jnp.bfloat16)
    kv_col_weight = jnp.einsum(
        "rd,rc->dc", seq_input, kv_col_grad, preferred_element_type=jnp.float32
    )
    kv_input_parts = lax.all_to_all(
        jnp.einsum("rc,dc->rd", kv_col_grad, head_kv, preferred_element_type=jnp.float32)
        .astype(jnp.bfloat16)
        .reshape(group_size, own_rows, width),
        GROUP_AXES,
        split_axis=0,
        concat_axis=0,
        tiled=True,
    )
    attn_input_grad = jnp.sum(
        attn_row_grad.reshape(EXPERTS * slot_cap, width)[attn_index] * attn_pair_kept[:, :, None],
        axis=1,
    )
    attn_input_grad = attn_input_grad + jnp.sum(kv_input_parts.astype(jnp.float32), axis=0)
    attn_input_grad = attn_input_grad + jnp.dot(
        attn_logit_grad, router_one.astype(jnp.float32).T, precision=lax.Precision.HIGHEST
    )
    attn_router_own = jnp.dot(
        attn_input.astype(jnp.float32).T, attn_logit_grad, precision=lax.Precision.HIGHEST
    )
    input_grad, gain_one_own = norm_back(
        attn_input_grad, gain_one.astype(jnp.float32), normed_one, inverse_one
    )
    input_grad = input_grad + hidden_grad
    grad_extras = jnp.concatenate(
        [gain_one_own[:, None], gain_two_own[:, None], attn_router_own, mlp_router_own], axis=1
    )
    packed_grad = jnp.concatenate(
        [
            kv_col_weight,
            jnp.pad(grad_extras, ((0, 0), (0, extra_pad - grad_extras.shape[1]))),
        ],
        axis=1,
    )
    group_sum = lax.psum_scatter(packed_grad, "grp", scatter_dimension=0, tiled=True)
    dealt = lax.all_to_all(
        group_sum.reshape(group_size, kv_rows, pair_cols + extra_pad),
        GROUP_AXES,
        split_axis=0,
        concat_axis=0,
        tiled=True,
    )
    kv_grad = jnp.transpose(
        dealt[:, :, :pair_cols].reshape(group_size, kv_rows, 2, head_cols), (1, 2, 0, 3)
    ).reshape(kv_rows, kv_width)
    extra_grad = jnp.sum(dealt[:, :, pair_cols:], axis=0)
    gain_one_grad = extra_grad[:, 0]
    gain_two_grad = extra_grad[:, 1]
    attn_router_grad = extra_grad[:, 2 : 2 + EXPERTS]
    mlp_router_grad = extra_grad[:, 2 + EXPERTS : 2 + 2 * EXPERTS]
    both_full = lax.all_gather(
        jnp.concatenate(
            [own_output.astype(jnp.bfloat16), input_grad.astype(jnp.bfloat16)], axis=1
        ),
        "expert",
        axis=0,
        tiled=True,
    )
    mixed_full, input_full = both_full[:, :width], both_full[:, width:]
    return (
        mixed_full,
        input_full,
        gain_one_grad,
        kv_grad,
        attn_router_grad,
        query_grad,
        output_grad,
        gain_two_grad,
        mlp_router_grad,
        gate_grad,
        up_grad,
        down_grad,
    )


def solution(mesh):
    seq_size, halves = mesh.devices.shape
    grouped = jax.sharding.Mesh(
        mesh.devices.reshape(EXPERTS, seq_size // EXPERTS, halves), ALL_AXES
    )
    return jax.shard_map(
        shards,
        mesh=grouped,
        in_specs=(
            P(SEQ_AXES, None),
            P(ALL_AXES),
            P(ALL_AXES, None),
            P(ALL_AXES, None),
            P(None, ALL_AXES),
            P(ALL_AXES, None),
            P(ALL_AXES),
            P(ALL_AXES, None),
            P(None, ALL_AXES),
            P(None, ALL_AXES),
            P(ALL_AXES, None),
            P(SEQ_AXES, None),
            P(SEQ_AXES, None),
            P(SEQ_AXES, None),
            P(SEQ_AXES, None),
        ),
        out_specs=(
            P(SEQ_AXES, None),
            P(SEQ_AXES, None),
            P(ALL_AXES),
            P(ALL_AXES, None),
            P(ALL_AXES, None),
            P(None, ALL_AXES),
            P(ALL_AXES, None),
            P(ALL_AXES),
            P(ALL_AXES, None),
            P(None, ALL_AXES),
            P(None, ALL_AXES),
            P(ALL_AXES, None),
        ),
        check_vma=False,
    )
```

```python
import functools
import math

import jax
import jax.numpy as jnp
from jax import lax
from jax.experimental import pallas as pl
from jax.sharding import PartitionSpec as P

ALL_AXES = ("grp", "sub", "expert")
SEQ_AXES = ("grp", "sub")
GROUP_AXES = ("sub", "expert")
KV_HEADS = 16
HEAD = 128
EXPERTS = 8
TOPK = 2
PIECES = 8
BLOCK = 256


epsilon = 1e-06
masked_score = -1e30


def _scores(q, k, qb, scale):
    s = lax.dot_general(q, k, (((1,), (1,)), ((), ())), preferred_element_type=jnp.float32) * scale
    kblock = lax.broadcasted_iota(jnp.int32, s.shape, 1) // BLOCK
    return jnp.where(kblock <= qb, s, masked_score)

def _fwd_kernel(scale, q_ref, k_ref, v_ref, qb_ref, o_ref, lse_ref):
    s = _scores(q_ref[...], k_ref[...], qb_ref[...], scale)
    largest = jnp.max(s, axis=-1, keepdims=True)
    weights = jnp.exp(s - largest)
    totals = jnp.sum(weights, axis=-1, keepdims=True)
    probs = weights / totals
    o_ref[...] = jnp.dot(probs.astype(jnp.bfloat16), v_ref[...],
                         preferred_element_type=jnp.float32).astype(o_ref.dtype)
    lse_ref[...] = largest + jnp.log(totals)

def _bwd_kernel(scale, q_ref, k_ref, v_ref, qb_ref, lse_ref, do_ref, dq_ref, dk_ref, dv_ref):
    q = q_ref[...]; k = k_ref[...]; v = v_ref[...]; do = do_ref[...]
    probs = jnp.exp(_scores(q, k, qb_ref[...], scale) - lse_ref[...])
    dp = lax.dot_general(do, v, (((1,), (1,)), ((), ())), preferred_element_type=jnp.float32)
    inner = jnp.sum(probs * dp, axis=-1, keepdims=True)
    ds = (probs * (dp - inner)).astype(jnp.bfloat16)
    dv_ref[...] = lax.dot_general(probs.astype(jnp.bfloat16), do, (((0,), (0,)), ((), ())),
                                  preferred_element_type=jnp.float32)
    dk_ref[...] = lax.dot_general(ds, q, (((0,), (0,)), ((), ())),
                                  preferred_element_type=jnp.float32) * scale
    dq_ref[...] = jnp.dot(ds, k, preferred_element_type=jnp.float32) * scale

def attn_fwd(q, k, v, qb):
    n, rows, d = q.shape; keys = k.shape[1]
    scale = 1.0 / math.sqrt(d)
    rspec = pl.BlockSpec((None, rows, d), lambda i: (i, 0, 0))
    kspec = pl.BlockSpec((None, keys, d), lambda i: (i, 0, 0))
    cspec = pl.BlockSpec((None, rows, 1), lambda i: (i, 0, 0))
    return pl.pallas_call(
        functools.partial(_fwd_kernel, scale),
        grid=(n,),
        in_specs=[rspec, kspec, kspec, cspec],
        out_specs=[rspec, cspec],
        out_shape=[jax.ShapeDtypeStruct((n, rows, d), jnp.bfloat16),
                   jax.ShapeDtypeStruct((n, rows, 1), jnp.float32)],
        cost_estimate=pl.CostEstimate(flops=4 * n * rows * keys * d,
                                      transcendentals=n * rows * keys,
                                      bytes_accessed=2 * n * (2 * rows * d + 2 * keys * d)),
    )(q, k, v, qb)

def attn_bwd(q, k, v, qb, lse, do):
    n, rows, d = q.shape; keys = k.shape[1]
    scale = 1.0 / math.sqrt(d)
    rspec = pl.BlockSpec((None, rows, d), lambda i: (i, 0, 0))
    kspec = pl.BlockSpec((None, keys, d), lambda i: (i, 0, 0))
    cspec = pl.BlockSpec((None, rows, 1), lambda i: (i, 0, 0))
    return pl.pallas_call(
        functools.partial(_bwd_kernel, scale),
        grid=(n,),
        in_specs=[rspec, kspec, kspec, cspec, cspec, rspec],
        out_specs=[rspec, kspec, kspec],
        out_shape=[jax.ShapeDtypeStruct((n, rows, d), jnp.float32),
                   jax.ShapeDtypeStruct((n, keys, d), jnp.float32),
                   jax.ShapeDtypeStruct((n, keys, d), jnp.float32)],
        cost_estimate=pl.CostEstimate(flops=10 * n * rows * keys * d,
                                      transcendentals=n * rows * keys,
                                      bytes_accessed=2 * n * (3 * rows * d + 2 * keys * d) + 8 * n * (rows * d + 2 * keys * d)),
    )(q, k, v, qb, lse, do)


def rope_tables(positions, head_size):
    half_size = head_size // 2
    frequency = jnp.exp(
        jnp.arange(half_size, dtype=jnp.float32) * (-2.0 * math.log(10000.0) / head_size)
    )
    angles = positions.astype(jnp.float32)[:, None] * frequency[None, :]
    return (jnp.cos(angles)[:, None, :], jnp.sin(angles)[:, None, :])


def rotate(values, cosines, sines):
    half_size = values.shape[-1] // 2
    first = values[..., :half_size]
    second = values[..., half_size:]
    return jnp.concatenate(
        [first * cosines - second * sines, second * cosines + first * sines], axis=-1
    )


def rotate_back(grads, cosines, sines):
    half_size = grads.shape[-1] // 2
    first = grads[..., :half_size]
    second = grads[..., half_size:]
    return jnp.concatenate(
        [first * cosines + second * sines, second * cosines - first * sines], axis=-1
    )


def slot_table(expert_ids, ranks, slot_cap):
    block_rows = expert_ids.shape[0]
    expert_range = jnp.arange(EXPERTS, dtype=jnp.int32)
    member = jnp.sum(
        (expert_ids[:, :, None] == expert_range[None, None, :]).astype(jnp.int32), axis=1
    )
    earlier = (ranks[:, None] < ranks[None, :]).astype(jnp.int32)
    places = jnp.sum(earlier[:, :, None] * member[:, None, :], axis=0)
    kept = member * (places < slot_cap).astype(jnp.int32)
    slot_range = jnp.arange(slot_cap, dtype=jnp.int32)
    landing = kept[:, :, None] * (places[:, :, None] == slot_range[None, None, :]).astype(jnp.int32)
    row_range = jnp.arange(block_rows, dtype=jnp.int32)
    slot_token = jnp.sum(landing * row_range[:, None, None], axis=0)
    slot_valid = jnp.sum(landing, axis=0)
    return (places, kept, slot_token, slot_valid)


def pair_index(expert_ids, places, kept, slot_cap):
    chosen_place = jnp.take_along_axis(places, expert_ids, axis=1)
    chosen_kept = jnp.take_along_axis(kept, expert_ids, axis=1)
    return (
        expert_ids * slot_cap + jnp.minimum(chosen_place, slot_cap - 1),
        chosen_kept.astype(jnp.float32),
    )


def pair_gates(logits, expert_ids):
    return jax.nn.softmax(jnp.take_along_axis(logits, expert_ids, axis=1), axis=-1)


def expert_onehot(expert_ids):
    expert_range = jnp.arange(EXPERTS, dtype=jnp.int32)
    return (expert_ids[:, :, None] == expert_range[None, None, :]).astype(jnp.float32)


def gates_back(gates, gate_grads, expert_ids):
    inner = jnp.sum(gates * gate_grads, axis=1, keepdims=True)
    chosen_grads = gates * (gate_grads - inner)
    return jnp.sum(chosen_grads[:, :, None] * expert_onehot(expert_ids), axis=1)


def slot_gates(gates, pair_kept, expert_ids, slot_token, slot_valid):
    per_expert = jnp.sum((gates * pair_kept)[:, :, None] * expert_onehot(expert_ids), axis=1)
    return jnp.take_along_axis(per_expert.T, slot_token, axis=1) * slot_valid.astype(jnp.float32)


def pick_slots(values, slot_token, slot_valid):
    return jnp.where(slot_valid[:, :, None] > 0, values[slot_token], jnp.zeros((), values.dtype))


def fan_out(slot_values, group_size):
    experts_here, slot_cap, width = slot_values.shape
    spread_out = jnp.broadcast_to(slot_values[:, None], (experts_here, group_size, slot_cap, width))
    return spread_out.reshape(experts_here * group_size, slot_cap, width)


def fold_group(received, group_size):
    count, slot_cap, width = received.shape
    return jnp.sum(received.reshape(count // group_size, group_size, slot_cap, width), axis=1)


def norm_back(normed_grad, gain, normed, inverse):
    scaled = normed_grad * gain
    gain_grad = jnp.sum(normed_grad * normed, axis=0)
    input_grad = inverse * (scaled - normed * jnp.mean(scaled * normed, axis=-1, keepdims=True))
    return (input_grad, gain_grad)


def shards(
    tokens,
    attn_gain,
    kv_weight,
    attn_router,
    query_weight,
    output_weight,
    mlp_gain,
    mlp_router,
    gate_weight,
    up_weight,
    down_weight,
    attn_experts,
    mlp_experts,
    priority,
    cotangent,
):
    devices = lax.axis_size(ALL_AXES)
    halves = lax.axis_size("expert")
    device_index = lax.axis_index(ALL_AXES)
    half_index = lax.axis_index("expert")
    seq_tokens, width = tokens.shape
    own_rows = seq_tokens // halves
    group_size = devices // EXPERTS
    head_cols = query_weight.shape[1]
    local_heads = head_cols // HEAD
    key_cols = KV_HEADS * HEAD
    all_tokens = own_rows * devices
    seq_length = seq_tokens * PIECES
    sequences = all_tokens // seq_length
    slot_cap = (9 * TOPK * own_rows + 8 * EXPERTS - 1) // (8 * EXPERTS)
    slot_rows = devices * slot_cap
    seq_rows = slot_rows // sequences
    my_expert = device_index // group_size
    groups = lax.axis_size("grp")

    def dispatch(slot_values):
        by_group = lax.all_to_all(slot_values, "grp", split_axis=0, concat_axis=0, tiled=True)
        return lax.all_gather(
            by_group.reshape(groups * slot_cap, width), GROUP_AXES, axis=0, tiled=True
        )

    def combine(partial_value):
        parts = lax.all_to_all(
            partial_value.astype(jnp.bfloat16).reshape(group_size, groups * slot_cap, width),
            GROUP_AXES,
            split_axis=0,
            concat_axis=0,
            tiled=True,
        )
        summed = jnp.sum(parts.astype(jnp.float32), axis=0).reshape(groups, slot_cap, width)
        return lax.all_to_all(summed, "grp", split_axis=0, concat_axis=0, tiled=True)

    def combine_scattered(partial_value):
        summed = lax.psum_scatter(
            partial_value.astype(jnp.bfloat16), GROUP_AXES, scatter_dimension=0, tiled=True
        )
        return lax.all_to_all(
            summed.astype(jnp.float32).reshape(groups, slot_cap, width),
            "grp",
            split_axis=0,
            concat_axis=0,
            tiled=True,
        )

    def to_rows(per_head):
        parts = lax.all_to_all(
            per_head.reshape(group_size, groups * slot_cap, head_cols),
            GROUP_AXES,
            split_axis=0,
            concat_axis=0,
            tiled=True,
        )
        return jnp.swapaxes(parts, 0, 1).reshape(groups * slot_cap, group_size * head_cols)

    def to_owners(row_values):
        return lax.all_to_all(
            row_values.reshape(groups, slot_cap, width), "grp", split_axis=0, concat_axis=0, tiled=True
        )

    def to_gj(rows):
        shaped = rows.reshape((group_size, groups, slot_cap) + rows.shape[1:])
        return jnp.swapaxes(shaped, 0, 1).reshape(rows.shape)

    def to_jg(rows):
        shaped = rows.reshape((groups, group_size, slot_cap) + rows.shape[1:])
        return jnp.swapaxes(shaped, 0, 1).reshape(rows.shape)
    scale = 1.0 / math.sqrt(HEAD)

    start_row = half_index * own_rows
    own_input = lax.dynamic_slice_in_dim(tokens, start_row, own_rows, 0).astype(jnp.float32)
    own_cotangent = lax.dynamic_slice_in_dim(cotangent, start_row, own_rows, 0).astype(jnp.float32)
    own_attn = lax.dynamic_slice_in_dim(attn_experts, start_row, own_rows, 0)
    own_mlp = lax.dynamic_slice_in_dim(mlp_experts, start_row, own_rows, 0)
    own_rank = lax.dynamic_slice_in_dim(priority[0], start_row, own_rows, 0)
    token_order = jnp.arange(own_rows, dtype=jnp.int32)

    kv_rows, kv_width = kv_weight.shape
    id_cols = own_rows * TOPK // kv_rows
    extras = jnp.concatenate(
        [
            attn_gain[:, None],
            mlp_gain[:, None],
            attn_router,
            mlp_router,
            own_attn.reshape(kv_rows, id_cols).astype(jnp.bfloat16),
        ],
        axis=1,
    )
    extra_cols = extras.shape[1]
    extra_pad = -(-extra_cols // 128) * 128
    pair_cols = 2 * head_cols
    head_blocks = jnp.transpose(
        kv_weight.reshape(kv_rows, 2, group_size, head_cols), (2, 0, 1, 3)
    ).reshape(group_size, kv_rows, pair_cols)
    padded_extras = jnp.pad(extras, ((0, 0), (0, extra_pad - extra_cols)))
    dealt_rows = lax.all_to_all(
        jnp.concatenate(
            [
                head_blocks,
                jnp.broadcast_to(padded_extras[None], (group_size, kv_rows, extra_pad)),
            ],
            axis=2,
        ),
        GROUP_AXES,
        split_axis=0,
        concat_axis=0,
        tiled=True,
    )
    gathered = lax.all_to_all(
        jnp.broadcast_to(
            dealt_rows.reshape(1, group_size * kv_rows, pair_cols + extra_pad),
            (groups, group_size * kv_rows, pair_cols + extra_pad),
        ),
        "grp",
        split_axis=0,
        concat_axis=0,
        tiled=True,
    ).reshape(devices * kv_rows, pair_cols + extra_pad)
    head_kv = gathered[:, :pair_cols]
    gain_one = gathered[:, pair_cols]
    gain_two = gathered[:, pair_cols + 1]
    router_one = gathered[:, pair_cols + 2 : pair_cols + 2 + EXPERTS]
    router_two = gathered[:, pair_cols + 2 + EXPERTS : pair_cols + 2 + 2 * EXPERTS]
    routes_all = gathered[:, pair_cols + 2 + 2 * EXPERTS : pair_cols + extra_cols].astype(jnp.int32)
    inverse_one = lax.rsqrt(jnp.mean(own_input * own_input, axis=-1, keepdims=True) + epsilon)
    normed_one = own_input * inverse_one
    attn_input = (normed_one * gain_one.astype(jnp.float32)).astype(jnp.bfloat16)
    attn_logits = jnp.dot(attn_input, router_one, preferred_element_type=jnp.float32)
    seq_input = lax.all_gather(attn_input, GROUP_AXES, axis=0, tiled=True)
    seq_kv = jnp.dot(seq_input, head_kv, preferred_element_type=jnp.float32)
    seq_cos, seq_sin = rope_tables(jnp.arange(seq_length, dtype=jnp.int32), HEAD)
    seq_pair = jnp.concatenate(
        [
            rotate(seq_kv[:, :head_cols].reshape(seq_length, local_heads, HEAD), seq_cos, seq_sin)
            .reshape(seq_length, head_cols)
            .astype(jnp.bfloat16),
            seq_kv[:, head_cols:].astype(jnp.bfloat16),
        ],
        axis=1,
    )
    all_pairs = lax.all_to_all(
        jnp.broadcast_to(seq_pair[None], (groups,) + seq_pair.shape),
        "grp",
        split_axis=0,
        concat_axis=0,
        tiled=True,
    ).reshape(groups * seq_length, 2 * head_cols)
    seq_keys = all_pairs[:, :head_cols].reshape(sequences, seq_length, local_heads, HEAD)
    seq_values = all_pairs[:, head_cols:].reshape(sequences, seq_length, local_heads, HEAD)
    attn_places, attn_kept, attn_token, attn_valid = slot_table(own_attn, token_order, slot_cap)
    mlp_places, mlp_kept, mlp_token, mlp_valid = slot_table(own_mlp, own_rank, slot_cap)
    block_routes = routes_all.reshape(devices, own_rows, TOPK)
    dest_tables = jax.vmap(lambda block_ids: slot_table(block_ids, token_order, slot_cap)[2])(
        block_routes
    )
    dest_token = jnp.take(dest_tables, my_expert, axis=1)
    attn_rows = dispatch(pick_slots(attn_input, attn_token, attn_valid))
    queries = to_gj(jnp.dot(attn_rows, query_weight, preferred_element_type=jnp.float32))
    slot_positions = (
        (jnp.arange(devices, dtype=jnp.int32)[:, None] * own_rows + dest_token) % seq_length
    ).reshape(slot_rows)
    slot_cos, slot_sin = rope_tables(slot_positions, HEAD)
    rotated = rotate(queries.reshape(slot_rows, local_heads, HEAD), slot_cos, slot_sin).astype(
        jnp.bfloat16
    )
    seq_queries = rotated.reshape(sequences, seq_rows, local_heads, HEAD)
    query_blocks = (slot_positions // BLOCK).reshape(sequences, seq_rows)
    key_blocks = jnp.arange(seq_length, dtype=jnp.int32) // BLOCK

    attn_mixed, log_totals = attn_fwd(
        seq_queries.reshape(sequences, seq_rows, HEAD),
        seq_keys.reshape(sequences, seq_length, HEAD),
        seq_values.reshape(sequences, seq_length, HEAD),
        query_blocks[:, :, None],
    )
    mixed_rows = to_jg(attn_mixed.reshape(slot_rows, head_cols))
    output_stack = lax.all_gather(output_weight, GROUP_AXES, axis=0, tiled=True)
    attn_slots = to_owners(
        jnp.dot(to_rows(mixed_rows), output_stack, preferred_element_type=jnp.float32)
    )
    attn_gates = pair_gates(attn_logits, own_attn)
    attn_index, attn_pair_kept = pair_index(own_attn, attn_places, attn_kept, slot_cap)
    attn_picked = attn_slots.reshape(EXPERTS * slot_cap, width)[attn_index]
    hidden_state = own_input + jnp.sum(
        attn_picked * (attn_gates * attn_pair_kept)[:, :, None], axis=1
    )
    inverse_two = lax.rsqrt(jnp.mean(hidden_state * hidden_state, axis=-1, keepdims=True) + epsilon)
    normed_two = hidden_state * inverse_two
    mlp_input = (normed_two * gain_two.astype(jnp.float32)).astype(jnp.bfloat16)
    query_stack = lax.all_gather(query_weight, GROUP_AXES, axis=1, tiled=True)
    mlp_input, query_stack = lax.optimization_barrier((mlp_input, query_stack))
    mlp_logits = jnp.dot(mlp_input, router_two, preferred_element_type=jnp.float32)
    mlp_gates = pair_gates(mlp_logits, own_mlp)
    mlp_index, mlp_pair_kept = pair_index(own_mlp, mlp_places, mlp_kept, slot_cap)
    mlp_slot_grad = (
        own_cotangent[mlp_token]
        * slot_gates(mlp_gates, mlp_pair_kept, own_mlp, mlp_token, mlp_valid)[:, :, None]
    ).astype(jnp.bfloat16)
    mlp_by_group = lax.all_to_all(
        jnp.concatenate([pick_slots(mlp_input, mlp_token, mlp_valid), mlp_slot_grad], axis=1),
        "grp",
        split_axis=0,
        concat_axis=0,
        tiled=True,
    )
    mlp_rows = lax.all_gather(
        mlp_by_group[:, :slot_cap].reshape(groups * slot_cap, width),
        GROUP_AXES,
        axis=0,
        tiled=True,
    )
    down_rows = lax.all_gather(
        mlp_by_group[:, slot_cap:].reshape(groups * slot_cap, width),
        GROUP_AXES,
        axis=0,
        tiled=True,
    )
    gate_pre = jnp.dot(mlp_rows, gate_weight, preferred_element_type=jnp.float32)
    up_pre = jnp.dot(mlp_rows, up_weight, preferred_element_type=jnp.float32)
    activated = jax.nn.silu(gate_pre)
    inner_rows = (activated * up_pre).astype(jnp.bfloat16)
    mlp_partial = jnp.dot(inner_rows, down_weight, preferred_element_type=jnp.float32)
    mlp_slots = combine_scattered(mlp_partial)
    mlp_picked = mlp_slots.reshape(EXPERTS * slot_cap, width)[mlp_index]
    own_output = hidden_state + jnp.sum(
        mlp_picked * (mlp_gates * mlp_pair_kept)[:, :, None], axis=1
    )
    mlp_gate_grad = jnp.sum(mlp_picked * own_cotangent[:, None, :], axis=-1) * mlp_pair_kept
    mlp_logit_grad = gates_back(mlp_gates, mlp_gate_grad, own_mlp)
    inner_grad = jnp.einsum("rd,fd->rf", down_rows, down_weight, preferred_element_type=jnp.float32)
    down_grad = jnp.einsum("rf,rd->fd", inner_rows, down_rows, preferred_element_type=jnp.float32)
    sigmoid_gate = jax.nn.sigmoid(gate_pre)
    gate_pre_grad = (
        inner_grad * up_pre * sigmoid_gate * (1.0 + gate_pre * (1.0 - sigmoid_gate))
    ).astype(jnp.bfloat16)
    up_pre_grad = (inner_grad * activated).astype(jnp.bfloat16)
    gate_grad = jnp.einsum("rd,rf->df", mlp_rows, gate_pre_grad, preferred_element_type=jnp.float32)
    up_grad = jnp.einsum("rd,rf->df", mlp_rows, up_pre_grad, preferred_element_type=jnp.float32)
    row_grad = jnp.einsum(
        "rf,df->rd", gate_pre_grad, gate_weight, preferred_element_type=jnp.float32
    ) + jnp.einsum("rf,df->rd", up_pre_grad, up_weight, preferred_element_type=jnp.float32)
    mlp_row_grad = combine(row_grad)
    mlp_input_grad = jnp.sum(
        mlp_row_grad.reshape(EXPERTS * slot_cap, width)[mlp_index] * mlp_pair_kept[:, :, None],
        axis=1,
    )
    mlp_input_grad = mlp_input_grad + jnp.dot(
        mlp_logit_grad, router_two.astype(jnp.float32).T, precision=lax.Precision.HIGHEST
    )
    mlp_router_own = jnp.dot(
        mlp_input.astype(jnp.float32).T, mlp_logit_grad, precision=lax.Precision.HIGHEST
    )
    hidden_grad, gain_two_own = norm_back(
        mlp_input_grad, gain_two.astype(jnp.float32), normed_two, inverse_two
    )
    hidden_grad = hidden_grad + own_cotangent
    attn_gate_grad = jnp.sum(attn_picked * hidden_grad[:, None, :], axis=-1) * attn_pair_kept
    attn_logit_grad = gates_back(attn_gates, attn_gate_grad, own_attn)
    attn_slot_grad = (
        hidden_grad[attn_token]
        * slot_gates(attn_gates, attn_pair_kept, own_attn, attn_token, attn_valid)[:, :, None]
    ).astype(jnp.bfloat16)
    out_rows = dispatch(attn_slot_grad)
    output_grad = jnp.einsum("rw,rd->wd", mixed_rows, out_rows, preferred_element_type=jnp.float32)
    mixed_grad = jnp.einsum(
        "rd,wd->rw", out_rows, output_weight, preferred_element_type=jnp.float32
    ).astype(jnp.bfloat16)
    seq_mixed_grad = to_gj(mixed_grad).reshape(sequences, seq_rows, local_heads, HEAD)

    seq_query_grad, seq_key_grad, seq_value_grad = attn_bwd(
        seq_queries.reshape(sequences, seq_rows, HEAD),
        seq_keys.reshape(sequences, seq_length, HEAD),
        seq_values.reshape(sequences, seq_length, HEAD),
        query_blocks[:, :, None],
        log_totals,
        seq_mixed_grad.reshape(sequences, seq_rows, HEAD),
    )
    query_rot_grad = to_jg(
        rotate_back(seq_query_grad.reshape(slot_rows, local_heads, HEAD), slot_cos, slot_sin)
        .reshape(slot_rows, head_cols)
        .astype(jnp.bfloat16)
    )
    query_grad = jnp.einsum(
        "rd,rw->dw", attn_rows, query_rot_grad, preferred_element_type=jnp.float32
    )
    attn_row_grad = to_owners(
        jnp.einsum(
            "rw,dw->rd", to_rows(query_rot_grad), query_stack, preferred_element_type=jnp.float32
        )
    )
    pair_back = lax.all_to_all(
        jnp.concatenate([seq_key_grad, seq_value_grad], axis=2).astype(jnp.bfloat16),
        "grp",
        split_axis=0,
        concat_axis=0,
        tiled=True,
    )
    seq_pair_grad = jnp.sum(pair_back.astype(jnp.float32), axis=0)
    kv_col_grad = jnp.concatenate(
        [
            rotate_back(
                seq_pair_grad[:, :head_cols].reshape(seq_length, local_heads, HEAD),
                seq_cos,
                seq_sin,
            ).reshape(seq_length, head_cols),
            seq_pair_grad[:, head_cols:],
        ],
        axis=1,
    ).astype(jnp.bfloat16)
    kv_col_weight = jnp.einsum(
        "rd,rc->dc", seq_input, kv_col_grad, preferred_element_type=jnp.float32
    )
    kv_input_parts = lax.all_to_all(
        jnp.einsum("rc,dc->rd", kv_col_grad, head_kv, preferred_element_type=jnp.float32)
        .astype(jnp.bfloat16)
        .reshape(group_size, own_rows, width),
        GROUP_AXES,
        split_axis=0,
        concat_axis=0,
        tiled=True,
    )
    attn_input_grad = jnp.sum(
        attn_row_grad.reshape(EXPERTS * slot_cap, width)[attn_index] * attn_pair_kept[:, :, None],
        axis=1,
    )
    attn_input_grad = attn_input_grad + jnp.sum(kv_input_parts.astype(jnp.float32), axis=0)
    attn_input_grad = attn_input_grad + jnp.dot(
        attn_logit_grad, router_one.astype(jnp.float32).T, precision=lax.Precision.HIGHEST
    )
    attn_router_own = jnp.dot(
        attn_input.astype(jnp.float32).T, attn_logit_grad, precision=lax.Precision.HIGHEST
    )
    input_grad, gain_one_own = norm_back(
        attn_input_grad, gain_one.astype(jnp.float32), normed_one, inverse_one
    )
    input_grad = input_grad + hidden_grad
    grad_extras = jnp.concatenate(
        [gain_one_own[:, None], gain_two_own[:, None], attn_router_own, mlp_router_own], axis=1
    )
    packed_grad = jnp.concatenate(
        [
            kv_col_weight,
            jnp.pad(grad_extras, ((0, 0), (0, extra_pad - grad_extras.shape[1]))),
        ],
        axis=1,
    )
    group_sum = lax.psum_scatter(packed_grad, "grp", scatter_dimension=0, tiled=True)
    dealt = lax.all_to_all(
        group_sum.reshape(group_size, kv_rows, pair_cols + extra_pad),
        GROUP_AXES,
        split_axis=0,
        concat_axis=0,
        tiled=True,
    )
    kv_grad = jnp.transpose(
        dealt[:, :, :pair_cols].reshape(group_size, kv_rows, 2, head_cols), (1, 2, 0, 3)
    ).reshape(kv_rows, kv_width)
    extra_grad = jnp.sum(dealt[:, :, pair_cols:], axis=0)
    gain_one_grad = extra_grad[:, 0]
    gain_two_grad = extra_grad[:, 1]
    attn_router_grad = extra_grad[:, 2 : 2 + EXPERTS]
    mlp_router_grad = extra_grad[:, 2 + EXPERTS : 2 + 2 * EXPERTS]
    both_full = lax.all_gather(
        jnp.concatenate(
            [own_output.astype(jnp.bfloat16), input_grad.astype(jnp.bfloat16)], axis=1
        ),
        "expert",
        axis=0,
        tiled=True,
    )
    mixed_full, input_full = both_full[:, :width], both_full[:, width:]
    return (
        mixed_full,
        input_full,
        gain_one_grad,
        kv_grad,
        attn_router_grad,
        query_grad,
        output_grad,
        gain_two_grad,
        mlp_router_grad,
        gate_grad,
        up_grad,
        down_grad,
    )


def solution(mesh):
    seq_size, halves = mesh.devices.shape
    grouped = jax.sharding.Mesh(
        mesh.devices.reshape(EXPERTS, seq_size // EXPERTS, halves), ALL_AXES
    )
    return jax.shard_map(
        shards,
        mesh=grouped,
        in_specs=(
            P(SEQ_AXES, None),
            P(ALL_AXES),
            P(ALL_AXES, None),
            P(ALL_AXES, None),
            P(None, ALL_AXES),
            P(ALL_AXES, None),
            P(ALL_AXES),
            P(ALL_AXES, None),
            P(None, ALL_AXES),
            P(None, ALL_AXES),
            P(ALL_AXES, None),
            P(SEQ_AXES, None),
            P(SEQ_AXES, None),
            P(SEQ_AXES, None),
            P(SEQ_AXES, None),
        ),
        out_specs=(
            P(SEQ_AXES, None),
            P(SEQ_AXES, None),
            P(ALL_AXES),
            P(ALL_AXES, None),
            P(ALL_AXES, None),
            P(None, ALL_AXES),
            P(ALL_AXES, None),
            P(ALL_AXES),
            P(ALL_AXES, None),
            P(None, ALL_AXES),
            P(None, ALL_AXES),
            P(ALL_AXES, None),
        ),
        check_vma=False,
    )
```

```python
import functools
import math

import jax
import jax.numpy as jnp
from jax import lax
from jax.experimental import pallas as pl
from jax.sharding import PartitionSpec as P

ALL_AXES = ("grp", "sub", "expert")
SEQ_AXES = ("grp", "sub")
GROUP_AXES = ("sub", "expert")
KV_HEADS = 16
HEAD = 128
EXPERTS = 8
TOPK = 2
PIECES = 8
BLOCK = 256


epsilon = 1e-06
masked_score = -1e30


def _scores(q, k, qb, scale):
    s = lax.dot_general(q, k, (((1,), (1,)), ((), ())), preferred_element_type=jnp.float32) * scale
    kblock = lax.broadcasted_iota(jnp.int32, s.shape, 1) // BLOCK
    return jnp.where(kblock <= qb, s, masked_score)

def _fwd_kernel(scale, q_ref, k_ref, v_ref, qb_ref, o_ref, lse_ref):
    s = _scores(q_ref[...], k_ref[...], qb_ref[...], scale)
    largest = jnp.max(s, axis=-1, keepdims=True)
    weights = jnp.exp(s - largest)
    totals = jnp.sum(weights, axis=-1, keepdims=True)
    probs = weights / totals
    o_ref[...] = jnp.dot(probs.astype(jnp.bfloat16), v_ref[...],
                         preferred_element_type=jnp.float32).astype(o_ref.dtype)
    lse_ref[...] = largest + jnp.log(totals)

def _bwd_kernel(scale, q_ref, k_ref, v_ref, qb_ref, lse_ref, do_ref, dq_ref, dk_ref, dv_ref):
    q = q_ref[...]; k = k_ref[...]; v = v_ref[...]; do = do_ref[...]
    probs = jnp.exp(_scores(q, k, qb_ref[...], scale) - lse_ref[...])
    dp = lax.dot_general(do, v, (((1,), (1,)), ((), ())), preferred_element_type=jnp.float32)
    inner = jnp.sum(probs * dp, axis=-1, keepdims=True)
    ds = (probs * (dp - inner)).astype(jnp.bfloat16)
    dv_ref[...] = lax.dot_general(probs.astype(jnp.bfloat16), do, (((0,), (0,)), ((), ())),
                                  preferred_element_type=jnp.float32)
    dk_ref[...] = lax.dot_general(ds, q, (((0,), (0,)), ((), ())),
                                  preferred_element_type=jnp.float32) * scale
    dq_ref[...] = jnp.dot(ds, k, preferred_element_type=jnp.float32) * scale

def attn_fwd(q, k, v, qb):
    n, rows, d = q.shape; keys = k.shape[1]
    scale = 1.0 / math.sqrt(d)
    rspec = pl.BlockSpec((None, rows, d), lambda i: (i, 0, 0))
    kspec = pl.BlockSpec((None, keys, d), lambda i: (i, 0, 0))
    cspec = pl.BlockSpec((None, rows, 1), lambda i: (i, 0, 0))
    return pl.pallas_call(
        functools.partial(_fwd_kernel, scale),
        grid=(n,),
        in_specs=[rspec, kspec, kspec, cspec],
        out_specs=[rspec, cspec],
        out_shape=[jax.ShapeDtypeStruct((n, rows, d), jnp.bfloat16),
                   jax.ShapeDtypeStruct((n, rows, 1), jnp.float32)],
        cost_estimate=pl.CostEstimate(flops=4 * n * rows * keys * d,
                                      transcendentals=n * rows * keys,
                                      bytes_accessed=2 * n * (2 * rows * d + 2 * keys * d)),
    )(q, k, v, qb)

def attn_bwd(q, k, v, qb, lse, do):
    n, rows, d = q.shape; keys = k.shape[1]
    scale = 1.0 / math.sqrt(d)
    rspec = pl.BlockSpec((None, rows, d), lambda i: (i, 0, 0))
    kspec = pl.BlockSpec((None, keys, d), lambda i: (i, 0, 0))
    cspec = pl.BlockSpec((None, rows, 1), lambda i: (i, 0, 0))
    return pl.pallas_call(
        functools.partial(_bwd_kernel, scale),
        grid=(n,),
        in_specs=[rspec, kspec, kspec, cspec, cspec, rspec],
        out_specs=[rspec, kspec, kspec],
        out_shape=[jax.ShapeDtypeStruct((n, rows, d), jnp.float32),
                   jax.ShapeDtypeStruct((n, keys, d), jnp.float32),
                   jax.ShapeDtypeStruct((n, keys, d), jnp.float32)],
        cost_estimate=pl.CostEstimate(flops=10 * n * rows * keys * d,
                                      transcendentals=n * rows * keys,
                                      bytes_accessed=2 * n * (3 * rows * d + 2 * keys * d) + 8 * n * (rows * d + 2 * keys * d)),
    )(q, k, v, qb, lse, do)


def rope_tables(positions, head_size):
    half_size = head_size // 2
    frequency = jnp.exp(
        jnp.arange(half_size, dtype=jnp.float32) * (-2.0 * math.log(10000.0) / head_size)
    )
    angles = positions.astype(jnp.float32)[:, None] * frequency[None, :]
    return (jnp.cos(angles)[:, None, :], jnp.sin(angles)[:, None, :])


def rotate(values, cosines, sines):
    half_size = values.shape[-1] // 2
    first = values[..., :half_size]
    second = values[..., half_size:]
    return jnp.concatenate(
        [first * cosines - second * sines, second * cosines + first * sines], axis=-1
    )


def rotate_back(grads, cosines, sines):
    half_size = grads.shape[-1] // 2
    first = grads[..., :half_size]
    second = grads[..., half_size:]
    return jnp.concatenate(
        [first * cosines + second * sines, second * cosines - first * sines], axis=-1
    )


def slot_table(expert_ids, ranks, slot_cap):
    block_rows = expert_ids.shape[0]
    expert_range = jnp.arange(EXPERTS, dtype=jnp.int32)
    member = jnp.sum(
        (expert_ids[:, :, None] == expert_range[None, None, :]).astype(jnp.int32), axis=1
    )
    earlier = (ranks[:, None] < ranks[None, :]).astype(jnp.int32)
    places = jnp.sum(earlier[:, :, None] * member[:, None, :], axis=0)
    kept = member * (places < slot_cap).astype(jnp.int32)
    slot_range = jnp.arange(slot_cap, dtype=jnp.int32)
    landing = kept[:, :, None] * (places[:, :, None] == slot_range[None, None, :]).astype(jnp.int32)
    row_range = jnp.arange(block_rows, dtype=jnp.int32)
    slot_token = jnp.sum(landing * row_range[:, None, None], axis=0)
    slot_valid = jnp.sum(landing, axis=0)
    return (places, kept, slot_token, slot_valid)


def pair_index(expert_ids, places, kept, slot_cap):
    chosen_place = jnp.take_along_axis(places, expert_ids, axis=1)
    chosen_kept = jnp.take_along_axis(kept, expert_ids, axis=1)
    return (
        expert_ids * slot_cap + jnp.minimum(chosen_place, slot_cap - 1),
        chosen_kept.astype(jnp.float32),
    )


def pair_gates(logits, expert_ids):
    return jax.nn.softmax(jnp.take_along_axis(logits, expert_ids, axis=1), axis=-1)


def expert_onehot(expert_ids):
    expert_range = jnp.arange(EXPERTS, dtype=jnp.int32)
    return (expert_ids[:, :, None] == expert_range[None, None, :]).astype(jnp.float32)


def gates_back(gates, gate_grads, expert_ids):
    inner = jnp.sum(gates * gate_grads, axis=1, keepdims=True)
    chosen_grads = gates * (gate_grads - inner)
    return jnp.sum(chosen_grads[:, :, None] * expert_onehot(expert_ids), axis=1)


def slot_gates(gates, pair_kept, expert_ids, slot_token, slot_valid):
    per_expert = jnp.sum((gates * pair_kept)[:, :, None] * expert_onehot(expert_ids), axis=1)
    return jnp.take_along_axis(per_expert.T, slot_token, axis=1) * slot_valid.astype(jnp.float32)


def pick_slots(values, slot_token, slot_valid):
    return jnp.where(slot_valid[:, :, None] > 0, values[slot_token], jnp.zeros((), values.dtype))


def fan_out(slot_values, group_size):
    experts_here, slot_cap, width = slot_values.shape
    spread_out = jnp.broadcast_to(slot_values[:, None], (experts_here, group_size, slot_cap, width))
    return spread_out.reshape(experts_here * group_size, slot_cap, width)


def fold_group(received, group_size):
    count, slot_cap, width = received.shape
    return jnp.sum(received.reshape(count // group_size, group_size, slot_cap, width), axis=1)


def norm_back(normed_grad, gain, normed, inverse):
    scaled = normed_grad * gain
    gain_grad = jnp.sum(normed_grad * normed, axis=0)
    input_grad = inverse * (scaled - normed * jnp.mean(scaled * normed, axis=-1, keepdims=True))
    return (input_grad, gain_grad)


def shards(
    tokens,
    attn_gain,
    kv_weight,
    attn_router,
    query_weight,
    output_weight,
    mlp_gain,
    mlp_router,
    gate_weight,
    up_weight,
    down_weight,
    attn_experts,
    mlp_experts,
    priority,
    cotangent,
):
    devices = lax.axis_size(ALL_AXES)
    halves = lax.axis_size("expert")
    device_index = lax.axis_index(ALL_AXES)
    half_index = lax.axis_index("expert")
    seq_tokens, width = tokens.shape
    own_rows = seq_tokens // halves
    group_size = devices // EXPERTS
    head_cols = query_weight.shape[1]
    local_heads = head_cols // HEAD
    key_cols = KV_HEADS * HEAD
    all_tokens = own_rows * devices
    seq_length = seq_tokens * PIECES
    sequences = all_tokens // seq_length
    slot_cap = (9 * TOPK * own_rows + 8 * EXPERTS - 1) // (8 * EXPERTS)
    slot_rows = devices * slot_cap
    seq_rows = slot_rows // sequences
    my_expert = device_index // group_size
    groups = lax.axis_size("grp")

    def dispatch(slot_values):
        by_group = lax.all_to_all(slot_values, "grp", split_axis=0, concat_axis=0, tiled=True)
        return lax.all_gather(
            by_group.reshape(groups * slot_cap, width), GROUP_AXES, axis=0, tiled=True
        )

    def combine(partial_value):
        parts = lax.all_to_all(
            partial_value.astype(jnp.bfloat16).reshape(group_size, groups * slot_cap, width),
            GROUP_AXES,
            split_axis=0,
            concat_axis=0,
            tiled=True,
        )
        summed = jnp.sum(parts.astype(jnp.float32), axis=0).reshape(groups, slot_cap, width)
        return lax.all_to_all(summed, "grp", split_axis=0, concat_axis=0, tiled=True)

    def combine_scattered(partial_value):
        summed = lax.psum_scatter(
            partial_value.astype(jnp.bfloat16), GROUP_AXES, scatter_dimension=0, tiled=True
        )
        return lax.all_to_all(
            summed.astype(jnp.float32).reshape(groups, slot_cap, width),
            "grp",
            split_axis=0,
            concat_axis=0,
            tiled=True,
        )

    def to_rows(per_head):
        parts = lax.all_to_all(
            per_head.reshape(group_size, groups * slot_cap, head_cols),
            GROUP_AXES,
            split_axis=0,
            concat_axis=0,
            tiled=True,
        )
        return jnp.swapaxes(parts, 0, 1).reshape(groups * slot_cap, group_size * head_cols)

    def to_owners(row_values):
        return lax.all_to_all(
            row_values.reshape(groups, slot_cap, width), "grp", split_axis=0, concat_axis=0, tiled=True
        )

    def to_gj(rows):
        shaped = rows.reshape((group_size, groups, slot_cap) + rows.shape[1:])
        return jnp.swapaxes(shaped, 0, 1).reshape(rows.shape)

    def to_jg(rows):
        shaped = rows.reshape((groups, group_size, slot_cap) + rows.shape[1:])
        return jnp.swapaxes(shaped, 0, 1).reshape(rows.shape)
    scale = 1.0 / math.sqrt(HEAD)

    start_row = half_index * own_rows
    own_input = lax.dynamic_slice_in_dim(tokens, start_row, own_rows, 0).astype(jnp.float32)
    own_cotangent = lax.dynamic_slice_in_dim(cotangent, start_row, own_rows, 0).astype(jnp.float32)
    own_attn = lax.dynamic_slice_in_dim(attn_experts, start_row, own_rows, 0)
    own_mlp = lax.dynamic_slice_in_dim(mlp_experts, start_row, own_rows, 0)
    own_rank = lax.dynamic_slice_in_dim(priority[0], start_row, own_rows, 0)
    token_order = jnp.arange(own_rows, dtype=jnp.int32)

    kv_rows, kv_width = kv_weight.shape
    id_cols = own_rows * TOPK // kv_rows
    extras = jnp.concatenate(
        [
            attn_gain[:, None],
            mlp_gain[:, None],
            attn_router,
            mlp_router,
            own_attn.reshape(kv_rows, id_cols).astype(jnp.bfloat16),
        ],
        axis=1,
    )
    extra_cols = extras.shape[1]
    extra_pad = -(-extra_cols // 128) * 128
    pair_cols = 2 * head_cols
    head_blocks = jnp.transpose(
        kv_weight.reshape(kv_rows, 2, group_size, head_cols), (2, 0, 1, 3)
    ).reshape(group_size, kv_rows, pair_cols)
    padded_extras = jnp.pad(extras, ((0, 0), (0, extra_pad - extra_cols)))
    dealt_rows = lax.all_to_all(
        jnp.concatenate(
            [
                head_blocks,
                jnp.broadcast_to(padded_extras[None], (group_size, kv_rows, extra_pad)),
            ],
            axis=2,
        ),
        GROUP_AXES,
        split_axis=0,
        concat_axis=0,
        tiled=True,
    )
    gathered = lax.all_to_all(
        jnp.broadcast_to(
            dealt_rows.reshape(1, group_size * kv_rows, pair_cols + extra_pad),
            (groups, group_size * kv_rows, pair_cols + extra_pad),
        ),
        "grp",
        split_axis=0,
        concat_axis=0,
        tiled=True,
    ).reshape(devices * kv_rows, pair_cols + extra_pad)
    head_kv = gathered[:, :pair_cols]
    gain_one = gathered[:, pair_cols]
    gain_two = gathered[:, pair_cols + 1]
    router_one = gathered[:, pair_cols + 2 : pair_cols + 2 + EXPERTS]
    router_two = gathered[:, pair_cols + 2 + EXPERTS : pair_cols + 2 + 2 * EXPERTS]
    routes_all = gathered[:, pair_cols + 2 + 2 * EXPERTS : pair_cols + extra_cols].astype(jnp.int32)
    inverse_one = lax.rsqrt(jnp.mean(own_input * own_input, axis=-1, keepdims=True) + epsilon)
    normed_one = own_input * inverse_one
    attn_input = (normed_one * gain_one.astype(jnp.float32)).astype(jnp.bfloat16)
    attn_logits = jnp.dot(attn_input, router_one, preferred_element_type=jnp.float32)
    seq_input = lax.all_to_all(
        jnp.broadcast_to(attn_input[None], (group_size,) + attn_input.shape),
        GROUP_AXES,
        split_axis=0,
        concat_axis=0,
        tiled=True,
    ).reshape(group_size * own_rows, width)
    seq_kv = jnp.dot(seq_input, head_kv, preferred_element_type=jnp.float32)
    seq_cos, seq_sin = rope_tables(jnp.arange(seq_length, dtype=jnp.int32), HEAD)
    seq_pair = jnp.concatenate(
        [
            rotate(seq_kv[:, :head_cols].reshape(seq_length, local_heads, HEAD), seq_cos, seq_sin)
            .reshape(seq_length, head_cols)
            .astype(jnp.bfloat16),
            seq_kv[:, head_cols:].astype(jnp.bfloat16),
        ],
        axis=1,
    )
    all_pairs = lax.all_to_all(
        jnp.broadcast_to(seq_pair[None], (groups,) + seq_pair.shape),
        "grp",
        split_axis=0,
        concat_axis=0,
        tiled=True,
    ).reshape(groups * seq_length, 2 * head_cols)
    seq_keys = all_pairs[:, :head_cols].reshape(sequences, seq_length, local_heads, HEAD)
    seq_values = all_pairs[:, head_cols:].reshape(sequences, seq_length, local_heads, HEAD)
    attn_places, attn_kept, attn_token, attn_valid = slot_table(own_attn, token_order, slot_cap)
    mlp_places, mlp_kept, mlp_token, mlp_valid = slot_table(own_mlp, own_rank, slot_cap)
    block_routes = routes_all.reshape(devices, own_rows, TOPK)
    dest_tables = jax.vmap(lambda block_ids: slot_table(block_ids, token_order, slot_cap)[2])(
        block_routes
    )
    dest_token = jnp.take(dest_tables, my_expert, axis=1)
    attn_rows = dispatch(pick_slots(attn_input, attn_token, attn_valid))
    queries = to_gj(jnp.dot(attn_rows, query_weight, preferred_element_type=jnp.float32))
    slot_positions = (
        (jnp.arange(devices, dtype=jnp.int32)[:, None] * own_rows + dest_token) % seq_length
    ).reshape(slot_rows)
    slot_cos, slot_sin = rope_tables(slot_positions, HEAD)
    rotated = rotate(queries.reshape(slot_rows, local_heads, HEAD), slot_cos, slot_sin).astype(
        jnp.bfloat16
    )
    seq_queries = rotated.reshape(sequences, seq_rows, local_heads, HEAD)
    query_blocks = (slot_positions // BLOCK).reshape(sequences, seq_rows)
    key_blocks = jnp.arange(seq_length, dtype=jnp.int32) // BLOCK

    attn_mixed, log_totals = attn_fwd(
        seq_queries.reshape(sequences, seq_rows, HEAD),
        seq_keys.reshape(sequences, seq_length, HEAD),
        seq_values.reshape(sequences, seq_length, HEAD),
        query_blocks[:, :, None],
    )
    mixed_rows = to_jg(attn_mixed.reshape(slot_rows, head_cols))
    output_stack = lax.all_gather(output_weight, GROUP_AXES, axis=0, tiled=True)
    attn_slots = to_owners(
        jnp.dot(to_rows(mixed_rows), output_stack, preferred_element_type=jnp.float32)
    )
    attn_gates = pair_gates(attn_logits, own_attn)
    attn_index, attn_pair_kept = pair_index(own_attn, attn_places, attn_kept, slot_cap)
    attn_picked = attn_slots.reshape(EXPERTS * slot_cap, width)[attn_index]
    hidden_state = own_input + jnp.sum(
        attn_picked * (attn_gates * attn_pair_kept)[:, :, None], axis=1
    )
    inverse_two = lax.rsqrt(jnp.mean(hidden_state * hidden_state, axis=-1, keepdims=True) + epsilon)
    normed_two = hidden_state * inverse_two
    mlp_input = (normed_two * gain_two.astype(jnp.float32)).astype(jnp.bfloat16)
    mlp_logits = jnp.dot(mlp_input, router_two, preferred_element_type=jnp.float32)
    mlp_gates = pair_gates(mlp_logits, own_mlp)
    mlp_index, mlp_pair_kept = pair_index(own_mlp, mlp_places, mlp_kept, slot_cap)
    mlp_slot_grad = (
        own_cotangent[mlp_token]
        * slot_gates(mlp_gates, mlp_pair_kept, own_mlp, mlp_token, mlp_valid)[:, :, None]
    ).astype(jnp.bfloat16)
    mlp_by_group = lax.all_to_all(
        jnp.concatenate([pick_slots(mlp_input, mlp_token, mlp_valid), mlp_slot_grad], axis=1),
        "grp",
        split_axis=0,
        concat_axis=0,
        tiled=True,
    )
    mlp_rows = lax.all_gather(
        mlp_by_group[:, :slot_cap].reshape(groups * slot_cap, width),
        GROUP_AXES,
        axis=0,
        tiled=True,
    )
    down_rows = lax.all_gather(
        mlp_by_group[:, slot_cap:].reshape(groups * slot_cap, width),
        GROUP_AXES,
        axis=0,
        tiled=True,
    )
    gate_pre = jnp.dot(mlp_rows, gate_weight, preferred_element_type=jnp.float32)
    up_pre = jnp.dot(mlp_rows, up_weight, preferred_element_type=jnp.float32)
    activated = jax.nn.silu(gate_pre)
    inner_rows = (activated * up_pre).astype(jnp.bfloat16)
    mlp_partial = jnp.dot(inner_rows, down_weight, preferred_element_type=jnp.float32)
    mlp_slots = combine_scattered(mlp_partial)
    query_stack = lax.all_gather(query_weight, GROUP_AXES, axis=1, tiled=True)
    mlp_slots, query_stack = lax.optimization_barrier((mlp_slots, query_stack))
    mlp_picked = mlp_slots.reshape(EXPERTS * slot_cap, width)[mlp_index]
    own_output = hidden_state + jnp.sum(
        mlp_picked * (mlp_gates * mlp_pair_kept)[:, :, None], axis=1
    )
    mixed_full = lax.all_gather(own_output.astype(jnp.bfloat16), "expert", axis=0, tiled=True)
    mlp_gate_grad = jnp.sum(mlp_picked * own_cotangent[:, None, :], axis=-1) * mlp_pair_kept
    mlp_logit_grad = gates_back(mlp_gates, mlp_gate_grad, own_mlp)
    inner_grad = jnp.einsum("rd,fd->rf", down_rows, down_weight, preferred_element_type=jnp.float32)
    down_grad = jnp.einsum("rf,rd->fd", inner_rows, down_rows, preferred_element_type=jnp.float32)
    sigmoid_gate = jax.nn.sigmoid(gate_pre)
    gate_pre_grad = (
        inner_grad * up_pre * sigmoid_gate * (1.0 + gate_pre * (1.0 - sigmoid_gate))
    ).astype(jnp.bfloat16)
    up_pre_grad = (inner_grad * activated).astype(jnp.bfloat16)
    gate_grad = jnp.einsum("rd,rf->df", mlp_rows, gate_pre_grad, preferred_element_type=jnp.float32)
    up_grad = jnp.einsum("rd,rf->df", mlp_rows, up_pre_grad, preferred_element_type=jnp.float32)
    row_grad = jnp.einsum(
        "rf,df->rd", gate_pre_grad, gate_weight, preferred_element_type=jnp.float32
    ) + jnp.einsum("rf,df->rd", up_pre_grad, up_weight, preferred_element_type=jnp.float32)
    mlp_row_grad = combine(row_grad)
    mlp_input_grad = jnp.sum(
        mlp_row_grad.reshape(EXPERTS * slot_cap, width)[mlp_index] * mlp_pair_kept[:, :, None],
        axis=1,
    )
    mlp_input_grad = mlp_input_grad + jnp.dot(
        mlp_logit_grad, router_two.astype(jnp.float32).T, precision=lax.Precision.HIGHEST
    )
    mlp_router_own = jnp.dot(
        mlp_input.astype(jnp.float32).T, mlp_logit_grad, precision=lax.Precision.HIGHEST
    )
    hidden_grad, gain_two_own = norm_back(
        mlp_input_grad, gain_two.astype(jnp.float32), normed_two, inverse_two
    )
    hidden_grad = hidden_grad + own_cotangent
    attn_gate_grad = jnp.sum(attn_picked * hidden_grad[:, None, :], axis=-1) * attn_pair_kept
    attn_logit_grad = gates_back(attn_gates, attn_gate_grad, own_attn)
    attn_slot_grad = (
        hidden_grad[attn_token]
        * slot_gates(attn_gates, attn_pair_kept, own_attn, attn_token, attn_valid)[:, :, None]
    ).astype(jnp.bfloat16)
    out_rows = dispatch(attn_slot_grad)
    output_grad = jnp.einsum("rw,rd->wd", mixed_rows, out_rows, preferred_element_type=jnp.float32)
    mixed_grad = jnp.einsum(
        "rd,wd->rw", out_rows, output_weight, preferred_element_type=jnp.float32
    ).astype(jnp.bfloat16)
    seq_mixed_grad = to_gj(mixed_grad).reshape(sequences, seq_rows, local_heads, HEAD)

    seq_query_grad, seq_key_grad, seq_value_grad = attn_bwd(
        seq_queries.reshape(sequences, seq_rows, HEAD),
        seq_keys.reshape(sequences, seq_length, HEAD),
        seq_values.reshape(sequences, seq_length, HEAD),
        query_blocks[:, :, None],
        log_totals,
        seq_mixed_grad.reshape(sequences, seq_rows, HEAD),
    )
    query_rot_grad = to_jg(
        rotate_back(seq_query_grad.reshape(slot_rows, local_heads, HEAD), slot_cos, slot_sin)
        .reshape(slot_rows, head_cols)
        .astype(jnp.bfloat16)
    )
    query_grad = jnp.einsum(
        "rd,rw->dw", attn_rows, query_rot_grad, preferred_element_type=jnp.float32
    )
    attn_row_grad = to_owners(
        jnp.einsum(
            "rw,dw->rd", to_rows(query_rot_grad), query_stack, preferred_element_type=jnp.float32
        )
    )
    pair_back = lax.all_to_all(
        jnp.concatenate([seq_key_grad, seq_value_grad], axis=2).astype(jnp.bfloat16),
        "grp",
        split_axis=0,
        concat_axis=0,
        tiled=True,
    )
    seq_pair_grad = jnp.sum(pair_back.astype(jnp.float32), axis=0)
    kv_col_grad = jnp.concatenate(
        [
            rotate_back(
                seq_pair_grad[:, :head_cols].reshape(seq_length, local_heads, HEAD),
                seq_cos,
                seq_sin,
            ).reshape(seq_length, head_cols),
            seq_pair_grad[:, head_cols:],
        ],
        axis=1,
    ).astype(jnp.bfloat16)
    kv_col_weight = jnp.einsum(
        "rd,rc->dc", seq_input, kv_col_grad, preferred_element_type=jnp.float32
    )
    kv_input_parts = lax.all_to_all(
        jnp.einsum("rc,dc->rd", kv_col_grad, head_kv, preferred_element_type=jnp.float32)
        .astype(jnp.bfloat16)
        .reshape(group_size, own_rows, width),
        GROUP_AXES,
        split_axis=0,
        concat_axis=0,
        tiled=True,
    )
    attn_input_grad = jnp.sum(
        attn_row_grad.reshape(EXPERTS * slot_cap, width)[attn_index] * attn_pair_kept[:, :, None],
        axis=1,
    )
    attn_input_grad = attn_input_grad + jnp.sum(kv_input_parts.astype(jnp.float32), axis=0)
    attn_input_grad = attn_input_grad + jnp.dot(
        attn_logit_grad, router_one.astype(jnp.float32).T, precision=lax.Precision.HIGHEST
    )
    attn_router_own = jnp.dot(
        attn_input.astype(jnp.float32).T, attn_logit_grad, precision=lax.Precision.HIGHEST
    )
    input_grad, gain_one_own = norm_back(
        attn_input_grad, gain_one.astype(jnp.float32), normed_one, inverse_one
    )
    input_grad = input_grad + hidden_grad
    grad_extras = jnp.concatenate(
        [gain_one_own[:, None], gain_two_own[:, None], attn_router_own, mlp_router_own], axis=1
    )
    packed_grad = jnp.concatenate(
        [
            kv_col_weight,
            jnp.pad(grad_extras, ((0, 0), (0, extra_pad - grad_extras.shape[1]))),
        ],
        axis=1,
    )
    group_sum = lax.psum_scatter(packed_grad, "grp", scatter_dimension=0, tiled=True)
    dealt = lax.all_to_all(
        group_sum.reshape(group_size, kv_rows, pair_cols + extra_pad),
        GROUP_AXES,
        split_axis=0,
        concat_axis=0,
        tiled=True,
    )
    kv_grad = jnp.transpose(
        dealt[:, :, :pair_cols].reshape(group_size, kv_rows, 2, head_cols), (1, 2, 0, 3)
    ).reshape(kv_rows, kv_width)
    extra_grad = jnp.sum(dealt[:, :, pair_cols:], axis=0)
    gain_one_grad = extra_grad[:, 0]
    gain_two_grad = extra_grad[:, 1]
    attn_router_grad = extra_grad[:, 2 : 2 + EXPERTS]
    mlp_router_grad = extra_grad[:, 2 + EXPERTS : 2 + 2 * EXPERTS]
    input_full = lax.all_gather(input_grad.astype(jnp.bfloat16), "expert", axis=0, tiled=True)
    return (
        mixed_full,
        input_full,
        gain_one_grad,
        kv_grad,
        attn_router_grad,
        query_grad,
        output_grad,
        gain_two_grad,
        mlp_router_grad,
        gate_grad,
        up_grad,
        down_grad,
    )


def solution(mesh):
    seq_size, halves = mesh.devices.shape
    grouped = jax.sharding.Mesh(
        mesh.devices.reshape(EXPERTS, seq_size // EXPERTS, halves), ALL_AXES
    )
    return jax.shard_map(
        shards,
        mesh=grouped,
        in_specs=(
            P(SEQ_AXES, None),
            P(ALL_AXES),
            P(ALL_AXES, None),
            P(ALL_AXES, None),
            P(None, ALL_AXES),
            P(ALL_AXES, None),
            P(ALL_AXES),
            P(ALL_AXES, None),
            P(None, ALL_AXES),
            P(None, ALL_AXES),
            P(ALL_AXES, None),
            P(SEQ_AXES, None),
            P(SEQ_AXES, None),
            P(SEQ_AXES, None),
            P(SEQ_AXES, None),
        ),
        out_specs=(
            P(SEQ_AXES, None),
            P(SEQ_AXES, None),
            P(ALL_AXES),
            P(ALL_AXES, None),
            P(ALL_AXES, None),
            P(None, ALL_AXES),
            P(ALL_AXES, None),
            P(ALL_AXES),
            P(ALL_AXES, None),
            P(None, ALL_AXES),
            P(None, ALL_AXES),
            P(ALL_AXES, None),
        ),
        check_vma=False,
    )
```

```python
import functools
import math

import jax
import jax.numpy as jnp
from jax import lax
from jax.experimental import pallas as pl
from jax.sharding import PartitionSpec as P

ALL_AXES = ("grp", "sub", "expert")
SEQ_AXES = ("grp", "sub")
GROUP_AXES = ("sub", "expert")
KV_HEADS = 16
HEAD = 128
EXPERTS = 8
TOPK = 2
PIECES = 8
BLOCK = 256


epsilon = 1e-06
masked_score = -1e30


def _scores(q, k, qb, scale):
    s = lax.dot_general(q, k, (((1,), (1,)), ((), ())), preferred_element_type=jnp.float32) * scale
    kblock = lax.broadcasted_iota(jnp.int32, s.shape, 1) // BLOCK
    return jnp.where(kblock <= qb, s, masked_score)

def _fwd_kernel(scale, q_ref, k_ref, v_ref, qb_ref, o_ref, lse_ref):
    s = _scores(q_ref[...], k_ref[...], qb_ref[...], scale)
    largest = jnp.max(s, axis=-1, keepdims=True)
    weights = jnp.exp(s - largest)
    totals = jnp.sum(weights, axis=-1, keepdims=True)
    probs = weights / totals
    o_ref[...] = jnp.dot(probs.astype(jnp.bfloat16), v_ref[...],
                         preferred_element_type=jnp.float32).astype(o_ref.dtype)
    lse_ref[...] = largest + jnp.log(totals)

def _bwd_kernel(scale, q_ref, k_ref, v_ref, qb_ref, lse_ref, do_ref, dq_ref, dk_ref, dv_ref):
    q = q_ref[...]; k = k_ref[...]; v = v_ref[...]; do = do_ref[...]
    probs = jnp.exp(_scores(q, k, qb_ref[...], scale) - lse_ref[...])
    dp = lax.dot_general(do, v, (((1,), (1,)), ((), ())), preferred_element_type=jnp.float32)
    inner = jnp.sum(probs * dp, axis=-1, keepdims=True)
    ds = (probs * (dp - inner)).astype(jnp.bfloat16)
    dv_ref[...] = lax.dot_general(probs.astype(jnp.bfloat16), do, (((0,), (0,)), ((), ())),
                                  preferred_element_type=jnp.float32)
    dk_ref[...] = lax.dot_general(ds, q, (((0,), (0,)), ((), ())),
                                  preferred_element_type=jnp.float32) * scale
    dq_ref[...] = jnp.dot(ds, k, preferred_element_type=jnp.float32) * scale

def attn_fwd(q, k, v, qb):
    n, rows, d = q.shape; keys = k.shape[1]
    scale = 1.0 / math.sqrt(d)
    rspec = pl.BlockSpec((None, rows, d), lambda i: (i, 0, 0))
    kspec = pl.BlockSpec((None, keys, d), lambda i: (i, 0, 0))
    cspec = pl.BlockSpec((None, rows, 1), lambda i: (i, 0, 0))
    return pl.pallas_call(
        functools.partial(_fwd_kernel, scale),
        grid=(n,),
        in_specs=[rspec, kspec, kspec, cspec],
        out_specs=[rspec, cspec],
        out_shape=[jax.ShapeDtypeStruct((n, rows, d), jnp.bfloat16),
                   jax.ShapeDtypeStruct((n, rows, 1), jnp.float32)],
        cost_estimate=pl.CostEstimate(flops=4 * n * rows * keys * d,
                                      transcendentals=n * rows * keys,
                                      bytes_accessed=2 * n * (2 * rows * d + 2 * keys * d)),
    )(q, k, v, qb)

def attn_bwd(q, k, v, qb, lse, do):
    n, rows, d = q.shape; keys = k.shape[1]
    scale = 1.0 / math.sqrt(d)
    rspec = pl.BlockSpec((None, rows, d), lambda i: (i, 0, 0))
    kspec = pl.BlockSpec((None, keys, d), lambda i: (i, 0, 0))
    cspec = pl.BlockSpec((None, rows, 1), lambda i: (i, 0, 0))
    return pl.pallas_call(
        functools.partial(_bwd_kernel, scale),
        grid=(n,),
        in_specs=[rspec, kspec, kspec, cspec, cspec, rspec],
        out_specs=[rspec, kspec, kspec],
        out_shape=[jax.ShapeDtypeStruct((n, rows, d), jnp.float32),
                   jax.ShapeDtypeStruct((n, keys, d), jnp.float32),
                   jax.ShapeDtypeStruct((n, keys, d), jnp.float32)],
        cost_estimate=pl.CostEstimate(flops=10 * n * rows * keys * d,
                                      transcendentals=n * rows * keys,
                                      bytes_accessed=2 * n * (3 * rows * d + 2 * keys * d) + 8 * n * (rows * d + 2 * keys * d)),
    )(q, k, v, qb, lse, do)


def rope_tables(positions, head_size):
    half_size = head_size // 2
    frequency = jnp.exp(
        jnp.arange(half_size, dtype=jnp.float32) * (-2.0 * math.log(10000.0) / head_size)
    )
    angles = positions.astype(jnp.float32)[:, None] * frequency[None, :]
    return (jnp.cos(angles)[:, None, :], jnp.sin(angles)[:, None, :])


def rotate(values, cosines, sines):
    half_size = values.shape[-1] // 2
    first = values[..., :half_size]
    second = values[..., half_size:]
    return jnp.concatenate(
        [first * cosines - second * sines, second * cosines + first * sines], axis=-1
    )


def rotate_back(grads, cosines, sines):
    half_size = grads.shape[-1] // 2
    first = grads[..., :half_size]
    second = grads[..., half_size:]
    return jnp.concatenate(
        [first * cosines + second * sines, second * cosines - first * sines], axis=-1
    )


def slot_table(expert_ids, ranks, slot_cap):
    block_rows = expert_ids.shape[0]
    expert_range = jnp.arange(EXPERTS, dtype=jnp.int32)
    member = jnp.sum(
        (expert_ids[:, :, None] == expert_range[None, None, :]).astype(jnp.int32), axis=1
    )
    earlier = (ranks[:, None] < ranks[None, :]).astype(jnp.int32)
    places = jnp.sum(earlier[:, :, None] * member[:, None, :], axis=0)
    kept = member * (places < slot_cap).astype(jnp.int32)
    slot_range = jnp.arange(slot_cap, dtype=jnp.int32)
    landing = kept[:, :, None] * (places[:, :, None] == slot_range[None, None, :]).astype(jnp.int32)
    row_range = jnp.arange(block_rows, dtype=jnp.int32)
    slot_token = jnp.sum(landing * row_range[:, None, None], axis=0)
    slot_valid = jnp.sum(landing, axis=0)
    return (places, kept, slot_token, slot_valid)


def pair_index(expert_ids, places, kept, slot_cap):
    chosen_place = jnp.take_along_axis(places, expert_ids, axis=1)
    chosen_kept = jnp.take_along_axis(kept, expert_ids, axis=1)
    return (
        expert_ids * slot_cap + jnp.minimum(chosen_place, slot_cap - 1),
        chosen_kept.astype(jnp.float32),
    )


def pair_gates(logits, expert_ids):
    return jax.nn.softmax(jnp.take_along_axis(logits, expert_ids, axis=1), axis=-1)


def expert_onehot(expert_ids):
    expert_range = jnp.arange(EXPERTS, dtype=jnp.int32)
    return (expert_ids[:, :, None] == expert_range[None, None, :]).astype(jnp.float32)


def gates_back(gates, gate_grads, expert_ids):
    inner = jnp.sum(gates * gate_grads, axis=1, keepdims=True)
    chosen_grads = gates * (gate_grads - inner)
    return jnp.sum(chosen_grads[:, :, None] * expert_onehot(expert_ids), axis=1)


def slot_gates(gates, pair_kept, expert_ids, slot_token, slot_valid):
    per_expert = jnp.sum((gates * pair_kept)[:, :, None] * expert_onehot(expert_ids), axis=1)
    return jnp.take_along_axis(per_expert.T, slot_token, axis=1) * slot_valid.astype(jnp.float32)


def pick_slots(values, slot_token, slot_valid):
    return jnp.where(slot_valid[:, :, None] > 0, values[slot_token], jnp.zeros((), values.dtype))


def fan_out(slot_values, group_size):
    experts_here, slot_cap, width = slot_values.shape
    spread_out = jnp.broadcast_to(slot_values[:, None], (experts_here, group_size, slot_cap, width))
    return spread_out.reshape(experts_here * group_size, slot_cap, width)


def fold_group(received, group_size):
    count, slot_cap, width = received.shape
    return jnp.sum(received.reshape(count // group_size, group_size, slot_cap, width), axis=1)


def norm_back(normed_grad, gain, normed, inverse):
    scaled = normed_grad * gain
    gain_grad = jnp.sum(normed_grad * normed, axis=0)
    input_grad = inverse * (scaled - normed * jnp.mean(scaled * normed, axis=-1, keepdims=True))
    return (input_grad, gain_grad)


def shards(
    tokens,
    attn_gain,
    kv_weight,
    attn_router,
    query_weight,
    output_weight,
    mlp_gain,
    mlp_router,
    gate_weight,
    up_weight,
    down_weight,
    attn_experts,
    mlp_experts,
    priority,
    cotangent,
):
    devices = lax.axis_size(ALL_AXES)
    halves = lax.axis_size("expert")
    device_index = lax.axis_index(ALL_AXES)
    half_index = lax.axis_index("expert")
    seq_tokens, width = tokens.shape
    own_rows = seq_tokens // halves
    group_size = devices // EXPERTS
    head_cols = query_weight.shape[1]
    local_heads = head_cols // HEAD
    key_cols = KV_HEADS * HEAD
    all_tokens = own_rows * devices
    seq_length = seq_tokens * PIECES
    sequences = all_tokens // seq_length
    slot_cap = (9 * TOPK * own_rows + 8 * EXPERTS - 1) // (8 * EXPERTS)
    slot_rows = devices * slot_cap
    seq_rows = slot_rows // sequences
    my_expert = device_index // group_size
    groups = lax.axis_size("grp")

    def dispatch(slot_values):
        by_group = lax.all_to_all(slot_values, "grp", split_axis=0, concat_axis=0, tiled=True)
        return lax.all_gather(
            by_group.reshape(groups * slot_cap, width), GROUP_AXES, axis=0, tiled=True
        )

    def combine(partial_value):
        parts = lax.all_to_all(
            partial_value.astype(jnp.bfloat16).reshape(group_size, groups * slot_cap, width),
            GROUP_AXES,
            split_axis=0,
            concat_axis=0,
            tiled=True,
        )
        summed = jnp.sum(parts.astype(jnp.float32), axis=0).reshape(groups, slot_cap, width)
        return lax.all_to_all(summed, "grp", split_axis=0, concat_axis=0, tiled=True)

    def combine_scattered(partial_value):
        summed = lax.psum_scatter(
            partial_value.astype(jnp.bfloat16), GROUP_AXES, scatter_dimension=0, tiled=True
        )
        return lax.all_to_all(
            summed.astype(jnp.float32).reshape(groups, slot_cap, width),
            "grp",
            split_axis=0,
            concat_axis=0,
            tiled=True,
        )

    def to_rows(per_head):
        parts = lax.all_to_all(
            per_head.reshape(group_size, groups * slot_cap, head_cols),
            GROUP_AXES,
            split_axis=0,
            concat_axis=0,
            tiled=True,
        )
        return jnp.swapaxes(parts, 0, 1).reshape(groups * slot_cap, group_size * head_cols)

    def to_owners(row_values):
        return lax.all_to_all(
            row_values.reshape(groups, slot_cap, width), "grp", split_axis=0, concat_axis=0, tiled=True
        )

    def to_gj(rows):
        shaped = rows.reshape((group_size, groups, slot_cap) + rows.shape[1:])
        return jnp.swapaxes(shaped, 0, 1).reshape(rows.shape)

    def to_jg(rows):
        shaped = rows.reshape((groups, group_size, slot_cap) + rows.shape[1:])
        return jnp.swapaxes(shaped, 0, 1).reshape(rows.shape)
    scale = 1.0 / math.sqrt(HEAD)

    start_row = half_index * own_rows
    own_input = lax.dynamic_slice_in_dim(tokens, start_row, own_rows, 0).astype(jnp.float32)
    own_cotangent = lax.dynamic_slice_in_dim(cotangent, start_row, own_rows, 0).astype(jnp.float32)
    own_attn = lax.dynamic_slice_in_dim(attn_experts, start_row, own_rows, 0)
    own_mlp = lax.dynamic_slice_in_dim(mlp_experts, start_row, own_rows, 0)
    own_rank = lax.dynamic_slice_in_dim(priority[0], start_row, own_rows, 0)
    token_order = jnp.arange(own_rows, dtype=jnp.int32)

    kv_rows, kv_width = kv_weight.shape
    id_cols = own_rows * TOPK // kv_rows
    extras = jnp.concatenate(
        [
            attn_gain[:, None],
            mlp_gain[:, None],
            attn_router,
            mlp_router,
            own_attn.reshape(kv_rows, id_cols).astype(jnp.bfloat16),
        ],
        axis=1,
    )
    extra_cols = extras.shape[1]
    extra_pad = -(-extra_cols // 128) * 128
    pair_cols = 2 * head_cols
    head_blocks = jnp.transpose(
        kv_weight.reshape(kv_rows, 2, group_size, head_cols), (2, 0, 1, 3)
    ).reshape(group_size, kv_rows, pair_cols)
    padded_extras = jnp.pad(extras, ((0, 0), (0, extra_pad - extra_cols)))
    dealt_rows = lax.all_to_all(
        jnp.concatenate(
            [
                head_blocks,
                jnp.broadcast_to(padded_extras[None], (group_size, kv_rows, extra_pad)),
            ],
            axis=2,
        ),
        GROUP_AXES,
        split_axis=0,
        concat_axis=0,
        tiled=True,
    )
    gathered = lax.all_to_all(
        jnp.broadcast_to(
            dealt_rows.reshape(1, group_size * kv_rows, pair_cols + extra_pad),
            (groups, group_size * kv_rows, pair_cols + extra_pad),
        ),
        "grp",
        split_axis=0,
        concat_axis=0,
        tiled=True,
    ).reshape(devices * kv_rows, pair_cols + extra_pad)
    head_kv = gathered[:, :pair_cols]
    gain_one = gathered[:, pair_cols]
    gain_two = gathered[:, pair_cols + 1]
    router_one = gathered[:, pair_cols + 2 : pair_cols + 2 + EXPERTS]
    router_two = gathered[:, pair_cols + 2 + EXPERTS : pair_cols + 2 + 2 * EXPERTS]
    routes_all = gathered[:, pair_cols + 2 + 2 * EXPERTS : pair_cols + extra_cols].astype(jnp.int32)
    inverse_one = lax.rsqrt(jnp.mean(own_input * own_input, axis=-1, keepdims=True) + epsilon)
    normed_one = own_input * inverse_one
    attn_input = (normed_one * gain_one.astype(jnp.float32)).astype(jnp.bfloat16)
    attn_logits = jnp.dot(attn_input, router_one, preferred_element_type=jnp.float32)
    seq_input = lax.all_gather(attn_input, GROUP_AXES, axis=0, tiled=True)
    seq_kv = jnp.dot(seq_input, head_kv, preferred_element_type=jnp.float32)
    seq_cos, seq_sin = rope_tables(jnp.arange(seq_length, dtype=jnp.int32), HEAD)
    seq_pair = jnp.concatenate(
        [
            rotate(seq_kv[:, :head_cols].reshape(seq_length, local_heads, HEAD), seq_cos, seq_sin)
            .reshape(seq_length, head_cols)
            .astype(jnp.bfloat16),
            seq_kv[:, head_cols:].astype(jnp.bfloat16),
        ],
        axis=1,
    )
    all_pairs = lax.all_to_all(
        jnp.broadcast_to(seq_pair[None], (groups,) + seq_pair.shape),
        "grp",
        split_axis=0,
        concat_axis=0,
        tiled=True,
    ).reshape(groups * seq_length, 2 * head_cols)
    seq_keys = all_pairs[:, :head_cols].reshape(sequences, seq_length, local_heads, HEAD)
    seq_values = all_pairs[:, head_cols:].reshape(sequences, seq_length, local_heads, HEAD)
    attn_places, attn_kept, attn_token, attn_valid = slot_table(own_attn, token_order, slot_cap)
    mlp_places, mlp_kept, mlp_token, mlp_valid = slot_table(own_mlp, own_rank, slot_cap)
    block_routes = routes_all.reshape(devices, own_rows, TOPK)
    dest_tables = jax.vmap(lambda block_ids: slot_table(block_ids, token_order, slot_cap)[2])(
        block_routes
    )
    dest_token = jnp.take(dest_tables, my_expert, axis=1)
    attn_rows = dispatch(pick_slots(attn_input, attn_token, attn_valid))
    queries = to_gj(jnp.dot(attn_rows, query_weight, preferred_element_type=jnp.float32))
    slot_positions = (
        (jnp.arange(devices, dtype=jnp.int32)[:, None] * own_rows + dest_token) % seq_length
    ).reshape(slot_rows)
    slot_cos, slot_sin = rope_tables(slot_positions, HEAD)
    rotated = rotate(queries.reshape(slot_rows, local_heads, HEAD), slot_cos, slot_sin).astype(
        jnp.bfloat16
    )
    seq_queries = rotated.reshape(sequences, seq_rows, local_heads, HEAD)
    query_blocks = (slot_positions // BLOCK).reshape(sequences, seq_rows)
    key_blocks = jnp.arange(seq_length, dtype=jnp.int32) // BLOCK

    attn_mixed, log_totals = attn_fwd(
        seq_queries.reshape(sequences, seq_rows, HEAD),
        seq_keys.reshape(sequences, seq_length, HEAD),
        seq_values.reshape(sequences, seq_length, HEAD),
        query_blocks[:, :, None],
    )
    mixed_rows = to_jg(attn_mixed.reshape(slot_rows, head_cols))
    output_stack = lax.all_gather(output_weight, GROUP_AXES, axis=0, tiled=True)
    attn_slots = to_owners(
        jnp.dot(to_rows(mixed_rows), output_stack, preferred_element_type=jnp.float32)
    )
    attn_gates = pair_gates(attn_logits, own_attn)
    attn_index, attn_pair_kept = pair_index(own_attn, attn_places, attn_kept, slot_cap)
    attn_picked = attn_slots.reshape(EXPERTS * slot_cap, width)[attn_index]
    hidden_state = own_input + jnp.sum(
        attn_picked * (attn_gates * attn_pair_kept)[:, :, None], axis=1
    )
    inverse_two = lax.rsqrt(jnp.mean(hidden_state * hidden_state, axis=-1, keepdims=True) + epsilon)
    normed_two = hidden_state * inverse_two
    mlp_input = (normed_two * gain_two.astype(jnp.float32)).astype(jnp.bfloat16)
    mlp_logits = jnp.dot(mlp_input, router_two, preferred_element_type=jnp.float32)
    mlp_gates = pair_gates(mlp_logits, own_mlp)
    mlp_index, mlp_pair_kept = pair_index(own_mlp, mlp_places, mlp_kept, slot_cap)
    mlp_slot_grad = (
        own_cotangent[mlp_token]
        * slot_gates(mlp_gates, mlp_pair_kept, own_mlp, mlp_token, mlp_valid)[:, :, None]
    ).astype(jnp.bfloat16)
    mlp_by_group = lax.all_to_all(
        jnp.concatenate([pick_slots(mlp_input, mlp_token, mlp_valid), mlp_slot_grad], axis=1),
        "grp",
        split_axis=0,
        concat_axis=0,
        tiled=True,
    )
    mlp_rows = lax.all_gather(
        mlp_by_group[:, :slot_cap].reshape(groups * slot_cap, width),
        GROUP_AXES,
        axis=0,
        tiled=True,
    )
    down_rows = lax.all_gather(
        mlp_by_group[:, slot_cap:].reshape(groups * slot_cap, width),
        GROUP_AXES,
        axis=0,
        tiled=True,
    )
    gate_pre = jnp.dot(mlp_rows, gate_weight, preferred_element_type=jnp.float32)
    up_pre = jnp.dot(mlp_rows, up_weight, preferred_element_type=jnp.float32)
    activated = jax.nn.silu(gate_pre)
    inner_rows = (activated * up_pre).astype(jnp.bfloat16)
    mlp_partial = jnp.dot(inner_rows, down_weight, preferred_element_type=jnp.float32)
    mlp_slots = combine_scattered(mlp_partial)
    query_stack = lax.all_gather(query_weight, GROUP_AXES, axis=1, tiled=True)
    mlp_slots, query_stack = lax.optimization_barrier((mlp_slots, query_stack))
    mlp_picked = mlp_slots.reshape(EXPERTS * slot_cap, width)[mlp_index]
    own_output = hidden_state + jnp.sum(
        mlp_picked * (mlp_gates * mlp_pair_kept)[:, :, None], axis=1
    )
    mlp_gate_grad = jnp.sum(mlp_picked * own_cotangent[:, None, :], axis=-1) * mlp_pair_kept
    mlp_logit_grad = gates_back(mlp_gates, mlp_gate_grad, own_mlp)
    inner_grad = jnp.einsum("rd,fd->rf", down_rows, down_weight, preferred_element_type=jnp.float32)
    down_grad = jnp.einsum("rf,rd->fd", inner_rows, down_rows, preferred_element_type=jnp.float32)
    sigmoid_gate = jax.nn.sigmoid(gate_pre)
    gate_pre_grad = (
        inner_grad * up_pre * sigmoid_gate * (1.0 + gate_pre * (1.0 - sigmoid_gate))
    ).astype(jnp.bfloat16)
    up_pre_grad = (inner_grad * activated).astype(jnp.bfloat16)
    gate_grad = jnp.einsum("rd,rf->df", mlp_rows, gate_pre_grad, preferred_element_type=jnp.float32)
    up_grad = jnp.einsum("rd,rf->df", mlp_rows, up_pre_grad, preferred_element_type=jnp.float32)
    row_grad = jnp.einsum(
        "rf,df->rd", gate_pre_grad, gate_weight, preferred_element_type=jnp.float32
    ) + jnp.einsum("rf,df->rd", up_pre_grad, up_weight, preferred_element_type=jnp.float32)
    mlp_row_grad = combine(row_grad)
    mlp_input_grad = jnp.sum(
        mlp_row_grad.reshape(EXPERTS * slot_cap, width)[mlp_index] * mlp_pair_kept[:, :, None],
        axis=1,
    )
    mlp_input_grad = mlp_input_grad + jnp.dot(
        mlp_logit_grad, router_two.astype(jnp.float32).T, precision=lax.Precision.HIGHEST
    )
    mlp_router_own = jnp.dot(
        mlp_input.astype(jnp.float32).T, mlp_logit_grad, precision=lax.Precision.HIGHEST
    )
    hidden_grad, gain_two_own = norm_back(
        mlp_input_grad, gain_two.astype(jnp.float32), normed_two, inverse_two
    )
    hidden_grad = hidden_grad + own_cotangent
    attn_gate_grad = jnp.sum(attn_picked * hidden_grad[:, None, :], axis=-1) * attn_pair_kept
    attn_logit_grad = gates_back(attn_gates, attn_gate_grad, own_attn)
    attn_slot_grad = (
        hidden_grad[attn_token]
        * slot_gates(attn_gates, attn_pair_kept, own_attn, attn_token, attn_valid)[:, :, None]
    ).astype(jnp.bfloat16)
    out_rows = dispatch(attn_slot_grad)
    output_grad = jnp.einsum("rw,rd->wd", mixed_rows, out_rows, preferred_element_type=jnp.float32)
    mixed_grad = jnp.einsum(
        "rd,wd->rw", out_rows, output_weight, preferred_element_type=jnp.float32
    ).astype(jnp.bfloat16)
    seq_mixed_grad = to_gj(mixed_grad).reshape(sequences, seq_rows, local_heads, HEAD)

    seq_query_grad, seq_key_grad, seq_value_grad = attn_bwd(
        seq_queries.reshape(sequences, seq_rows, HEAD),
        seq_keys.reshape(sequences, seq_length, HEAD),
        seq_values.reshape(sequences, seq_length, HEAD),
        query_blocks[:, :, None],
        log_totals,
        seq_mixed_grad.reshape(sequences, seq_rows, HEAD),
    )
    query_rot_grad = to_jg(
        rotate_back(seq_query_grad.reshape(slot_rows, local_heads, HEAD), slot_cos, slot_sin)
        .reshape(slot_rows, head_cols)
        .astype(jnp.bfloat16)
    )
    query_grad = jnp.einsum(
        "rd,rw->dw", attn_rows, query_rot_grad, preferred_element_type=jnp.float32
    )
    attn_row_grad = to_owners(
        jnp.einsum(
            "rw,dw->rd", to_rows(query_rot_grad), query_stack, preferred_element_type=jnp.float32
        )
    )
    pair_back = lax.all_to_all(
        jnp.concatenate([seq_key_grad, seq_value_grad], axis=2).astype(jnp.bfloat16),
        "grp",
        split_axis=0,
        concat_axis=0,
        tiled=True,
    )
    seq_pair_grad = jnp.sum(pair_back.astype(jnp.float32), axis=0)
    kv_col_grad = jnp.concatenate(
        [
            rotate_back(
                seq_pair_grad[:, :head_cols].reshape(seq_length, local_heads, HEAD),
                seq_cos,
                seq_sin,
            ).reshape(seq_length, head_cols),
            seq_pair_grad[:, head_cols:],
        ],
        axis=1,
    ).astype(jnp.bfloat16)
    kv_col_weight = jnp.einsum(
        "rd,rc->dc", seq_input, kv_col_grad, preferred_element_type=jnp.float32
    )
    kv_sum = lax.psum_scatter(kv_col_weight, "grp", scatter_dimension=0, tiled=True)
    kv_dealt = lax.all_to_all(
        kv_sum.reshape(group_size, kv_rows, pair_cols),
        GROUP_AXES,
        split_axis=0,
        concat_axis=0,
        tiled=True,
    )
    kv_grad = jnp.transpose(
        kv_dealt.reshape(group_size, kv_rows, 2, head_cols), (1, 2, 0, 3)
    ).reshape(kv_rows, kv_width)
    kv_input_parts = lax.all_to_all(
        jnp.einsum("rc,dc->rd", kv_col_grad, head_kv, preferred_element_type=jnp.float32)
        .astype(jnp.bfloat16)
        .reshape(group_size, own_rows, width),
        GROUP_AXES,
        split_axis=0,
        concat_axis=0,
        tiled=True,
    )
    attn_input_grad = jnp.sum(
        attn_row_grad.reshape(EXPERTS * slot_cap, width)[attn_index] * attn_pair_kept[:, :, None],
        axis=1,
    )
    attn_input_grad = attn_input_grad + jnp.sum(kv_input_parts.astype(jnp.float32), axis=0)
    attn_input_grad = attn_input_grad + jnp.dot(
        attn_logit_grad, router_one.astype(jnp.float32).T, precision=lax.Precision.HIGHEST
    )
    attn_router_own = jnp.dot(
        attn_input.astype(jnp.float32).T, attn_logit_grad, precision=lax.Precision.HIGHEST
    )
    input_grad, gain_one_own = norm_back(
        attn_input_grad, gain_one.astype(jnp.float32), normed_one, inverse_one
    )
    input_grad = input_grad + hidden_grad
    grad_extras = jnp.concatenate(
        [gain_one_own[:, None], gain_two_own[:, None], attn_router_own, mlp_router_own], axis=1
    )
    extra_sum = lax.psum_scatter(
        jnp.pad(grad_extras, ((0, 0), (0, extra_pad - grad_extras.shape[1]))),
        "grp",
        scatter_dimension=0,
        tiled=True,
    )
    extra_grad = jnp.sum(
        lax.all_to_all(
            extra_sum.reshape(group_size, kv_rows, extra_pad),
            GROUP_AXES,
            split_axis=0,
            concat_axis=0,
            tiled=True,
        ),
        axis=0,
    )
    gain_one_grad = extra_grad[:, 0]
    gain_two_grad = extra_grad[:, 1]
    attn_router_grad = extra_grad[:, 2 : 2 + EXPERTS]
    mlp_router_grad = extra_grad[:, 2 + EXPERTS : 2 + 2 * EXPERTS]
    both_full = lax.all_gather(
        jnp.concatenate(
            [own_output.astype(jnp.bfloat16), input_grad.astype(jnp.bfloat16)], axis=1
        ),
        "expert",
        axis=0,
        tiled=True,
    )
    mixed_full, input_full = both_full[:, :width], both_full[:, width:]
    return (
        mixed_full,
        input_full,
        gain_one_grad,
        kv_grad,
        attn_router_grad,
        query_grad,
        output_grad,
        gain_two_grad,
        mlp_router_grad,
        gate_grad,
        up_grad,
        down_grad,
    )


def solution(mesh):
    seq_size, halves = mesh.devices.shape
    grouped = jax.sharding.Mesh(
        mesh.devices.reshape(EXPERTS, seq_size // EXPERTS, halves), ALL_AXES
    )
    return jax.shard_map(
        shards,
        mesh=grouped,
        in_specs=(
            P(SEQ_AXES, None),
            P(ALL_AXES),
            P(ALL_AXES, None),
            P(ALL_AXES, None),
            P(None, ALL_AXES),
            P(ALL_AXES, None),
            P(ALL_AXES),
            P(ALL_AXES, None),
            P(None, ALL_AXES),
            P(None, ALL_AXES),
            P(ALL_AXES, None),
            P(SEQ_AXES, None),
            P(SEQ_AXES, None),
            P(SEQ_AXES, None),
            P(SEQ_AXES, None),
        ),
        out_specs=(
            P(SEQ_AXES, None),
            P(SEQ_AXES, None),
            P(ALL_AXES),
            P(ALL_AXES, None),
            P(ALL_AXES, None),
            P(None, ALL_AXES),
            P(ALL_AXES, None),
            P(ALL_AXES),
            P(ALL_AXES, None),
            P(None, ALL_AXES),
            P(None, ALL_AXES),
            P(ALL_AXES, None),
        ),
        check_vma=False,
    )
```

```python
import functools
import math

import jax
import jax.numpy as jnp
from jax import lax
from jax.experimental import pallas as pl
from jax.sharding import PartitionSpec as P

ALL_AXES = ("grp", "sub", "expert")
SEQ_AXES = ("grp", "sub")
GROUP_AXES = ("sub", "expert")
KV_HEADS = 16
HEAD = 128
EXPERTS = 8
TOPK = 2
PIECES = 8
BLOCK = 256


epsilon = 1e-06
masked_score = -1e30


def _scores(q, k, qb, scale):
    s = lax.dot_general(q, k, (((1,), (1,)), ((), ())), preferred_element_type=jnp.float32) * scale
    kblock = lax.broadcasted_iota(jnp.int32, s.shape, 1) // BLOCK
    return jnp.where(kblock <= qb, s, masked_score)

def _fwd_kernel(scale, q_ref, k_ref, v_ref, qb_ref, o_ref, lse_ref):
    s = _scores(q_ref[...], k_ref[...], qb_ref[...], scale)
    largest = jnp.max(s, axis=-1, keepdims=True)
    weights = jnp.exp(s - largest)
    totals = jnp.sum(weights, axis=-1, keepdims=True)
    probs = weights / totals
    o_ref[...] = jnp.dot(probs.astype(jnp.bfloat16), v_ref[...],
                         preferred_element_type=jnp.float32).astype(o_ref.dtype)
    lse_ref[...] = largest + jnp.log(totals)

def _bwd_kernel(scale, q_ref, k_ref, v_ref, qb_ref, lse_ref, do_ref, dq_ref, dk_ref, dv_ref):
    q = q_ref[...]; k = k_ref[...]; v = v_ref[...]; do = do_ref[...]
    probs = jnp.exp(_scores(q, k, qb_ref[...], scale) - lse_ref[...])
    dp = lax.dot_general(do, v, (((1,), (1,)), ((), ())), preferred_element_type=jnp.float32)
    inner = jnp.sum(probs * dp, axis=-1, keepdims=True)
    ds = (probs * (dp - inner)).astype(jnp.bfloat16)
    dv_ref[...] = lax.dot_general(probs.astype(jnp.bfloat16), do, (((0,), (0,)), ((), ())),
                                  preferred_element_type=jnp.float32)
    dk_ref[...] = lax.dot_general(ds, q, (((0,), (0,)), ((), ())),
                                  preferred_element_type=jnp.float32) * scale
    dq_ref[...] = jnp.dot(ds, k, preferred_element_type=jnp.float32) * scale

def attn_fwd(q, k, v, qb):
    n, rows, d = q.shape; keys = k.shape[1]
    scale = 1.0 / math.sqrt(d)
    rspec = pl.BlockSpec((None, rows, d), lambda i: (i, 0, 0))
    kspec = pl.BlockSpec((None, keys, d), lambda i: (i, 0, 0))
    cspec = pl.BlockSpec((None, rows, 1), lambda i: (i, 0, 0))
    return pl.pallas_call(
        functools.partial(_fwd_kernel, scale),
        grid=(n,),
        in_specs=[rspec, kspec, kspec, cspec],
        out_specs=[rspec, cspec],
        out_shape=[jax.ShapeDtypeStruct((n, rows, d), jnp.bfloat16),
                   jax.ShapeDtypeStruct((n, rows, 1), jnp.float32)],
        cost_estimate=pl.CostEstimate(flops=4 * n * rows * keys * d,
                                      transcendentals=n * rows * keys,
                                      bytes_accessed=2 * n * (2 * rows * d + 2 * keys * d)),
    )(q, k, v, qb)

def attn_bwd(q, k, v, qb, lse, do):
    n, rows, d = q.shape; keys = k.shape[1]
    scale = 1.0 / math.sqrt(d)
    rspec = pl.BlockSpec((None, rows, d), lambda i: (i, 0, 0))
    kspec = pl.BlockSpec((None, keys, d), lambda i: (i, 0, 0))
    cspec = pl.BlockSpec((None, rows, 1), lambda i: (i, 0, 0))
    return pl.pallas_call(
        functools.partial(_bwd_kernel, scale),
        grid=(n,),
        in_specs=[rspec, kspec, kspec, cspec, cspec, rspec],
        out_specs=[rspec, kspec, kspec],
        out_shape=[jax.ShapeDtypeStruct((n, rows, d), jnp.float32),
                   jax.ShapeDtypeStruct((n, keys, d), jnp.float32),
                   jax.ShapeDtypeStruct((n, keys, d), jnp.float32)],
        cost_estimate=pl.CostEstimate(flops=10 * n * rows * keys * d,
                                      transcendentals=n * rows * keys,
                                      bytes_accessed=2 * n * (3 * rows * d + 2 * keys * d) + 8 * n * (rows * d + 2 * keys * d)),
    )(q, k, v, qb, lse, do)


def rope_tables(positions, head_size):
    half_size = head_size // 2
    frequency = jnp.exp(
        jnp.arange(half_size, dtype=jnp.float32) * (-2.0 * math.log(10000.0) / head_size)
    )
    angles = positions.astype(jnp.float32)[:, None] * frequency[None, :]
    return (jnp.cos(angles)[:, None, :], jnp.sin(angles)[:, None, :])


def rotate(values, cosines, sines):
    half_size = values.shape[-1] // 2
    first = values[..., :half_size]
    second = values[..., half_size:]
    return jnp.concatenate(
        [first * cosines - second * sines, second * cosines + first * sines], axis=-1
    )


def rotate_back(grads, cosines, sines):
    half_size = grads.shape[-1] // 2
    first = grads[..., :half_size]
    second = grads[..., half_size:]
    return jnp.concatenate(
        [first * cosines + second * sines, second * cosines - first * sines], axis=-1
    )


def slot_table(expert_ids, ranks, slot_cap):
    block_rows = expert_ids.shape[0]
    expert_range = jnp.arange(EXPERTS, dtype=jnp.int32)
    member = jnp.sum(
        (expert_ids[:, :, None] == expert_range[None, None, :]).astype(jnp.int32), axis=1
    )
    earlier = (ranks[:, None] < ranks[None, :]).astype(jnp.int32)
    places = jnp.sum(earlier[:, :, None] * member[:, None, :], axis=0)
    kept = member * (places < slot_cap).astype(jnp.int32)
    slot_range = jnp.arange(slot_cap, dtype=jnp.int32)
    landing = kept[:, :, None] * (places[:, :, None] == slot_range[None, None, :]).astype(jnp.int32)
    row_range = jnp.arange(block_rows, dtype=jnp.int32)
    slot_token = jnp.sum(landing * row_range[:, None, None], axis=0)
    slot_valid = jnp.sum(landing, axis=0)
    return (places, kept, slot_token, slot_valid)


def pair_index(expert_ids, places, kept, slot_cap):
    chosen_place = jnp.take_along_axis(places, expert_ids, axis=1)
    chosen_kept = jnp.take_along_axis(kept, expert_ids, axis=1)
    return (
        expert_ids * slot_cap + jnp.minimum(chosen_place, slot_cap - 1),
        chosen_kept.astype(jnp.float32),
    )


def pair_gates(logits, expert_ids):
    return jax.nn.softmax(jnp.take_along_axis(logits, expert_ids, axis=1), axis=-1)


def expert_onehot(expert_ids):
    expert_range = jnp.arange(EXPERTS, dtype=jnp.int32)
    return (expert_ids[:, :, None] == expert_range[None, None, :]).astype(jnp.float32)


def gates_back(gates, gate_grads, expert_ids):
    inner = jnp.sum(gates * gate_grads, axis=1, keepdims=True)
    chosen_grads = gates * (gate_grads - inner)
    return jnp.sum(chosen_grads[:, :, None] * expert_onehot(expert_ids), axis=1)


def slot_gates(gates, pair_kept, expert_ids, slot_token, slot_valid):
    per_expert = jnp.sum((gates * pair_kept)[:, :, None] * expert_onehot(expert_ids), axis=1)
    return jnp.take_along_axis(per_expert.T, slot_token, axis=1) * slot_valid.astype(jnp.float32)


def pick_slots(values, slot_token, slot_valid):
    return jnp.where(slot_valid[:, :, None] > 0, values[slot_token], jnp.zeros((), values.dtype))


def fan_out(slot_values, group_size):
    experts_here, slot_cap, width = slot_values.shape
    spread_out = jnp.broadcast_to(slot_values[:, None], (experts_here, group_size, slot_cap, width))
    return spread_out.reshape(experts_here * group_size, slot_cap, width)


def fold_group(received, group_size):
    count, slot_cap, width = received.shape
    return jnp.sum(received.reshape(count // group_size, group_size, slot_cap, width), axis=1)


def norm_back(normed_grad, gain, normed, inverse):
    scaled = normed_grad * gain
    gain_grad = jnp.sum(normed_grad * normed, axis=0)
    input_grad = inverse * (scaled - normed * jnp.mean(scaled * normed, axis=-1, keepdims=True))
    return (input_grad, gain_grad)


def shards(
    tokens,
    attn_gain,
    kv_weight,
    attn_router,
    query_weight,
    output_weight,
    mlp_gain,
    mlp_router,
    gate_weight,
    up_weight,
    down_weight,
    attn_experts,
    mlp_experts,
    priority,
    cotangent,
):
    devices = lax.axis_size(ALL_AXES)
    halves = lax.axis_size("expert")
    device_index = lax.axis_index(ALL_AXES)
    half_index = lax.axis_index("expert")
    seq_tokens, width = tokens.shape
    own_rows = seq_tokens // halves
    group_size = devices // EXPERTS
    head_cols = query_weight.shape[1]
    local_heads = head_cols // HEAD
    key_cols = KV_HEADS * HEAD
    all_tokens = own_rows * devices
    seq_length = seq_tokens * PIECES
    sequences = all_tokens // seq_length
    slot_cap = (9 * TOPK * own_rows + 8 * EXPERTS - 1) // (8 * EXPERTS)
    slot_rows = devices * slot_cap
    seq_rows = slot_rows // sequences
    my_expert = device_index // group_size
    groups = lax.axis_size("grp")

    def dispatch(slot_values):
        by_group = lax.all_to_all(slot_values, "grp", split_axis=0, concat_axis=0, tiled=True)
        return lax.all_gather(
            by_group.reshape(groups * slot_cap, width), GROUP_AXES, axis=0, tiled=True
        )

    def combine(partial_value):
        parts = lax.all_to_all(
            partial_value.astype(jnp.bfloat16).reshape(group_size, groups * slot_cap, width),
            GROUP_AXES,
            split_axis=0,
            concat_axis=0,
            tiled=True,
        )
        summed = jnp.sum(parts.astype(jnp.float32), axis=0).reshape(groups, slot_cap, width)
        return lax.all_to_all(
            summed.astype(jnp.bfloat16), "grp", split_axis=0, concat_axis=0, tiled=True
        ).astype(jnp.float32)

    def combine_scattered(partial_value):
        summed = lax.psum_scatter(
            partial_value.astype(jnp.bfloat16), GROUP_AXES, scatter_dimension=0, tiled=True
        )
        return lax.all_to_all(
            summed.reshape(groups, slot_cap, width), "grp", split_axis=0, concat_axis=0, tiled=True
        ).astype(jnp.float32)

    def to_rows(per_head):
        parts = lax.all_to_all(
            per_head.reshape(group_size, groups * slot_cap, head_cols),
            GROUP_AXES,
            split_axis=0,
            concat_axis=0,
            tiled=True,
        )
        return jnp.swapaxes(parts, 0, 1).reshape(groups * slot_cap, group_size * head_cols)

    def to_owners(row_values):
        return lax.all_to_all(
            row_values.astype(jnp.bfloat16).reshape(groups, slot_cap, width),
            "grp",
            split_axis=0,
            concat_axis=0,
            tiled=True,
        ).astype(jnp.float32)

    def to_gj(rows):
        shaped = rows.reshape((group_size, groups, slot_cap) + rows.shape[1:])
        return jnp.swapaxes(shaped, 0, 1).reshape(rows.shape)

    def to_jg(rows):
        shaped = rows.reshape((groups, group_size, slot_cap) + rows.shape[1:])
        return jnp.swapaxes(shaped, 0, 1).reshape(rows.shape)
    scale = 1.0 / math.sqrt(HEAD)

    start_row = half_index * own_rows
    own_input = lax.dynamic_slice_in_dim(tokens, start_row, own_rows, 0).astype(jnp.float32)
    own_cotangent = lax.dynamic_slice_in_dim(cotangent, start_row, own_rows, 0).astype(jnp.float32)
    own_attn = lax.dynamic_slice_in_dim(attn_experts, start_row, own_rows, 0)
    own_mlp = lax.dynamic_slice_in_dim(mlp_experts, start_row, own_rows, 0)
    own_rank = lax.dynamic_slice_in_dim(priority[0], start_row, own_rows, 0)
    token_order = jnp.arange(own_rows, dtype=jnp.int32)

    kv_rows, kv_width = kv_weight.shape
    id_cols = own_rows * TOPK // kv_rows
    extras = jnp.concatenate(
        [
            attn_gain[:, None],
            mlp_gain[:, None],
            attn_router,
            mlp_router,
            own_attn.reshape(kv_rows, id_cols).astype(jnp.bfloat16),
        ],
        axis=1,
    )
    extra_cols = extras.shape[1]
    extra_pad = -(-extra_cols // 128) * 128
    pair_cols = 2 * head_cols
    head_blocks = jnp.transpose(
        kv_weight.reshape(kv_rows, 2, group_size, head_cols), (2, 0, 1, 3)
    ).reshape(group_size, kv_rows, pair_cols)
    padded_extras = jnp.pad(extras, ((0, 0), (0, extra_pad - extra_cols)))
    dealt_rows = lax.all_to_all(
        jnp.concatenate(
            [
                head_blocks,
                jnp.broadcast_to(padded_extras[None], (group_size, kv_rows, extra_pad)),
            ],
            axis=2,
        ),
        GROUP_AXES,
        split_axis=0,
        concat_axis=0,
        tiled=True,
    )
    gathered = lax.all_to_all(
        jnp.broadcast_to(
            dealt_rows.reshape(1, group_size * kv_rows, pair_cols + extra_pad),
            (groups, group_size * kv_rows, pair_cols + extra_pad),
        ),
        "grp",
        split_axis=0,
        concat_axis=0,
        tiled=True,
    ).reshape(devices * kv_rows, pair_cols + extra_pad)
    head_kv = gathered[:, :pair_cols]
    gain_one = gathered[:, pair_cols]
    gain_two = gathered[:, pair_cols + 1]
    router_one = gathered[:, pair_cols + 2 : pair_cols + 2 + EXPERTS]
    router_two = gathered[:, pair_cols + 2 + EXPERTS : pair_cols + 2 + 2 * EXPERTS]
    routes_all = gathered[:, pair_cols + 2 + 2 * EXPERTS : pair_cols + extra_cols].astype(jnp.int32)
    inverse_one = lax.rsqrt(jnp.mean(own_input * own_input, axis=-1, keepdims=True) + epsilon)
    normed_one = own_input * inverse_one
    attn_input = (normed_one * gain_one.astype(jnp.float32)).astype(jnp.bfloat16)
    attn_logits = jnp.dot(attn_input, router_one, preferred_element_type=jnp.float32)
    seq_input = lax.all_gather(attn_input, GROUP_AXES, axis=0, tiled=True)
    seq_kv = jnp.dot(seq_input, head_kv, preferred_element_type=jnp.float32)
    seq_cos, seq_sin = rope_tables(jnp.arange(seq_length, dtype=jnp.int32), HEAD)
    seq_pair = jnp.concatenate(
        [
            rotate(seq_kv[:, :head_cols].reshape(seq_length, local_heads, HEAD), seq_cos, seq_sin)
            .reshape(seq_length, head_cols)
            .astype(jnp.bfloat16),
            seq_kv[:, head_cols:].astype(jnp.bfloat16),
        ],
        axis=1,
    )
    all_pairs = lax.all_to_all(
        jnp.broadcast_to(seq_pair[None], (groups,) + seq_pair.shape),
        "grp",
        split_axis=0,
        concat_axis=0,
        tiled=True,
    ).reshape(groups * seq_length, 2 * head_cols)
    seq_keys = all_pairs[:, :head_cols].reshape(sequences, seq_length, local_heads, HEAD)
    seq_values = all_pairs[:, head_cols:].reshape(sequences, seq_length, local_heads, HEAD)
    attn_places, attn_kept, attn_token, attn_valid = slot_table(own_attn, token_order, slot_cap)
    mlp_places, mlp_kept, mlp_token, mlp_valid = slot_table(own_mlp, own_rank, slot_cap)
    block_routes = routes_all.reshape(devices, own_rows, TOPK)
    dest_tables = jax.vmap(lambda block_ids: slot_table(block_ids, token_order, slot_cap)[2])(
        block_routes
    )
    dest_token = jnp.take(dest_tables, my_expert, axis=1)
    attn_rows = dispatch(pick_slots(attn_input, attn_token, attn_valid))
    queries = to_gj(jnp.dot(attn_rows, query_weight, preferred_element_type=jnp.float32))
    slot_positions = (
        (jnp.arange(devices, dtype=jnp.int32)[:, None] * own_rows + dest_token) % seq_length
    ).reshape(slot_rows)
    slot_cos, slot_sin = rope_tables(slot_positions, HEAD)
    rotated = rotate(queries.reshape(slot_rows, local_heads, HEAD), slot_cos, slot_sin).astype(
        jnp.bfloat16
    )
    seq_queries = rotated.reshape(sequences, seq_rows, local_heads, HEAD)
    query_blocks = (slot_positions // BLOCK).reshape(sequences, seq_rows)
    key_blocks = jnp.arange(seq_length, dtype=jnp.int32) // BLOCK

    attn_mixed, log_totals = attn_fwd(
        seq_queries.reshape(sequences, seq_rows, HEAD),
        seq_keys.reshape(sequences, seq_length, HEAD),
        seq_values.reshape(sequences, seq_length, HEAD),
        query_blocks[:, :, None],
    )
    mixed_rows = to_jg(attn_mixed.reshape(slot_rows, head_cols))
    output_stack = lax.all_gather(output_weight, GROUP_AXES, axis=0, tiled=True)
    attn_slots = to_owners(
        jnp.dot(to_rows(mixed_rows), output_stack, preferred_element_type=jnp.float32)
    )
    attn_gates = pair_gates(attn_logits, own_attn)
    attn_index, attn_pair_kept = pair_index(own_attn, attn_places, attn_kept, slot_cap)
    attn_picked = attn_slots.reshape(EXPERTS * slot_cap, width)[attn_index]
    hidden_state = own_input + jnp.sum(
        attn_picked * (attn_gates * attn_pair_kept)[:, :, None], axis=1
    )
    inverse_two = lax.rsqrt(jnp.mean(hidden_state * hidden_state, axis=-1, keepdims=True) + epsilon)
    normed_two = hidden_state * inverse_two
    mlp_input = (normed_two * gain_two.astype(jnp.float32)).astype(jnp.bfloat16)
    mlp_logits = jnp.dot(mlp_input, router_two, preferred_element_type=jnp.float32)
    mlp_gates = pair_gates(mlp_logits, own_mlp)
    mlp_index, mlp_pair_kept = pair_index(own_mlp, mlp_places, mlp_kept, slot_cap)
    mlp_slot_grad = (
        own_cotangent[mlp_token]
        * slot_gates(mlp_gates, mlp_pair_kept, own_mlp, mlp_token, mlp_valid)[:, :, None]
    ).astype(jnp.bfloat16)
    mlp_by_group = lax.all_to_all(
        jnp.concatenate([pick_slots(mlp_input, mlp_token, mlp_valid), mlp_slot_grad], axis=1),
        "grp",
        split_axis=0,
        concat_axis=0,
        tiled=True,
    )
    mlp_rows = lax.all_gather(
        mlp_by_group[:, :slot_cap].reshape(groups * slot_cap, width),
        GROUP_AXES,
        axis=0,
        tiled=True,
    )
    down_rows = lax.all_gather(
        mlp_by_group[:, slot_cap:].reshape(groups * slot_cap, width),
        GROUP_AXES,
        axis=0,
        tiled=True,
    )
    gate_pre = jnp.dot(mlp_rows, gate_weight, preferred_element_type=jnp.float32)
    up_pre = jnp.dot(mlp_rows, up_weight, preferred_element_type=jnp.float32)
    activated = jax.nn.silu(gate_pre)
    inner_rows = (activated * up_pre).astype(jnp.bfloat16)
    mlp_partial = jnp.dot(inner_rows, down_weight, preferred_element_type=jnp.float32)
    mlp_slots = combine_scattered(mlp_partial)
    query_stack = lax.all_gather(query_weight, GROUP_AXES, axis=1, tiled=True)
    mlp_slots, query_stack = lax.optimization_barrier((mlp_slots, query_stack))
    mlp_picked = mlp_slots.reshape(EXPERTS * slot_cap, width)[mlp_index]
    own_output = hidden_state + jnp.sum(
        mlp_picked * (mlp_gates * mlp_pair_kept)[:, :, None], axis=1
    )
    mlp_gate_grad = jnp.sum(mlp_picked * own_cotangent[:, None, :], axis=-1) * mlp_pair_kept
    mlp_logit_grad = gates_back(mlp_gates, mlp_gate_grad, own_mlp)
    inner_grad = jnp.einsum("rd,fd->rf", down_rows, down_weight, preferred_element_type=jnp.float32)
    down_grad = jnp.einsum("rf,rd->fd", inner_rows, down_rows, preferred_element_type=jnp.float32)
    sigmoid_gate = jax.nn.sigmoid(gate_pre)
    gate_pre_grad = (
        inner_grad * up_pre * sigmoid_gate * (1.0 + gate_pre * (1.0 - sigmoid_gate))
    ).astype(jnp.bfloat16)
    up_pre_grad = (inner_grad * activated).astype(jnp.bfloat16)
    gate_grad = jnp.einsum("rd,rf->df", mlp_rows, gate_pre_grad, preferred_element_type=jnp.float32)
    up_grad = jnp.einsum("rd,rf->df", mlp_rows, up_pre_grad, preferred_element_type=jnp.float32)
    row_grad = jnp.einsum(
        "rf,df->rd", gate_pre_grad, gate_weight, preferred_element_type=jnp.float32
    ) + jnp.einsum("rf,df->rd", up_pre_grad, up_weight, preferred_element_type=jnp.float32)
    mlp_row_grad = combine(row_grad)
    mlp_input_grad = jnp.sum(
        mlp_row_grad.reshape(EXPERTS * slot_cap, width)[mlp_index] * mlp_pair_kept[:, :, None],
        axis=1,
    )
    mlp_input_grad = mlp_input_grad + jnp.dot(
        mlp_logit_grad, router_two.astype(jnp.float32).T, precision=lax.Precision.HIGHEST
    )
    mlp_router_own = jnp.dot(
        mlp_input.astype(jnp.float32).T, mlp_logit_grad, precision=lax.Precision.HIGHEST
    )
    hidden_grad, gain_two_own = norm_back(
        mlp_input_grad, gain_two.astype(jnp.float32), normed_two, inverse_two
    )
    hidden_grad = hidden_grad + own_cotangent
    attn_gate_grad = jnp.sum(attn_picked * hidden_grad[:, None, :], axis=-1) * attn_pair_kept
    attn_logit_grad = gates_back(attn_gates, attn_gate_grad, own_attn)
    attn_slot_grad = (
        hidden_grad[attn_token]
        * slot_gates(attn_gates, attn_pair_kept, own_attn, attn_token, attn_valid)[:, :, None]
    ).astype(jnp.bfloat16)
    out_rows = dispatch(attn_slot_grad)
    output_grad = jnp.einsum("rw,rd->wd", mixed_rows, out_rows, preferred_element_type=jnp.float32)
    mixed_grad = jnp.einsum(
        "rd,wd->rw", out_rows, output_weight, preferred_element_type=jnp.float32
    ).astype(jnp.bfloat16)
    seq_mixed_grad = to_gj(mixed_grad).reshape(sequences, seq_rows, local_heads, HEAD)

    seq_query_grad, seq_key_grad, seq_value_grad = attn_bwd(
        seq_queries.reshape(sequences, seq_rows, HEAD),
        seq_keys.reshape(sequences, seq_length, HEAD),
        seq_values.reshape(sequences, seq_length, HEAD),
        query_blocks[:, :, None],
        log_totals,
        seq_mixed_grad.reshape(sequences, seq_rows, HEAD),
    )
    query_rot_grad = to_jg(
        rotate_back(seq_query_grad.reshape(slot_rows, local_heads, HEAD), slot_cos, slot_sin)
        .reshape(slot_rows, head_cols)
        .astype(jnp.bfloat16)
    )
    query_grad = jnp.einsum(
        "rd,rw->dw", attn_rows, query_rot_grad, preferred_element_type=jnp.float32
    )
    attn_row_grad = to_owners(
        jnp.einsum(
            "rw,dw->rd", to_rows(query_rot_grad), query_stack, preferred_element_type=jnp.float32
        )
    )
    pair_back = lax.all_to_all(
        jnp.concatenate([seq_key_grad, seq_value_grad], axis=2).astype(jnp.bfloat16),
        "grp",
        split_axis=0,
        concat_axis=0,
        tiled=True,
    )
    seq_pair_grad = jnp.sum(pair_back.astype(jnp.float32), axis=0)
    kv_col_grad = jnp.concatenate(
        [
            rotate_back(
                seq_pair_grad[:, :head_cols].reshape(seq_length, local_heads, HEAD),
                seq_cos,
                seq_sin,
            ).reshape(seq_length, head_cols),
            seq_pair_grad[:, head_cols:],
        ],
        axis=1,
    ).astype(jnp.bfloat16)
    kv_col_weight = jnp.einsum(
        "rd,rc->dc", seq_input, kv_col_grad, preferred_element_type=jnp.float32
    )
    kv_input_parts = lax.all_to_all(
        jnp.einsum("rc,dc->rd", kv_col_grad, head_kv, preferred_element_type=jnp.float32)
        .astype(jnp.bfloat16)
        .reshape(group_size, own_rows, width),
        GROUP_AXES,
        split_axis=0,
        concat_axis=0,
        tiled=True,
    )
    attn_input_grad = jnp.sum(
        attn_row_grad.reshape(EXPERTS * slot_cap, width)[attn_index] * attn_pair_kept[:, :, None],
        axis=1,
    )
    attn_input_grad = attn_input_grad + jnp.sum(kv_input_parts.astype(jnp.float32), axis=0)
    attn_input_grad = attn_input_grad + jnp.dot(
        attn_logit_grad, router_one.astype(jnp.float32).T, precision=lax.Precision.HIGHEST
    )
    attn_router_own = jnp.dot(
        attn_input.astype(jnp.float32).T, attn_logit_grad, precision=lax.Precision.HIGHEST
    )
    input_grad, gain_one_own = norm_back(
        attn_input_grad, gain_one.astype(jnp.float32), normed_one, inverse_one
    )
    input_grad = input_grad + hidden_grad
    grad_extras = jnp.concatenate(
        [gain_one_own[:, None], gain_two_own[:, None], attn_router_own, mlp_router_own], axis=1
    )
    packed_grad = jnp.concatenate(
        [
            kv_col_weight,
            jnp.pad(grad_extras, ((0, 0), (0, extra_pad - grad_extras.shape[1]))),
        ],
        axis=1,
    )
    group_sum = lax.psum_scatter(packed_grad, "grp", scatter_dimension=0, tiled=True)
    dealt = lax.all_to_all(
        group_sum.reshape(group_size, kv_rows, pair_cols + extra_pad),
        GROUP_AXES,
        split_axis=0,
        concat_axis=0,
        tiled=True,
    )
    kv_grad = jnp.transpose(
        dealt[:, :, :pair_cols].reshape(group_size, kv_rows, 2, head_cols), (1, 2, 0, 3)
    ).reshape(kv_rows, kv_width)
    extra_grad = jnp.sum(dealt[:, :, pair_cols:], axis=0)
    gain_one_grad = extra_grad[:, 0]
    gain_two_grad = extra_grad[:, 1]
    attn_router_grad = extra_grad[:, 2 : 2 + EXPERTS]
    mlp_router_grad = extra_grad[:, 2 + EXPERTS : 2 + 2 * EXPERTS]
    both_full = lax.all_gather(
        jnp.concatenate(
            [own_output.astype(jnp.bfloat16), input_grad.astype(jnp.bfloat16)], axis=1
        ),
        "expert",
        axis=0,
        tiled=True,
    )
    mixed_full, input_full = both_full[:, :width], both_full[:, width:]
    return (
        mixed_full,
        input_full,
        gain_one_grad,
        kv_grad,
        attn_router_grad,
        query_grad,
        output_grad,
        gain_two_grad,
        mlp_router_grad,
        gate_grad,
        up_grad,
        down_grad,
    )


def solution(mesh):
    seq_size, halves = mesh.devices.shape
    grouped = jax.sharding.Mesh(
        mesh.devices.reshape(EXPERTS, seq_size // EXPERTS, halves), ALL_AXES
    )
    return jax.shard_map(
        shards,
        mesh=grouped,
        in_specs=(
            P(SEQ_AXES, None),
            P(ALL_AXES),
            P(ALL_AXES, None),
            P(ALL_AXES, None),
            P(None, ALL_AXES),
            P(ALL_AXES, None),
            P(ALL_AXES),
            P(ALL_AXES, None),
            P(None, ALL_AXES),
            P(None, ALL_AXES),
            P(ALL_AXES, None),
            P(SEQ_AXES, None),
            P(SEQ_AXES, None),
            P(SEQ_AXES, None),
            P(SEQ_AXES, None),
        ),
        out_specs=(
            P(SEQ_AXES, None),
            P(SEQ_AXES, None),
            P(ALL_AXES),
            P(ALL_AXES, None),
            P(ALL_AXES, None),
            P(None, ALL_AXES),
            P(ALL_AXES, None),
            P(ALL_AXES),
            P(ALL_AXES, None),
            P(None, ALL_AXES),
            P(None, ALL_AXES),
            P(ALL_AXES, None),
        ),
        check_vma=False,
    )
```

```python
import functools
import math

import jax
import jax.numpy as jnp
from jax import lax
from jax.experimental import pallas as pl
from jax.sharding import PartitionSpec as P

ALL_AXES = ("grp", "sub", "expert")
SEQ_AXES = ("grp", "sub")
GROUP_AXES = ("sub", "expert")
KV_HEADS = 16
HEAD = 128
EXPERTS = 8
TOPK = 2
PIECES = 8
BLOCK = 256


epsilon = 1e-06
masked_score = -1e30


def _scores(q, k, qb, scale):
    s = lax.dot_general(q, k, (((1,), (1,)), ((), ())), preferred_element_type=jnp.float32) * scale
    kblock = lax.broadcasted_iota(jnp.int32, s.shape, 1) // BLOCK
    return jnp.where(kblock <= qb, s, masked_score)

def _fwd_kernel(scale, q_ref, k_ref, v_ref, qb_ref, o_ref, lse_ref):
    s = _scores(q_ref[...], k_ref[...], qb_ref[...], scale)
    largest = jnp.max(s, axis=-1, keepdims=True)
    weights = jnp.exp(s - largest)
    totals = jnp.sum(weights, axis=-1, keepdims=True)
    probs = weights / totals
    o_ref[...] = jnp.dot(probs.astype(jnp.bfloat16), v_ref[...],
                         preferred_element_type=jnp.float32).astype(o_ref.dtype)
    lse_ref[...] = largest + jnp.log(totals)

def _bwd_kernel(scale, q_ref, k_ref, v_ref, qb_ref, lse_ref, do_ref, dq_ref, dk_ref, dv_ref):
    q = q_ref[...]; k = k_ref[...]; v = v_ref[...]; do = do_ref[...]
    probs = jnp.exp(_scores(q, k, qb_ref[...], scale) - lse_ref[...])
    dp = lax.dot_general(do, v, (((1,), (1,)), ((), ())), preferred_element_type=jnp.float32)
    inner = jnp.sum(probs * dp, axis=-1, keepdims=True)
    ds = (probs * (dp - inner)).astype(jnp.bfloat16)
    dv_ref[...] = lax.dot_general(probs.astype(jnp.bfloat16), do, (((0,), (0,)), ((), ())),
                                  preferred_element_type=jnp.float32)
    dk_ref[...] = lax.dot_general(ds, q, (((0,), (0,)), ((), ())),
                                  preferred_element_type=jnp.float32) * scale
    dq_ref[...] = jnp.dot(ds, k, preferred_element_type=jnp.float32) * scale

def attn_fwd(q, k, v, qb):
    n, rows, d = q.shape; keys = k.shape[1]
    scale = 1.0 / math.sqrt(d)
    rspec = pl.BlockSpec((None, rows, d), lambda i: (i, 0, 0))
    kspec = pl.BlockSpec((None, keys, d), lambda i: (i, 0, 0))
    cspec = pl.BlockSpec((None, rows, 1), lambda i: (i, 0, 0))
    return pl.pallas_call(
        functools.partial(_fwd_kernel, scale),
        grid=(n,),
        in_specs=[rspec, kspec, kspec, cspec],
        out_specs=[rspec, cspec],
        out_shape=[jax.ShapeDtypeStruct((n, rows, d), jnp.bfloat16),
                   jax.ShapeDtypeStruct((n, rows, 1), jnp.float32)],
        cost_estimate=pl.CostEstimate(flops=4 * n * rows * keys * d,
                                      transcendentals=n * rows * keys,
                                      bytes_accessed=2 * n * (2 * rows * d + 2 * keys * d)),
    )(q, k, v, qb)

def attn_bwd(q, k, v, qb, lse, do):
    n, rows, d = q.shape; keys = k.shape[1]
    scale = 1.0 / math.sqrt(d)
    rspec = pl.BlockSpec((None, rows, d), lambda i: (i, 0, 0))
    kspec = pl.BlockSpec((None, keys, d), lambda i: (i, 0, 0))
    cspec = pl.BlockSpec((None, rows, 1), lambda i: (i, 0, 0))
    return pl.pallas_call(
        functools.partial(_bwd_kernel, scale),
        grid=(n,),
        in_specs=[rspec, kspec, kspec, cspec, cspec, rspec],
        out_specs=[rspec, kspec, kspec],
        out_shape=[jax.ShapeDtypeStruct((n, rows, d), jnp.float32),
                   jax.ShapeDtypeStruct((n, keys, d), jnp.float32),
                   jax.ShapeDtypeStruct((n, keys, d), jnp.float32)],
        cost_estimate=pl.CostEstimate(flops=10 * n * rows * keys * d,
                                      transcendentals=n * rows * keys,
                                      bytes_accessed=2 * n * (3 * rows * d + 2 * keys * d) + 8 * n * (rows * d + 2 * keys * d)),
    )(q, k, v, qb, lse, do)


def rope_tables(positions, head_size):
    half_size = head_size // 2
    frequency = jnp.exp(
        jnp.arange(half_size, dtype=jnp.float32) * (-2.0 * math.log(10000.0) / head_size)
    )
    angles = positions.astype(jnp.float32)[:, None] * frequency[None, :]
    return (jnp.cos(angles)[:, None, :], jnp.sin(angles)[:, None, :])


def rotate(values, cosines, sines):
    half_size = values.shape[-1] // 2
    first = values[..., :half_size]
    second = values[..., half_size:]
    return jnp.concatenate(
        [first * cosines - second * sines, second * cosines + first * sines], axis=-1
    )


def rotate_back(grads, cosines, sines):
    half_size = grads.shape[-1] // 2
    first = grads[..., :half_size]
    second = grads[..., half_size:]
    return jnp.concatenate(
        [first * cosines + second * sines, second * cosines - first * sines], axis=-1
    )


def slot_table(expert_ids, ranks, slot_cap):
    block_rows = expert_ids.shape[0]
    expert_range = jnp.arange(EXPERTS, dtype=jnp.int32)
    member = jnp.sum(
        (expert_ids[:, :, None] == expert_range[None, None, :]).astype(jnp.int32), axis=1
    )
    earlier = (ranks[:, None] < ranks[None, :]).astype(jnp.int32)
    places = jnp.sum(earlier[:, :, None] * member[:, None, :], axis=0)
    kept = member * (places < slot_cap).astype(jnp.int32)
    slot_range = jnp.arange(slot_cap, dtype=jnp.int32)
    landing = kept[:, :, None] * (places[:, :, None] == slot_range[None, None, :]).astype(jnp.int32)
    row_range = jnp.arange(block_rows, dtype=jnp.int32)
    slot_token = jnp.sum(landing * row_range[:, None, None], axis=0)
    slot_valid = jnp.sum(landing, axis=0)
    return (places, kept, slot_token, slot_valid)


def pair_index(expert_ids, places, kept, slot_cap):
    chosen_place = jnp.take_along_axis(places, expert_ids, axis=1)
    chosen_kept = jnp.take_along_axis(kept, expert_ids, axis=1)
    return (
        expert_ids * slot_cap + jnp.minimum(chosen_place, slot_cap - 1),
        chosen_kept.astype(jnp.float32),
    )


def pair_gates(logits, expert_ids):
    return jax.nn.softmax(jnp.take_along_axis(logits, expert_ids, axis=1), axis=-1)


def expert_onehot(expert_ids):
    expert_range = jnp.arange(EXPERTS, dtype=jnp.int32)
    return (expert_ids[:, :, None] == expert_range[None, None, :]).astype(jnp.float32)


def gates_back(gates, gate_grads, expert_ids):
    inner = jnp.sum(gates * gate_grads, axis=1, keepdims=True)
    chosen_grads = gates * (gate_grads - inner)
    return jnp.sum(chosen_grads[:, :, None] * expert_onehot(expert_ids), axis=1)


def slot_gates(gates, pair_kept, expert_ids, slot_token, slot_valid):
    per_expert = jnp.sum((gates * pair_kept)[:, :, None] * expert_onehot(expert_ids), axis=1)
    return jnp.take_along_axis(per_expert.T, slot_token, axis=1) * slot_valid.astype(jnp.float32)


def pick_slots(values, slot_token, slot_valid):
    return jnp.where(slot_valid[:, :, None] > 0, values[slot_token], jnp.zeros((), values.dtype))


def fan_out(slot_values, group_size):
    experts_here, slot_cap, width = slot_values.shape
    spread_out = jnp.broadcast_to(slot_values[:, None], (experts_here, group_size, slot_cap, width))
    return spread_out.reshape(experts_here * group_size, slot_cap, width)


def fold_group(received, group_size):
    count, slot_cap, width = received.shape
    return jnp.sum(received.reshape(count // group_size, group_size, slot_cap, width), axis=1)


def norm_back(normed_grad, gain, normed, inverse):
    scaled = normed_grad * gain
    gain_grad = jnp.sum(normed_grad * normed, axis=0)
    input_grad = inverse * (scaled - normed * jnp.mean(scaled * normed, axis=-1, keepdims=True))
    return (input_grad, gain_grad)


def shards(
    tokens,
    attn_gain,
    kv_weight,
    attn_router,
    query_weight,
    output_weight,
    mlp_gain,
    mlp_router,
    gate_weight,
    up_weight,
    down_weight,
    attn_experts,
    mlp_experts,
    priority,
    cotangent,
):
    devices = lax.axis_size(ALL_AXES)
    halves = lax.axis_size("expert")
    device_index = lax.axis_index(ALL_AXES)
    half_index = lax.axis_index("expert")
    seq_tokens, width = tokens.shape
    own_rows = seq_tokens // halves
    group_size = devices // EXPERTS
    head_cols = query_weight.shape[1]
    local_heads = head_cols // HEAD
    key_cols = KV_HEADS * HEAD
    all_tokens = own_rows * devices
    seq_length = seq_tokens * PIECES
    sequences = all_tokens // seq_length
    slot_cap = (9 * TOPK * own_rows + 8 * EXPERTS - 1) // (8 * EXPERTS)
    slot_rows = devices * slot_cap
    seq_rows = slot_rows // sequences
    my_expert = device_index // group_size
    groups = lax.axis_size("grp")

    def dispatch(slot_values):
        by_group = lax.all_to_all(slot_values, "grp", split_axis=0, concat_axis=0, tiled=True)
        return lax.all_gather(
            by_group.reshape(groups * slot_cap, width), GROUP_AXES, axis=0, tiled=True
        )

    def combine(partial_value):
        parts = lax.all_to_all(
            partial_value.astype(jnp.bfloat16).reshape(group_size, groups * slot_cap, width),
            GROUP_AXES,
            split_axis=0,
            concat_axis=0,
            tiled=True,
        )
        summed = jnp.sum(parts.astype(jnp.float32), axis=0).reshape(groups, slot_cap, width)
        return lax.all_to_all(
            summed.astype(jnp.bfloat16), "grp", split_axis=0, concat_axis=0, tiled=True
        ).astype(jnp.float32)

    def combine_scattered(partial_value):
        summed = lax.psum_scatter(
            partial_value.astype(jnp.bfloat16), GROUP_AXES, scatter_dimension=0, tiled=True
        )
        return lax.all_to_all(
            summed.reshape(groups, slot_cap, width), "grp", split_axis=0, concat_axis=0, tiled=True
        ).astype(jnp.float32)

    def to_rows(per_head):
        parts = lax.all_to_all(
            per_head.reshape(group_size, groups * slot_cap, head_cols),
            GROUP_AXES,
            split_axis=0,
            concat_axis=0,
            tiled=True,
        )
        return jnp.swapaxes(parts, 0, 1).reshape(groups * slot_cap, group_size * head_cols)

    def to_owners(row_values):
        return lax.all_to_all(
            row_values.astype(jnp.bfloat16).reshape(groups, slot_cap, width),
            "grp",
            split_axis=0,
            concat_axis=0,
            tiled=True,
        ).astype(jnp.float32)

    def to_gj(rows):
        shaped = rows.reshape((group_size, groups, slot_cap) + rows.shape[1:])
        return jnp.swapaxes(shaped, 0, 1).reshape(rows.shape)

    def to_jg(rows):
        shaped = rows.reshape((groups, group_size, slot_cap) + rows.shape[1:])
        return jnp.swapaxes(shaped, 0, 1).reshape(rows.shape)
    scale = 1.0 / math.sqrt(HEAD)

    start_row = half_index * own_rows
    own_input = lax.dynamic_slice_in_dim(tokens, start_row, own_rows, 0).astype(jnp.float32)
    own_cotangent = lax.dynamic_slice_in_dim(cotangent, start_row, own_rows, 0).astype(jnp.float32)
    own_attn = lax.dynamic_slice_in_dim(attn_experts, start_row, own_rows, 0)
    own_mlp = lax.dynamic_slice_in_dim(mlp_experts, start_row, own_rows, 0)
    own_rank = lax.dynamic_slice_in_dim(priority[0], start_row, own_rows, 0)
    token_order = jnp.arange(own_rows, dtype=jnp.int32)

    kv_rows, kv_width = kv_weight.shape
    id_cols = own_rows * TOPK // kv_rows
    extras = jnp.concatenate(
        [
            attn_gain[:, None],
            mlp_gain[:, None],
            attn_router,
            mlp_router,
            own_attn.reshape(kv_rows, id_cols).astype(jnp.bfloat16),
        ],
        axis=1,
    )
    extra_cols = extras.shape[1]
    extra_pad = -(-extra_cols // 128) * 128
    pair_cols = 2 * head_cols
    head_blocks = jnp.transpose(
        kv_weight.reshape(kv_rows, 2, group_size, head_cols), (2, 0, 1, 3)
    ).reshape(group_size, kv_rows, pair_cols)
    padded_extras = jnp.pad(extras, ((0, 0), (0, extra_pad - extra_cols)))
    dealt_rows = lax.all_to_all(
        jnp.concatenate(
            [
                head_blocks,
                jnp.broadcast_to(padded_extras[None], (group_size, kv_rows, extra_pad)),
            ],
            axis=2,
        ),
        GROUP_AXES,
        split_axis=0,
        concat_axis=0,
        tiled=True,
    )
    gathered = lax.all_to_all(
        jnp.broadcast_to(
            dealt_rows.reshape(1, group_size * kv_rows, pair_cols + extra_pad),
            (groups, group_size * kv_rows, pair_cols + extra_pad),
        ),
        "grp",
        split_axis=0,
        concat_axis=0,
        tiled=True,
    ).reshape(devices * kv_rows, pair_cols + extra_pad)
    head_kv = gathered[:, :pair_cols]
    gain_one = gathered[:, pair_cols]
    gain_two = gathered[:, pair_cols + 1]
    router_one = gathered[:, pair_cols + 2 : pair_cols + 2 + EXPERTS]
    router_two = gathered[:, pair_cols + 2 + EXPERTS : pair_cols + 2 + 2 * EXPERTS]
    routes_all = gathered[:, pair_cols + 2 + 2 * EXPERTS : pair_cols + extra_cols].astype(jnp.int32)
    inverse_one = lax.rsqrt(jnp.mean(own_input * own_input, axis=-1, keepdims=True) + epsilon)
    normed_one = own_input * inverse_one
    attn_input = (normed_one * gain_one.astype(jnp.float32)).astype(jnp.bfloat16)
    attn_logits = jnp.dot(attn_input, router_one, preferred_element_type=jnp.float32)
    seq_input = lax.all_gather(attn_input, GROUP_AXES, axis=0, tiled=True)
    seq_kv = jnp.dot(seq_input, head_kv, preferred_element_type=jnp.float32)
    seq_cos, seq_sin = rope_tables(jnp.arange(seq_length, dtype=jnp.int32), HEAD)
    seq_pair = jnp.concatenate(
        [
            rotate(seq_kv[:, :head_cols].reshape(seq_length, local_heads, HEAD), seq_cos, seq_sin)
            .reshape(seq_length, head_cols)
            .astype(jnp.bfloat16),
            seq_kv[:, head_cols:].astype(jnp.bfloat16),
        ],
        axis=1,
    )
    all_pairs = lax.all_to_all(
        jnp.broadcast_to(seq_pair[None], (groups,) + seq_pair.shape),
        "grp",
        split_axis=0,
        concat_axis=0,
        tiled=True,
    ).reshape(groups * seq_length, 2 * head_cols)
    seq_keys = all_pairs[:, :head_cols].reshape(sequences, seq_length, local_heads, HEAD)
    seq_values = all_pairs[:, head_cols:].reshape(sequences, seq_length, local_heads, HEAD)
    attn_places, attn_kept, attn_token, attn_valid = slot_table(own_attn, token_order, slot_cap)
    mlp_places, mlp_kept, mlp_token, mlp_valid = slot_table(own_mlp, own_rank, slot_cap)
    block_routes = routes_all.reshape(devices, own_rows, TOPK)
    dest_tables = jax.vmap(lambda block_ids: slot_table(block_ids, token_order, slot_cap)[2])(
        block_routes
    )
    dest_token = jnp.take(dest_tables, my_expert, axis=1)
    attn_rows = dispatch(pick_slots(attn_input, attn_token, attn_valid))
    queries = to_gj(jnp.dot(attn_rows, query_weight, preferred_element_type=jnp.float32))
    slot_positions = (
        (jnp.arange(devices, dtype=jnp.int32)[:, None] * own_rows + dest_token) % seq_length
    ).reshape(slot_rows)
    slot_cos, slot_sin = rope_tables(slot_positions, HEAD)
    rotated = rotate(queries.reshape(slot_rows, local_heads, HEAD), slot_cos, slot_sin).astype(
        jnp.bfloat16
    )
    seq_queries = rotated.reshape(sequences, seq_rows, local_heads, HEAD)
    query_blocks = (slot_positions // BLOCK).reshape(sequences, seq_rows)
    key_blocks = jnp.arange(seq_length, dtype=jnp.int32) // BLOCK

    attn_mixed, log_totals = attn_fwd(
        seq_queries.reshape(sequences, seq_rows, HEAD),
        seq_keys.reshape(sequences, seq_length, HEAD),
        seq_values.reshape(sequences, seq_length, HEAD),
        query_blocks[:, :, None],
    )
    mixed_rows = to_jg(attn_mixed.reshape(slot_rows, head_cols))
    output_stack = lax.all_gather(output_weight, GROUP_AXES, axis=0, tiled=True)
    attn_slots = to_owners(
        jnp.dot(to_rows(mixed_rows), output_stack, preferred_element_type=jnp.float32)
    )
    attn_gates = pair_gates(attn_logits, own_attn)
    attn_index, attn_pair_kept = pair_index(own_attn, attn_places, attn_kept, slot_cap)
    attn_picked = attn_slots.reshape(EXPERTS * slot_cap, width)[attn_index]
    hidden_state = own_input + jnp.sum(
        attn_picked * (attn_gates * attn_pair_kept)[:, :, None], axis=1
    )
    inverse_two = lax.rsqrt(jnp.mean(hidden_state * hidden_state, axis=-1, keepdims=True) + epsilon)
    normed_two = hidden_state * inverse_two
    mlp_input = (normed_two * gain_two.astype(jnp.float32)).astype(jnp.bfloat16)
    query_high = lax.all_gather(query_weight[: width // 2], GROUP_AXES, axis=1, tiled=True)
    mlp_input, query_high = lax.optimization_barrier((mlp_input, query_high))
    mlp_logits = jnp.dot(mlp_input, router_two, preferred_element_type=jnp.float32)
    mlp_gates = pair_gates(mlp_logits, own_mlp)
    mlp_index, mlp_pair_kept = pair_index(own_mlp, mlp_places, mlp_kept, slot_cap)
    mlp_slot_grad = (
        own_cotangent[mlp_token]
        * slot_gates(mlp_gates, mlp_pair_kept, own_mlp, mlp_token, mlp_valid)[:, :, None]
    ).astype(jnp.bfloat16)
    mlp_by_group = lax.all_to_all(
        jnp.concatenate([pick_slots(mlp_input, mlp_token, mlp_valid), mlp_slot_grad], axis=1),
        "grp",
        split_axis=0,
        concat_axis=0,
        tiled=True,
    )
    mlp_rows = lax.all_gather(
        mlp_by_group[:, :slot_cap].reshape(groups * slot_cap, width),
        GROUP_AXES,
        axis=0,
        tiled=True,
    )
    down_rows = lax.all_gather(
        mlp_by_group[:, slot_cap:].reshape(groups * slot_cap, width),
        GROUP_AXES,
        axis=0,
        tiled=True,
    )
    gate_pre = jnp.dot(mlp_rows, gate_weight, preferred_element_type=jnp.float32)
    up_pre = jnp.dot(mlp_rows, up_weight, preferred_element_type=jnp.float32)
    activated = jax.nn.silu(gate_pre)
    inner_rows = (activated * up_pre).astype(jnp.bfloat16)
    mlp_partial = jnp.dot(inner_rows, down_weight, preferred_element_type=jnp.float32)
    mlp_slots = combine_scattered(mlp_partial)
    query_low = lax.all_gather(query_weight[width // 2 :], GROUP_AXES, axis=1, tiled=True)
    mlp_slots, query_low = lax.optimization_barrier((mlp_slots, query_low))
    mlp_picked = mlp_slots.reshape(EXPERTS * slot_cap, width)[mlp_index]
    own_output = hidden_state + jnp.sum(
        mlp_picked * (mlp_gates * mlp_pair_kept)[:, :, None], axis=1
    )
    mlp_gate_grad = jnp.sum(mlp_picked * own_cotangent[:, None, :], axis=-1) * mlp_pair_kept
    mlp_logit_grad = gates_back(mlp_gates, mlp_gate_grad, own_mlp)
    inner_grad = jnp.einsum("rd,fd->rf", down_rows, down_weight, preferred_element_type=jnp.float32)
    down_grad = jnp.einsum("rf,rd->fd", inner_rows, down_rows, preferred_element_type=jnp.float32)
    sigmoid_gate = jax.nn.sigmoid(gate_pre)
    gate_pre_grad = (
        inner_grad * up_pre * sigmoid_gate * (1.0 + gate_pre * (1.0 - sigmoid_gate))
    ).astype(jnp.bfloat16)
    up_pre_grad = (inner_grad * activated).astype(jnp.bfloat16)
    gate_grad = jnp.einsum("rd,rf->df", mlp_rows, gate_pre_grad, preferred_element_type=jnp.float32)
    up_grad = jnp.einsum("rd,rf->df", mlp_rows, up_pre_grad, preferred_element_type=jnp.float32)
    row_grad = jnp.einsum(
        "rf,df->rd", gate_pre_grad, gate_weight, preferred_element_type=jnp.float32
    ) + jnp.einsum("rf,df->rd", up_pre_grad, up_weight, preferred_element_type=jnp.float32)
    mlp_row_grad = combine(row_grad)
    mlp_input_grad = jnp.sum(
        mlp_row_grad.reshape(EXPERTS * slot_cap, width)[mlp_index] * mlp_pair_kept[:, :, None],
        axis=1,
    )
    mlp_input_grad = mlp_input_grad + jnp.dot(
        mlp_logit_grad, router_two.astype(jnp.float32).T, precision=lax.Precision.HIGHEST
    )
    mlp_router_own = jnp.dot(
        mlp_input.astype(jnp.float32).T, mlp_logit_grad, precision=lax.Precision.HIGHEST
    )
    hidden_grad, gain_two_own = norm_back(
        mlp_input_grad, gain_two.astype(jnp.float32), normed_two, inverse_two
    )
    hidden_grad = hidden_grad + own_cotangent
    attn_gate_grad = jnp.sum(attn_picked * hidden_grad[:, None, :], axis=-1) * attn_pair_kept
    attn_logit_grad = gates_back(attn_gates, attn_gate_grad, own_attn)
    attn_slot_grad = (
        hidden_grad[attn_token]
        * slot_gates(attn_gates, attn_pair_kept, own_attn, attn_token, attn_valid)[:, :, None]
    ).astype(jnp.bfloat16)
    out_rows = dispatch(attn_slot_grad)
    output_grad = jnp.einsum("rw,rd->wd", mixed_rows, out_rows, preferred_element_type=jnp.float32)
    mixed_grad = jnp.einsum(
        "rd,wd->rw", out_rows, output_weight, preferred_element_type=jnp.float32
    ).astype(jnp.bfloat16)
    seq_mixed_grad = to_gj(mixed_grad).reshape(sequences, seq_rows, local_heads, HEAD)

    seq_query_grad, seq_key_grad, seq_value_grad = attn_bwd(
        seq_queries.reshape(sequences, seq_rows, HEAD),
        seq_keys.reshape(sequences, seq_length, HEAD),
        seq_values.reshape(sequences, seq_length, HEAD),
        query_blocks[:, :, None],
        log_totals,
        seq_mixed_grad.reshape(sequences, seq_rows, HEAD),
    )
    query_rot_grad = to_jg(
        rotate_back(seq_query_grad.reshape(slot_rows, local_heads, HEAD), slot_cos, slot_sin)
        .reshape(slot_rows, head_cols)
        .astype(jnp.bfloat16)
    )
    query_grad = jnp.einsum(
        "rd,rw->dw", attn_rows, query_rot_grad, preferred_element_type=jnp.float32
    )
    query_rows = to_rows(query_rot_grad)
    attn_row_grad = to_owners(
        jnp.concatenate(
            [
                jnp.einsum("rw,dw->rd", query_rows, query_high, preferred_element_type=jnp.float32),
                jnp.einsum("rw,dw->rd", query_rows, query_low, preferred_element_type=jnp.float32),
            ],
            axis=1,
        )
    )
    pair_back = lax.all_to_all(
        jnp.concatenate([seq_key_grad, seq_value_grad], axis=2).astype(jnp.bfloat16),
        "grp",
        split_axis=0,
        concat_axis=0,
        tiled=True,
    )
    seq_pair_grad = jnp.sum(pair_back.astype(jnp.float32), axis=0)
    kv_col_grad = jnp.concatenate(
        [
            rotate_back(
                seq_pair_grad[:, :head_cols].reshape(seq_length, local_heads, HEAD),
                seq_cos,
                seq_sin,
            ).reshape(seq_length, head_cols),
            seq_pair_grad[:, head_cols:],
        ],
        axis=1,
    ).astype(jnp.bfloat16)
    kv_col_weight = jnp.einsum(
        "rd,rc->dc", seq_input, kv_col_grad, preferred_element_type=jnp.float32
    )
    kv_input_parts = lax.all_to_all(
        jnp.einsum("rc,dc->rd", kv_col_grad, head_kv, preferred_element_type=jnp.float32)
        .astype(jnp.bfloat16)
        .reshape(group_size, own_rows, width),
        GROUP_AXES,
        split_axis=0,
        concat_axis=0,
        tiled=True,
    )
    attn_input_grad = jnp.sum(
        attn_row_grad.reshape(EXPERTS * slot_cap, width)[attn_index] * attn_pair_kept[:, :, None],
        axis=1,
    )
    attn_input_grad = attn_input_grad + jnp.sum(kv_input_parts.astype(jnp.float32), axis=0)
    attn_input_grad = attn_input_grad + jnp.dot(
        attn_logit_grad, router_one.astype(jnp.float32).T, precision=lax.Precision.HIGHEST
    )
    attn_router_own = jnp.dot(
        attn_input.astype(jnp.float32).T, attn_logit_grad, precision=lax.Precision.HIGHEST
    )
    input_grad, gain_one_own = norm_back(
        attn_input_grad, gain_one.astype(jnp.float32), normed_one, inverse_one
    )
    input_grad = input_grad + hidden_grad
    grad_extras = jnp.concatenate(
        [gain_one_own[:, None], gain_two_own[:, None], attn_router_own, mlp_router_own], axis=1
    )
    packed_grad = jnp.concatenate(
        [
            kv_col_weight,
            jnp.pad(grad_extras, ((0, 0), (0, extra_pad - grad_extras.shape[1]))),
        ],
        axis=1,
    )
    group_sum = lax.psum_scatter(packed_grad, "grp", scatter_dimension=0, tiled=True)
    dealt = lax.all_to_all(
        group_sum.reshape(group_size, kv_rows, pair_cols + extra_pad),
        GROUP_AXES,
        split_axis=0,
        concat_axis=0,
        tiled=True,
    )
    kv_grad = jnp.transpose(
        dealt[:, :, :pair_cols].reshape(group_size, kv_rows, 2, head_cols), (1, 2, 0, 3)
    ).reshape(kv_rows, kv_width)
    extra_grad = jnp.sum(dealt[:, :, pair_cols:], axis=0)
    gain_one_grad = extra_grad[:, 0]
    gain_two_grad = extra_grad[:, 1]
    attn_router_grad = extra_grad[:, 2 : 2 + EXPERTS]
    mlp_router_grad = extra_grad[:, 2 + EXPERTS : 2 + 2 * EXPERTS]
    both_full = lax.all_gather(
        jnp.concatenate(
            [own_output.astype(jnp.bfloat16), input_grad.astype(jnp.bfloat16)], axis=1
        ),
        "expert",
        axis=0,
        tiled=True,
    )
    mixed_full, input_full = both_full[:, :width], both_full[:, width:]
    return (
        mixed_full,
        input_full,
        gain_one_grad,
        kv_grad,
        attn_router_grad,
        query_grad,
        output_grad,
        gain_two_grad,
        mlp_router_grad,
        gate_grad,
        up_grad,
        down_grad,
    )


def solution(mesh):
    seq_size, halves = mesh.devices.shape
    grouped = jax.sharding.Mesh(
        mesh.devices.reshape(EXPERTS, seq_size // EXPERTS, halves), ALL_AXES
    )
    return jax.shard_map(
        shards,
        mesh=grouped,
        in_specs=(
            P(SEQ_AXES, None),
            P(ALL_AXES),
            P(ALL_AXES, None),
            P(ALL_AXES, None),
            P(None, ALL_AXES),
            P(ALL_AXES, None),
            P(ALL_AXES),
            P(ALL_AXES, None),
            P(None, ALL_AXES),
            P(None, ALL_AXES),
            P(ALL_AXES, None),
            P(SEQ_AXES, None),
            P(SEQ_AXES, None),
            P(SEQ_AXES, None),
            P(SEQ_AXES, None),
        ),
        out_specs=(
            P(SEQ_AXES, None),
            P(SEQ_AXES, None),
            P(ALL_AXES),
            P(ALL_AXES, None),
            P(ALL_AXES, None),
            P(None, ALL_AXES),
            P(ALL_AXES, None),
            P(ALL_AXES),
            P(ALL_AXES, None),
            P(None, ALL_AXES),
            P(None, ALL_AXES),
            P(ALL_AXES, None),
        ),
        check_vma=False,
    )
```

```python
import functools
import math

import jax
import jax.numpy as jnp
from jax import lax
from jax.experimental import pallas as pl
from jax.sharding import PartitionSpec as P

ALL_AXES = ("grp", "sub", "expert")
SEQ_AXES = ("grp", "sub")
GROUP_AXES = ("sub", "expert")
KV_HEADS = 16
HEAD = 128
EXPERTS = 8
TOPK = 2
PIECES = 8
BLOCK = 256


epsilon = 1e-06
masked_score = -1e30


def _scores(q, k, qb, scale):
    s = lax.dot_general(q, k, (((1,), (1,)), ((), ())), preferred_element_type=jnp.float32) * scale
    kblock = lax.broadcasted_iota(jnp.int32, s.shape, 1) // BLOCK
    return jnp.where(kblock <= qb, s, masked_score)

def _fwd_kernel(scale, q_ref, k_ref, v_ref, qb_ref, o_ref, lse_ref):
    s = _scores(q_ref[...], k_ref[...], qb_ref[...], scale)
    largest = jnp.max(s, axis=-1, keepdims=True)
    weights = jnp.exp(s - largest)
    totals = jnp.sum(weights, axis=-1, keepdims=True)
    probs = weights / totals
    o_ref[...] = jnp.dot(probs.astype(jnp.bfloat16), v_ref[...],
                         preferred_element_type=jnp.float32).astype(o_ref.dtype)
    lse_ref[...] = largest + jnp.log(totals)

def _bwd_kernel(scale, q_ref, k_ref, v_ref, qb_ref, lse_ref, do_ref, dq_ref, dkv_ref):
    q = q_ref[...]; k = k_ref[...]; v = v_ref[...]; do = do_ref[...]
    probs = jnp.exp(_scores(q, k, qb_ref[...], scale) - lse_ref[...])
    dp = lax.dot_general(do, v, (((1,), (1,)), ((), ())), preferred_element_type=jnp.float32)
    inner = jnp.sum(probs * dp, axis=-1, keepdims=True)
    ds = (probs * (dp - inner)).astype(jnp.bfloat16)
    d = q.shape[1]
    dkv_ref[:, d:] = lax.dot_general(probs.astype(jnp.bfloat16), do, (((0,), (0,)), ((), ())),
                                     preferred_element_type=jnp.float32).astype(dkv_ref.dtype)
    dkv_ref[:, :d] = (lax.dot_general(ds, q, (((0,), (0,)), ((), ())),
                                      preferred_element_type=jnp.float32) * scale).astype(dkv_ref.dtype)
    dq_ref[...] = jnp.dot(ds, k, preferred_element_type=jnp.float32) * scale

def attn_fwd(q, k, v, qb):
    n, rows, d = q.shape; keys = k.shape[1]
    scale = 1.0 / math.sqrt(d)
    rspec = pl.BlockSpec((None, rows, d), lambda i: (i, 0, 0))
    kspec = pl.BlockSpec((None, keys, d), lambda i: (i, 0, 0))
    cspec = pl.BlockSpec((None, rows, 1), lambda i: (i, 0, 0))
    return pl.pallas_call(
        functools.partial(_fwd_kernel, scale),
        grid=(n,),
        in_specs=[rspec, kspec, kspec, cspec],
        out_specs=[rspec, cspec],
        out_shape=[jax.ShapeDtypeStruct((n, rows, d), jnp.bfloat16),
                   jax.ShapeDtypeStruct((n, rows, 1), jnp.float32)],
        cost_estimate=pl.CostEstimate(flops=4 * n * rows * keys * d,
                                      transcendentals=n * rows * keys,
                                      bytes_accessed=2 * n * (2 * rows * d + 2 * keys * d)),
    )(q, k, v, qb)

def attn_bwd(q, k, v, qb, lse, do):
    n, rows, d = q.shape; keys = k.shape[1]
    scale = 1.0 / math.sqrt(d)
    rspec = pl.BlockSpec((None, rows, d), lambda i: (i, 0, 0))
    kspec = pl.BlockSpec((None, keys, d), lambda i: (i, 0, 0))
    cspec = pl.BlockSpec((None, rows, 1), lambda i: (i, 0, 0))
    return pl.pallas_call(
        functools.partial(_bwd_kernel, scale),
        grid=(n,),
        in_specs=[rspec, kspec, kspec, cspec, cspec, rspec],
        out_specs=[rspec, pl.BlockSpec((None, keys, 2 * d), lambda i: (i, 0, 0))],
        out_shape=[jax.ShapeDtypeStruct((n, rows, d), jnp.float32),
                   jax.ShapeDtypeStruct((n, keys, 2 * d), jnp.bfloat16)],
        cost_estimate=pl.CostEstimate(flops=10 * n * rows * keys * d,
                                      transcendentals=n * rows * keys,
                                      bytes_accessed=2 * n * (3 * rows * d + 2 * keys * d) + 8 * n * (rows * d + 2 * keys * d)),
    )(q, k, v, qb, lse, do)


def rope_tables(positions, head_size):
    half_size = head_size // 2
    frequency = jnp.exp(
        jnp.arange(half_size, dtype=jnp.float32) * (-2.0 * math.log(10000.0) / head_size)
    )
    angles = positions.astype(jnp.float32)[:, None] * frequency[None, :]
    return (jnp.cos(angles)[:, None, :], jnp.sin(angles)[:, None, :])


def rotate(values, cosines, sines):
    half_size = values.shape[-1] // 2
    first = values[..., :half_size]
    second = values[..., half_size:]
    return jnp.concatenate(
        [first * cosines - second * sines, second * cosines + first * sines], axis=-1
    )


def rotate_back(grads, cosines, sines):
    half_size = grads.shape[-1] // 2
    first = grads[..., :half_size]
    second = grads[..., half_size:]
    return jnp.concatenate(
        [first * cosines + second * sines, second * cosines - first * sines], axis=-1
    )


def slot_table(expert_ids, ranks, slot_cap):
    block_rows = expert_ids.shape[0]
    expert_range = jnp.arange(EXPERTS, dtype=jnp.int32)
    member = jnp.sum(
        (expert_ids[:, :, None] == expert_range[None, None, :]).astype(jnp.int32), axis=1
    )
    earlier = (ranks[:, None] < ranks[None, :]).astype(jnp.int32)
    places = jnp.sum(earlier[:, :, None] * member[:, None, :], axis=0)
    kept = member * (places < slot_cap).astype(jnp.int32)
    slot_range = jnp.arange(slot_cap, dtype=jnp.int32)
    landing = kept[:, :, None] * (places[:, :, None] == slot_range[None, None, :]).astype(jnp.int32)
    row_range = jnp.arange(block_rows, dtype=jnp.int32)
    slot_token = jnp.sum(landing * row_range[:, None, None], axis=0)
    slot_valid = jnp.sum(landing, axis=0)
    return (places, kept, slot_token, slot_valid)


def pair_index(expert_ids, places, kept, slot_cap):
    chosen_place = jnp.take_along_axis(places, expert_ids, axis=1)
    chosen_kept = jnp.take_along_axis(kept, expert_ids, axis=1)
    return (
        expert_ids * slot_cap + jnp.minimum(chosen_place, slot_cap - 1),
        chosen_kept.astype(jnp.float32),
    )


def pair_gates(logits, expert_ids):
    return jax.nn.softmax(jnp.take_along_axis(logits, expert_ids, axis=1), axis=-1)


def expert_onehot(expert_ids):
    expert_range = jnp.arange(EXPERTS, dtype=jnp.int32)
    return (expert_ids[:, :, None] == expert_range[None, None, :]).astype(jnp.float32)


def gates_back(gates, gate_grads, expert_ids):
    inner = jnp.sum(gates * gate_grads, axis=1, keepdims=True)
    chosen_grads = gates * (gate_grads - inner)
    return jnp.sum(chosen_grads[:, :, None] * expert_onehot(expert_ids), axis=1)


def slot_gates(gates, pair_kept, expert_ids, slot_token, slot_valid):
    per_expert = jnp.sum((gates * pair_kept)[:, :, None] * expert_onehot(expert_ids), axis=1)
    return jnp.take_along_axis(per_expert.T, slot_token, axis=1) * slot_valid.astype(jnp.float32)


def pick_slots(values, slot_token, slot_valid):
    return jnp.where(slot_valid[:, :, None] > 0, values[slot_token], jnp.zeros((), values.dtype))


def fan_out(slot_values, group_size):
    experts_here, slot_cap, width = slot_values.shape
    spread_out = jnp.broadcast_to(slot_values[:, None], (experts_here, group_size, slot_cap, width))
    return spread_out.reshape(experts_here * group_size, slot_cap, width)


def fold_group(received, group_size):
    count, slot_cap, width = received.shape
    return jnp.sum(received.reshape(count // group_size, group_size, slot_cap, width), axis=1)


def norm_back(normed_grad, gain, normed, inverse):
    scaled = normed_grad * gain
    gain_grad = jnp.sum(normed_grad * normed, axis=0)
    input_grad = inverse * (scaled - normed * jnp.mean(scaled * normed, axis=-1, keepdims=True))
    return (input_grad, gain_grad)


def shards(
    tokens,
    attn_gain,
    kv_weight,
    attn_router,
    query_weight,
    output_weight,
    mlp_gain,
    mlp_router,
    gate_weight,
    up_weight,
    down_weight,
    attn_experts,
    mlp_experts,
    priority,
    cotangent,
):
    devices = lax.axis_size(ALL_AXES)
    halves = lax.axis_size("expert")
    device_index = lax.axis_index(ALL_AXES)
    half_index = lax.axis_index("expert")
    seq_tokens, width = tokens.shape
    own_rows = seq_tokens // halves
    group_size = devices // EXPERTS
    head_cols = query_weight.shape[1]
    local_heads = head_cols // HEAD
    key_cols = KV_HEADS * HEAD
    all_tokens = own_rows * devices
    seq_length = seq_tokens * PIECES
    sequences = all_tokens // seq_length
    slot_cap = (9 * TOPK * own_rows + 8 * EXPERTS - 1) // (8 * EXPERTS)
    slot_rows = devices * slot_cap
    seq_rows = slot_rows // sequences
    my_expert = device_index // group_size
    groups = lax.axis_size("grp")

    def dispatch(slot_values):
        by_group = lax.all_to_all(slot_values, "grp", split_axis=0, concat_axis=0, tiled=True)
        return lax.all_gather(
            by_group.reshape(groups * slot_cap, width), GROUP_AXES, axis=0, tiled=True
        )

    def combine(partial_value):
        parts = lax.all_to_all(
            partial_value.astype(jnp.bfloat16).reshape(group_size, groups * slot_cap, width),
            GROUP_AXES,
            split_axis=0,
            concat_axis=0,
            tiled=True,
        )
        summed = jnp.sum(parts.astype(jnp.float32), axis=0).reshape(groups, slot_cap, width)
        return lax.all_to_all(
            summed.astype(jnp.bfloat16), "grp", split_axis=0, concat_axis=0, tiled=True
        ).astype(jnp.float32)

    def combine_scattered(partial_value):
        summed = lax.psum_scatter(
            partial_value.astype(jnp.bfloat16), GROUP_AXES, scatter_dimension=0, tiled=True
        )
        return lax.all_to_all(
            summed.reshape(groups, slot_cap, width), "grp", split_axis=0, concat_axis=0, tiled=True
        ).astype(jnp.float32)

    def to_rows(per_head):
        parts = lax.all_to_all(
            per_head.reshape(group_size, groups * slot_cap, head_cols),
            GROUP_AXES,
            split_axis=0,
            concat_axis=0,
            tiled=True,
        )
        return jnp.swapaxes(parts, 0, 1).reshape(groups * slot_cap, group_size * head_cols)

    def to_owners(row_values):
        return lax.all_to_all(
            row_values.astype(jnp.bfloat16).reshape(groups, slot_cap, width),
            "grp",
            split_axis=0,
            concat_axis=0,
            tiled=True,
        ).astype(jnp.float32)

    def to_gj(rows):
        shaped = rows.reshape((group_size, groups, slot_cap) + rows.shape[1:])
        return jnp.swapaxes(shaped, 0, 1).reshape(rows.shape)

    def to_jg(rows):
        shaped = rows.reshape((groups, group_size, slot_cap) + rows.shape[1:])
        return jnp.swapaxes(shaped, 0, 1).reshape(rows.shape)
    scale = 1.0 / math.sqrt(HEAD)

    start_row = half_index * own_rows
    own_input = lax.dynamic_slice_in_dim(tokens, start_row, own_rows, 0).astype(jnp.float32)
    own_cotangent = lax.dynamic_slice_in_dim(cotangent, start_row, own_rows, 0).astype(jnp.float32)
    own_attn = lax.dynamic_slice_in_dim(attn_experts, start_row, own_rows, 0)
    own_mlp = lax.dynamic_slice_in_dim(mlp_experts, start_row, own_rows, 0)
    own_rank = lax.dynamic_slice_in_dim(priority[0], start_row, own_rows, 0)
    token_order = jnp.arange(own_rows, dtype=jnp.int32)

    kv_rows, kv_width = kv_weight.shape
    id_cols = own_rows * TOPK // kv_rows
    extras = jnp.concatenate(
        [
            attn_gain[:, None],
            mlp_gain[:, None],
            attn_router,
            mlp_router,
            own_attn.reshape(kv_rows, id_cols).astype(jnp.bfloat16),
        ],
        axis=1,
    )
    extra_cols = extras.shape[1]
    extra_pad = -(-extra_cols // 128) * 128
    pair_cols = 2 * head_cols
    head_blocks = jnp.transpose(
        kv_weight.reshape(kv_rows, 2, group_size, head_cols), (2, 0, 1, 3)
    ).reshape(group_size, kv_rows, pair_cols)
    padded_extras = jnp.pad(extras, ((0, 0), (0, extra_pad - extra_cols)))
    dealt_rows = lax.all_to_all(
        jnp.concatenate(
            [
                head_blocks,
                jnp.broadcast_to(padded_extras[None], (group_size, kv_rows, extra_pad)),
            ],
            axis=2,
        ),
        GROUP_AXES,
        split_axis=0,
        concat_axis=0,
        tiled=True,
    )
    gathered = lax.all_to_all(
        jnp.broadcast_to(
            dealt_rows.reshape(1, group_size * kv_rows, pair_cols + extra_pad),
            (groups, group_size * kv_rows, pair_cols + extra_pad),
        ),
        "grp",
        split_axis=0,
        concat_axis=0,
        tiled=True,
    ).reshape(devices * kv_rows, pair_cols + extra_pad)
    head_kv = gathered[:, :pair_cols]
    gain_one = gathered[:, pair_cols]
    gain_two = gathered[:, pair_cols + 1]
    router_one = gathered[:, pair_cols + 2 : pair_cols + 2 + EXPERTS]
    router_two = gathered[:, pair_cols + 2 + EXPERTS : pair_cols + 2 + 2 * EXPERTS]
    routes_all = gathered[:, pair_cols + 2 + 2 * EXPERTS : pair_cols + extra_cols].astype(jnp.int32)
    inverse_one = lax.rsqrt(jnp.mean(own_input * own_input, axis=-1, keepdims=True) + epsilon)
    normed_one = own_input * inverse_one
    attn_input = (normed_one * gain_one.astype(jnp.float32)).astype(jnp.bfloat16)
    attn_logits = jnp.dot(attn_input, router_one, preferred_element_type=jnp.float32)
    seq_input = lax.all_gather(attn_input, GROUP_AXES, axis=0, tiled=True)
    seq_kv = jnp.dot(seq_input, head_kv, preferred_element_type=jnp.float32)
    seq_cos, seq_sin = rope_tables(jnp.arange(seq_length, dtype=jnp.int32), HEAD)
    seq_pair = jnp.concatenate(
        [
            rotate(seq_kv[:, :head_cols].reshape(seq_length, local_heads, HEAD), seq_cos, seq_sin)
            .reshape(seq_length, head_cols)
            .astype(jnp.bfloat16),
            seq_kv[:, head_cols:].astype(jnp.bfloat16),
        ],
        axis=1,
    )
    all_pairs = lax.all_to_all(
        jnp.broadcast_to(seq_pair[None], (groups,) + seq_pair.shape),
        "grp",
        split_axis=0,
        concat_axis=0,
        tiled=True,
    ).reshape(groups * seq_length, 2 * head_cols)
    seq_keys = all_pairs[:, :head_cols].reshape(sequences, seq_length, local_heads, HEAD)
    seq_values = all_pairs[:, head_cols:].reshape(sequences, seq_length, local_heads, HEAD)
    attn_places, attn_kept, attn_token, attn_valid = slot_table(own_attn, token_order, slot_cap)
    mlp_places, mlp_kept, mlp_token, mlp_valid = slot_table(own_mlp, own_rank, slot_cap)
    block_routes = routes_all.reshape(devices, own_rows, TOPK)
    dest_tables = jax.vmap(lambda block_ids: slot_table(block_ids, token_order, slot_cap)[2])(
        block_routes
    )
    dest_token = jnp.take(dest_tables, my_expert, axis=1)
    attn_rows = dispatch(pick_slots(attn_input, attn_token, attn_valid))
    queries = to_gj(jnp.dot(attn_rows, query_weight, preferred_element_type=jnp.float32))
    slot_positions = (
        (jnp.arange(devices, dtype=jnp.int32)[:, None] * own_rows + dest_token) % seq_length
    ).reshape(slot_rows)
    slot_cos, slot_sin = rope_tables(slot_positions, HEAD)
    rotated = rotate(queries.reshape(slot_rows, local_heads, HEAD), slot_cos, slot_sin).astype(
        jnp.bfloat16
    )
    seq_queries = rotated.reshape(sequences, seq_rows, local_heads, HEAD)
    query_blocks = (slot_positions // BLOCK).reshape(sequences, seq_rows)
    key_blocks = jnp.arange(seq_length, dtype=jnp.int32) // BLOCK

    attn_mixed, log_totals = attn_fwd(
        seq_queries.reshape(sequences, seq_rows, HEAD),
        seq_keys.reshape(sequences, seq_length, HEAD),
        seq_values.reshape(sequences, seq_length, HEAD),
        query_blocks[:, :, None],
    )
    mixed_rows = to_jg(attn_mixed.reshape(slot_rows, head_cols))
    output_stack = lax.all_gather(output_weight, GROUP_AXES, axis=0, tiled=True)
    attn_slots = to_owners(
        jnp.dot(to_rows(mixed_rows), output_stack, preferred_element_type=jnp.float32)
    )
    attn_gates = pair_gates(attn_logits, own_attn)
    attn_index, attn_pair_kept = pair_index(own_attn, attn_places, attn_kept, slot_cap)
    attn_picked = attn_slots.reshape(EXPERTS * slot_cap, width)[attn_index]
    hidden_state = own_input + jnp.sum(
        attn_picked * (attn_gates * attn_pair_kept)[:, :, None], axis=1
    )
    inverse_two = lax.rsqrt(jnp.mean(hidden_state * hidden_state, axis=-1, keepdims=True) + epsilon)
    normed_two = hidden_state * inverse_two
    mlp_input = (normed_two * gain_two.astype(jnp.float32)).astype(jnp.bfloat16)
    mlp_logits = jnp.dot(mlp_input, router_two, preferred_element_type=jnp.float32)
    mlp_gates = pair_gates(mlp_logits, own_mlp)
    mlp_index, mlp_pair_kept = pair_index(own_mlp, mlp_places, mlp_kept, slot_cap)
    mlp_slot_grad = (
        own_cotangent[mlp_token]
        * slot_gates(mlp_gates, mlp_pair_kept, own_mlp, mlp_token, mlp_valid)[:, :, None]
    ).astype(jnp.bfloat16)
    mlp_by_group = lax.all_to_all(
        jnp.concatenate([pick_slots(mlp_input, mlp_token, mlp_valid), mlp_slot_grad], axis=1),
        "grp",
        split_axis=0,
        concat_axis=0,
        tiled=True,
    )
    mlp_rows = lax.all_gather(
        mlp_by_group[:, :slot_cap].reshape(groups * slot_cap, width),
        GROUP_AXES,
        axis=0,
        tiled=True,
    )
    down_rows = lax.all_gather(
        mlp_by_group[:, slot_cap:].reshape(groups * slot_cap, width),
        GROUP_AXES,
        axis=0,
        tiled=True,
    )
    gate_pre = jnp.dot(mlp_rows, gate_weight, preferred_element_type=jnp.float32)
    up_pre = jnp.dot(mlp_rows, up_weight, preferred_element_type=jnp.float32)
    activated = jax.nn.silu(gate_pre)
    inner_rows = (activated * up_pre).astype(jnp.bfloat16)
    mlp_partial = jnp.dot(inner_rows, down_weight, preferred_element_type=jnp.float32)
    mlp_slots = combine_scattered(mlp_partial)
    query_stack = lax.all_gather(query_weight, GROUP_AXES, axis=1, tiled=True)
    mlp_slots, query_stack = lax.optimization_barrier((mlp_slots, query_stack))
    mlp_picked = mlp_slots.reshape(EXPERTS * slot_cap, width)[mlp_index]
    own_output = hidden_state + jnp.sum(
        mlp_picked * (mlp_gates * mlp_pair_kept)[:, :, None], axis=1
    )
    mlp_gate_grad = jnp.sum(mlp_picked * own_cotangent[:, None, :], axis=-1) * mlp_pair_kept
    mlp_logit_grad = gates_back(mlp_gates, mlp_gate_grad, own_mlp)
    inner_grad = jnp.einsum("rd,fd->rf", down_rows, down_weight, preferred_element_type=jnp.float32)
    down_grad = jnp.einsum("rf,rd->fd", inner_rows, down_rows, preferred_element_type=jnp.float32)
    sigmoid_gate = jax.nn.sigmoid(gate_pre)
    gate_pre_grad = (
        inner_grad * up_pre * sigmoid_gate * (1.0 + gate_pre * (1.0 - sigmoid_gate))
    ).astype(jnp.bfloat16)
    up_pre_grad = (inner_grad * activated).astype(jnp.bfloat16)
    gate_grad = jnp.einsum("rd,rf->df", mlp_rows, gate_pre_grad, preferred_element_type=jnp.float32)
    up_grad = jnp.einsum("rd,rf->df", mlp_rows, up_pre_grad, preferred_element_type=jnp.float32)
    row_grad = jnp.einsum(
        "rf,df->rd", gate_pre_grad, gate_weight, preferred_element_type=jnp.float32
    ) + jnp.einsum("rf,df->rd", up_pre_grad, up_weight, preferred_element_type=jnp.float32)
    mlp_row_grad = combine(row_grad)
    mlp_input_grad = jnp.sum(
        mlp_row_grad.reshape(EXPERTS * slot_cap, width)[mlp_index] * mlp_pair_kept[:, :, None],
        axis=1,
    )
    mlp_input_grad = mlp_input_grad + jnp.dot(
        mlp_logit_grad, router_two.astype(jnp.float32).T, precision=lax.Precision.HIGHEST
    )
    mlp_router_own = jnp.dot(
        mlp_input.astype(jnp.float32).T, mlp_logit_grad, precision=lax.Precision.HIGHEST
    )
    hidden_grad, gain_two_own = norm_back(
        mlp_input_grad, gain_two.astype(jnp.float32), normed_two, inverse_two
    )
    hidden_grad = hidden_grad + own_cotangent
    attn_gate_grad = jnp.sum(attn_picked * hidden_grad[:, None, :], axis=-1) * attn_pair_kept
    attn_logit_grad = gates_back(attn_gates, attn_gate_grad, own_attn)
    attn_slot_grad = (
        hidden_grad[attn_token]
        * slot_gates(attn_gates, attn_pair_kept, own_attn, attn_token, attn_valid)[:, :, None]
    ).astype(jnp.bfloat16)
    out_rows = dispatch(attn_slot_grad)
    output_grad = jnp.einsum("rw,rd->wd", mixed_rows, out_rows, preferred_element_type=jnp.float32)
    mixed_grad = jnp.einsum(
        "rd,wd->rw", out_rows, output_weight, preferred_element_type=jnp.float32
    ).astype(jnp.bfloat16)
    seq_mixed_grad = to_gj(mixed_grad).reshape(sequences, seq_rows, local_heads, HEAD)

    seq_query_grad, seq_pair_back = attn_bwd(
        seq_queries.reshape(sequences, seq_rows, HEAD),
        seq_keys.reshape(sequences, seq_length, HEAD),
        seq_values.reshape(sequences, seq_length, HEAD),
        query_blocks[:, :, None],
        log_totals,
        seq_mixed_grad.reshape(sequences, seq_rows, HEAD),
    )
    query_rot_grad = to_jg(
        rotate_back(seq_query_grad.reshape(slot_rows, local_heads, HEAD), slot_cos, slot_sin)
        .reshape(slot_rows, head_cols)
        .astype(jnp.bfloat16)
    )
    query_grad = jnp.einsum(
        "rd,rw->dw", attn_rows, query_rot_grad, preferred_element_type=jnp.float32
    )
    attn_row_grad = to_owners(
        jnp.einsum(
            "rw,dw->rd", to_rows(query_rot_grad), query_stack, preferred_element_type=jnp.float32
        )
    )
    pair_back = lax.all_to_all(
        seq_pair_back,
        "grp",
        split_axis=0,
        concat_axis=0,
        tiled=True,
    )
    seq_pair_grad = jnp.sum(pair_back.astype(jnp.float32), axis=0)
    kv_col_grad = jnp.concatenate(
        [
            rotate_back(
                seq_pair_grad[:, :head_cols].reshape(seq_length, local_heads, HEAD),
                seq_cos,
                seq_sin,
            ).reshape(seq_length, head_cols),
            seq_pair_grad[:, head_cols:],
        ],
        axis=1,
    ).astype(jnp.bfloat16)
    kv_col_weight = jnp.einsum(
        "rd,rc->dc", seq_input, kv_col_grad, preferred_element_type=jnp.float32
    )
    kv_input_parts = lax.all_to_all(
        jnp.einsum("rc,dc->rd", kv_col_grad, head_kv, preferred_element_type=jnp.float32)
        .astype(jnp.bfloat16)
        .reshape(group_size, own_rows, width),
        GROUP_AXES,
        split_axis=0,
        concat_axis=0,
        tiled=True,
    )
    attn_input_grad = jnp.sum(
        attn_row_grad.reshape(EXPERTS * slot_cap, width)[attn_index] * attn_pair_kept[:, :, None],
        axis=1,
    )
    attn_input_grad = attn_input_grad + jnp.sum(kv_input_parts.astype(jnp.float32), axis=0)
    attn_input_grad = attn_input_grad + jnp.dot(
        attn_logit_grad, router_one.astype(jnp.float32).T, precision=lax.Precision.HIGHEST
    )
    attn_router_own = jnp.dot(
        attn_input.astype(jnp.float32).T, attn_logit_grad, precision=lax.Precision.HIGHEST
    )
    input_grad, gain_one_own = norm_back(
        attn_input_grad, gain_one.astype(jnp.float32), normed_one, inverse_one
    )
    input_grad = input_grad + hidden_grad
    grad_extras = jnp.concatenate(
        [gain_one_own[:, None], gain_two_own[:, None], attn_router_own, mlp_router_own], axis=1
    )
    packed_grad = jnp.concatenate(
        [
            kv_col_weight,
            jnp.pad(grad_extras, ((0, 0), (0, extra_pad - grad_extras.shape[1]))),
        ],
        axis=1,
    )
    group_sum = lax.psum_scatter(packed_grad, "grp", scatter_dimension=0, tiled=True)
    dealt = lax.all_to_all(
        group_sum.reshape(group_size, kv_rows, pair_cols + extra_pad),
        GROUP_AXES,
        split_axis=0,
        concat_axis=0,
        tiled=True,
    )
    kv_grad = jnp.transpose(
        dealt[:, :, :pair_cols].reshape(group_size, kv_rows, 2, head_cols), (1, 2, 0, 3)
    ).reshape(kv_rows, kv_width)
    extra_grad = jnp.sum(dealt[:, :, pair_cols:], axis=0)
    gain_one_grad = extra_grad[:, 0]
    gain_two_grad = extra_grad[:, 1]
    attn_router_grad = extra_grad[:, 2 : 2 + EXPERTS]
    mlp_router_grad = extra_grad[:, 2 + EXPERTS : 2 + 2 * EXPERTS]
    both_full = lax.all_gather(
        jnp.concatenate(
            [own_output.astype(jnp.bfloat16), input_grad.astype(jnp.bfloat16)], axis=1
        ),
        "expert",
        axis=0,
        tiled=True,
    )
    mixed_full, input_full = both_full[:, :width], both_full[:, width:]
    return (
        mixed_full,
        input_full,
        gain_one_grad,
        kv_grad,
        attn_router_grad,
        query_grad,
        output_grad,
        gain_two_grad,
        mlp_router_grad,
        gate_grad,
        up_grad,
        down_grad,
    )


def solution(mesh):
    seq_size, halves = mesh.devices.shape
    grouped = jax.sharding.Mesh(
        mesh.devices.reshape(EXPERTS, seq_size // EXPERTS, halves), ALL_AXES
    )
    return jax.shard_map(
        shards,
        mesh=grouped,
        in_specs=(
            P(SEQ_AXES, None),
            P(ALL_AXES),
            P(ALL_AXES, None),
            P(ALL_AXES, None),
            P(None, ALL_AXES),
            P(ALL_AXES, None),
            P(ALL_AXES),
            P(ALL_AXES, None),
            P(None, ALL_AXES),
            P(None, ALL_AXES),
            P(ALL_AXES, None),
            P(SEQ_AXES, None),
            P(SEQ_AXES, None),
            P(SEQ_AXES, None),
            P(SEQ_AXES, None),
        ),
        out_specs=(
            P(SEQ_AXES, None),
            P(SEQ_AXES, None),
            P(ALL_AXES),
            P(ALL_AXES, None),
            P(ALL_AXES, None),
            P(None, ALL_AXES),
            P(ALL_AXES, None),
            P(ALL_AXES),
            P(ALL_AXES, None),
            P(None, ALL_AXES),
            P(None, ALL_AXES),
            P(ALL_AXES, None),
        ),
        check_vma=False,
    )
```

```python
import functools
import math

import jax
import jax.numpy as jnp
from jax import lax
from jax.experimental import pallas as pl
from jax.sharding import PartitionSpec as P

ALL_AXES = ("grp", "sub", "expert")
SEQ_AXES = ("grp", "sub")
GROUP_AXES = ("sub", "expert")
KV_HEADS = 16
HEAD = 128
EXPERTS = 8
TOPK = 2
PIECES = 8
BLOCK = 256


epsilon = 1e-06
masked_score = -1e30


def _scores(q, k, qb, scale):
    s = lax.dot_general(q, k, (((1,), (1,)), ((), ())), preferred_element_type=jnp.float32) * scale
    kblock = lax.broadcasted_iota(jnp.int32, s.shape, 1) // BLOCK
    return jnp.where(kblock <= qb, s, masked_score)

def _fwd_kernel(scale, q_ref, k_ref, v_ref, qb_ref, o_ref, lse_ref):
    s = _scores(q_ref[...], k_ref[...], qb_ref[...], scale)
    largest = jnp.max(s, axis=-1, keepdims=True)
    weights = jnp.exp(s - largest)
    totals = jnp.sum(weights, axis=-1, keepdims=True)
    probs = weights / totals
    o_ref[...] = jnp.dot(probs.astype(jnp.bfloat16), v_ref[...],
                         preferred_element_type=jnp.float32).astype(o_ref.dtype)
    lse_ref[...] = largest + jnp.log(totals)

def _bwd_kernel(scale, q_ref, k_ref, v_ref, qb_ref, lse_ref, do_ref, dq_ref, dk_ref, dv_ref):
    q = q_ref[...]; k = k_ref[...]; v = v_ref[...]; do = do_ref[...]
    probs = jnp.exp(_scores(q, k, qb_ref[...], scale) - lse_ref[...])
    dp = lax.dot_general(do, v, (((1,), (1,)), ((), ())), preferred_element_type=jnp.float32)
    inner = jnp.sum(probs * dp, axis=-1, keepdims=True)
    ds = (probs * (dp - inner)).astype(jnp.bfloat16)
    dv_ref[...] = lax.dot_general(probs.astype(jnp.bfloat16), do, (((0,), (0,)), ((), ())),
                                  preferred_element_type=jnp.float32)
    dk_ref[...] = lax.dot_general(ds, q, (((0,), (0,)), ((), ())),
                                  preferred_element_type=jnp.float32) * scale
    dq_ref[...] = jnp.dot(ds, k, preferred_element_type=jnp.float32) * scale

def attn_fwd(q, k, v, qb):
    n, rows, d = q.shape; keys = k.shape[1]
    scale = 1.0 / math.sqrt(d)
    rspec = pl.BlockSpec((None, rows, d), lambda i: (i, 0, 0))
    kspec = pl.BlockSpec((None, keys, d), lambda i: (i, 0, 0))
    cspec = pl.BlockSpec((None, rows, 1), lambda i: (i, 0, 0))
    return pl.pallas_call(
        functools.partial(_fwd_kernel, scale),
        grid=(n,),
        in_specs=[rspec, kspec, kspec, cspec],
        out_specs=[rspec, cspec],
        out_shape=[jax.ShapeDtypeStruct((n, rows, d), jnp.bfloat16),
                   jax.ShapeDtypeStruct((n, rows, 1), jnp.float32)],
        cost_estimate=pl.CostEstimate(flops=4 * n * rows * keys * d,
                                      transcendentals=n * rows * keys,
                                      bytes_accessed=2 * n * (2 * rows * d + 2 * keys * d)),
    )(q, k, v, qb)

def attn_bwd(q, k, v, qb, lse, do):
    n, rows, d = q.shape; keys = k.shape[1]
    scale = 1.0 / math.sqrt(d)
    rspec = pl.BlockSpec((None, rows, d), lambda i: (i, 0, 0))
    kspec = pl.BlockSpec((None, keys, d), lambda i: (i, 0, 0))
    cspec = pl.BlockSpec((None, rows, 1), lambda i: (i, 0, 0))
    return pl.pallas_call(
        functools.partial(_bwd_kernel, scale),
        grid=(n,),
        in_specs=[rspec, kspec, kspec, cspec, cspec, rspec],
        out_specs=[rspec, kspec, kspec],
        out_shape=[jax.ShapeDtypeStruct((n, rows, d), jnp.float32),
                   jax.ShapeDtypeStruct((n, keys, d), jnp.float32),
                   jax.ShapeDtypeStruct((n, keys, d), jnp.float32)],
        cost_estimate=pl.CostEstimate(flops=10 * n * rows * keys * d,
                                      transcendentals=n * rows * keys,
                                      bytes_accessed=2 * n * (3 * rows * d + 2 * keys * d) + 8 * n * (rows * d + 2 * keys * d)),
    )(q, k, v, qb, lse, do)


def rope_tables(positions, head_size):
    half_size = head_size // 2
    frequency = jnp.exp(
        jnp.arange(half_size, dtype=jnp.float32) * (-2.0 * math.log(10000.0) / head_size)
    )
    angles = positions.astype(jnp.float32)[:, None] * frequency[None, :]
    return (jnp.cos(angles)[:, None, :], jnp.sin(angles)[:, None, :])


def rotate(values, cosines, sines):
    half_size = values.shape[-1] // 2
    first = values[..., :half_size]
    second = values[..., half_size:]
    return jnp.concatenate(
        [first * cosines - second * sines, second * cosines + first * sines], axis=-1
    )


def rotate_back(grads, cosines, sines):
    half_size = grads.shape[-1] // 2
    first = grads[..., :half_size]
    second = grads[..., half_size:]
    return jnp.concatenate(
        [first * cosines + second * sines, second * cosines - first * sines], axis=-1
    )


def slot_table(expert_ids, ranks, slot_cap):
    block_rows = expert_ids.shape[0]
    expert_range = jnp.arange(EXPERTS, dtype=jnp.int32)
    member = jnp.sum(
        (expert_ids[:, :, None] == expert_range[None, None, :]).astype(jnp.int32), axis=1
    )
    earlier = (ranks[:, None] < ranks[None, :]).astype(jnp.int32)
    places = jnp.sum(earlier[:, :, None] * member[:, None, :], axis=0)
    kept = member * (places < slot_cap).astype(jnp.int32)
    slot_range = jnp.arange(slot_cap, dtype=jnp.int32)
    landing = kept[:, :, None] * (places[:, :, None] == slot_range[None, None, :]).astype(jnp.int32)
    row_range = jnp.arange(block_rows, dtype=jnp.int32)
    slot_token = jnp.sum(landing * row_range[:, None, None], axis=0)
    slot_valid = jnp.sum(landing, axis=0)
    return (places, kept, slot_token, slot_valid)


def pair_index(expert_ids, places, kept, slot_cap):
    chosen_place = jnp.take_along_axis(places, expert_ids, axis=1)
    chosen_kept = jnp.take_along_axis(kept, expert_ids, axis=1)
    return (
        expert_ids * slot_cap + jnp.minimum(chosen_place, slot_cap - 1),
        chosen_kept.astype(jnp.float32),
    )


def pair_gates(logits, expert_ids):
    return jax.nn.softmax(jnp.take_along_axis(logits, expert_ids, axis=1), axis=-1)


def expert_onehot(expert_ids):
    expert_range = jnp.arange(EXPERTS, dtype=jnp.int32)
    return (expert_ids[:, :, None] == expert_range[None, None, :]).astype(jnp.float32)


def gates_back(gates, gate_grads, expert_ids):
    inner = jnp.sum(gates * gate_grads, axis=1, keepdims=True)
    chosen_grads = gates * (gate_grads - inner)
    return jnp.sum(chosen_grads[:, :, None] * expert_onehot(expert_ids), axis=1)


def slot_gates(gates, pair_kept, expert_ids, slot_token, slot_valid):
    per_expert = jnp.sum((gates * pair_kept)[:, :, None] * expert_onehot(expert_ids), axis=1)
    return jnp.take_along_axis(per_expert.T, slot_token, axis=1) * slot_valid.astype(jnp.float32)


def pick_slots(values, slot_token, slot_valid):
    return jnp.where(slot_valid[:, :, None] > 0, values[slot_token], jnp.zeros((), values.dtype))


def fan_out(slot_values, group_size):
    experts_here, slot_cap, width = slot_values.shape
    spread_out = jnp.broadcast_to(slot_values[:, None], (experts_here, group_size, slot_cap, width))
    return spread_out.reshape(experts_here * group_size, slot_cap, width)


def fold_group(received, group_size):
    count, slot_cap, width = received.shape
    return jnp.sum(received.reshape(count // group_size, group_size, slot_cap, width), axis=1)


def norm_back(normed_grad, gain, normed, inverse):
    scaled = normed_grad * gain
    gain_grad = jnp.sum(normed_grad * normed, axis=0)
    input_grad = inverse * (scaled - normed * jnp.mean(scaled * normed, axis=-1, keepdims=True))
    return (input_grad, gain_grad)


def shards(
    tokens,
    attn_gain,
    kv_weight,
    attn_router,
    query_weight,
    output_weight,
    mlp_gain,
    mlp_router,
    gate_weight,
    up_weight,
    down_weight,
    attn_experts,
    mlp_experts,
    priority,
    cotangent,
):
    devices = lax.axis_size(ALL_AXES)
    halves = lax.axis_size("expert")
    device_index = lax.axis_index(ALL_AXES)
    half_index = lax.axis_index("expert")
    seq_tokens, width = tokens.shape
    own_rows = seq_tokens // halves
    group_size = devices // EXPERTS
    head_cols = query_weight.shape[1]
    local_heads = head_cols // HEAD
    key_cols = KV_HEADS * HEAD
    all_tokens = own_rows * devices
    seq_length = seq_tokens * PIECES
    sequences = all_tokens // seq_length
    slot_cap = (9 * TOPK * own_rows + 8 * EXPERTS - 1) // (8 * EXPERTS)
    slot_rows = devices * slot_cap
    seq_rows = slot_rows // sequences
    my_expert = device_index // group_size
    groups = lax.axis_size("grp")

    def dispatch(slot_values):
        by_group = lax.all_to_all(slot_values, "grp", split_axis=0, concat_axis=0, tiled=True)
        return lax.all_gather(
            by_group.reshape(groups * slot_cap, width), GROUP_AXES, axis=0, tiled=True
        )

    def combine(partial_value):
        parts = lax.all_to_all(
            partial_value.astype(jnp.bfloat16).reshape(group_size, groups * slot_cap, width),
            GROUP_AXES,
            split_axis=0,
            concat_axis=0,
            tiled=True,
        )
        summed = jnp.sum(parts.astype(jnp.float32), axis=0).reshape(groups, slot_cap, width)
        return lax.all_to_all(
            summed.astype(jnp.bfloat16), "grp", split_axis=0, concat_axis=0, tiled=True
        ).astype(jnp.float32)

    def combine_scattered(partial_value):
        summed = lax.psum_scatter(
            partial_value.astype(jnp.bfloat16), GROUP_AXES, scatter_dimension=0, tiled=True
        )
        return lax.all_to_all(
            summed.reshape(groups, slot_cap, width), "grp", split_axis=0, concat_axis=0, tiled=True
        ).astype(jnp.float32)

    def to_rows(per_head):
        parts = lax.all_to_all(
            per_head.reshape(group_size, groups * slot_cap, head_cols),
            GROUP_AXES,
            split_axis=0,
            concat_axis=0,
            tiled=True,
        )
        return jnp.swapaxes(parts, 0, 1).reshape(groups * slot_cap, group_size * head_cols)

    def to_owners(row_values):
        return lax.all_to_all(
            row_values.astype(jnp.bfloat16).reshape(groups, slot_cap, width),
            "grp",
            split_axis=0,
            concat_axis=0,
            tiled=True,
        ).astype(jnp.float32)

    def to_gj(rows):
        shaped = rows.reshape((group_size, groups, slot_cap) + rows.shape[1:])
        return jnp.swapaxes(shaped, 0, 1).reshape(rows.shape)

    def to_jg(rows):
        shaped = rows.reshape((groups, group_size, slot_cap) + rows.shape[1:])
        return jnp.swapaxes(shaped, 0, 1).reshape(rows.shape)
    scale = 1.0 / math.sqrt(HEAD)

    start_row = half_index * own_rows
    own_input = lax.dynamic_slice_in_dim(tokens, start_row, own_rows, 0).astype(jnp.float32)
    own_cotangent = lax.dynamic_slice_in_dim(cotangent, start_row, own_rows, 0).astype(jnp.float32)
    own_attn = lax.dynamic_slice_in_dim(attn_experts, start_row, own_rows, 0)
    own_mlp = lax.dynamic_slice_in_dim(mlp_experts, start_row, own_rows, 0)
    own_rank = lax.dynamic_slice_in_dim(priority[0], start_row, own_rows, 0)
    token_order = jnp.arange(own_rows, dtype=jnp.int32)

    kv_rows, kv_width = kv_weight.shape
    id_cols = own_rows * TOPK // kv_rows
    extras = jnp.concatenate(
        [
            attn_gain[:, None],
            mlp_gain[:, None],
            attn_router,
            mlp_router,
            own_attn.reshape(kv_rows, id_cols).astype(jnp.bfloat16),
        ],
        axis=1,
    )
    extra_cols = extras.shape[1]
    extra_pad = -(-extra_cols // 128) * 128
    pair_cols = 2 * head_cols
    head_blocks = jnp.transpose(
        kv_weight.reshape(kv_rows, 2, group_size, head_cols), (2, 0, 1, 3)
    ).reshape(group_size, kv_rows, pair_cols)
    padded_extras = jnp.pad(extras, ((0, 0), (0, extra_pad - extra_cols)))
    dealt_rows = lax.all_to_all(
        jnp.concatenate(
            [
                head_blocks,
                jnp.broadcast_to(padded_extras[None], (group_size, kv_rows, extra_pad)),
            ],
            axis=2,
        ),
        GROUP_AXES,
        split_axis=0,
        concat_axis=0,
        tiled=True,
    )
    gathered = lax.all_to_all(
        jnp.broadcast_to(
            dealt_rows.reshape(1, group_size * kv_rows, pair_cols + extra_pad),
            (groups, group_size * kv_rows, pair_cols + extra_pad),
        ),
        "grp",
        split_axis=0,
        concat_axis=0,
        tiled=True,
    ).reshape(devices * kv_rows, pair_cols + extra_pad)
    head_kv = gathered[:, :pair_cols]
    gain_one = gathered[:, pair_cols]
    gain_two = gathered[:, pair_cols + 1]
    router_one = gathered[:, pair_cols + 2 : pair_cols + 2 + EXPERTS]
    router_two = gathered[:, pair_cols + 2 + EXPERTS : pair_cols + 2 + 2 * EXPERTS]
    routes_all = gathered[:, pair_cols + 2 + 2 * EXPERTS : pair_cols + extra_cols].astype(jnp.int32)
    inverse_one = lax.rsqrt(jnp.mean(own_input * own_input, axis=-1, keepdims=True) + epsilon)
    normed_one = own_input * inverse_one
    attn_input = (normed_one * gain_one.astype(jnp.float32)).astype(jnp.bfloat16)
    attn_logits = jnp.dot(attn_input, router_one, preferred_element_type=jnp.float32)
    seq_input = lax.all_gather(attn_input, GROUP_AXES, axis=0, tiled=True)
    seq_kv = jnp.dot(seq_input, head_kv, preferred_element_type=jnp.float32)
    seq_cos, seq_sin = rope_tables(jnp.arange(seq_length, dtype=jnp.int32), HEAD)
    seq_pair = jnp.concatenate(
        [
            rotate(seq_kv[:, :head_cols].reshape(seq_length, local_heads, HEAD), seq_cos, seq_sin)
            .reshape(seq_length, head_cols)
            .astype(jnp.bfloat16),
            seq_kv[:, head_cols:].astype(jnp.bfloat16),
        ],
        axis=1,
    )
    all_pairs = lax.all_to_all(
        jnp.broadcast_to(seq_pair[None], (groups,) + seq_pair.shape),
        "grp",
        split_axis=0,
        concat_axis=0,
        tiled=True,
    ).reshape(groups * seq_length, 2 * head_cols)
    seq_keys = all_pairs[:, :head_cols].reshape(sequences, seq_length, local_heads, HEAD)
    seq_values = all_pairs[:, head_cols:].reshape(sequences, seq_length, local_heads, HEAD)
    attn_places, attn_kept, attn_token, attn_valid = slot_table(own_attn, token_order, slot_cap)
    mlp_places, mlp_kept, mlp_token, mlp_valid = slot_table(own_mlp, own_rank, slot_cap)
    block_routes = routes_all.reshape(devices, own_rows, TOPK)
    dest_tables = jax.vmap(lambda block_ids: slot_table(block_ids, token_order, slot_cap)[2])(
        block_routes
    )
    dest_token = jnp.take(dest_tables, my_expert, axis=1)
    attn_rows = dispatch(pick_slots(attn_input, attn_token, attn_valid))
    queries = to_gj(jnp.dot(attn_rows, query_weight, preferred_element_type=jnp.float32))
    slot_positions = (
        (jnp.arange(devices, dtype=jnp.int32)[:, None] * own_rows + dest_token) % seq_length
    ).reshape(slot_rows)
    slot_cos, slot_sin = rope_tables(slot_positions, HEAD)
    rotated = rotate(queries.reshape(slot_rows, local_heads, HEAD), slot_cos, slot_sin).astype(
        jnp.bfloat16
    )
    seq_queries = rotated.reshape(sequences, seq_rows, local_heads, HEAD)
    query_blocks = (slot_positions // BLOCK).reshape(sequences, seq_rows)
    key_blocks = jnp.arange(seq_length, dtype=jnp.int32) // BLOCK

    attn_mixed, log_totals = attn_fwd(
        seq_queries.reshape(sequences, seq_rows, HEAD),
        seq_keys.reshape(sequences, seq_length, HEAD),
        seq_values.reshape(sequences, seq_length, HEAD),
        query_blocks[:, :, None],
    )
    mixed_rows = to_jg(attn_mixed.reshape(slot_rows, head_cols))
    output_stack = lax.all_gather(output_weight, GROUP_AXES, axis=0, tiled=True)
    attn_slots = to_owners(
        jnp.dot(to_rows(mixed_rows), output_stack, preferred_element_type=jnp.float32)
    )
    attn_gates = pair_gates(attn_logits, own_attn)
    attn_index, attn_pair_kept = pair_index(own_attn, attn_places, attn_kept, slot_cap)
    attn_picked = attn_slots.reshape(EXPERTS * slot_cap, width)[attn_index]
    hidden_state = own_input + jnp.sum(
        attn_picked * (attn_gates * attn_pair_kept)[:, :, None], axis=1
    )
    inverse_two = lax.rsqrt(jnp.mean(hidden_state * hidden_state, axis=-1, keepdims=True) + epsilon)
    normed_two = hidden_state * inverse_two
    mlp_input = (normed_two * gain_two.astype(jnp.float32)).astype(jnp.bfloat16)
    mlp_logits = jnp.dot(mlp_input, router_two, preferred_element_type=jnp.float32)
    mlp_gates = pair_gates(mlp_logits, own_mlp)
    mlp_index, mlp_pair_kept = pair_index(own_mlp, mlp_places, mlp_kept, slot_cap)
    mlp_slot_grad = (
        own_cotangent[mlp_token]
        * slot_gates(mlp_gates, mlp_pair_kept, own_mlp, mlp_token, mlp_valid)[:, :, None]
    ).astype(jnp.bfloat16)
    mlp_by_group = lax.all_to_all(
        jnp.concatenate([pick_slots(mlp_input, mlp_token, mlp_valid), mlp_slot_grad], axis=1),
        "grp",
        split_axis=0,
        concat_axis=0,
        tiled=True,
    )
    mlp_rows = lax.all_gather(
        mlp_by_group[:, :slot_cap].reshape(groups * slot_cap, width),
        GROUP_AXES,
        axis=0,
        tiled=True,
    )
    down_rows = lax.all_gather(
        mlp_by_group[:, slot_cap:].reshape(groups * slot_cap, width),
        GROUP_AXES,
        axis=0,
        tiled=True,
    )
    gate_pre = jnp.dot(mlp_rows, gate_weight, preferred_element_type=jnp.float32)
    up_pre = jnp.dot(mlp_rows, up_weight, preferred_element_type=jnp.float32)
    activated = jax.nn.silu(gate_pre)
    inner_rows = (activated * up_pre).astype(jnp.bfloat16)
    mlp_partial = jnp.dot(inner_rows, down_weight, preferred_element_type=jnp.float32)
    mlp_slots = combine_scattered(mlp_partial)
    query_stack = lax.all_gather(query_weight, GROUP_AXES, axis=1, tiled=True)
    mlp_slots, query_stack = lax.optimization_barrier((mlp_slots, query_stack))
    mlp_picked = mlp_slots.reshape(EXPERTS * slot_cap, width)[mlp_index]
    own_output = hidden_state + jnp.sum(
        mlp_picked * (mlp_gates * mlp_pair_kept)[:, :, None], axis=1
    )
    mlp_gate_grad = jnp.sum(mlp_picked * own_cotangent[:, None, :], axis=-1) * mlp_pair_kept
    mlp_logit_grad = gates_back(mlp_gates, mlp_gate_grad, own_mlp)
    inner_grad = jnp.einsum("rd,fd->rf", down_rows, down_weight, preferred_element_type=jnp.float32)
    down_grad = jnp.einsum("rf,rd->fd", inner_rows, down_rows, preferred_element_type=jnp.float32)
    sigmoid_gate = jax.nn.sigmoid(gate_pre)
    gate_pre_grad = (
        inner_grad * up_pre * sigmoid_gate * (1.0 + gate_pre * (1.0 - sigmoid_gate))
    ).astype(jnp.bfloat16)
    up_pre_grad = (inner_grad * activated).astype(jnp.bfloat16)
    gate_grad = jnp.einsum("rd,rf->df", mlp_rows, gate_pre_grad, preferred_element_type=jnp.float32)
    up_grad = jnp.einsum("rd,rf->df", mlp_rows, up_pre_grad, preferred_element_type=jnp.float32)
    row_grad = jnp.einsum(
        "rf,df->rd", gate_pre_grad, gate_weight, preferred_element_type=jnp.float32
    ) + jnp.einsum("rf,df->rd", up_pre_grad, up_weight, preferred_element_type=jnp.float32)
    mlp_row_grad = combine(row_grad)
    mlp_input_grad = jnp.sum(
        mlp_row_grad.reshape(EXPERTS * slot_cap, width)[mlp_index] * mlp_pair_kept[:, :, None],
        axis=1,
    )
    mlp_input_grad = mlp_input_grad + jnp.dot(
        mlp_logit_grad, router_two.astype(jnp.float32).T, precision=lax.Precision.HIGHEST
    )
    mlp_router_own = jnp.dot(
        mlp_input.astype(jnp.float32).T, mlp_logit_grad, precision=lax.Precision.HIGHEST
    )
    hidden_grad, gain_two_own = norm_back(
        mlp_input_grad, gain_two.astype(jnp.float32), normed_two, inverse_two
    )
    hidden_grad = hidden_grad + own_cotangent
    attn_gate_grad = jnp.sum(attn_picked * hidden_grad[:, None, :], axis=-1) * attn_pair_kept
    attn_logit_grad = gates_back(attn_gates, attn_gate_grad, own_attn)
    attn_slot_grad = (
        hidden_grad[attn_token]
        * slot_gates(attn_gates, attn_pair_kept, own_attn, attn_token, attn_valid)[:, :, None]
    ).astype(jnp.bfloat16)
    out_rows = dispatch(attn_slot_grad)
    output_grad = jnp.einsum("rw,rd->wd", mixed_rows, out_rows, preferred_element_type=jnp.float32)
    mixed_grad = jnp.einsum(
        "rd,wd->rw", out_rows, output_weight, preferred_element_type=jnp.float32
    ).astype(jnp.bfloat16)
    seq_mixed_grad = to_gj(mixed_grad).reshape(sequences, seq_rows, local_heads, HEAD)

    seq_query_grad, seq_key_grad, seq_value_grad = attn_bwd(
        seq_queries.reshape(sequences, seq_rows, HEAD),
        seq_keys.reshape(sequences, seq_length, HEAD),
        seq_values.reshape(sequences, seq_length, HEAD),
        query_blocks[:, :, None],
        log_totals,
        seq_mixed_grad.reshape(sequences, seq_rows, HEAD),
    )
    query_rot_grad = to_jg(
        rotate_back(seq_query_grad.reshape(slot_rows, local_heads, HEAD), slot_cos, slot_sin)
        .reshape(slot_rows, head_cols)
        .astype(jnp.bfloat16)
    )
    query_grad = jnp.einsum(
        "rd,rw->dw", attn_rows, query_rot_grad, preferred_element_type=jnp.float32
    )
    attn_row_grad = to_owners(
        jnp.einsum(
            "rw,dw->rd", to_rows(query_rot_grad), query_stack, preferred_element_type=jnp.float32
        )
    )
    pair_back = lax.all_to_all(
        jnp.concatenate([seq_key_grad, seq_value_grad], axis=2).astype(jnp.bfloat16),
        "grp",
        split_axis=0,
        concat_axis=0,
        tiled=True,
    )
    seq_pair_grad = jnp.sum(pair_back.astype(jnp.float32), axis=0)
    kv_col_grad = jnp.concatenate(
        [
            rotate_back(
                seq_pair_grad[:, :head_cols].reshape(seq_length, local_heads, HEAD),
                seq_cos,
                seq_sin,
            ).reshape(seq_length, head_cols),
            seq_pair_grad[:, head_cols:],
        ],
        axis=1,
    ).astype(jnp.bfloat16)
    kv_col_weight = jnp.einsum(
        "rd,rc->dc", seq_input, kv_col_grad, preferred_element_type=jnp.float32
    )
    kv_input_parts = lax.all_to_all(
        jnp.einsum("rc,dc->rd", kv_col_grad, head_kv, preferred_element_type=jnp.float32)
        .astype(jnp.bfloat16)
        .reshape(group_size, own_rows, width),
        GROUP_AXES,
        split_axis=0,
        concat_axis=0,
        tiled=True,
    )
    attn_input_grad = jnp.sum(
        attn_row_grad.reshape(EXPERTS * slot_cap, width)[attn_index] * attn_pair_kept[:, :, None],
        axis=1,
    )
    attn_input_grad = attn_input_grad + jnp.sum(kv_input_parts.astype(jnp.float32), axis=0)
    attn_input_grad = attn_input_grad + jnp.dot(
        attn_logit_grad, router_one.astype(jnp.float32).T, precision=lax.Precision.HIGHEST
    )
    attn_router_own = jnp.dot(
        attn_input.astype(jnp.float32).T, attn_logit_grad, precision=lax.Precision.HIGHEST
    )
    input_grad, gain_one_own = norm_back(
        attn_input_grad, gain_one.astype(jnp.float32), normed_one, inverse_one
    )
    input_grad = input_grad + hidden_grad
    grad_extras = jnp.concatenate(
        [gain_one_own[:, None], gain_two_own[:, None], attn_router_own, mlp_router_own], axis=1
    )
    packed_grad = jnp.concatenate(
        [
            kv_col_weight,
            jnp.pad(grad_extras, ((0, 0), (0, extra_pad - grad_extras.shape[1]))),
        ],
        axis=1,
    )
    group_sum = lax.psum_scatter(packed_grad, "grp", scatter_dimension=0, tiled=True)
    dealt = lax.all_to_all(
        group_sum.reshape(group_size, kv_rows, pair_cols + extra_pad),
        GROUP_AXES,
        split_axis=0,
        concat_axis=0,
        tiled=True,
    )
    kv_grad = jnp.transpose(
        dealt[:, :, :pair_cols].reshape(group_size, kv_rows, 2, head_cols), (1, 2, 0, 3)
    ).reshape(kv_rows, kv_width)
    extra_grad = jnp.sum(dealt[:, :, pair_cols:], axis=0)
    gain_one_grad = extra_grad[:, 0]
    gain_two_grad = extra_grad[:, 1]
    attn_router_grad = extra_grad[:, 2 : 2 + EXPERTS]
    mlp_router_grad = extra_grad[:, 2 + EXPERTS : 2 + 2 * EXPERTS]
    both_own = jnp.concatenate(
        [own_output.astype(jnp.bfloat16), input_grad.astype(jnp.bfloat16)], axis=1
    )
    both_full = lax.all_to_all(
        jnp.broadcast_to(both_own[None], (halves,) + both_own.shape),
        "expert",
        split_axis=0,
        concat_axis=0,
        tiled=True,
    ).reshape(halves * own_rows, 2 * width)
    mixed_full, input_full = both_full[:, :width], both_full[:, width:]
    return (
        mixed_full,
        input_full,
        gain_one_grad,
        kv_grad,
        attn_router_grad,
        query_grad,
        output_grad,
        gain_two_grad,
        mlp_router_grad,
        gate_grad,
        up_grad,
        down_grad,
    )


def solution(mesh):
    seq_size, halves = mesh.devices.shape
    grouped = jax.sharding.Mesh(
        mesh.devices.reshape(EXPERTS, seq_size // EXPERTS, halves), ALL_AXES
    )
    return jax.shard_map(
        shards,
        mesh=grouped,
        in_specs=(
            P(SEQ_AXES, None),
            P(ALL_AXES),
            P(ALL_AXES, None),
            P(ALL_AXES, None),
            P(None, ALL_AXES),
            P(ALL_AXES, None),
            P(ALL_AXES),
            P(ALL_AXES, None),
            P(None, ALL_AXES),
            P(None, ALL_AXES),
            P(ALL_AXES, None),
            P(SEQ_AXES, None),
            P(SEQ_AXES, None),
            P(SEQ_AXES, None),
            P(SEQ_AXES, None),
        ),
        out_specs=(
            P(SEQ_AXES, None),
            P(SEQ_AXES, None),
            P(ALL_AXES),
            P(ALL_AXES, None),
            P(ALL_AXES, None),
            P(None, ALL_AXES),
            P(ALL_AXES, None),
            P(ALL_AXES),
            P(ALL_AXES, None),
            P(None, ALL_AXES),
            P(None, ALL_AXES),
            P(ALL_AXES, None),
        ),
        check_vma=False,
    )
```

```python
import functools
import math

import jax
import jax.numpy as jnp
from jax import lax
from jax.experimental import pallas as pl
from jax.sharding import PartitionSpec as P

ALL_AXES = ("grp", "sub", "expert")
SEQ_AXES = ("grp", "sub")
GROUP_AXES = ("sub", "expert")
KV_HEADS = 16
HEAD = 128
EXPERTS = 8
TOPK = 2
PIECES = 8
BLOCK = 256


epsilon = 1e-06
masked_score = -1e30


def _scores(q, k, qb, scale):
    s = lax.dot_general(q, k, (((1,), (1,)), ((), ())), preferred_element_type=jnp.float32) * scale
    kblock = lax.broadcasted_iota(jnp.int32, s.shape, 1) // BLOCK
    return jnp.where(kblock <= qb, s, masked_score)

def _fwd_kernel(scale, q_ref, k_ref, v_ref, qb_ref, o_ref, lse_ref):
    s = _scores(q_ref[...], k_ref[...], qb_ref[...], scale)
    largest = jnp.max(s, axis=-1, keepdims=True)
    weights = jnp.exp(s - largest)
    totals = jnp.sum(weights, axis=-1, keepdims=True)
    probs = weights / totals
    o_ref[...] = jnp.dot(probs.astype(jnp.bfloat16), v_ref[...],
                         preferred_element_type=jnp.float32).astype(o_ref.dtype)
    lse_ref[...] = largest + jnp.log(totals)

def _bwd_kernel(scale, q_ref, k_ref, v_ref, qb_ref, lse_ref, do_ref, dq_ref, dkv_ref):
    q = q_ref[...]; k = k_ref[...]; v = v_ref[...]; do = do_ref[...]
    probs = jnp.exp(_scores(q, k, qb_ref[...], scale) - lse_ref[...])
    dp = lax.dot_general(do, v, (((1,), (1,)), ((), ())), preferred_element_type=jnp.float32)
    inner = jnp.sum(probs * dp, axis=-1, keepdims=True)
    ds = (probs * (dp - inner)).astype(jnp.bfloat16)
    d = q.shape[1]
    dkv_ref[:, d:] = lax.dot_general(probs.astype(jnp.bfloat16), do, (((0,), (0,)), ((), ())),
                                     preferred_element_type=jnp.float32).astype(dkv_ref.dtype)
    dkv_ref[:, :d] = (lax.dot_general(ds, q, (((0,), (0,)), ((), ())),
                                      preferred_element_type=jnp.float32) * scale).astype(dkv_ref.dtype)
    dq_ref[...] = jnp.dot(ds, k, preferred_element_type=jnp.float32) * scale

def attn_fwd(q, k, v, qb):
    n, rows, d = q.shape; keys = k.shape[1]
    scale = 1.0 / math.sqrt(d)
    rspec = pl.BlockSpec((None, rows, d), lambda i: (i, 0, 0))
    kspec = pl.BlockSpec((None, keys, d), lambda i: (i, 0, 0))
    cspec = pl.BlockSpec((None, rows, 1), lambda i: (i, 0, 0))
    return pl.pallas_call(
        functools.partial(_fwd_kernel, scale),
        grid=(n,),
        in_specs=[rspec, kspec, kspec, cspec],
        out_specs=[rspec, cspec],
        out_shape=[jax.ShapeDtypeStruct((n, rows, d), jnp.bfloat16),
                   jax.ShapeDtypeStruct((n, rows, 1), jnp.float32)],
        cost_estimate=pl.CostEstimate(flops=4 * n * rows * keys * d,
                                      transcendentals=n * rows * keys,
                                      bytes_accessed=2 * n * (2 * rows * d + 2 * keys * d)),
    )(q, k, v, qb)

def attn_bwd(q, k, v, qb, lse, do):
    n, rows, d = q.shape; keys = k.shape[1]
    scale = 1.0 / math.sqrt(d)
    rspec = pl.BlockSpec((None, rows, d), lambda i: (i, 0, 0))
    kspec = pl.BlockSpec((None, keys, d), lambda i: (i, 0, 0))
    cspec = pl.BlockSpec((None, rows, 1), lambda i: (i, 0, 0))
    return pl.pallas_call(
        functools.partial(_bwd_kernel, scale),
        grid=(n,),
        in_specs=[rspec, kspec, kspec, cspec, cspec, rspec],
        out_specs=[rspec, pl.BlockSpec((None, keys, 2 * d), lambda i: (i, 0, 0))],
        out_shape=[jax.ShapeDtypeStruct((n, rows, d), jnp.float32),
                   jax.ShapeDtypeStruct((n, keys, 2 * d), jnp.bfloat16)],
        cost_estimate=pl.CostEstimate(flops=10 * n * rows * keys * d,
                                      transcendentals=n * rows * keys,
                                      bytes_accessed=2 * n * (3 * rows * d + 2 * keys * d) + 8 * n * (rows * d + 2 * keys * d)),
    )(q, k, v, qb, lse, do)


def rope_tables(positions, head_size):
    half_size = head_size // 2
    frequency = jnp.exp(
        jnp.arange(half_size, dtype=jnp.float32) * (-2.0 * math.log(10000.0) / head_size)
    )
    angles = positions.astype(jnp.float32)[:, None] * frequency[None, :]
    return (jnp.cos(angles)[:, None, :], jnp.sin(angles)[:, None, :])


def rotate(values, cosines, sines):
    half_size = values.shape[-1] // 2
    first = values[..., :half_size]
    second = values[..., half_size:]
    return jnp.concatenate(
        [first * cosines - second * sines, second * cosines + first * sines], axis=-1
    )


def rotate_back(grads, cosines, sines):
    half_size = grads.shape[-1] // 2
    first = grads[..., :half_size]
    second = grads[..., half_size:]
    return jnp.concatenate(
        [first * cosines + second * sines, second * cosines - first * sines], axis=-1
    )


def slot_table(expert_ids, ranks, slot_cap):
    block_rows = expert_ids.shape[0]
    expert_range = jnp.arange(EXPERTS, dtype=jnp.int32)
    member = jnp.sum(
        (expert_ids[:, :, None] == expert_range[None, None, :]).astype(jnp.int32), axis=1
    )
    earlier = (ranks[:, None] < ranks[None, :]).astype(jnp.int32)
    places = jnp.sum(earlier[:, :, None] * member[:, None, :], axis=0)
    kept = member * (places < slot_cap).astype(jnp.int32)
    slot_range = jnp.arange(slot_cap, dtype=jnp.int32)
    landing = kept[:, :, None] * (places[:, :, None] == slot_range[None, None, :]).astype(jnp.int32)
    row_range = jnp.arange(block_rows, dtype=jnp.int32)
    slot_token = jnp.sum(landing * row_range[:, None, None], axis=0)
    slot_valid = jnp.sum(landing, axis=0)
    return (places, kept, slot_token, slot_valid)


def pair_index(expert_ids, places, kept, slot_cap):
    chosen_place = jnp.take_along_axis(places, expert_ids, axis=1)
    chosen_kept = jnp.take_along_axis(kept, expert_ids, axis=1)
    return (
        expert_ids * slot_cap + jnp.minimum(chosen_place, slot_cap - 1),
        chosen_kept.astype(jnp.float32),
    )


def pair_gates(logits, expert_ids):
    return jax.nn.softmax(jnp.take_along_axis(logits, expert_ids, axis=1), axis=-1)


def expert_onehot(expert_ids):
    expert_range = jnp.arange(EXPERTS, dtype=jnp.int32)
    return (expert_ids[:, :, None] == expert_range[None, None, :]).astype(jnp.float32)


def gates_back(gates, gate_grads, expert_ids):
    inner = jnp.sum(gates * gate_grads, axis=1, keepdims=True)
    chosen_grads = gates * (gate_grads - inner)
    return jnp.sum(chosen_grads[:, :, None] * expert_onehot(expert_ids), axis=1)


def slot_gates(gates, pair_kept, expert_ids, slot_token, slot_valid):
    per_expert = jnp.sum((gates * pair_kept)[:, :, None] * expert_onehot(expert_ids), axis=1)
    return jnp.take_along_axis(per_expert.T, slot_token, axis=1) * slot_valid.astype(jnp.float32)


def pick_slots(values, slot_token, slot_valid):
    return jnp.where(slot_valid[:, :, None] > 0, values[slot_token], jnp.zeros((), values.dtype))


def fan_out(slot_values, group_size):
    experts_here, slot_cap, width = slot_values.shape
    spread_out = jnp.broadcast_to(slot_values[:, None], (experts_here, group_size, slot_cap, width))
    return spread_out.reshape(experts_here * group_size, slot_cap, width)


def fold_group(received, group_size):
    count, slot_cap, width = received.shape
    return jnp.sum(received.reshape(count // group_size, group_size, slot_cap, width), axis=1)


def norm_back(normed_grad, gain, normed, inverse):
    scaled = normed_grad * gain
    gain_grad = jnp.sum(normed_grad * normed, axis=0)
    input_grad = inverse * (scaled - normed * jnp.mean(scaled * normed, axis=-1, keepdims=True))
    return (input_grad, gain_grad)


def shards(
    tokens,
    attn_gain,
    kv_weight,
    attn_router,
    query_weight,
    output_weight,
    mlp_gain,
    mlp_router,
    gate_weight,
    up_weight,
    down_weight,
    attn_experts,
    mlp_experts,
    priority,
    cotangent,
):
    devices = lax.axis_size(ALL_AXES)
    halves = lax.axis_size("expert")
    device_index = lax.axis_index(ALL_AXES)
    half_index = lax.axis_index("expert")
    seq_tokens, width = tokens.shape
    own_rows = seq_tokens // halves
    group_size = devices // EXPERTS
    head_cols = query_weight.shape[1]
    local_heads = head_cols // HEAD
    key_cols = KV_HEADS * HEAD
    all_tokens = own_rows * devices
    seq_length = seq_tokens * PIECES
    sequences = all_tokens // seq_length
    slot_cap = (9 * TOPK * own_rows + 8 * EXPERTS - 1) // (8 * EXPERTS)
    slot_rows = devices * slot_cap
    seq_rows = slot_rows // sequences
    my_expert = device_index // group_size
    groups = lax.axis_size("grp")

    def dispatch(slot_values):
        by_group = lax.all_to_all(slot_values, "grp", split_axis=0, concat_axis=0, tiled=True)
        return lax.all_gather(
            by_group.reshape(groups * slot_cap, width), GROUP_AXES, axis=0, tiled=True
        )

    def combine(partial_value):
        parts = lax.all_to_all(
            partial_value.astype(jnp.bfloat16).reshape(group_size, groups * slot_cap, width),
            GROUP_AXES,
            split_axis=0,
            concat_axis=0,
            tiled=True,
        )
        summed = jnp.sum(parts.astype(jnp.float32), axis=0).reshape(groups, slot_cap, width)
        return lax.all_to_all(
            summed.astype(jnp.bfloat16), "grp", split_axis=0, concat_axis=0, tiled=True
        ).astype(jnp.float32)

    def combine_scattered(partial_value):
        summed = lax.psum_scatter(
            partial_value.astype(jnp.bfloat16), GROUP_AXES, scatter_dimension=0, tiled=True
        )
        return lax.all_to_all(
            summed.reshape(groups, slot_cap, width), "grp", split_axis=0, concat_axis=0, tiled=True
        ).astype(jnp.float32)

    def to_rows(per_head):
        parts = lax.all_to_all(
            per_head.reshape(group_size, groups * slot_cap, head_cols),
            GROUP_AXES,
            split_axis=0,
            concat_axis=0,
            tiled=True,
        )
        return jnp.swapaxes(parts, 0, 1).reshape(groups * slot_cap, group_size * head_cols)

    def to_owners(row_values):
        return lax.all_to_all(
            row_values.astype(jnp.bfloat16).reshape(groups, slot_cap, width),
            "grp",
            split_axis=0,
            concat_axis=0,
            tiled=True,
        ).astype(jnp.float32)

    def to_gj(rows):
        shaped = rows.reshape((group_size, groups, slot_cap) + rows.shape[1:])
        return jnp.swapaxes(shaped, 0, 1).reshape(rows.shape)

    def to_jg(rows):
        shaped = rows.reshape((groups, group_size, slot_cap) + rows.shape[1:])
        return jnp.swapaxes(shaped, 0, 1).reshape(rows.shape)
    scale = 1.0 / math.sqrt(HEAD)

    start_row = half_index * own_rows
    own_input = lax.dynamic_slice_in_dim(tokens, start_row, own_rows, 0).astype(jnp.float32)
    own_cotangent = lax.dynamic_slice_in_dim(cotangent, start_row, own_rows, 0).astype(jnp.float32)
    own_attn = lax.dynamic_slice_in_dim(attn_experts, start_row, own_rows, 0)
    own_mlp = lax.dynamic_slice_in_dim(mlp_experts, start_row, own_rows, 0)
    own_rank = lax.dynamic_slice_in_dim(priority[0], start_row, own_rows, 0)
    token_order = jnp.arange(own_rows, dtype=jnp.int32)

    kv_rows, kv_width = kv_weight.shape
    id_cols = own_rows * TOPK // kv_rows
    extras = jnp.concatenate(
        [
            attn_gain[:, None],
            mlp_gain[:, None],
            attn_router,
            mlp_router,
            own_attn.reshape(kv_rows, id_cols).astype(jnp.bfloat16),
        ],
        axis=1,
    )
    extra_cols = extras.shape[1]
    extra_pad = -(-extra_cols // 128) * 128
    pair_cols = 2 * head_cols
    head_blocks = jnp.transpose(
        kv_weight.reshape(kv_rows, 2, group_size, head_cols), (2, 0, 1, 3)
    ).reshape(group_size, kv_rows, pair_cols)
    padded_extras = jnp.pad(extras, ((0, 0), (0, extra_pad - extra_cols)))
    dealt_rows = lax.all_to_all(
        jnp.concatenate(
            [
                head_blocks,
                jnp.broadcast_to(padded_extras[None], (group_size, kv_rows, extra_pad)),
            ],
            axis=2,
        ),
        GROUP_AXES,
        split_axis=0,
        concat_axis=0,
        tiled=True,
    )
    gathered = lax.all_to_all(
        jnp.broadcast_to(
            dealt_rows.reshape(1, group_size * kv_rows, pair_cols + extra_pad),
            (groups, group_size * kv_rows, pair_cols + extra_pad),
        ),
        "grp",
        split_axis=0,
        concat_axis=0,
        tiled=True,
    ).reshape(devices * kv_rows, pair_cols + extra_pad)
    head_kv = gathered[:, :pair_cols]
    gain_one = gathered[:, pair_cols]
    gain_two = gathered[:, pair_cols + 1]
    router_one = gathered[:, pair_cols + 2 : pair_cols + 2 + EXPERTS]
    router_two = gathered[:, pair_cols + 2 + EXPERTS : pair_cols + 2 + 2 * EXPERTS]
    routes_all = gathered[:, pair_cols + 2 + 2 * EXPERTS : pair_cols + extra_cols].astype(jnp.int32)
    inverse_one = lax.rsqrt(jnp.mean(own_input * own_input, axis=-1, keepdims=True) + epsilon)
    normed_one = own_input * inverse_one
    attn_input = (normed_one * gain_one.astype(jnp.float32)).astype(jnp.bfloat16)
    attn_logits = jnp.dot(attn_input, router_one, preferred_element_type=jnp.float32)
    seq_input = lax.all_gather(attn_input, GROUP_AXES, axis=0, tiled=True)
    seq_kv = jnp.dot(seq_input, head_kv, preferred_element_type=jnp.float32)
    seq_cos, seq_sin = rope_tables(jnp.arange(seq_length, dtype=jnp.int32), HEAD)
    seq_pair = jnp.concatenate(
        [
            rotate(seq_kv[:, :head_cols].reshape(seq_length, local_heads, HEAD), seq_cos, seq_sin)
            .reshape(seq_length, head_cols)
            .astype(jnp.bfloat16),
            seq_kv[:, head_cols:].astype(jnp.bfloat16),
        ],
        axis=1,
    )
    all_pairs = lax.all_to_all(
        jnp.broadcast_to(seq_pair[None], (groups,) + seq_pair.shape),
        "grp",
        split_axis=0,
        concat_axis=0,
        tiled=True,
    ).reshape(groups * seq_length, 2 * head_cols)
    seq_keys = all_pairs[:, :head_cols].reshape(sequences, seq_length, local_heads, HEAD)
    seq_values = all_pairs[:, head_cols:].reshape(sequences, seq_length, local_heads, HEAD)
    attn_places, attn_kept, attn_token, attn_valid = slot_table(own_attn, token_order, slot_cap)
    mlp_places, mlp_kept, mlp_token, mlp_valid = slot_table(own_mlp, own_rank, slot_cap)
    block_routes = routes_all.reshape(devices, own_rows, TOPK)
    dest_tables = jax.vmap(lambda block_ids: slot_table(block_ids, token_order, slot_cap)[2])(
        block_routes
    )
    dest_token = jnp.take(dest_tables, my_expert, axis=1)
    attn_rows = dispatch(pick_slots(attn_input, attn_token, attn_valid))
    queries = to_gj(jnp.dot(attn_rows, query_weight, preferred_element_type=jnp.float32))
    slot_positions = (
        (jnp.arange(devices, dtype=jnp.int32)[:, None] * own_rows + dest_token) % seq_length
    ).reshape(slot_rows)
    slot_cos, slot_sin = rope_tables(slot_positions, HEAD)
    rotated = rotate(queries.reshape(slot_rows, local_heads, HEAD), slot_cos, slot_sin).astype(
        jnp.bfloat16
    )
    seq_queries = rotated.reshape(sequences, seq_rows, local_heads, HEAD)
    query_blocks = (slot_positions // BLOCK).reshape(sequences, seq_rows)
    key_blocks = jnp.arange(seq_length, dtype=jnp.int32) // BLOCK

    attn_mixed, log_totals = attn_fwd(
        seq_queries.reshape(sequences, seq_rows, HEAD),
        seq_keys.reshape(sequences, seq_length, HEAD),
        seq_values.reshape(sequences, seq_length, HEAD),
        query_blocks[:, :, None],
    )
    mixed_rows = to_jg(attn_mixed.reshape(slot_rows, head_cols))
    output_stack = lax.all_gather(output_weight, GROUP_AXES, axis=0, tiled=True)
    attn_slots = to_owners(
        jnp.dot(to_rows(mixed_rows), output_stack, preferred_element_type=jnp.float32)
    )
    attn_gates = pair_gates(attn_logits, own_attn)
    attn_index, attn_pair_kept = pair_index(own_attn, attn_places, attn_kept, slot_cap)
    attn_picked = attn_slots.reshape(EXPERTS * slot_cap, width)[attn_index]
    hidden_state = own_input + jnp.sum(
        attn_picked * (attn_gates * attn_pair_kept)[:, :, None], axis=1
    )
    inverse_two = lax.rsqrt(jnp.mean(hidden_state * hidden_state, axis=-1, keepdims=True) + epsilon)
    normed_two = hidden_state * inverse_two
    mlp_input = (normed_two * gain_two.astype(jnp.float32)).astype(jnp.bfloat16)
    mlp_logits = jnp.dot(mlp_input, router_two, preferred_element_type=jnp.float32)
    mlp_gates = pair_gates(mlp_logits, own_mlp)
    mlp_index, mlp_pair_kept = pair_index(own_mlp, mlp_places, mlp_kept, slot_cap)
    mlp_slot_grad = (
        own_cotangent[mlp_token]
        * slot_gates(mlp_gates, mlp_pair_kept, own_mlp, mlp_token, mlp_valid)[:, :, None]
    ).astype(jnp.bfloat16)
    mlp_by_group = lax.all_to_all(
        jnp.concatenate([pick_slots(mlp_input, mlp_token, mlp_valid), mlp_slot_grad], axis=1),
        "grp",
        split_axis=0,
        concat_axis=0,
        tiled=True,
    )
    mlp_rows = lax.all_gather(
        mlp_by_group[:, :slot_cap].reshape(groups * slot_cap, width),
        GROUP_AXES,
        axis=0,
        tiled=True,
    )
    down_rows = lax.all_gather(
        mlp_by_group[:, slot_cap:].reshape(groups * slot_cap, width),
        GROUP_AXES,
        axis=0,
        tiled=True,
    )
    gate_pre = jnp.dot(mlp_rows, gate_weight, preferred_element_type=jnp.float32)
    up_pre = jnp.dot(mlp_rows, up_weight, preferred_element_type=jnp.float32)
    activated = jax.nn.silu(gate_pre)
    inner_rows = (activated * up_pre).astype(jnp.bfloat16)
    mlp_partial = jnp.dot(inner_rows, down_weight, preferred_element_type=jnp.float32)
    mlp_slots = combine_scattered(mlp_partial)
    query_stack = lax.all_gather(query_weight, GROUP_AXES, axis=1, tiled=True)
    mlp_slots, query_stack = lax.optimization_barrier((mlp_slots, query_stack))
    mlp_picked = mlp_slots.reshape(EXPERTS * slot_cap, width)[mlp_index]
    own_output = hidden_state + jnp.sum(
        mlp_picked * (mlp_gates * mlp_pair_kept)[:, :, None], axis=1
    )
    mlp_gate_grad = jnp.sum(mlp_picked * own_cotangent[:, None, :], axis=-1) * mlp_pair_kept
    mlp_logit_grad = gates_back(mlp_gates, mlp_gate_grad, own_mlp)
    inner_grad = jnp.einsum("rd,fd->rf", down_rows, down_weight, preferred_element_type=jnp.float32)
    down_grad = jnp.einsum("rf,rd->fd", inner_rows, down_rows, preferred_element_type=jnp.float32)
    sigmoid_gate = jax.nn.sigmoid(gate_pre)
    gate_pre_grad = (
        inner_grad * up_pre * sigmoid_gate * (1.0 + gate_pre * (1.0 - sigmoid_gate))
    ).astype(jnp.bfloat16)
    up_pre_grad = (inner_grad * activated).astype(jnp.bfloat16)
    gate_grad = jnp.einsum("rd,rf->df", mlp_rows, gate_pre_grad, preferred_element_type=jnp.float32)
    up_grad = jnp.einsum("rd,rf->df", mlp_rows, up_pre_grad, preferred_element_type=jnp.float32)
    row_grad = jnp.einsum(
        "rf,df->rd", gate_pre_grad, gate_weight, preferred_element_type=jnp.float32
    ) + jnp.einsum("rf,df->rd", up_pre_grad, up_weight, preferred_element_type=jnp.float32)
    mlp_row_grad = combine(row_grad)
    mlp_input_grad = jnp.sum(
        mlp_row_grad.reshape(EXPERTS * slot_cap, width)[mlp_index] * mlp_pair_kept[:, :, None],
        axis=1,
    )
    mlp_input_grad = mlp_input_grad + jnp.dot(
        mlp_logit_grad, router_two.astype(jnp.float32).T, precision=lax.Precision.HIGHEST
    )
    mlp_router_own = jnp.dot(
        mlp_input.astype(jnp.float32).T, mlp_logit_grad, precision=lax.Precision.HIGHEST
    )
    hidden_grad, gain_two_own = norm_back(
        mlp_input_grad, gain_two.astype(jnp.float32), normed_two, inverse_two
    )
    hidden_grad = hidden_grad + own_cotangent
    attn_gate_grad = jnp.sum(attn_picked * hidden_grad[:, None, :], axis=-1) * attn_pair_kept
    attn_logit_grad = gates_back(attn_gates, attn_gate_grad, own_attn)
    attn_slot_grad = (
        hidden_grad[attn_token]
        * slot_gates(attn_gates, attn_pair_kept, own_attn, attn_token, attn_valid)[:, :, None]
    ).astype(jnp.bfloat16)
    out_rows = dispatch(attn_slot_grad)
    output_grad = jnp.einsum("rw,rd->wd", mixed_rows, out_rows, preferred_element_type=jnp.float32)
    mixed_grad = jnp.einsum(
        "rd,wd->rw", out_rows, output_weight, preferred_element_type=jnp.float32
    ).astype(jnp.bfloat16)
    seq_mixed_grad = to_gj(mixed_grad).reshape(sequences, seq_rows, local_heads, HEAD)

    seq_query_grad, seq_pair_back = attn_bwd(
        seq_queries.reshape(sequences, seq_rows, HEAD),
        seq_keys.reshape(sequences, seq_length, HEAD),
        seq_values.reshape(sequences, seq_length, HEAD),
        query_blocks[:, :, None],
        log_totals,
        seq_mixed_grad.reshape(sequences, seq_rows, HEAD),
    )
    query_rot_grad = to_jg(
        rotate_back(seq_query_grad.reshape(slot_rows, local_heads, HEAD), slot_cos, slot_sin)
        .reshape(slot_rows, head_cols)
        .astype(jnp.bfloat16)
    )
    query_grad = jnp.einsum(
        "rd,rw->dw", attn_rows, query_rot_grad, preferred_element_type=jnp.float32
    )
    attn_row_grad = to_owners(
        jnp.einsum(
            "rw,dw->rd", to_rows(query_rot_grad), query_stack, preferred_element_type=jnp.float32
        )
    )
    pair_back = lax.all_to_all(
        seq_pair_back,
        "grp",
        split_axis=0,
        concat_axis=0,
        tiled=True,
    )
    seq_pair_grad = jnp.sum(pair_back.astype(jnp.float32), axis=0)
    kv_col_grad = jnp.concatenate(
        [
            rotate_back(
                seq_pair_grad[:, :head_cols].reshape(seq_length, local_heads, HEAD),
                seq_cos,
                seq_sin,
            ).reshape(seq_length, head_cols),
            seq_pair_grad[:, head_cols:],
        ],
        axis=1,
    ).astype(jnp.bfloat16)
    kv_col_weight = jnp.einsum(
        "rd,rc->dc", seq_input, kv_col_grad, preferred_element_type=jnp.float32
    )
    kv_input_parts = lax.all_to_all(
        jnp.einsum("rc,dc->rd", kv_col_grad, head_kv, preferred_element_type=jnp.float32)
        .astype(jnp.bfloat16)
        .reshape(group_size, own_rows, width),
        GROUP_AXES,
        split_axis=0,
        concat_axis=0,
        tiled=True,
    )
    attn_input_grad = jnp.sum(
        attn_row_grad.reshape(EXPERTS * slot_cap, width)[attn_index] * attn_pair_kept[:, :, None],
        axis=1,
    )
    attn_input_grad = attn_input_grad + jnp.sum(kv_input_parts.astype(jnp.float32), axis=0)
    attn_input_grad = attn_input_grad + jnp.dot(
        attn_logit_grad, router_one.astype(jnp.float32).T, precision=lax.Precision.HIGHEST
    )
    attn_router_own = jnp.dot(
        attn_input.astype(jnp.float32).T, attn_logit_grad, precision=lax.Precision.HIGHEST
    )
    input_grad, gain_one_own = norm_back(
        attn_input_grad, gain_one.astype(jnp.float32), normed_one, inverse_one
    )
    input_grad = input_grad + hidden_grad
    grad_extras = jnp.concatenate(
        [gain_one_own[:, None], gain_two_own[:, None], attn_router_own, mlp_router_own], axis=1
    )
    packed_grad = jnp.concatenate(
        [
            kv_col_weight,
            jnp.pad(grad_extras, ((0, 0), (0, extra_pad - grad_extras.shape[1]))),
        ],
        axis=1,
    )
    group_sum = lax.psum_scatter(packed_grad, "grp", scatter_dimension=0, tiled=True)
    dealt = lax.all_to_all(
        group_sum.reshape(group_size, kv_rows, pair_cols + extra_pad),
        GROUP_AXES,
        split_axis=0,
        concat_axis=0,
        tiled=True,
    )
    kv_grad = jnp.transpose(
        dealt[:, :, :pair_cols].reshape(group_size, kv_rows, 2, head_cols), (1, 2, 0, 3)
    ).reshape(kv_rows, kv_width)
    extra_grad = jnp.sum(dealt[:, :, pair_cols:], axis=0)
    gain_one_grad = extra_grad[:, 0]
    gain_two_grad = extra_grad[:, 1]
    attn_router_grad = extra_grad[:, 2 : 2 + EXPERTS]
    mlp_router_grad = extra_grad[:, 2 + EXPERTS : 2 + 2 * EXPERTS]
    both_own = jnp.concatenate(
        [own_output.astype(jnp.bfloat16), input_grad.astype(jnp.bfloat16)], axis=1
    )
    both_full = lax.all_to_all(
        jnp.broadcast_to(both_own[None], (halves,) + both_own.shape),
        "expert",
        split_axis=0,
        concat_axis=0,
        tiled=True,
    ).reshape(halves * own_rows, 2 * width)
    mixed_full, input_full = both_full[:, :width], both_full[:, width:]
    return (
        mixed_full,
        input_full,
        gain_one_grad,
        kv_grad,
        attn_router_grad,
        query_grad,
        output_grad,
        gain_two_grad,
        mlp_router_grad,
        gate_grad,
        up_grad,
        down_grad,
    )


def solution(mesh):
    seq_size, halves = mesh.devices.shape
    grouped = jax.sharding.Mesh(
        mesh.devices.reshape(EXPERTS, seq_size // EXPERTS, halves), ALL_AXES
    )
    return jax.shard_map(
        shards,
        mesh=grouped,
        in_specs=(
            P(SEQ_AXES, None),
            P(ALL_AXES),
            P(ALL_AXES, None),
            P(ALL_AXES, None),
            P(None, ALL_AXES),
            P(ALL_AXES, None),
            P(ALL_AXES),
            P(ALL_AXES, None),
            P(None, ALL_AXES),
            P(None, ALL_AXES),
            P(ALL_AXES, None),
            P(SEQ_AXES, None),
            P(SEQ_AXES, None),
            P(SEQ_AXES, None),
            P(SEQ_AXES, None),
        ),
        out_specs=(
            P(SEQ_AXES, None),
            P(SEQ_AXES, None),
            P(ALL_AXES),
            P(ALL_AXES, None),
            P(ALL_AXES, None),
            P(None, ALL_AXES),
            P(ALL_AXES, None),
            P(ALL_AXES),
            P(ALL_AXES, None),
            P(None, ALL_AXES),
            P(None, ALL_AXES),
            P(ALL_AXES, None),
        ),
        check_vma=False,
    )
```
